32 devices in a mesh: seq: 8 (over z, y), shard: 4 (over x, core).
Axes of the slice: x: 2, y: 2, z: 4, core: 2. Of those that a mesh axis runs over, the one named last changes fastest.
Arguments:
- tokens: bfloat16 [4, 2048, 512], P('shard', 'seq'), may hold values from -6 to 6
- cotangent: bfloat16 [4, 2048, 512], P('shard', 'seq'), may hold values from -6 to 6
- positions: int32 [4, 2048], P('shard'), may hold values from 0 to 2047, as said below
- lengths: int32 [4, 4], P('shard'), may hold values from 1 to 1952, as said below
- mixer_gain: float32 [512], P('shard'), may hold values from 0.5 to 1.5
- input_weight: float32 [512, 2048], P(None, 'shard'), may hold values from -0.25 to 0.25
- kernel_weight: float32 [4, 1024], P(None, 'shard'), may hold values from -3 to 3
- kernel_bias: float32 [1024], P('shard'), may hold values from -3 to 3
- select_weight: float32 [1024, 64], P('shard'), may hold values from -0.1875 to 0.1875
- step_weight: float32 [32, 1024], P(None, 'shard'), may hold values from -1 to 1
- step_bias: float32 [1024], P('shard'), may hold values from -7 to -3
- decay_log: float32 [1024, 16], P('shard'), may hold values from -2 to 1
- skip_scale: float32 [1024], P('shard'), may hold values from 0.2 to 1.5
- output_weight: float32 [1024, 512], P('shard'), may hold values from -0.1875 to 0.1875
- attention_gain: float32 [512], P('shard'), may hold values from 0.5 to 1.5
- heads_weight: float32 [512, 1536], P(None, 'shard'), may hold values from -0.25 to 0.25
- merge_weight: float32 [512, 512], P('shard'), may hold values from -4 to 4
Outputs:
- output: bfloat16 [4, 2048, 512], P('shard', 'seq')
- token_grad: float32 [4, 2048, 512], P('shard', 'seq')
- mixer_gain_grad: float32 [512], P('shard')
- input_weight_grad: float32 [512, 2048], P(None, 'shard')
- kernel_weight_grad: float32 [4, 1024], P(None, 'shard')
- kernel_bias_grad: float32 [1024], P('shard')
- select_weight_grad: float32 [1024, 64], P('shard')
- step_weight_grad: float32 [32, 1024], P(None, 'shard')
- step_bias_grad: float32 [1024], P('shard')
- decay_log_grad: float32 [1024, 16], P('shard')
- skip_scale_grad: float32 [1024], P('shard')
- output_weight_grad: float32 [1024, 512], P('shard')
- attention_gain_grad: float32 [512], P('shard')
- heads_weight_grad: float32 [512, 1536], P(None, 'shard')
- merge_weight_grad: float32 [512, 512], P('shard')
The draws below stay inside these ranges and needn't reach their ends.
Inputs may be any that keep to these rules, and one draw needn't show every extreme that they name: Each row is a permutation of the positions of its group; rows j * 256 + i * 32 to j * 256 + (i + 1) * 32 - 1 hold positions of i * 256 to (i + 1) * 256 - 1, for every i and j below 8. `lengths`: each row sums to 2048; all entries but one are at most 64; the remaining one, at a place drawn from the seed, equals the stated maximum, so that it starts among the group's first 256 positions and ends among its last 256.
All inputs are finite; a program needn't handle non-finite values.
Results may differ from the reference program's by a relative error of at most 0.028.
Values may be sent and summed in bfloat16 or wider, within the bound.
A program may use at most 256 MiB of HBM per device.

```python
import math
import jax
import jax.numpy as jnp
from jax import lax

D = 512
DI = 1024
RANK = 32
HEADS = 8
STATE = 16
HEAD_DIM = 64
CONV = 4
SCAN_BLOCK = 16
NSEQ = 4
TOK_DEV = 256
SPANS = 8
GROUPS = 4
GROUP_TOK = 2048
SHARE = 32


def draw_positions(key, part):

    def one_group(group_key):
        base = jnp.broadcast_to(jnp.arange(TOK_DEV, dtype=jnp.int32)[None, :], (SPANS, TOK_DEV))
        mixed = jax.random.permutation(group_key, base, axis=1, independent=True)
        mixed = mixed + (jnp.arange(SPANS, dtype=jnp.int32) * TOK_DEV)[:, None]
        blocks = mixed.reshape(SPANS, SPANS, SHARE)
        return jnp.transpose(blocks, (1, 0, 2)).reshape(GROUP_TOK)
    return jax.vmap(one_group)(jax.random.split(key, GROUPS))


def draw_lengths(key, part):

    def one_group(group_key):
        pick_key, size_key = jax.random.split(group_key)
        half_share = TOK_DEV // NSEQ // 2
        extra = jax.random.randint(size_key, (NSEQ - 1,), 0, half_share // 2 + 1, dtype=jnp.int32)
        shorts = half_share + extra - jnp.roll(extra, 1)
        longest = jax.random.randint(pick_key, (), 0, NSEQ, dtype=jnp.int32)
        slots = jnp.arange(NSEQ, dtype=jnp.int32)
        is_long = slots == longest
        order = jnp.clip(slots - (slots > longest).astype(jnp.int32), 0, NSEQ - 2)
        picked = jnp.sum((order[:, None] == jnp.arange(NSEQ - 1, dtype=jnp.int32)[None, :]).astype(jnp.int32) * shorts[None, :], axis=1)
        remaining = GROUP_TOK - (NSEQ - 1) * half_share
        return jnp.where(is_long, remaining, picked).astype(jnp.int32)
    return jax.vmap(one_group)(jax.random.split(key, GROUPS))


def block_levels(key, extent, pieces, low, largest):
    def one(dim, blocks):
        heights = jax.random.uniform(jax.random.fold_in(jax.random.fold_in(key, 6), dim), (blocks,), jnp.float32, low / len(pieces), largest / len(pieces))
        return jnp.repeat(jnp.exp(heights), extent[dim] // blocks).reshape((-1,) + (1,) * (len(extent) - dim - 1))

    level = one(*pieces[0])
    for cut in pieces[1:]:
        level = level * one(*cut)
    return level


def bell_draw(own_key, extent, width, limit, cuts=(), kind=jnp.bfloat16):
    values = width * jax.random.normal(own_key, extent, jnp.float32)
    if cuts:
        values = values * block_levels(own_key, extent, cuts, -0.22, 0.18)
    return jnp.clip(values, -limit, limit).astype(kind)


def setup_inputs(seed: int = 0) -> dict:
    splits = jax.random.split(jax.random.key(seed), 18)
    tokens = bell_draw(splits[0], (GROUPS, GROUP_TOK, D), 1.0, 6.0, ((0, 4), (1, 8)))
    cotangent = bell_draw(splits[1], (GROUPS, GROUP_TOK, D), 1.0, 6.0, ((0, 4), (1, 8)))
    positions = draw_positions(jax.random.fold_in(splits[17], 71), 0)
    lengths = draw_lengths(jax.random.fold_in(splits[17], 71), 0)
    mixer_gain = jnp.clip(1.0 + 0.1 * jax.random.normal(splits[4], (D,), jnp.float32), 0.5, 1.5)
    input_weight = bell_draw(splits[5], (D, 2 * DI), D ** -0.5, 0.25, ((1, 4),), jnp.float32)
    kernel_weight = bell_draw(splits[6], (CONV, DI), CONV ** -0.5, 3.0, ((1, 4),), jnp.float32)
    kernel_bias = bell_draw(splits[7], (DI,), 0.5, 3.0, ((0, 4),), jnp.float32)
    select_weight = bell_draw(splits[8], (DI, RANK + 2 * STATE), DI ** -0.5, 0.1875, ((0, 4),), jnp.float32)
    step_weight = bell_draw(splits[9], (RANK, DI), RANK ** -0.5, 1.0, ((1, 4),), jnp.float32)
    step_bias = jnp.clip(-7.0 + 4.0 * jax.random.uniform(splits[10], (DI,), jnp.float32) ** block_levels(splits[10], (DI,), ((0, 4),), -0.2, 0.2), -7.0, -3.0)
    decay_log = jnp.clip(-2.0 + 3.0 * jax.random.uniform(splits[11], (DI, STATE), jnp.float32) ** block_levels(splits[11], (DI, STATE), ((0, 4),), -0.2, 0.2), -2.0, 1.0)
    skip_scale = jnp.clip(0.2 + 1.3 * jax.random.uniform(splits[12], (DI,), jnp.float32) ** block_levels(splits[12], (DI,), ((0, 4),), -0.2, 0.2), 0.2, 1.5)
    output_weight = bell_draw(splits[13], (DI, D), DI ** -0.5, 0.1875, ((0, 4),), jnp.float32)
    attention_gain = jnp.clip(1.0 + 0.1 * jax.random.normal(splits[14], (D,), jnp.float32), 0.5, 1.5)
    heads_weight = bell_draw(splits[15], (D, 3 * D), D ** -0.5, 0.25, ((1, 4),), jnp.float32)
    merge_weight = bell_draw(splits[16], (D, D), 2 ** -0.5, 4.0, ((0, 4),), jnp.float32)
    return {"tokens": tokens, "cotangent": cotangent, "positions": positions, "lengths": lengths, "mixer_gain": mixer_gain, "input_weight": input_weight, "kernel_weight": kernel_weight, "kernel_bias": kernel_bias, "select_weight": select_weight, "step_weight": step_weight, "step_bias": step_bias, "decay_log": decay_log, "skip_scale": skip_scale, "output_weight": output_weight, "attention_gain": attention_gain, "heads_weight": heads_weight, "merge_weight": merge_weight}


@jax.custom_vjp
def low(v):
    return lax.optimization_barrier(v.astype(jnp.bfloat16)).astype(jnp.float32)

@jax.custom_vjp
def low_back(v):
    return v

def low_keep(v):
    return (low(v), None)

def low_pass(kept, grad):
    return (grad,)

def back_keep(v):
    return (v, None)

def back_low(kept, grad):
    return (low(grad),)
low.defvjp(low_keep, low_pass)
low_back.defvjp(back_keep, back_low)
EPS = 1e-05
NEG = -1e+30

def matmul(left, right):
    return jnp.dot(left, right, precision=lax.Precision.HIGHEST, preferred_element_type=jnp.float32)

def rms_norm(value, gain):
    inverse = lax.rsqrt(lax.optimization_barrier(jnp.mean(value * value, axis=-1, keepdims=True)) + EPS)
    return value * inverse * gain

def segment_info(lengths, places):
    ends = jnp.cumsum(lengths)
    starts = ends - lengths
    segment = lax.optimization_barrier(jnp.sum((places[:, None] >= ends[None, :]).astype(jnp.int32), axis=1))
    begin = lax.optimization_barrier(jnp.sum((places[:, None] == starts[None, :]).astype(jnp.int32), axis=1))
    return (segment, begin)

def state_scan(amat, initial, delta, drive, bmat, cmat, keep):
    total_rows = delta.shape[0]
    blocks = total_rows // SCAN_BLOCK

    def one_block(state_now, inputs):
        block_delta, block_drive, block_b, block_c, block_keep = inputs
        outputs = []
        for offset in range(SCAN_BLOCK):
            decay_now = jnp.exp(block_delta[offset][:, None] * amat) * block_keep[offset]
            state_now = decay_now * state_now + (block_delta[offset] * block_drive[offset])[:, None] * block_b[offset][None, :]
            outputs.append(lax.optimization_barrier(jnp.sum(state_now * block_c[offset][None, :], axis=1)))
        return (state_now, jnp.stack(outputs))
    shaped = tuple((member.reshape((blocks, SCAN_BLOCK) + member.shape[1:]) for member in (delta, drive, bmat, cmat, keep)))
    final_state, outputs = lax.scan(jax.checkpoint(one_block), initial, shaped)
    return (outputs.reshape(total_rows, delta.shape[1]), final_state)

def attention(qkv, segment):
    total_rows = qkv.shape[0]
    block_rows = math.gcd(total_rows, 512)
    blocks = total_rows // block_rows
    queries = qkv[:, :D].reshape(total_rows, HEADS, HEAD_DIM)
    key_rows = qkv[:, D:2 * D].reshape(total_rows, HEADS, HEAD_DIM)
    value_rows = qkv[:, 2 * D:].reshape(total_rows, HEADS, HEAD_DIM)
    places = jnp.arange(total_rows, dtype=jnp.int32)
    score_scale = 1.0 / math.sqrt(HEAD_DIM)

    def one_block(inputs):
        block_q, block_pos, block_seg = inputs
        raw_score = low_back(jnp.einsum('qhd,khd->hqk', block_q, key_rows, precision=lax.Precision.HIGHEST) * score_scale)
        allowed = ((places[None, :] <= block_pos[:, None]) & (segment[None, :] == block_seg[:, None]))[None]
        masked = jnp.where(allowed, raw_score, NEG)
        row_max = lax.optimization_barrier(jnp.max(masked, axis=-1, keepdims=True))
        exp_rows = jnp.exp(masked - row_max) * allowed.astype(jnp.float32)
        prob_rows = low(exp_rows / lax.optimization_barrier(jnp.sum(exp_rows, axis=-1, keepdims=True)))
        return low_back(low(jnp.einsum('hqk,khd->qhd', prob_rows, value_rows, precision=lax.Precision.HIGHEST)))
    shaped = (queries.reshape(blocks, block_rows, HEADS, HEAD_DIM), places.reshape(blocks, block_rows), segment.reshape(blocks, block_rows))
    context = lax.map(jax.checkpoint(one_block), shaped)
    return context.reshape(total_rows, D)

def layer(inputs, weights, segment, begin):
    gain_first, input_full, kernel_full, kernel_offset, select_full, step_full, step_offset, decay_full, skip_full, output_full, gain_second, heads_full, merge_full = tuple((low(member) for member in weights))
    total_rows = inputs.shape[0]
    xn1 = low(rms_norm(inputs, gain_first))
    xz = low_back(matmul(xn1, input_full))
    xin = xz[:, :DI]
    zgate = xz[:, DI:]
    conv_pre = kernel_offset + jnp.zeros_like(xin)
    for offset in range(CONV):
        lagged = CONV - 1 - offset
        shifted = jnp.concatenate([jnp.zeros((lagged, DI), jnp.float32), xin[:total_rows - lagged]], axis=0)
        prior = jnp.concatenate([jnp.full((lagged,), -1, jnp.int32), segment[:total_rows - lagged]], axis=0)
        conv_pre = conv_pre + kernel_full[offset] * shifted * (prior == segment).astype(jnp.float32)[:, None]
    u_value = low(jax.nn.silu(conv_pre))
    xdbl = low_back(matmul(u_value, select_full))
    step_low = low(xdbl[:, :RANK])
    bmat = xdbl[:, RANK:RANK + STATE]
    cmat = xdbl[:, RANK + STATE:]
    delta = jax.nn.softplus(low_back(matmul(step_low, step_full) + step_offset))
    amat = -jnp.exp(decay_full)
    keep = (1 - begin).astype(jnp.float32)
    ys, _ = state_scan(amat, jnp.zeros((DI, STATE), jnp.float32), delta, u_value, bmat, cmat, keep)
    gated = low_back(low((ys + skip_full * u_value) * jax.nn.silu(zgate)))
    x_one = inputs + low_back(matmul(gated, output_full))
    xn2 = low(rms_norm(x_one, gain_second))
    qkv = low_back(low(matmul(xn2, heads_full)))
    context = attention(qkv, segment)
    return x_one + low_back(matmul(context, merge_full))

def reference(tokens, cotangent, positions, lengths, mixer_gain, input_weight, kernel_weight, kernel_bias, select_weight, step_weight, step_bias, decay_log, skip_scale, output_weight, attention_gain, heads_weight, merge_weight):
    params = (mixer_gain, input_weight, kernel_weight, kernel_bias, select_weight, step_weight, step_bias, decay_log, skip_scale, output_weight, attention_gain, heads_weight, merge_weight)
    places = jnp.arange(GROUP_TOK, dtype=jnp.int32)

    def one_group(totals, group):
        group_tokens, group_cot, group_pos, group_len = group
        segment, begin = segment_info(group_len, places)

        def given_order(inputs, weights):
            return layer(inputs, weights, segment, begin)[group_pos]
        result, pull = jax.vjp(given_order, group_tokens.astype(jnp.float32), params)
        input_grad, weight_grads = pull(group_cot.astype(jnp.float32))
        totals = tuple((before + added for before, added in zip(totals, weight_grads)))
        return (totals, (result.astype(jnp.bfloat16), input_grad))
    zeros = tuple((jnp.zeros_like(member) for member in params))
    totals, (output, token_grad) = lax.scan(one_group, zeros, (tokens, cotangent, positions, lengths))
    return (output, token_grad, totals[0], totals[1], totals[2], totals[3], totals[4], totals[5], totals[6], totals[7], totals[8], totals[9], totals[10], totals[11], totals[12])
```

```python
import functools
import math

import jax
import jax.numpy as jnp
from jax import lax
from jax.experimental import pallas as pl
from jax.experimental.pallas import tpu as pltpu
from jax.sharding import PartitionSpec as P

D = 512
DI = 1024
RANK = 32
HEADS = 8
STATE = 16
HEAD_DIM = 64
CONV = 4
CHUNKS = 8
LANES = 128
GROUPS_CH = DI // LANES
EDGE = (CONV - 1) * CHUNKS

SEL = 0
STEP = RANK + 2 * STATE
DEC = STEP + RANK
TAPS = DEC + STATE
BIAS = TAPS + CONV
STEPB = BIAS + 1
SKIP = STEPB + 1
GAINS = SKIP + 1
PACK = 128

EPS = 1e-05
NEG = -1e30
CUT = 1e30
F32 = jnp.float32
BF16 = jnp.bfloat16

VMEM = pl.BlockSpec(memory_space=pltpu.VMEM)
SMEM = pl.BlockSpec(memory_space=pltpu.SMEM)


def params(**more):
    return pltpu.CompilerParams(vmem_limit_bytes=56 << 20, **more)


def dot_nn(left, right):
    return lax.dot_general(left, right, (((1,), (0,)), ((), ())), preferred_element_type=F32)


def dot_nt(left, right):
    return lax.dot_general(left, right, (((1,), (1,)), ((), ())), preferred_element_type=F32)


def dot_tn(left, right):
    return lax.dot_general(left, right, (((0,), (0,)), ((), ())), preferred_element_type=F32)


def row_places(rows, steps):
    return (rows & (CHUNKS - 1)) * steps + (rows >> 3)


def starts_of(lengths_ref, nseq):
    starts = [jnp.int32(0)]
    for k in range(nseq - 1):
        starts.append(starts[-1] + lengths_ref[k])
    return starts


def start_of(places, starts):
    first = jnp.zeros_like(places)
    for start in starts[1:]:
        first = jnp.where(places >= start, start, first)
    return first


def begin_of(places, starts):
    found = places == starts[0]
    for start in starts[1:]:
        found = found | (places == start)
    return found


def norm(value):
    return lax.rsqrt(jnp.mean(value * value, axis=-1, keepdims=True) + EPS)


def silu_slope(value):
    s = jax.nn.sigmoid(value)
    return s * (1.0 + value * (1.0 - s))


def tile(step):
    return pl.ds(pl.multiple_of(step * CHUNKS, CHUNKS), CHUNKS)


def lanes_of(group):
    return pl.ds(pl.multiple_of(group * LANES, LANES), LANES)


def spread_decay(packed_ref, amat_ref, spread_ref):
    amat = -jnp.exp(packed_ref[DEC : DEC + STATE, :].astype(F32))
    amat_ref[...] = amat
    for st in range(STATE):
        spread_ref[st * CHUNKS : (st + 1) * CHUNKS, :] = jnp.broadcast_to(
            amat[st : st + 1, :], (CHUNKS, DI)
        )


def spread_columns(source_ref, first, target_ref, steps):
    def one(step, carry):
        values = source_ref[tile(step), :]
        base = step * (STATE * CHUNKS)
        for st in range(STATE):
            at = pl.ds(pl.multiple_of(base + st * CHUNKS, CHUNKS), CHUNKS)
            column = values[:, first + st : first + st + 1]
            target_ref[at, :] = jnp.broadcast_to(column, (CHUNKS, LANES))
        return carry

    lax.fori_loop(0, steps, one, 0)


def state_at(step, st):
    return pl.ds(pl.multiple_of(step * (STATE * CHUNKS) + st * CHUNKS, CHUNKS), CHUNKS)


def exponent_steps(delta_ref, lengths_ref, my, nseq, target_ref, steps):
    starts = starts_of(lengths_ref, nseq)
    total = steps * CHUNKS

    def one(step, carry):
        rows = lax.broadcasted_iota(jnp.int32, (CHUNKS, 1), 0) * steps + step + my * total
        target_ref[tile(step), :] = jnp.where(
            begin_of(rows, starts), CUT, delta_ref[tile(step), :]
        )
        return carry

    lax.fori_loop(0, steps, one, 0)


def first_kernel(
    steps,
    nseq,
    lengths_ref,
    my_ref,
    tokens_ref,
    edge_ref,
    wi_ref,
    packed_ref,
    gains_ref,
    ext_ref,
    zgate_ref,
    conv_ref,
    u_ref,
    delta_ref,
    xdbl_ref,
    ends_ref,
    totals_ref,
    send_ref,
    cut_ref,
    du_ref,
    bx_ref,
    amat_ref,
    spread_ref,
):
    my = my_ref[0]
    rows = steps * CHUNKS
    starts = starts_of(lengths_ref, nseq)
    gain = gains_ref[0:1, :].astype(F32)
    x = tokens_ref[...].astype(F32)
    xn1 = (x * norm(x) * gain).astype(BF16)
    before = edge_ref[...].astype(F32)
    edge_n = (before * norm(before) * gain).astype(BF16)
    ext_ref[EDGE:, :] = dot_nt(xn1, wi_ref[0:DI, :])
    zgate_ref[...] = dot_nt(xn1, wi_ref[DI:, :])
    edge_x = dot_nt(edge_n, wi_ref[0:DI, :])
    count = edge_ref.shape[0]
    chunk = lax.broadcasted_iota(jnp.int32, (CHUNKS, DI), 0)
    for k in range(CONV - 1):
        late = (steps - CONV + 1 + k) * CHUNKS + EDGE
        moved = pltpu.roll(ext_ref[late : late + CHUNKS, :], 1, 0)
        at = count - CONV + 1 + k
        ext_ref[k * CHUNKS : (k + 1) * CHUNKS, :] = jnp.where(
            chunk == 0, jnp.broadcast_to(edge_x[at : at + 1, :], (CHUNKS, DI)), moved
        )
    small = packed_ref[DEC:PACK, :].astype(F32)
    taps = small[TAPS - DEC : TAPS - DEC + CONV, :]
    bias = small[BIAS - DEC : BIAS - DEC + 1, :]

    def conv_step(step, carry):
        places = lax.broadcasted_iota(jnp.int32, (CHUNKS, 1), 0) * steps + step + my * rows
        first = start_of(places, starts)
        total = jnp.broadcast_to(bias, (CHUNKS, DI))
        for k in range(CONV):
            at = pl.ds(pl.multiple_of((step + k) * CHUNKS, CHUNKS), CHUNKS)
            inside = places - (CONV - 1) + k >= first
            total = total + jnp.where(inside, taps[k : k + 1, :] * ext_ref[at, :], 0.0)
        conv_ref[tile(step), :] = total
        du_ref[tile(step), :] = total * jax.nn.sigmoid(total)
        return carry

    lax.fori_loop(0, steps, conv_step, 0)
    u = du_ref[...].astype(BF16)
    u_ref[...] = u
    xdbl = dot_nt(u, packed_ref[SEL : SEL + STEP, :])
    xdbl_ref[...] = xdbl
    delta_ref[...] = dot_nn(
        xdbl[:, :RANK].astype(BF16), packed_ref[STEP : STEP + RANK, :]
    )
    stepb = small[STEPB - DEC : STEPB - DEC + 1, :]

    def delta_step(step, total):
        places = lax.broadcasted_iota(jnp.int32, (CHUNKS, 1), 0) * steps + step + my * rows
        pre = delta_ref[tile(step), :] + stepb
        delta = jnp.maximum(pre, 0.0) + jnp.log1p(jnp.exp(-jnp.abs(pre)))
        delta_ref[tile(step), :] = delta
        cut = jnp.where(begin_of(places, starts), CUT, delta)
        cut_ref[tile(step), :] = cut
        du_ref[tile(step), :] = delta * du_ref[tile(step), :].astype(BF16).astype(F32)
        return total + cut

    totals_ref[...] = lax.fori_loop(0, steps, delta_step, jnp.zeros((CHUNKS, DI), F32))
    spread_decay(packed_ref, amat_ref, spread_ref)
    spread_columns(xdbl_ref, RANK, bx_ref, steps)

    def group_step(group, carry):
        lanes = lanes_of(group)
        amat = [spread_ref[st * CHUNKS : (st + 1) * CHUNKS, lanes] for st in range(STATE)]

        def step_fn(step, states):
            cut = cut_ref[tile(step), lanes]
            drive = du_ref[tile(step), lanes]
            return tuple(
                jnp.exp(cut * amat[st]) * states[st] + drive * bx_ref[state_at(step, st), :]
                for st in range(STATE)
            )

        states = lax.fori_loop(
            0, steps, step_fn, (jnp.zeros((CHUNKS, LANES), F32),) * STATE
        )
        for st in range(STATE):
            ends_ref[st, :, lanes] = states[st]
        return carry

    lax.fori_loop(0, GROUPS_CH, group_step, 0)
    amat = amat_ref[...]
    state = jnp.zeros((STATE, DI), F32)
    for k in range(CHUNKS):
        state = jnp.exp(amat * totals_ref[k : k + 1, :]) * state + ends_ref[:, k, :]
    send_ref[0:STATE, :] = state
    send_ref[STATE:, :] = jnp.broadcast_to(
        jnp.sum(totals_ref[...], axis=0, keepdims=True), (CHUNKS, DI)
    )


def lane_low(rows):
    return lax.broadcasted_iota(jnp.int32, (rows, LANES), 1) < HEAD_DIM


def pick_rows(index_ref, rows, steps):
    places = row_places(lax.broadcasted_iota(jnp.int32, (rows, 1), 0), steps)
    return (index_ref[...] == places).astype(F32).astype(BF16)


def second_kernel(
    steps,
    nseq,
    spans,
    lengths_ref,
    my_ref,
    tokens_ref,
    packed_ref,
    gains_ref,
    wo_ref,
    wh_ref,
    wm_ref,
    given_ref,
    index_ref,
    states_ref,
    ends_ref,
    totals_ref,
    delta_ref,
    u_ref,
    xdbl_ref,
    zgate_ref,
    yfull_ref,
    gated_ref,
    x1_ref,
    init_ref,
    dout_ref,
    parts_ref,
    cut_ref,
    du_ref,
    bx_ref,
    cx_ref,
    amat_ref,
    spread_ref,
):
    my = my_ref[0]
    rows = steps * CHUNKS
    spread_decay(packed_ref, amat_ref, spread_ref)
    exponent_steps(delta_ref, lengths_ref, my, nseq, cut_ref, steps)
    du_ref[...] = delta_ref[...] * u_ref[...].astype(F32)
    spread_columns(xdbl_ref, RANK, bx_ref, steps)
    spread_columns(xdbl_ref, RANK + STATE, cx_ref, steps)
    amat = amat_ref[...]

    def chain(k, state):
        decay = jnp.exp(amat * states_ref[k, STATE : STATE + 1, :])
        return decay * state + states_ref[k, 0:STATE, :]

    state = lax.fori_loop(0, my, chain, jnp.zeros((STATE, DI), F32))
    for k in range(CHUNKS):
        init_ref[:, k, :] = state
        if k < CHUNKS - 1:
            state = jnp.exp(amat * totals_ref[k : k + 1, :]) * state + ends_ref[:, k, :]

    def group_step(group, carry):
        lanes = lanes_of(group)
        amat_g = [spread_ref[st * CHUNKS : (st + 1) * CHUNKS, lanes] for st in range(STATE)]

        def step_fn(step, states):
            cut = cut_ref[tile(step), lanes]
            drive = du_ref[tile(step), lanes]
            new = tuple(
                jnp.exp(cut * amat_g[st]) * states[st] + drive * bx_ref[state_at(step, st), :]
                for st in range(STATE)
            )
            terms = [new[st] * cx_ref[state_at(step, st), :] for st in range(STATE)]
            while len(terms) > 1:
                terms = [a + b for a, b in zip(terms[::2], terms[1::2])]
            yfull_ref[tile(step), lanes] = terms[0]
            return new

        lax.fori_loop(
            0, steps, step_fn, tuple(init_ref[st, :, lanes] for st in range(STATE))
        )
        return carry

    lax.fori_loop(0, GROUPS_CH, group_step, 0)
    skip = packed_ref[DEC:PACK, :].astype(F32)[SKIP - DEC : SKIP - DEC + 1, :]

    def gate_step(pair, carry):
        at = pl.ds(pl.multiple_of(pair * 2 * CHUNKS, 2 * CHUNKS), 2 * CHUNKS)
        yfull = yfull_ref[at, :] + skip * u_ref[at, :].astype(F32)
        yfull_ref[at, :] = yfull
        gate = zgate_ref[at, :]
        gated_ref[at, :] = (yfull * (gate * jax.nn.sigmoid(gate))).astype(BF16)
        return carry

    lax.fori_loop(0, steps // 2, gate_step, 0)
    x1 = tokens_ref[...].astype(F32) + dot_nn(gated_ref[...], wo_ref[...])
    x1_ref[...] = x1
    xn2 = (x1 * norm(x1) * gains_ref[1:2, :].astype(F32)).astype(BF16)
    dout = dot_nn(pick_rows(index_ref, rows, steps), given_ref[...]).astype(BF16)
    dout_ref[...] = dout
    dcontext = dot_nt(dout, wm_ref[...]).astype(BF16).astype(F32)
    qkv = dot_nt(xn2, wh_ref[...]).astype(BF16).astype(F32)
    low = lane_low(rows)
    scale = 1.0 / math.sqrt(HEAD_DIM)
    ratio = spans // HEADS
    part = rows // ratio
    for pair in range(HEADS // 2):
        at = pair * LANES
        q = qkv[:, at : at + LANES] * scale
        k = qkv[:, D + at : D + at + LANES]
        v = qkv[:, 2 * D + at : 2 * D + at + LANES]
        d = dcontext[:, at : at + LANES]
        for odd in range(2):
            if odd:
                qd = jnp.where(low, pltpu.roll(q, HEAD_DIM, 1), d)
                kv = jnp.where(low, pltpu.roll(k, HEAD_DIM, 1), v)
            else:
                qd = jnp.where(low, q, pltpu.roll(d, HEAD_DIM, 1))
                kv = jnp.where(low, k, pltpu.roll(v, HEAD_DIM, 1))
            qd = qd.astype(BF16)
            kv = kv.astype(BF16)
            for sub in range(ratio):
                to = (2 * pair + odd) * ratio + sub
                parts_ref[to, 0:part, :] = qd[sub * part : (sub + 1) * part, :]
                parts_ref[to, part:, :] = kv


def attention_kernel(
    steps,
    nseq,
    ratio,
    lengths_ref,
    my_ref,
    parts_ref,
    out_ref,
    score_ref,
    dprob_ref,
    dkv_ref,
):
    block = pl.program_id(0)
    spans = pl.num_programs(0)
    rows = steps * CHUNKS
    part = rows // ratio
    sub = lax.rem(my_ref[0], ratio)
    starts = starts_of(lengths_ref, nseq)

    @pl.when(block == 0)
    def _():
        dkv_ref[...] = jnp.zeros_like(dkv_ref)

    qd = parts_ref[block, 0:part, :]
    low = lane_low(part)
    qd_float = qd.astype(F32)
    both = jnp.concatenate(
        [jnp.where(low, qd_float, 0.0), jnp.where(low, 0.0, qd_float)], axis=0
    ).astype(BF16)
    own = lax.broadcasted_iota(jnp.int32, (part, 1), 0) + sub * part
    query = row_places(own, steps) + block * rows
    first = start_of(query, starts)
    key_local = row_places(lax.broadcasted_iota(jnp.int32, (1, rows), 1), steps)

    def scores(at, top):
        kv = parts_ref[at, part:, :]
        joint = dot_nt(both, kv)
        key = key_local + at * rows
        allowed = (key <= query) & (key >= first)
        score = jnp.where(allowed, joint[:part], NEG)
        score_ref[at] = score
        dprob_ref[at] = joint[part:]
        return jnp.maximum(top, jnp.max(score, axis=1, keepdims=True))

    top = lax.fori_loop(0, block + 1, scores, jnp.full((part, 1), NEG, F32))

    def weigh(at, carry):
        total, context = carry
        prob = jnp.exp(score_ref[at] - top)
        score_ref[at] = prob
        context = context + dot_nn(prob.astype(BF16), parts_ref[at, part:, :])
        return (total + jnp.sum(prob, axis=1, keepdims=True), context)

    total, context = lax.fori_loop(
        0,
        block + 1,
        weigh,
        (jnp.zeros((part, 1), F32), jnp.zeros((part, LANES), F32)),
    )
    inverse = 1.0 / total
    context = context * inverse
    datt = jnp.sum(jnp.where(low, 0.0, context * qd_float), axis=1, keepdims=True)
    key_low = lane_low(rows)

    def back(at, dquery):
        prob = score_ref[at] * inverse
        dscore = (prob * (dprob_ref[at] - datt)).astype(BF16)
        dkv_ref[at] += jnp.where(key_low, dot_tn(dscore, qd), dot_tn(prob.astype(BF16), qd))
        return dquery + dot_nn(dscore, parts_ref[at, part:, :])

    dquery = lax.fori_loop(0, block + 1, back, jnp.zeros((part, LANES), F32))
    scale = 1.0 / math.sqrt(HEAD_DIM)
    out_ref[block, 0:part, :] = jnp.where(low, dquery * scale, context).astype(BF16)

    @pl.when(block == spans - 1)
    def _():
        out_ref[:, part:, :] = dkv_ref[...].astype(BF16)


def third_kernel(
    steps,
    nseq,
    spans,
    lengths_ref,
    my_ref,
    parts_ref,
    gains_ref,
    packed_ref,
    wo_ref,
    wh_ref,
    wm_ref,
    index_ref,
    dout_ref,
    x1_ref,
    gated_ref,
    yfull_ref,
    zgate_ref,
    u_ref,
    delta_ref,
    xdbl_ref,
    totals_ref,
    given_ref,
    merge_grad_ref,
    heads_grad_ref,
    output_grad_ref,
    gain_grad_ref,
    dx1_ref,
    dys_ref,
    dzgate_ref,
    skip_grad_ref,
    ends_ref,
    send_ref,
    cut_ref,
    cx_ref,
    amat_ref,
    spread_ref,
):
    my = my_ref[0]
    rows = steps * CHUNKS
    ratio = spans // HEADS
    part = rows // ratio
    low = lane_low(rows)
    contexts, dqs, dks, dvs = [], [], [], []
    for pair in range(HEADS // 2):
        dqc, dkv = [], []
        for odd in range(2):
            base = (2 * pair + odd) * ratio
            dqc.append(
                jnp.concatenate(
                    [parts_ref[base + sub, 0:part, :].astype(F32) for sub in range(ratio)], axis=0
                )
            )
            dkv.append(sum(parts_ref[base + sub, part:, :].astype(F32) for sub in range(ratio)))
        dqs.append(jnp.where(low, dqc[0], pltpu.roll(dqc[1], HEAD_DIM, 1)))
        contexts.append(jnp.where(low, pltpu.roll(dqc[0], HEAD_DIM, 1), dqc[1]))
        dks.append(jnp.where(low, dkv[0], pltpu.roll(dkv[1], HEAD_DIM, 1)))
        dvs.append(jnp.where(low, pltpu.roll(dkv[0], HEAD_DIM, 1), dkv[1]))
    context = jnp.concatenate(contexts, axis=1).astype(BF16)
    dqkv = jnp.concatenate(dqs + dks + dvs, axis=1).astype(BF16)
    x1 = x1_ref[...]
    dout = dout_ref[...]
    x2 = (x1 + dot_nn(context, wm_ref[...])).astype(BF16)
    given_ref[...] = dot_tn(pick_rows(index_ref, rows, steps), x2).astype(BF16)
    merge_grad_ref[...] = dot_tn(context, dout).astype(BF16)
    gain = gains_ref[1:2, :].astype(F32)
    inverse = norm(x1)
    normal = x1 * inverse
    xn2 = (normal * gain).astype(BF16)
    heads_grad_ref[...] = dot_tn(dqkv, xn2).astype(BF16)
    dxn2 = dot_nn(dqkv, wh_ref[...])
    gain_grad_ref[...] = jnp.sum(dxn2 * normal, axis=0, keepdims=True)
    e2 = dxn2 * gain
    dx1 = dout.astype(F32) + inverse * (
        e2 - normal * jnp.mean(e2 * normal, axis=-1, keepdims=True)
    )
    dx1_ref[...] = dx1
    dmixed = dx1.astype(BF16)
    output_grad_ref[...] = dot_tn(gated_ref[...], dmixed).astype(BF16)
    dys_ref[...] = dot_nt(dmixed, wo_ref[...])

    def gate_step(pair, total):
        at = pl.ds(pl.multiple_of(pair * 2 * CHUNKS, 2 * CHUNKS), 2 * CHUNKS)
        dgated = dys_ref[at, :].astype(BF16).astype(F32)
        gate = zgate_ref[at, :]
        s = jax.nn.sigmoid(gate)
        dys = dgated * (gate * s)
        dys_ref[at, :] = dys
        dzgate_ref[at, :] = (dgated * yfull_ref[at, :] * (s * (1.0 + gate * (1.0 - s)))).astype(
            BF16
        )
        return total + dys * u_ref[at, :].astype(F32)

    total = lax.fori_loop(0, steps // 2, gate_step, jnp.zeros((2 * CHUNKS, DI), F32))
    skip_grad_ref[...] = jnp.sum(total, axis=0, keepdims=True)
    spread_decay(packed_ref, amat_ref, spread_ref)
    exponent_steps(delta_ref, lengths_ref, my, nseq, cut_ref, steps)
    spread_columns(xdbl_ref, RANK + STATE, cx_ref, steps)

    def group_step(group, carry):
        lanes = lanes_of(group)
        amat_g = [spread_ref[st * CHUNKS : (st + 1) * CHUNKS, lanes] for st in range(STATE)]

        def step_fn(turn, grads):
            step = steps - 1 - turn
            cut = cut_ref[tile(step), lanes]
            dys = dys_ref[tile(step), lanes]
            return tuple(
                jnp.exp(cut * amat_g[st]) * (grads[st] + dys * cx_ref[state_at(step, st), :])
                for st in range(STATE)
            )

        grads = lax.fori_loop(
            0, steps, step_fn, (jnp.zeros((CHUNKS, LANES), F32),) * STATE
        )
        for st in range(STATE):
            ends_ref[st, :, lanes] = grads[st]
        return carry

    lax.fori_loop(0, GROUPS_CH, group_step, 0)
    amat = amat_ref[...]
    state = jnp.zeros((STATE, DI), F32)
    for k in reversed(range(CHUNKS)):
        state = jnp.exp(amat * totals_ref[k : k + 1, :]) * state + ends_ref[:, k, :]
    send_ref[...] = state


def fourth_kernel(
    steps,
    nseq,
    spans,
    lengths_ref,
    my_ref,
    packed_ref,
    states_ref,
    grads_ref,
    init_ref,
    ends_ref,
    totals_ref,
    delta_ref,
    u_ref,
    xdbl_ref,
    dys_ref,
    conv_ref,
    ext_ref,
    skip_grad_ref,
    dext_ref,
    spill_ref,
    small_ref,
    cut_ref,
    du_ref,
    bx_ref,
    cx_ref,
    db_ref,
    dc_ref,
    decay_ref,
    kept_ref,
    state_ref,
    bgrad_ref,
    adelta_ref,
    arrive_ref,
    dxdbl_ref,
    amat_ref,
    spread_ref,
):
    my = my_ref[0]
    rows = steps * CHUNKS
    starts = starts_of(lengths_ref, nseq)
    spread_decay(packed_ref, amat_ref, spread_ref)
    exponent_steps(delta_ref, lengths_ref, my, nseq, cut_ref, steps)
    du_ref[...] = delta_ref[...] * u_ref[...].astype(F32)
    spread_columns(xdbl_ref, RANK, bx_ref, steps)
    spread_columns(xdbl_ref, RANK + STATE, cx_ref, steps)
    amat = amat_ref[...]

    def chain(turn, state):
        k = spans - 1 - turn
        decay = jnp.exp(amat * states_ref[k, STATE : STATE + 1, :])
        return decay * state + grads_ref[k]

    state = lax.fori_loop(0, spans - 1 - my, chain, jnp.zeros((STATE, DI), F32))
    for k in reversed(range(CHUNKS)):
        arrive_ref[:, k, :] = state
        if k:
            state = jnp.exp(amat * totals_ref[k : k + 1, :]) * state + ends_ref[:, k, :]
    db_ref[...] = jnp.zeros_like(db_ref)
    dc_ref[...] = jnp.zeros_like(dc_ref)
    half = STATE // 2

    def sum_of(terms):
        while len(terms) > 1:
            terms = [a + b for a, b in zip(terms[::2], terms[1::2])]
        return terms[0]

    def group_step(group, carry):
        lanes = lanes_of(group)
        for part in range(2):
            states = range(part * half, (part + 1) * half)
            amat_g = [spread_ref[st * CHUNKS : (st + 1) * CHUNKS, lanes] for st in states]

            def forward(step, held):
                cut = cut_ref[tile(step), lanes]
                drive = du_ref[tile(step), lanes]
                out = []
                for i, st in enumerate(states):
                    at = state_at(step, st)
                    decay = jnp.exp(cut * amat_g[i])
                    kept = decay * held[i]
                    new = kept + drive * bx_ref[at, :]
                    decay_ref[at, :] = decay
                    kept_ref[at, :] = kept
                    state_ref[at, :] = new
                    out.append(new)
                return tuple(out)

            lax.fori_loop(0, steps, forward, tuple(init_ref[st, :, lanes] for st in states))

            def backward(turn, held):
                grads, sums = held
                step = steps - 1 - turn
                delta = delta_ref[tile(step), lanes]
                drive = du_ref[tile(step), lanes]
                dys = dys_ref[tile(step), lanes]
                new, totals, by_b, by_a = [], [], [], []
                for i, st in enumerate(states):
                    at = state_at(step, st)
                    grad = grads[i] + dys * cx_ref[at, :]
                    new.append(decay_ref[at, :] * grad)
                    through = grad * kept_ref[at, :]
                    totals.append(sums[i] + through * delta)
                    by_a.append(amat_g[i] * through)
                    by_b.append(grad * bx_ref[at, :])
                    dc_ref[at, :] += state_ref[at, :] * dys
                    db_ref[at, :] += grad * drive
                if part:
                    bgrad_ref[tile(step), lanes] += sum_of(by_b)
                    adelta_ref[tile(step), lanes] += sum_of(by_a)
                else:
                    bgrad_ref[tile(step), lanes] = sum_of(by_b)
                    adelta_ref[tile(step), lanes] = sum_of(by_a)
                return (tuple(new), tuple(totals))

            _, sums = lax.fori_loop(
                0,
                steps,
                backward,
                (
                    tuple(arrive_ref[st, :, lanes] for st in states),
                    (jnp.zeros((CHUNKS, LANES), F32),) * half,
                ),
            )
            for i, st in enumerate(states):
                row = jnp.sum(sums[i], axis=0, keepdims=True)
                small_ref[DEC + st : DEC + st + 1, lanes] = row * amat_g[i][0:1, :]
        return carry

    lax.fori_loop(0, GROUPS_CH, group_step, 0)
    small = packed_ref[DEC:PACK, :].astype(F32)
    taps = small[TAPS - DEC : TAPS - DEC + CONV, :]
    skip = small[SKIP - DEC : SKIP - DEC + 1, :]

    def delta_step(step, total):
        at = tile(step)
        bgrad = bgrad_ref[at, :]
        delta = delta_ref[at, :]
        u = conv_ref[at, :]
        u = (u * jax.nn.sigmoid(u)).astype(BF16).astype(F32)
        ddelta = u * bgrad + adelta_ref[at, :]
        dtpre = (ddelta * (1.0 - jnp.exp(-delta))).astype(BF16).astype(F32)
        adelta_ref[at, :] = dtpre
        bgrad_ref[at, :] = dys_ref[at, :] * skip + delta * bgrad
        return total + dtpre

    total = lax.fori_loop(0, steps, delta_step, jnp.zeros((CHUNKS, DI), F32))
    small_ref[STEPB : STEPB + 1, :] = jnp.sum(total, axis=0, keepdims=True)
    small_ref[SKIP : SKIP + 1, :] = skip_grad_ref[...]
    small_ref[GAINS:, :] = jnp.zeros((PACK - GAINS, DI), F32)
    dtpre = adelta_ref[...].astype(BF16)
    steplow = xdbl_ref[:, 0:RANK].astype(BF16)
    small_ref[STEP : STEP + RANK, :] = dot_tn(steplow, dtpre)
    dxdbl_ref[:, 0:RANK] = dot_nt(dtpre, packed_ref[STEP : STEP + RANK, :])
    lane = lax.broadcasted_iota(jnp.int32, (CHUNKS, 2 * STATE), 1)

    def gather_step(step, carry):
        total = jnp.zeros((CHUNKS, 2 * STATE), F32)
        for st in range(STATE):
            at = state_at(step, st)
            total = jnp.where(lane == st, jnp.sum(db_ref[at, :], axis=1, keepdims=True), total)
            total = jnp.where(
                lane == STATE + st, jnp.sum(dc_ref[at, :], axis=1, keepdims=True), total
            )
        dxdbl_ref[tile(step), RANK:] = total
        return carry

    lax.fori_loop(0, steps, gather_step, 0)
    dxdbl = dxdbl_ref[...].astype(BF16)
    small_ref[SEL : SEL + STEP, :] = dot_tn(dxdbl, u_ref[...])
    bgrad_ref[...] += dot_nn(dxdbl, packed_ref[SEL : SEL + STEP, :])
    dext_ref[...] = jnp.zeros_like(dext_ref)
    zero = jnp.zeros((CHUNKS, DI), F32)

    def conv_step(step, totals):
        at = tile(step)
        dconv = bgrad_ref[at, :] * silu_slope(conv_ref[at, :])
        places = lax.broadcasted_iota(jnp.int32, (CHUNKS, 1), 0) * steps + step + my * rows
        first = start_of(places, starts)
        out = []
        for k in range(CONV):
            to = pl.ds(pl.multiple_of((step + k) * CHUNKS, CHUNKS), CHUNKS)
            inside = jnp.where(places - (CONV - 1) + k >= first, dconv, 0.0)
            out.append(totals[k] + inside * ext_ref[to, :])
            dext_ref[to, :] += taps[k : k + 1, :] * inside
        return tuple(out) + (totals[CONV] + dconv,)

    totals = lax.fori_loop(0, steps, conv_step, (zero,) * (CONV + 1))
    for k in range(CONV):
        small_ref[TAPS + k : TAPS + k + 1, :] = jnp.sum(totals[k], axis=0, keepdims=True)
    small_ref[BIAS : BIAS + 1, :] = jnp.sum(totals[CONV], axis=0, keepdims=True)
    chunk = lax.broadcasted_iota(jnp.int32, (CHUNKS, DI), 0)
    spill_ref[...] = jnp.zeros_like(spill_ref)
    for k in range(CONV - 1):
        block = dext_ref[k * CHUNKS : (k + 1) * CHUNKS, :]
        spill_ref[k : k + 1, :] = block[0:1, :]
        late = (steps - CONV + 1 + k) * CHUNKS + EDGE
        moved = pltpu.roll(block, CHUNKS - 1, 0)
        dext_ref[late : late + CHUNKS, :] += jnp.where(chunk < CHUNKS - 1, moved, 0.0)


def fifth_kernel(
    steps,
    tokens_ref,
    gains_ref,
    wi_ref,
    dext_ref,
    spill_ref,
    dzgate_ref,
    dx1_ref,
    token_grad_ref,
    input_grad_ref,
    gain_grad_ref,
    dxin_ref,
):
    rows = steps * CHUNKS
    gain = gains_ref[0:1, :].astype(F32)
    x = tokens_ref[...].astype(F32)
    inverse = norm(x)
    normal = x * inverse
    xn1 = (normal * gain).astype(BF16)
    dxin_ref[...] = dext_ref[EDGE:, :]
    for k in range(CONV - 1):
        at = (steps - CONV + 2 + k) * CHUNKS - 1
        dxin_ref[at : at + 1, :] += spill_ref[k : k + 1, :]
    dxin = dxin_ref[...].astype(BF16)
    dzgate = dzgate_ref[...]
    input_grad_ref[0:DI, :] = dot_tn(dxin, xn1).astype(BF16)
    input_grad_ref[DI:, :] = dot_tn(dzgate, xn1).astype(BF16)
    dxn1 = dot_nn(dxin, wi_ref[0:DI, :]) + dot_nn(dzgate, wi_ref[DI:, :])
    gain_grad_ref[...] = jnp.sum(dxn1 * normal, axis=0, keepdims=True)
    e1 = dxn1 * gain
    token_grad_ref[...] = dx1_ref[...] + inverse * (
        e1 - normal * jnp.mean(e1 * normal, axis=-1, keepdims=True)
    )


def shape(*dims, kind=F32):
    return jax.ShapeDtypeStruct(dims, kind)


def vmem(*dims, kind=F32):
    return pltpu.VMEM(dims, kind)


def call(kernel, name, outs, scratch, scalars, *args):
    return pl.pallas_call(
        kernel,
        out_shape=outs,
        in_specs=[SMEM] * len(scalars) + [VMEM] * len(args),
        out_specs=jax.tree.map(lambda _: VMEM, outs),
        scratch_shapes=scratch,
        compiler_params=params(),
        name=name,
    )(*scalars, *args)


def step_apart(value, axis, by):
    count = lax.axis_size(axis)
    first, last = (max(0, -by), min(count, count - by))
    return lax.ppermute(value, axis, [(source, source + by) for source in range(first, last)])


def per_device(
    tokens,
    cotangent,
    positions,
    lengths,
    mixer_gain,
    input_weight,
    kernel_weight,
    kernel_bias,
    select_weight,
    step_weight,
    step_bias,
    decay_log,
    skip_scale,
    output_weight,
    attention_gain,
    heads_weight,
    merge_weight,
):
    spans = lax.axis_size("seq")
    shards = lax.axis_size("shard")
    my = lax.axis_index("seq")
    rows = tokens.shape[1]
    steps = rows // CHUNKS
    share = rows // spans
    nseq = lengths.shape[1]
    ratio = spans // HEADS
    part = rows // ratio
    width = DI // shards

    def gathered(value):
        return lax.all_gather(value.astype(BF16), "shard", axis=0, tiled=True)

    edge = step_apart(tokens[0, rows - 2 * CHUNKS :], "seq", 1)
    packed = jnp.concatenate(
        [
            select_weight.T,
            step_weight,
            decay_log.T,
            kernel_weight,
            kernel_bias[None],
            step_bias[None],
            skip_scale[None],
            jnp.concatenate([mixer_gain, attention_gain])[None],
            jnp.zeros((PACK - GAINS - 1, width), F32),
        ],
        axis=0,
    )
    packed_all = gathered(packed[None])
    wi = gathered(input_weight.T)
    wo = gathered(output_weight)
    wh = gathered(heads_weight.T)
    wm = gathered(merge_weight)
    gains = (
        packed_all[:, GAINS, :].reshape(shards, 2, D // shards).transpose(1, 0, 2).reshape(2, D)
    )
    packed_w = packed_all.transpose(1, 0, 2).reshape(PACK, DI)
    given_cot = lax.all_to_all(
        cotangent[0].reshape(spans, share, D), "seq", split_axis=0, concat_axis=0, tiled=True
    ).reshape(rows, D)
    table = positions[0].reshape(spans, spans, share)
    index = (
        lax.dynamic_index_in_dim(table, my, axis=1, keepdims=False) - my * rows
    ).reshape(1, rows)
    x = tokens[0].reshape(CHUNKS, steps, D).transpose(1, 0, 2).reshape(rows, D)
    scalars = (lengths[0], my.astype(jnp.int32).reshape(1))

    spread = [vmem(STATE, DI), vmem(STATE * CHUNKS, DI)]
    columns = vmem(rows * STATE, LANES)
    plane = vmem(rows, DI)
    ext, zgate, conv, u, delta, xdbl, ends, totals, send = call(
        functools.partial(first_kernel, steps, nseq),
        "first",
        (
            shape(EDGE + rows, DI),
            shape(rows, DI),
            shape(rows, DI),
            shape(rows, DI, kind=BF16),
            shape(rows, DI),
            shape(rows, STEP),
            shape(STATE, CHUNKS, DI),
            shape(CHUNKS, DI),
            shape(STATE + CHUNKS, DI),
        ),
        [plane, plane, columns] + spread,
        scalars,
        x,
        edge,
        wi,
        packed_w,
        gains,
    )
    states = lax.all_gather(send, "seq")
    yfull, gated, x1, init, dout, parts = call(
        functools.partial(second_kernel, steps, nseq, spans),
        "second",
        (
            shape(rows, DI),
            shape(rows, DI, kind=BF16),
            shape(rows, D),
            shape(STATE, CHUNKS, DI),
            shape(rows, D, kind=BF16),
            shape(spans, part + rows, LANES, kind=BF16),
        ),
        [plane, plane, columns, columns] + spread,
        scalars,
        x,
        packed_w,
        gains,
        wo,
        wh,
        wm,
        given_cot,
        index,
        states,
        ends,
        totals,
        delta,
        u,
        xdbl,
        zgate,
    )
    parts = lax.all_to_all(parts, "seq", split_axis=0, concat_axis=0, tiled=True)
    whole = pl.BlockSpec((spans, part + rows, LANES), lambda i: (0, 0, 0))
    parts = pl.pallas_call(
        functools.partial(attention_kernel, steps, nseq, ratio),
        grid=(spans,),
        out_shape=shape(spans, part + rows, LANES, kind=BF16),
        in_specs=[SMEM, SMEM, whole],
        out_specs=whole,
        scratch_shapes=[
            vmem(spans, part, rows),
            vmem(spans, part, rows),
            vmem(spans, rows, LANES),
        ],
        compiler_params=params(),
        name="attention",
    )(*scalars, parts)
    parts = lax.all_to_all(parts, "seq", split_axis=0, concat_axis=0, tiled=True)
    (
        given,
        merge_grad,
        heads_grad,
        output_grad,
        gain_two_grad,
        dx1,
        dys,
        dzgate,
        skip_grad,
        back_ends,
        back_send,
    ) = call(
        functools.partial(third_kernel, steps, nseq, spans),
        "third",
        (
            shape(rows, D, kind=BF16),
            shape(D, D, kind=BF16),
            shape(3 * D, D, kind=BF16),
            shape(DI, D, kind=BF16),
            shape(1, D),
            shape(rows, D),
            shape(rows, DI),
            shape(rows, DI, kind=BF16),
            shape(1, DI),
            shape(STATE, CHUNKS, DI),
            shape(STATE, DI),
        ),
        [plane, columns] + spread,
        scalars,
        parts,
        gains,
        packed_w,
        wo,
        wh,
        wm,
        index,
        dout,
        x1,
        gated,
        yfull,
        zgate,
        u,
        delta,
        xdbl,
        totals,
    )
    output = lax.all_to_all(
        given.reshape(spans, share, D), "seq", split_axis=0, concat_axis=0, tiled=True
    ).reshape(rows, D)
    grads = lax.all_gather(back_send, "seq")
    dext, spill, small = call(
        functools.partial(fourth_kernel, steps, nseq, spans),
        "fourth",
        (shape(EDGE + rows, DI), shape(CHUNKS, DI), shape(PACK, DI)),
        [plane, plane]
        + [columns] * 7
        + [plane, plane, vmem(STATE, CHUNKS, DI), vmem(rows, STEP)]
        + spread,
        scalars,
        packed_w,
        states,
        grads,
        init,
        back_ends,
        totals,
        delta,
        u,
        xdbl,
        dys,
        conv,
        ext,
        skip_grad,
    )
    spill = step_apart(spill, "seq", -1)
    token_grad, input_grad, gain_one_grad = call(
        functools.partial(fifth_kernel, steps),
        "fifth",
        (shape(rows, D), shape(2 * DI, D, kind=BF16), shape(1, D)),
        [plane],
        (),
        x,
        gains,
        wi,
        dext,
        spill,
        dzgate,
        dx1,
    )
    token_grad = token_grad.reshape(steps, CHUNKS, D).transpose(1, 0, 2).reshape(rows, D)

    def scattered(value):
        return lax.psum_scatter(value.astype(BF16), "shard", scatter_dimension=0, tiled=True)

    gain_grads = (
        jnp.concatenate([gain_one_grad, gain_two_grad], axis=0)
        .reshape(2, shards, D // shards)
        .transpose(1, 0, 2)
        .reshape(shards, 1, width)
    )
    small = small.reshape(PACK, shards, width).transpose(1, 0, 2)
    small = jnp.concatenate([small[:, :GAINS], gain_grads], axis=1)
    sums = tuple(scattered(v) for v in (merge_grad, heads_grad, output_grad, input_grad, small))
    sums = tuple(lax.psum(v, "seq").astype(F32) for v in sums)
    merge_grad, heads_grad, output_grad, input_grad, small = sums
    small = small[0]
    gain_len = D // shards
    return (
        output[None],
        token_grad[None],
        small[GAINS, :gain_len],
        input_grad.T,
        small[TAPS : TAPS + CONV],
        small[BIAS],
        small[SEL : SEL + STEP].T,
        small[STEP : STEP + RANK],
        small[STEPB],
        small[DEC : DEC + STATE].T,
        small[SKIP],
        output_grad,
        small[GAINS, gain_len:],
        heads_grad.T,
        merge_grad,
    )


def solution(mesh):
    return jax.shard_map(
        per_device,
        mesh=mesh,
        in_specs=(
            P("shard", "seq", None),
            P("shard", "seq", None),
            P("shard", None),
            P("shard", None),
            P("shard"),
            P(None, "shard"),
            P(None, "shard"),
            P("shard"),
            P("shard", None),
            P(None, "shard"),
            P("shard"),
            P("shard", None),
            P("shard"),
            P("shard", None),
            P("shard"),
            P(None, "shard"),
            P("shard", None),
        ),
        out_specs=(
            P("shard", "seq", None),
            P("shard", "seq", None),
            P("shard"),
            P(None, "shard"),
            P(None, "shard"),
            P("shard"),
            P("shard", None),
            P(None, "shard"),
            P("shard"),
            P("shard", None),
            P("shard"),
            P("shard", None),
            P("shard"),
            P(None, "shard"),
            P("shard", None),
        ),
        check_vma=False,
    )
```

```python
import functools
import math

import jax
import jax.numpy as jnp
from jax import lax
from jax.experimental import pallas as pl
from jax.experimental.pallas import tpu as pltpu
from jax.sharding import PartitionSpec as P

D = 512
DI = 1024
RANK = 32
HEADS = 8
STATE = 16
HEAD_DIM = 64
CONV = 4
CHUNKS = 8
LANES = 128
GROUPS_CH = DI // LANES
EDGE = (CONV - 1) * CHUNKS

SEL = 0
STEP = RANK + 2 * STATE
DEC = STEP + RANK
TAPS = DEC + STATE
BIAS = TAPS + CONV
STEPB = BIAS + 1
SKIP = STEPB + 1
GAINS = SKIP + 1
PACK = 128

EPS = 1e-05
NEG = -1e30
CUT = 1e30
F32 = jnp.float32
BF16 = jnp.bfloat16

VMEM = pl.BlockSpec(memory_space=pltpu.VMEM)
SMEM = pl.BlockSpec(memory_space=pltpu.SMEM)


def params(**more):
    return pltpu.CompilerParams(vmem_limit_bytes=56 << 20, **more)


def dot_nn(left, right):
    return lax.dot_general(left, right, (((1,), (0,)), ((), ())), preferred_element_type=F32)


def dot_nt(left, right):
    return lax.dot_general(left, right, (((1,), (1,)), ((), ())), preferred_element_type=F32)


def dot_tn(left, right):
    return lax.dot_general(left, right, (((0,), (0,)), ((), ())), preferred_element_type=F32)


def row_places(rows, steps):
    return (rows & (CHUNKS - 1)) * steps + (rows >> 3)


def starts_of(lengths_ref, nseq):
    starts = [jnp.int32(0)]
    for k in range(nseq - 1):
        starts.append(starts[-1] + lengths_ref[k])
    return starts


def start_of(places, starts):
    first = jnp.zeros_like(places)
    for start in starts[1:]:
        first = jnp.where(places >= start, start, first)
    return first


def begin_of(places, starts):
    found = places == starts[0]
    for start in starts[1:]:
        found = found | (places == start)
    return found


def norm(value):
    return lax.rsqrt(jnp.mean(value * value, axis=-1, keepdims=True) + EPS)


def silu_slope(value):
    s = jax.nn.sigmoid(value)
    return s * (1.0 + value * (1.0 - s))


def tile(step):
    return pl.ds(pl.multiple_of(step * CHUNKS, CHUNKS), CHUNKS)


def lanes_of(group):
    return pl.ds(pl.multiple_of(group * LANES, LANES), LANES)


def spread_decay(packed_ref, amat_ref, spread_ref):
    amat = -jnp.exp(packed_ref[DEC : DEC + STATE, :].astype(F32))
    amat_ref[...] = amat
    for st in range(STATE):
        spread_ref[st * CHUNKS : (st + 1) * CHUNKS, :] = jnp.broadcast_to(
            amat[st : st + 1, :], (CHUNKS, DI)
        )


def spread_columns(source_ref, first, target_ref, steps):
    def one(step, carry):
        values = source_ref[tile(step), :]
        base = step * (STATE * CHUNKS)
        for st in range(STATE):
            at = pl.ds(pl.multiple_of(base + st * CHUNKS, CHUNKS), CHUNKS)
            column = values[:, first + st : first + st + 1]
            target_ref[at, :] = jnp.broadcast_to(column, (CHUNKS, LANES))
        return carry

    lax.fori_loop(0, steps, one, 0)


def state_at(step, st):
    return pl.ds(pl.multiple_of(step * (STATE * CHUNKS) + st * CHUNKS, CHUNKS), CHUNKS)


def exponent_steps(delta_ref, lengths_ref, my, nseq, target_ref, steps):
    starts = starts_of(lengths_ref, nseq)
    total = steps * CHUNKS

    def one(step, carry):
        rows = lax.broadcasted_iota(jnp.int32, (CHUNKS, 1), 0) * steps + step + my * total
        target_ref[tile(step), :] = jnp.where(
            begin_of(rows, starts), CUT, delta_ref[tile(step), :]
        )
        return carry

    lax.fori_loop(0, steps, one, 0)


def first_kernel(
    steps,
    nseq,
    lengths_ref,
    my_ref,
    tokens_ref,
    edge_ref,
    wi_ref,
    packed_ref,
    gains_ref,
    ext_ref,
    zgate_ref,
    conv_ref,
    u_ref,
    delta_ref,
    xdbl_ref,
    ends_ref,
    totals_ref,
    send_ref,
    total_ref,
    cut_ref,
    du_ref,
    bx_ref,
    amat_ref,
    spread_ref,
):
    my = my_ref[0]
    rows = steps * CHUNKS
    starts = starts_of(lengths_ref, nseq)
    gain = gains_ref[0:1, :].astype(F32)
    x = tokens_ref[...].astype(F32)
    xn1 = (x * norm(x) * gain).astype(BF16)
    before = edge_ref[...].astype(F32)
    edge_n = (before * norm(before) * gain).astype(BF16)
    ext_ref[EDGE:, :] = dot_nt(xn1, wi_ref[0:DI, :])
    zgate_ref[...] = dot_nt(xn1, wi_ref[DI:, :])
    edge_x = dot_nt(edge_n, wi_ref[0:DI, :])
    count = edge_ref.shape[0]
    chunk = lax.broadcasted_iota(jnp.int32, (CHUNKS, DI), 0)
    for k in range(CONV - 1):
        late = (steps - CONV + 1 + k) * CHUNKS + EDGE
        moved = pltpu.roll(ext_ref[late : late + CHUNKS, :], 1, 0)
        at = count - CONV + 1 + k
        ext_ref[k * CHUNKS : (k + 1) * CHUNKS, :] = jnp.where(
            chunk == 0, jnp.broadcast_to(edge_x[at : at + 1, :], (CHUNKS, DI)), moved
        )
    small = packed_ref[DEC:PACK, :].astype(F32)
    taps = small[TAPS - DEC : TAPS - DEC + CONV, :]
    bias = small[BIAS - DEC : BIAS - DEC + 1, :]

    def conv_step(step, carry):
        places = lax.broadcasted_iota(jnp.int32, (CHUNKS, 1), 0) * steps + step + my * rows
        first = start_of(places, starts)
        total = jnp.broadcast_to(bias, (CHUNKS, DI))
        for k in range(CONV):
            at = pl.ds(pl.multiple_of((step + k) * CHUNKS, CHUNKS), CHUNKS)
            inside = places - (CONV - 1) + k >= first
            total = total + jnp.where(inside, taps[k : k + 1, :] * ext_ref[at, :], 0.0)
        conv_ref[tile(step), :] = total
        du_ref[tile(step), :] = total * jax.nn.sigmoid(total)
        return carry

    lax.fori_loop(0, steps, conv_step, 0)
    u = du_ref[...].astype(BF16)
    u_ref[...] = u
    xdbl = dot_nt(u, packed_ref[SEL : SEL + STEP, :])
    xdbl_ref[...] = xdbl
    delta_ref[...] = dot_nn(
        xdbl[:, :RANK].astype(BF16), packed_ref[STEP : STEP + RANK, :]
    )
    stepb = small[STEPB - DEC : STEPB - DEC + 1, :]

    def delta_step(step, total):
        places = lax.broadcasted_iota(jnp.int32, (CHUNKS, 1), 0) * steps + step + my * rows
        pre = delta_ref[tile(step), :] + stepb
        delta = jnp.maximum(pre, 0.0) + jnp.log1p(jnp.exp(-jnp.abs(pre)))
        delta_ref[tile(step), :] = delta
        cut = jnp.where(begin_of(places, starts), CUT, delta)
        cut_ref[tile(step), :] = cut
        du_ref[tile(step), :] = delta * du_ref[tile(step), :].astype(BF16).astype(F32)
        return total + cut

    totals_ref[...] = lax.fori_loop(0, steps, delta_step, jnp.zeros((CHUNKS, DI), F32))
    spread_decay(packed_ref, amat_ref, spread_ref)
    spread_columns(xdbl_ref, RANK, bx_ref, steps)

    def group_step(group, carry):
        lanes = lanes_of(group)
        amat = [spread_ref[st * CHUNKS : (st + 1) * CHUNKS, lanes] for st in range(STATE)]

        def step_fn(step, states):
            cut = cut_ref[tile(step), lanes]
            drive = du_ref[tile(step), lanes]
            return tuple(
                jnp.exp(cut * amat[st]) * states[st] + drive * bx_ref[state_at(step, st), :]
                for st in range(STATE)
            )

        states = lax.fori_loop(
            0, steps, step_fn, (jnp.zeros((CHUNKS, LANES), F32),) * STATE
        )
        for st in range(STATE):
            ends_ref[st, :, lanes] = states[st]
        return carry

    lax.fori_loop(0, GROUPS_CH, group_step, 0)
    amat = amat_ref[...]
    state = jnp.zeros((STATE, DI), F32)
    for k in range(CHUNKS):
        state = jnp.exp(amat * totals_ref[k : k + 1, :]) * state + ends_ref[:, k, :]
    send_ref[...] = state.astype(BF16)
    total = jnp.sum(totals_ref[...], axis=0, keepdims=True)
    for group in range(GROUPS_CH):
        total_ref[group : group + 1, :] = total[:, group * LANES : (group + 1) * LANES]


def total_row(values):
    return jnp.concatenate([values[g : g + 1, :] for g in range(GROUPS_CH)], axis=1)


def lane_low(rows):
    return lax.broadcasted_iota(jnp.int32, (rows, LANES), 1) < HEAD_DIM


def pick_rows(index_ref, rows, steps):
    places = row_places(lax.broadcasted_iota(jnp.int32, (rows, 1), 0), steps)
    return (index_ref[...] == places).astype(F32).astype(BF16)


def second_kernel(
    steps,
    nseq,
    spans,
    lengths_ref,
    my_ref,
    tokens_ref,
    packed_ref,
    gains_ref,
    wo_ref,
    wh_ref,
    wm_ref,
    given_ref,
    index_ref,
    states_ref,
    span_totals_ref,
    ends_ref,
    totals_ref,
    delta_ref,
    u_ref,
    xdbl_ref,
    zgate_ref,
    yfull_ref,
    gated_ref,
    x1_ref,
    init_ref,
    dout_ref,
    parts_ref,
    cut_ref,
    du_ref,
    bx_ref,
    cx_ref,
    amat_ref,
    spread_ref,
):
    my = my_ref[0]
    rows = steps * CHUNKS
    spread_decay(packed_ref, amat_ref, spread_ref)
    exponent_steps(delta_ref, lengths_ref, my, nseq, cut_ref, steps)
    du_ref[...] = delta_ref[...] * u_ref[...].astype(F32)
    spread_columns(xdbl_ref, RANK, bx_ref, steps)
    spread_columns(xdbl_ref, RANK + STATE, cx_ref, steps)
    amat = amat_ref[...]

    def chain(k, state):
        decay = jnp.exp(amat * total_row(span_totals_ref[k]))
        return decay * state + states_ref[k].astype(F32)

    state = lax.fori_loop(0, my, chain, jnp.zeros((STATE, DI), F32))
    for k in range(CHUNKS):
        init_ref[:, k, :] = state
        if k < CHUNKS - 1:
            state = jnp.exp(amat * totals_ref[k : k + 1, :]) * state + ends_ref[:, k, :]

    def group_step(group, carry):
        lanes = lanes_of(group)
        amat_g = [spread_ref[st * CHUNKS : (st + 1) * CHUNKS, lanes] for st in range(STATE)]

        def step_fn(step, states):
            cut = cut_ref[tile(step), lanes]
            drive = du_ref[tile(step), lanes]
            new = tuple(
                jnp.exp(cut * amat_g[st]) * states[st] + drive * bx_ref[state_at(step, st), :]
                for st in range(STATE)
            )
            terms = [new[st] * cx_ref[state_at(step, st), :] for st in range(STATE)]
            while len(terms) > 1:
                terms = [a + b for a, b in zip(terms[::2], terms[1::2])]
            yfull_ref[tile(step), lanes] = terms[0]
            return new

        lax.fori_loop(
            0, steps, step_fn, tuple(init_ref[st, :, lanes] for st in range(STATE))
        )
        return carry

    lax.fori_loop(0, GROUPS_CH, group_step, 0)
    skip = packed_ref[DEC:PACK, :].astype(F32)[SKIP - DEC : SKIP - DEC + 1, :]

    def gate_step(pair, carry):
        at = pl.ds(pl.multiple_of(pair * 2 * CHUNKS, 2 * CHUNKS), 2 * CHUNKS)
        yfull = yfull_ref[at, :] + skip * u_ref[at, :].astype(F32)
        yfull_ref[at, :] = yfull
        gate = zgate_ref[at, :]
        gated_ref[at, :] = (yfull * (gate * jax.nn.sigmoid(gate))).astype(BF16)
        return carry

    lax.fori_loop(0, steps // 2, gate_step, 0)
    x1 = tokens_ref[...].astype(F32) + dot_nn(gated_ref[...], wo_ref[...])
    x1_ref[...] = x1
    xn2 = (x1 * norm(x1) * gains_ref[1:2, :].astype(F32)).astype(BF16)
    dout = dot_nn(pick_rows(index_ref, rows, steps), given_ref[...]).astype(BF16)
    dout_ref[...] = dout
    dcontext = dot_nt(dout, wm_ref[...]).astype(BF16).astype(F32)
    qkv = dot_nt(xn2, wh_ref[...]).astype(BF16).astype(F32)
    low = lane_low(rows)
    scale = 1.0 / math.sqrt(HEAD_DIM)
    ratio = spans // HEADS
    part = rows // ratio
    for pair in range(HEADS // 2):
        at = pair * LANES
        q = qkv[:, at : at + LANES] * scale
        k = qkv[:, D + at : D + at + LANES]
        v = qkv[:, 2 * D + at : 2 * D + at + LANES]
        d = dcontext[:, at : at + LANES]
        for odd in range(2):
            if odd:
                qd = jnp.where(low, pltpu.roll(q, HEAD_DIM, 1), d)
                kv = jnp.where(low, pltpu.roll(k, HEAD_DIM, 1), v)
            else:
                qd = jnp.where(low, q, pltpu.roll(d, HEAD_DIM, 1))
                kv = jnp.where(low, k, pltpu.roll(v, HEAD_DIM, 1))
            qd = qd.astype(BF16)
            kv = kv.astype(BF16)
            for sub in range(ratio):
                to = (2 * pair + odd) * ratio + sub
                parts_ref[to, 0:part, :] = qd[sub * part : (sub + 1) * part, :]
                parts_ref[to, part:, :] = kv


def attention_kernel(
    steps,
    nseq,
    ratio,
    lengths_ref,
    my_ref,
    parts_ref,
    out_ref,
    score_ref,
    dprob_ref,
    dkv_ref,
):
    block = pl.program_id(0)
    spans = pl.num_programs(0)
    rows = steps * CHUNKS
    part = rows // ratio
    sub = lax.rem(my_ref[0], ratio)
    starts = starts_of(lengths_ref, nseq)

    @pl.when(block == 0)
    def _():
        dkv_ref[...] = jnp.zeros_like(dkv_ref)

    qd = parts_ref[block, 0:part, :]
    low = lane_low(part)
    qd_float = qd.astype(F32)
    both = jnp.concatenate(
        [jnp.where(low, qd_float, 0.0), jnp.where(low, 0.0, qd_float)], axis=0
    ).astype(BF16)
    own = lax.broadcasted_iota(jnp.int32, (part, 1), 0) + sub * part
    query = row_places(own, steps) + block * rows
    first = start_of(query, starts)
    key_local = row_places(lax.broadcasted_iota(jnp.int32, (1, rows), 1), steps)

    def scores(at, top):
        kv = parts_ref[at, part:, :]
        joint = dot_nt(both, kv)
        key = key_local + at * rows
        allowed = (key <= query) & (key >= first)
        score = jnp.where(allowed, joint[:part], NEG)
        score_ref[at] = score
        dprob_ref[at] = joint[part:]
        return jnp.maximum(top, jnp.max(score, axis=1, keepdims=True))

    top = lax.fori_loop(0, block + 1, scores, jnp.full((part, 1), NEG, F32))

    def weigh(at, carry):
        total, context = carry
        prob = jnp.exp(score_ref[at] - top)
        score_ref[at] = prob
        context = context + dot_nn(prob.astype(BF16), parts_ref[at, part:, :])
        return (total + jnp.sum(prob, axis=1, keepdims=True), context)

    total, context = lax.fori_loop(
        0,
        block + 1,
        weigh,
        (jnp.zeros((part, 1), F32), jnp.zeros((part, LANES), F32)),
    )
    inverse = 1.0 / total
    context = context * inverse
    datt = jnp.sum(jnp.where(low, 0.0, context * qd_float), axis=1, keepdims=True)
    key_low = lane_low(rows)

    def back(at, dquery):
        prob = score_ref[at] * inverse
        dscore = (prob * (dprob_ref[at] - datt)).astype(BF16)
        dkv_ref[at] += jnp.where(key_low, dot_tn(dscore, qd), dot_tn(prob.astype(BF16), qd))
        return dquery + dot_nn(dscore, parts_ref[at, part:, :])

    dquery = lax.fori_loop(0, block + 1, back, jnp.zeros((part, LANES), F32))
    scale = 1.0 / math.sqrt(HEAD_DIM)
    out_ref[block, 0:part, :] = jnp.where(low, dquery * scale, context).astype(BF16)

    @pl.when(block == spans - 1)
    def _():
        out_ref[:, part:, :] = dkv_ref[...].astype(BF16)


def third_kernel(
    steps,
    nseq,
    spans,
    lengths_ref,
    my_ref,
    parts_ref,
    gains_ref,
    packed_ref,
    wo_ref,
    wh_ref,
    wm_ref,
    index_ref,
    dout_ref,
    x1_ref,
    gated_ref,
    yfull_ref,
    zgate_ref,
    u_ref,
    delta_ref,
    xdbl_ref,
    totals_ref,
    given_ref,
    merge_grad_ref,
    heads_grad_ref,
    output_grad_ref,
    gain_grad_ref,
    dx1_ref,
    dys_ref,
    dzgate_ref,
    skip_grad_ref,
    ends_ref,
    send_ref,
    cut_ref,
    cx_ref,
    amat_ref,
    spread_ref,
):
    my = my_ref[0]
    rows = steps * CHUNKS
    ratio = spans // HEADS
    part = rows // ratio
    low = lane_low(rows)
    contexts, dqs, dks, dvs = [], [], [], []
    for pair in range(HEADS // 2):
        dqc, dkv = [], []
        for odd in range(2):
            base = (2 * pair + odd) * ratio
            dqc.append(
                jnp.concatenate(
                    [parts_ref[base + sub, 0:part, :].astype(F32) for sub in range(ratio)], axis=0
                )
            )
            dkv.append(sum(parts_ref[base + sub, part:, :].astype(F32) for sub in range(ratio)))
        dqs.append(jnp.where(low, dqc[0], pltpu.roll(dqc[1], HEAD_DIM, 1)))
        contexts.append(jnp.where(low, pltpu.roll(dqc[0], HEAD_DIM, 1), dqc[1]))
        dks.append(jnp.where(low, dkv[0], pltpu.roll(dkv[1], HEAD_DIM, 1)))
        dvs.append(jnp.where(low, pltpu.roll(dkv[0], HEAD_DIM, 1), dkv[1]))
    context = jnp.concatenate(contexts, axis=1).astype(BF16)
    dqkv = jnp.concatenate(dqs + dks + dvs, axis=1).astype(BF16)
    x1 = x1_ref[...]
    dout = dout_ref[...]
    x2 = (x1 + dot_nn(context, wm_ref[...])).astype(BF16)
    given_ref[...] = dot_tn(pick_rows(index_ref, rows, steps), x2).astype(BF16)
    merge_grad_ref[...] = dot_tn(context, dout).astype(BF16)
    gain = gains_ref[1:2, :].astype(F32)
    inverse = norm(x1)
    normal = x1 * inverse
    xn2 = (normal * gain).astype(BF16)
    heads_grad_ref[...] = dot_tn(dqkv, xn2).astype(BF16)
    dxn2 = dot_nn(dqkv, wh_ref[...])
    gain_grad_ref[...] = jnp.sum(dxn2 * normal, axis=0, keepdims=True)
    e2 = dxn2 * gain
    dx1 = dout.astype(F32) + inverse * (
        e2 - normal * jnp.mean(e2 * normal, axis=-1, keepdims=True)
    )
    dx1_ref[...] = dx1
    dmixed = dx1.astype(BF16)
    output_grad_ref[...] = dot_tn(gated_ref[...], dmixed).astype(BF16)
    dys_ref[...] = dot_nt(dmixed, wo_ref[...])

    def gate_step(pair, total):
        at = pl.ds(pl.multiple_of(pair * 2 * CHUNKS, 2 * CHUNKS), 2 * CHUNKS)
        dgated = dys_ref[at, :].astype(BF16).astype(F32)
        gate = zgate_ref[at, :]
        s = jax.nn.sigmoid(gate)
        dys = dgated * (gate * s)
        dys_ref[at, :] = dys
        dzgate_ref[at, :] = (dgated * yfull_ref[at, :] * (s * (1.0 + gate * (1.0 - s)))).astype(
            BF16
        )
        return total + dys * u_ref[at, :].astype(F32)

    total = lax.fori_loop(0, steps // 2, gate_step, jnp.zeros((2 * CHUNKS, DI), F32))
    skip_grad_ref[...] = jnp.sum(total, axis=0, keepdims=True)
    spread_decay(packed_ref, amat_ref, spread_ref)
    exponent_steps(delta_ref, lengths_ref, my, nseq, cut_ref, steps)
    spread_columns(xdbl_ref, RANK + STATE, cx_ref, steps)

    def group_step(group, carry):
        lanes = lanes_of(group)
        amat_g = [spread_ref[st * CHUNKS : (st + 1) * CHUNKS, lanes] for st in range(STATE)]

        def step_fn(turn, grads):
            step = steps - 1 - turn
            cut = cut_ref[tile(step), lanes]
            dys = dys_ref[tile(step), lanes]
            return tuple(
                jnp.exp(cut * amat_g[st]) * (grads[st] + dys * cx_ref[state_at(step, st), :])
                for st in range(STATE)
            )

        grads = lax.fori_loop(
            0, steps, step_fn, (jnp.zeros((CHUNKS, LANES), F32),) * STATE
        )
        for st in range(STATE):
            ends_ref[st, :, lanes] = grads[st]
        return carry

    lax.fori_loop(0, GROUPS_CH, group_step, 0)
    amat = amat_ref[...]
    state = jnp.zeros((STATE, DI), F32)
    for k in reversed(range(CHUNKS)):
        state = jnp.exp(amat * totals_ref[k : k + 1, :]) * state + ends_ref[:, k, :]
    send_ref[...] = state.astype(BF16)


def fourth_kernel(
    steps,
    nseq,
    spans,
    lengths_ref,
    my_ref,
    packed_ref,
    span_totals_ref,
    grads_ref,
    init_ref,
    ends_ref,
    totals_ref,
    delta_ref,
    u_ref,
    xdbl_ref,
    dys_ref,
    conv_ref,
    ext_ref,
    skip_grad_ref,
    dext_ref,
    spill_ref,
    small_ref,
    cut_ref,
    du_ref,
    bx_ref,
    cx_ref,
    db_ref,
    dc_ref,
    decay_ref,
    kept_ref,
    state_ref,
    bgrad_ref,
    adelta_ref,
    arrive_ref,
    dxdbl_ref,
    amat_ref,
    spread_ref,
):
    my = my_ref[0]
    rows = steps * CHUNKS
    starts = starts_of(lengths_ref, nseq)
    spread_decay(packed_ref, amat_ref, spread_ref)
    exponent_steps(delta_ref, lengths_ref, my, nseq, cut_ref, steps)
    du_ref[...] = delta_ref[...] * u_ref[...].astype(F32)
    spread_columns(xdbl_ref, RANK, bx_ref, steps)
    spread_columns(xdbl_ref, RANK + STATE, cx_ref, steps)
    amat = amat_ref[...]

    def chain(turn, state):
        k = spans - 1 - turn
        decay = jnp.exp(amat * total_row(span_totals_ref[k]))
        return decay * state + grads_ref[k].astype(F32)

    state = lax.fori_loop(0, spans - 1 - my, chain, jnp.zeros((STATE, DI), F32))
    for k in reversed(range(CHUNKS)):
        arrive_ref[:, k, :] = state
        if k:
            state = jnp.exp(amat * totals_ref[k : k + 1, :]) * state + ends_ref[:, k, :]
    db_ref[...] = jnp.zeros_like(db_ref)
    dc_ref[...] = jnp.zeros_like(dc_ref)
    half = STATE // 2

    def sum_of(terms):
        while len(terms) > 1:
            terms = [a + b for a, b in zip(terms[::2], terms[1::2])]
        return terms[0]

    def group_step(group, carry):
        lanes = lanes_of(group)
        for part in range(2):
            states = range(part * half, (part + 1) * half)
            amat_g = [spread_ref[st * CHUNKS : (st + 1) * CHUNKS, lanes] for st in states]

            def forward(step, held):
                cut = cut_ref[tile(step), lanes]
                drive = du_ref[tile(step), lanes]
                out = []
                for i, st in enumerate(states):
                    at = state_at(step, st)
                    decay = jnp.exp(cut * amat_g[i])
                    kept = decay * held[i]
                    new = kept + drive * bx_ref[at, :]
                    decay_ref[at, :] = decay
                    kept_ref[at, :] = kept
                    state_ref[at, :] = new
                    out.append(new)
                return tuple(out)

            lax.fori_loop(0, steps, forward, tuple(init_ref[st, :, lanes] for st in states))

            def backward(turn, held):
                grads, sums = held
                step = steps - 1 - turn
                delta = delta_ref[tile(step), lanes]
                drive = du_ref[tile(step), lanes]
                dys = dys_ref[tile(step), lanes]
                new, totals, by_b, by_a = [], [], [], []
                for i, st in enumerate(states):
                    at = state_at(step, st)
                    grad = grads[i] + dys * cx_ref[at, :]
                    new.append(decay_ref[at, :] * grad)
                    through = grad * kept_ref[at, :]
                    totals.append(sums[i] + through * delta)
                    by_a.append(amat_g[i] * through)
                    by_b.append(grad * bx_ref[at, :])
                    dc_ref[at, :] += state_ref[at, :] * dys
                    db_ref[at, :] += grad * drive
                if part:
                    bgrad_ref[tile(step), lanes] += sum_of(by_b)
                    adelta_ref[tile(step), lanes] += sum_of(by_a)
                else:
                    bgrad_ref[tile(step), lanes] = sum_of(by_b)
                    adelta_ref[tile(step), lanes] = sum_of(by_a)
                return (tuple(new), tuple(totals))

            _, sums = lax.fori_loop(
                0,
                steps,
                backward,
                (
                    tuple(arrive_ref[st, :, lanes] for st in states),
                    (jnp.zeros((CHUNKS, LANES), F32),) * half,
                ),
            )
            for i, st in enumerate(states):
                row = jnp.sum(sums[i], axis=0, keepdims=True)
                small_ref[DEC + st : DEC + st + 1, lanes] = row * amat_g[i][0:1, :]
        return carry

    lax.fori_loop(0, GROUPS_CH, group_step, 0)
    small = packed_ref[DEC:PACK, :].astype(F32)
    taps = small[TAPS - DEC : TAPS - DEC + CONV, :]
    skip = small[SKIP - DEC : SKIP - DEC + 1, :]

    def delta_step(step, total):
        at = tile(step)
        bgrad = bgrad_ref[at, :]
        delta = delta_ref[at, :]
        u = conv_ref[at, :]
        u = (u * jax.nn.sigmoid(u)).astype(BF16).astype(F32)
        ddelta = u * bgrad + adelta_ref[at, :]
        dtpre = (ddelta * (1.0 - jnp.exp(-delta))).astype(BF16).astype(F32)
        adelta_ref[at, :] = dtpre
        bgrad_ref[at, :] = dys_ref[at, :] * skip + delta * bgrad
        return total + dtpre

    total = lax.fori_loop(0, steps, delta_step, jnp.zeros((CHUNKS, DI), F32))
    small_ref[STEPB : STEPB + 1, :] = jnp.sum(total, axis=0, keepdims=True)
    small_ref[SKIP : SKIP + 1, :] = skip_grad_ref[...]
    small_ref[GAINS:, :] = jnp.zeros((PACK - GAINS, DI), F32)
    dtpre = adelta_ref[...].astype(BF16)
    steplow = xdbl_ref[:, 0:RANK].astype(BF16)
    small_ref[STEP : STEP + RANK, :] = dot_tn(steplow, dtpre)
    dxdbl_ref[:, 0:RANK] = dot_nt(dtpre, packed_ref[STEP : STEP + RANK, :])
    lane = lax.broadcasted_iota(jnp.int32, (CHUNKS, 2 * STATE), 1)

    def gather_step(step, carry):
        total = jnp.zeros((CHUNKS, 2 * STATE), F32)
        for st in range(STATE):
            at = state_at(step, st)
            total = jnp.where(lane == st, jnp.sum(db_ref[at, :], axis=1, keepdims=True), total)
            total = jnp.where(
                lane == STATE + st, jnp.sum(dc_ref[at, :], axis=1, keepdims=True), total
            )
        dxdbl_ref[tile(step), RANK:] = total
        return carry

    lax.fori_loop(0, steps, gather_step, 0)
    dxdbl = dxdbl_ref[...].astype(BF16)
    small_ref[SEL : SEL + STEP, :] = dot_tn(dxdbl, u_ref[...])
    bgrad_ref[...] += dot_nn(dxdbl, packed_ref[SEL : SEL + STEP, :])
    dext_ref[...] = jnp.zeros_like(dext_ref)
    zero = jnp.zeros((CHUNKS, DI), F32)

    def conv_step(step, totals):
        at = tile(step)
        dconv = bgrad_ref[at, :] * silu_slope(conv_ref[at, :])
        places = lax.broadcasted_iota(jnp.int32, (CHUNKS, 1), 0) * steps + step + my * rows
        first = start_of(places, starts)
        out = []
        for k in range(CONV):
            to = pl.ds(pl.multiple_of((step + k) * CHUNKS, CHUNKS), CHUNKS)
            inside = jnp.where(places - (CONV - 1) + k >= first, dconv, 0.0)
            out.append(totals[k] + inside * ext_ref[to, :])
            dext_ref[to, :] += taps[k : k + 1, :] * inside
        return tuple(out) + (totals[CONV] + dconv,)

    totals = lax.fori_loop(0, steps, conv_step, (zero,) * (CONV + 1))
    for k in range(CONV):
        small_ref[TAPS + k : TAPS + k + 1, :] = jnp.sum(totals[k], axis=0, keepdims=True)
    small_ref[BIAS : BIAS + 1, :] = jnp.sum(totals[CONV], axis=0, keepdims=True)
    chunk = lax.broadcasted_iota(jnp.int32, (CHUNKS, DI), 0)
    spill_ref[...] = jnp.zeros_like(spill_ref)
    for k in range(CONV - 1):
        block = dext_ref[k * CHUNKS : (k + 1) * CHUNKS, :]
        spill_ref[k : k + 1, :] = block[0:1, :]
        late = (steps - CONV + 1 + k) * CHUNKS + EDGE
        moved = pltpu.roll(block, CHUNKS - 1, 0)
        dext_ref[late : late + CHUNKS, :] += jnp.where(chunk < CHUNKS - 1, moved, 0.0)


def fifth_kernel(
    steps,
    tokens_ref,
    gains_ref,
    wi_ref,
    dext_ref,
    spill_ref,
    dzgate_ref,
    dx1_ref,
    token_grad_ref,
    input_grad_ref,
    gain_grad_ref,
    dxin_ref,
):
    rows = steps * CHUNKS
    gain = gains_ref[0:1, :].astype(F32)
    x = tokens_ref[...].astype(F32)
    inverse = norm(x)
    normal = x * inverse
    xn1 = (normal * gain).astype(BF16)
    dxin_ref[...] = dext_ref[EDGE:, :]
    for k in range(CONV - 1):
        at = (steps - CONV + 2 + k) * CHUNKS - 1
        dxin_ref[at : at + 1, :] += spill_ref[k : k + 1, :]
    dxin = dxin_ref[...].astype(BF16)
    dzgate = dzgate_ref[...]
    input_grad_ref[0:DI, :] = dot_tn(dxin, xn1).astype(BF16)
    input_grad_ref[DI:, :] = dot_tn(dzgate, xn1).astype(BF16)
    dxn1 = dot_nn(dxin, wi_ref[0:DI, :]) + dot_nn(dzgate, wi_ref[DI:, :])
    gain_grad_ref[...] = jnp.sum(dxn1 * normal, axis=0, keepdims=True)
    e1 = dxn1 * gain
    token_grad_ref[...] = dx1_ref[...] + inverse * (
        e1 - normal * jnp.mean(e1 * normal, axis=-1, keepdims=True)
    )


def at_seq(index):
    return {"device_id": {"seq": index}, "device_id_type": pl.DeviceIdType.MESH}


def at_shard(index):
    return {"device_id": {"shard": index}, "device_id_type": pl.DeviceIdType.MESH}


def greet(peers):
    barrier = pltpu.get_barrier_semaphore()
    for peer in peers:
        pl.semaphore_signal(barrier, inc=1, **peer)
    pl.semaphore_wait(barrier, len(peers))


def shard_peers(shards):
    shard = lax.axis_index("shard")
    core, chip = lax.rem(shard, 2), lax.div(shard, 2)
    partner = chip * 2 + 1 - core
    others = [lax.rem(chip + by, shards // 2) * 2 + core for by in range(1, shards // 2)]
    return shard, core, chip, partner, others


def gather_kernel(count, shards, spans, *refs):
    pieces, (cot_ref, edge_ref) = refs[:count], refs[count : count + 2]
    wholes = refs[count + 2 : 2 * count + 2]
    given_ref, before_ref = refs[2 * count + 2 : 2 * count + 4]
    send_sem, recv_sem, pass_sem, own_sem, cot_send, cot_recv, edge_sem = refs[2 * count + 4 :]
    me = lax.axis_index("seq")
    shard, core, chip, partner, others = shard_peers(shards)
    greet(
        [at_shard(partner)]
        + [at_shard(other) for other in others]
        + [at_seq(lax.rem(me + by, spans)) for by in range(1, spans)]
    )
    copies = []
    for k in range(count):
        for i, to in enumerate(others + [partner]):
            copy = pltpu.make_async_remote_copy(
                src_ref=pieces[k],
                dst_ref=wholes[k].at[shard],
                send_sem=send_sem.at[k, i],
                recv_sem=recv_sem.at[k, i],
                **at_shard(to),
            )
            copy.start()
            copies.append(copy)
    local = [
        pltpu.make_async_copy(pieces[k], wholes[k].at[shard], own_sem.at[k]) for k in range(count)
    ] + [
        pltpu.make_async_copy(cot_ref.at[me], given_ref.at[me], own_sem.at[count]),
    ]
    for copy in local:
        copy.start()
    for by in range(1, spans):
        to = lax.rem(me + by, spans)
        copy = pltpu.make_async_remote_copy(
            src_ref=cot_ref.at[to],
            dst_ref=given_ref.at[me],
            send_sem=cot_send.at[by],
            recv_sem=cot_recv.at[by],
            **at_seq(to),
        )
        copy.start()
        copies.append(copy)
    edge = pltpu.make_async_remote_copy(
        src_ref=edge_ref,
        dst_ref=before_ref,
        send_sem=edge_sem.at[0],
        recv_sem=edge_sem.at[1],
        **at_seq(lax.rem(me + 1, spans)),
    )
    edge.start()
    passed = []
    far = len(others)
    for k in range(count):
        for i in range(far):
            copies[k * (far + 1) + i].wait_recv()
            came = lax.rem(chip + far - i, far + 1) * 2 + core
            copy = pltpu.make_async_remote_copy(
                src_ref=wholes[k].at[came],
                dst_ref=wholes[k].at[came],
                send_sem=pass_sem.at[0, k, i],
                recv_sem=pass_sem.at[1, k, i],
                **at_shard(partner),
            )
            copy.start()
            passed.append(copy)
    for k in range(count):
        for i in range(far):
            copies[k * (far + 1) + i].wait_send()
        copies[k * (far + 1) + far].wait()
    for copy in passed + local + copies[count * (far + 1) :] + [edge]:
        copy.wait()


def exchange_kernel(spans, count, *refs):
    mine, wholes = refs[:count], refs[count : 2 * count]
    send_sem, recv_sem, own_sem = refs[2 * count :]
    me = lax.axis_index("seq")
    greet([at_seq(lax.rem(me + by, spans)) for by in range(1, spans)])
    copies = []
    for by in range(1, spans):
        for k in range(count):
            copy = pltpu.make_async_remote_copy(
                src_ref=mine[k],
                dst_ref=wholes[k].at[me],
                send_sem=send_sem.at[k, by],
                recv_sem=recv_sem.at[k, by],
                **at_seq(lax.rem(me + by, spans)),
            )
            copy.start()
            copies.append(copy)
    for k in range(count):
        copy = pltpu.make_async_copy(mine[k], wholes[k].at[me], own_sem.at[k])
        copy.start()
        copies.append(copy)
    for copy in copies:
        copy.wait()


def reduce_kernel(count, shards, spans, *refs):
    grads, sums = refs[:count], refs[count : 2 * count]
    near, held, far, parts = (refs[(2 + i) * count : (3 + i) * count] for i in range(4))
    near_sem, far_sem, part_sem, last_sem = refs[6 * count :]
    me = lax.axis_index("seq")
    shard, core, chip, partner, others = shard_peers(shards)
    chips = shards // 2
    ring = [lax.rem(me + by, spans) for by in range(1, spans)]
    greet([at_shard(partner)] + [at_shard(o) for o in others] + [at_seq(to) for to in ring])

    def send(source, target, sems, at, to):
        copy = pltpu.make_async_remote_copy(
            src_ref=source, dst_ref=target, send_sem=sems.at[(0, *at)], recv_sem=sems.at[(1, *at)], **to
        )
        copy.start()
        return copy

    first = [
        [
            send(grads[k].at[x * 2 + 1 - core], near[k].at[x], near_sem, (k, x), at_shard(partner))
            for x in range(chips)
        ]
        for k in range(count)
    ]
    second = []
    for k in range(count):
        for x in range(chips):
            first[k][x].wait_recv()
            held[k][x] = (
                grads[k][x * 2 + core].astype(F32) + near[k][x].astype(F32)
            ).astype(BF16)
        second.append(
            [
                send(
                    held[k].at[lax.rem(chip + by, chips)],
                    far[k].at[by - 1],
                    far_sem,
                    (k, by),
                    at_shard(others[by - 1]),
                )
                for by in range(1, chips)
            ]
        )
    third = []
    for k in range(count):
        total = held[k][chip].astype(F32)
        for by in range(1, chips):
            second[k][by - 1].wait_recv()
            total = total + far[k][by - 1].astype(F32)
        near[k][0] = total.astype(BF16)
        third.append(
            [
                send(near[k].at[0, ring[by - 1]], parts[k].at[by], part_sem, (k, by), at_seq(ring[by - 1]))
                for by in range(1, spans)
            ]
        )
    fourth = []
    for k in range(count):
        total = near[k][0, me].astype(F32)
        for by in range(1, spans):
            third[k][by - 1].wait_recv()
            total = total + parts[k][by].astype(F32)
        sums[k][me] = total.astype(BF16)
        fourth.append(
            [
                send(sums[k].at[me], sums[k].at[me], last_sem, (k, by), at_seq(ring[by - 1]))
                for by in range(1, spans)
            ]
        )
    for group in first + second + third:
        for copy in group:
            copy.wait_send()
    for group in fourth:
        for copy in group:
            copy.wait()


def shape(*dims, kind=F32):
    return jax.ShapeDtypeStruct(dims, kind)


def vmem(*dims, kind=F32):
    return pltpu.VMEM(dims, kind)


def talk(kernel, name, number, outs, scratch, *args):
    return pl.pallas_call(
        kernel,
        out_shape=outs,
        in_specs=[VMEM] * len(args),
        out_specs=[VMEM] * len(outs),
        scratch_shapes=scratch,
        compiler_params=params(collective_id=number, has_side_effects=True),
        name=name,
    )(*args)


def exchanged(number, spans, *values):
    sems = [pltpu.SemaphoreType.DMA((len(values), spans))] * 2
    return talk(
        functools.partial(exchange_kernel, spans, len(values)),
        "exchange%d" % number,
        number,
        [shape(spans, *v.shape, kind=v.dtype) for v in values],
        sems + [pltpu.SemaphoreType.DMA((len(values),))],
        *values,
    )


def call(kernel, name, outs, scratch, scalars, *args):
    return pl.pallas_call(
        kernel,
        out_shape=outs,
        in_specs=[SMEM] * len(scalars) + [VMEM] * len(args),
        out_specs=jax.tree.map(lambda _: VMEM, outs),
        scratch_shapes=scratch,
        compiler_params=params(),
        name=name,
    )(*scalars, *args)


def step_apart(value, axis, by):
    count = lax.axis_size(axis)
    first, last = (max(0, -by), min(count, count - by))
    return lax.ppermute(value, axis, [(source, source + by) for source in range(first, last)])


def per_device(
    tokens,
    cotangent,
    positions,
    lengths,
    mixer_gain,
    input_weight,
    kernel_weight,
    kernel_bias,
    select_weight,
    step_weight,
    step_bias,
    decay_log,
    skip_scale,
    output_weight,
    attention_gain,
    heads_weight,
    merge_weight,
):
    spans = lax.axis_size("seq")
    shards = lax.axis_size("shard")
    my = lax.axis_index("seq")
    rows = tokens.shape[1]
    steps = rows // CHUNKS
    share = rows // spans
    nseq = lengths.shape[1]
    ratio = spans // HEADS
    part = rows // ratio
    width = DI // shards

    edge = tokens[0, rows - 2 * CHUNKS :]
    packed = jnp.concatenate(
        [
            select_weight.T,
            step_weight,
            decay_log.T,
            kernel_weight,
            kernel_bias[None],
            step_bias[None],
            skip_scale[None],
            jnp.concatenate([mixer_gain, attention_gain])[None],
            jnp.zeros((PACK - GAINS - 1, width), F32),
        ],
        axis=0,
    )
    pieces = [
        v.astype(BF16)
        for v in (input_weight.T, packed, output_weight, heads_weight.T, merge_weight)
    ]
    dma = pltpu.SemaphoreType.DMA
    count, far = len(pieces), shards // 2 - 1
    wi, packed_all, wo, wh, wm, given_cot, edge = talk(
        functools.partial(gather_kernel, count, shards, spans),
        "gather",
        0,
        [shape(shards, *v.shape, kind=BF16) for v in pieces]
        + [shape(spans, share, D, kind=BF16), shape(*edge.shape, kind=BF16)],
        [
            dma((count, far + 1)),
            dma((count, far + 1)),
            dma((2, count, far)),
            dma((count + 1,)),
            dma((spans,)),
            dma((spans,)),
            dma((2,)),
        ],
        *pieces,
        cotangent[0].reshape(spans, share, D),
        edge,
    )
    wi, wo, wh, wm = (v.reshape(-1, D) for v in (wi, wo, wh, wm))
    given_cot = given_cot.reshape(rows, D)
    gains = (
        packed_all[:, GAINS, :].reshape(shards, 2, D // shards).transpose(1, 0, 2).reshape(2, D)
    )
    packed_w = packed_all.transpose(1, 0, 2).reshape(PACK, DI)
    table = positions[0].reshape(spans, spans, share)
    index = (
        lax.dynamic_index_in_dim(table, my, axis=1, keepdims=False) - my * rows
    ).reshape(1, rows)
    x = tokens[0].reshape(CHUNKS, steps, D).transpose(1, 0, 2).reshape(rows, D)
    scalars = (lengths[0], my.astype(jnp.int32).reshape(1))

    spread = [vmem(STATE, DI), vmem(STATE * CHUNKS, DI)]
    columns = vmem(rows * STATE, LANES)
    plane = vmem(rows, DI)
    ext, zgate, conv, u, delta, xdbl, ends, totals, send, total = call(
        functools.partial(first_kernel, steps, nseq),
        "first",
        (
            shape(EDGE + rows, DI),
            shape(rows, DI),
            shape(rows, DI),
            shape(rows, DI, kind=BF16),
            shape(rows, DI),
            shape(rows, STEP),
            shape(STATE, CHUNKS, DI),
            shape(CHUNKS, DI),
            shape(STATE, DI, kind=BF16),
            shape(GROUPS_CH, LANES),
        ),
        [plane, plane, columns] + spread,
        scalars,
        x,
        edge,
        wi,
        packed_w,
        gains,
    )
    states, span_totals = exchanged(1, spans, send, total)
    yfull, gated, x1, init, dout, parts = call(
        functools.partial(second_kernel, steps, nseq, spans),
        "second",
        (
            shape(rows, DI),
            shape(rows, DI, kind=BF16),
            shape(rows, D),
            shape(STATE, CHUNKS, DI),
            shape(rows, D, kind=BF16),
            shape(spans, part + rows, LANES, kind=BF16),
        ),
        [plane, plane, columns, columns] + spread,
        scalars,
        x,
        packed_w,
        gains,
        wo,
        wh,
        wm,
        given_cot,
        index,
        states,
        span_totals,
        ends,
        totals,
        delta,
        u,
        xdbl,
        zgate,
    )
    parts = lax.all_to_all(parts, "seq", split_axis=0, concat_axis=0, tiled=True)
    whole = pl.BlockSpec((spans, part + rows, LANES), lambda i: (0, 0, 0))
    parts = pl.pallas_call(
        functools.partial(attention_kernel, steps, nseq, ratio),
        grid=(spans,),
        out_shape=shape(spans, part + rows, LANES, kind=BF16),
        in_specs=[SMEM, SMEM, whole],
        out_specs=whole,
        scratch_shapes=[
            vmem(spans, part, rows),
            vmem(spans, part, rows),
            vmem(spans, rows, LANES),
        ],
        compiler_params=params(),
        name="attention",
    )(*scalars, parts)
    parts = lax.all_to_all(parts, "seq", split_axis=0, concat_axis=0, tiled=True)
    (
        given,
        merge_grad,
        heads_grad,
        output_grad,
        gain_two_grad,
        dx1,
        dys,
        dzgate,
        skip_grad,
        back_ends,
        back_send,
    ) = call(
        functools.partial(third_kernel, steps, nseq, spans),
        "third",
        (
            shape(rows, D, kind=BF16),
            shape(D, D, kind=BF16),
            shape(3 * D, D, kind=BF16),
            shape(DI, D, kind=BF16),
            shape(1, D),
            shape(rows, D),
            shape(rows, DI),
            shape(rows, DI, kind=BF16),
            shape(1, DI),
            shape(STATE, CHUNKS, DI),
            shape(STATE, DI, kind=BF16),
        ),
        [plane, columns] + spread,
        scalars,
        parts,
        gains,
        packed_w,
        wo,
        wh,
        wm,
        index,
        dout,
        x1,
        gated,
        yfull,
        zgate,
        u,
        delta,
        xdbl,
        totals,
    )
    output = lax.all_to_all(
        given.reshape(spans, share, D), "seq", split_axis=0, concat_axis=0, tiled=True
    ).reshape(rows, D)
    (grads,) = exchanged(2, spans, back_send)
    dext, spill, small = call(
        functools.partial(fourth_kernel, steps, nseq, spans),
        "fourth",
        (shape(EDGE + rows, DI), shape(CHUNKS, DI), shape(PACK, DI)),
        [plane, plane]
        + [columns] * 7
        + [plane, plane, vmem(STATE, CHUNKS, DI), vmem(rows, STEP)]
        + spread,
        scalars,
        packed_w,
        span_totals,
        grads,
        init,
        back_ends,
        totals,
        delta,
        u,
        xdbl,
        dys,
        conv,
        ext,
        skip_grad,
    )
    spill = step_apart(spill, "seq", -1)
    token_grad, input_grad, gain_one_grad = call(
        functools.partial(fifth_kernel, steps),
        "fifth",
        (shape(rows, D), shape(2 * DI, D, kind=BF16), shape(1, D)),
        [plane],
        (),
        x,
        gains,
        wi,
        dext,
        spill,
        dzgate,
        dx1,
    )
    token_grad = token_grad.reshape(steps, CHUNKS, D).transpose(1, 0, 2).reshape(rows, D)

    gain_grads = (
        jnp.concatenate([gain_one_grad, gain_two_grad], axis=0)
        .reshape(2, shards, D // shards)
        .transpose(1, 0, 2)
        .reshape(shards, 1, width)
    )
    small = small.reshape(PACK, shards, width).transpose(1, 0, 2)
    small = jnp.concatenate(
        [small[:, :GAINS], gain_grads, jnp.zeros((shards, PACK - GAINS - 1, width), F32)], axis=1
    )
    grads = [
        v.astype(BF16).reshape(shards, spans, -1, v.shape[-1])
        for v in (merge_grad, heads_grad, output_grad, input_grad, small)
    ]
    count, chips = len(grads), shards // 2
    sums = talk(
        functools.partial(reduce_kernel, count, shards, spans),
        "reduce",
        3,
        [shape(*v.shape[1:], kind=BF16) for v in grads],
        [vmem(chips, *v.shape[1:], kind=BF16) for v in grads]
        + [vmem(chips, *v.shape[1:], kind=BF16) for v in grads]
        + [vmem(max(chips - 1, 1), *v.shape[1:], kind=BF16) for v in grads]
        + [vmem(*v.shape[1:], kind=BF16) for v in grads]
        + [dma((2, count, chips))] * 2
        + [dma((2, count, spans))] * 2,
        *grads,
    )
    merge_grad, heads_grad, output_grad, input_grad, small = (
        v.reshape(-1, v.shape[-1]).astype(F32) for v in sums
    )
    gain_len = D // shards
    return (
        output[None],
        token_grad[None],
        small[GAINS, :gain_len],
        input_grad.T,
        small[TAPS : TAPS + CONV],
        small[BIAS],
        small[SEL : SEL + STEP].T,
        small[STEP : STEP + RANK],
        small[STEPB],
        small[DEC : DEC + STATE].T,
        small[SKIP],
        output_grad,
        small[GAINS, gain_len:],
        heads_grad.T,
        merge_grad,
    )


def solution(mesh):
    return jax.shard_map(
        per_device,
        mesh=mesh,
        in_specs=(
            P("shard", "seq", None),
            P("shard", "seq", None),
            P("shard", None),
            P("shard", None),
            P("shard"),
            P(None, "shard"),
            P(None, "shard"),
            P("shard"),
            P("shard", None),
            P(None, "shard"),
            P("shard"),
            P("shard", None),
            P("shard"),
            P("shard", None),
            P("shard"),
            P(None, "shard"),
            P("shard", None),
        ),
        out_specs=(
            P("shard", "seq", None),
            P("shard", "seq", None),
            P("shard"),
            P(None, "shard"),
            P(None, "shard"),
            P("shard"),
            P("shard", None),
            P(None, "shard"),
            P("shard"),
            P("shard", None),
            P("shard"),
            P("shard", None),
            P("shard"),
            P(None, "shard"),
            P("shard", None),
        ),
        check_vma=False,
    )
```

```python
import functools
import math

import jax
import jax.numpy as jnp
from jax import lax
from jax.experimental import pallas as pl
from jax.experimental.pallas import tpu as pltpu
from jax.sharding import PartitionSpec as P

D = 512
DI = 1024
RANK = 32
HEADS = 8
STATE = 16
HEAD_DIM = 64
CONV = 4
CHUNKS = 8
LANES = 128
GROUPS_CH = DI // LANES
EDGE = (CONV - 1) * CHUNKS

SEL = 0
STEP = RANK + 2 * STATE
DEC = STEP + RANK
TAPS = DEC + STATE
BIAS = TAPS + CONV
STEPB = BIAS + 1
SKIP = STEPB + 1
GAINS = SKIP + 1
PACK = 128

EPS = 1e-05
NEG = -1e30
CUT = 1e30
F32 = jnp.float32
BF16 = jnp.bfloat16

VMEM = pl.BlockSpec(memory_space=pltpu.VMEM)
SMEM = pl.BlockSpec(memory_space=pltpu.SMEM)


def params(**more):
    return pltpu.CompilerParams(vmem_limit_bytes=56 << 20, **more)


def dot_nn(left, right):
    return lax.dot_general(left, right, (((1,), (0,)), ((), ())), preferred_element_type=F32)


def dot_nt(left, right):
    return lax.dot_general(left, right, (((1,), (1,)), ((), ())), preferred_element_type=F32)


def dot_tn(left, right):
    return lax.dot_general(left, right, (((0,), (0,)), ((), ())), preferred_element_type=F32)


def row_places(rows, steps):
    return (rows & (CHUNKS - 1)) * steps + (rows >> 3)


def starts_of(lengths_ref, nseq):
    starts = [jnp.int32(0)]
    for k in range(nseq - 1):
        starts.append(starts[-1] + lengths_ref[k])
    return starts


def start_of(places, starts):
    first = jnp.zeros_like(places)
    for start in starts[1:]:
        first = jnp.where(places >= start, start, first)
    return first


def begin_of(places, starts):
    found = places == starts[0]
    for start in starts[1:]:
        found = found | (places == start)
    return found


def norm(value):
    return lax.rsqrt(jnp.mean(value * value, axis=-1, keepdims=True) + EPS)


def silu_slope(value):
    s = jax.nn.sigmoid(value)
    return s * (1.0 + value * (1.0 - s))


def tile(step):
    return pl.ds(pl.multiple_of(step * CHUNKS, CHUNKS), CHUNKS)


def lanes_of(group):
    return pl.ds(pl.multiple_of(group * LANES, LANES), LANES)


def spread_decay(packed_ref, amat_ref, spread_ref):
    amat = -jnp.exp(packed_ref[DEC : DEC + STATE, :].astype(F32))
    amat_ref[...] = amat
    for st in range(STATE):
        spread_ref[st * CHUNKS : (st + 1) * CHUNKS, :] = jnp.broadcast_to(
            amat[st : st + 1, :], (CHUNKS, DI)
        )


def spread_columns(source_ref, first, target_ref, steps):
    def one(step, carry):
        values = source_ref[tile(step), :]
        base = step * (STATE * CHUNKS)
        for st in range(STATE):
            at = pl.ds(pl.multiple_of(base + st * CHUNKS, CHUNKS), CHUNKS)
            column = values[:, first + st : first + st + 1]
            target_ref[at, :] = jnp.broadcast_to(column, (CHUNKS, LANES))
        return carry

    lax.fori_loop(0, steps, one, 0)


def state_at(step, st):
    return pl.ds(pl.multiple_of(step * (STATE * CHUNKS) + st * CHUNKS, CHUNKS), CHUNKS)


def exponent_steps(delta_ref, lengths_ref, my, nseq, target_ref, steps):
    starts = starts_of(lengths_ref, nseq)
    total = steps * CHUNKS

    def one(step, carry):
        rows = lax.broadcasted_iota(jnp.int32, (CHUNKS, 1), 0) * steps + step + my * total
        target_ref[tile(step), :] = jnp.where(
            begin_of(rows, starts), CUT, delta_ref[tile(step), :]
        )
        return carry

    lax.fori_loop(0, steps, one, 0)


def at_seq(index):
    return {"device_id": {"seq": index}, "device_id_type": pl.DeviceIdType.MESH}


def at_shard(index):
    return {"device_id": {"shard": index}, "device_id_type": pl.DeviceIdType.MESH}


def greet(peers):
    barrier = pltpu.get_barrier_semaphore()
    for peer in peers:
        pl.semaphore_signal(barrier, inc=1, **peer)
    pl.semaphore_wait(barrier, len(peers))


def shard_peers(shards):
    shard = lax.axis_index("shard")
    core, chip = lax.rem(shard, 2), lax.div(shard, 2)
    partner = chip * 2 + 1 - core
    others = [lax.rem(chip + by, shards // 2) * 2 + core for by in range(1, shards // 2)]
    return shard, core, chip, partner, others


def start_kernel(
    steps,
    nseq,
    shards,
    spans,
    lengths_ref,
    tokens_ref,
    cot_ref,
    mixer_ref,
    attention_ref,
    select_ref,
    stepw_ref,
    decay_ref,
    taps_ref,
    bias_ref,
    stepb_ref,
    skip_ref,
    wi_ref,
    wo_ref,
    wh_ref,
    wm_ref,
    x_ref,
    wi_all,
    wo_all,
    wh_all,
    wm_all,
    packed_ref,
    gains_ref,
    given_ref,
    states_ref,
    span_totals_ref,
    ext_ref,
    zgate_ref,
    conv_ref,
    u_ref,
    delta_ref,
    xdbl_ref,
    ends_ref,
    totals_ref,
    row_ref,
    small_ref,
    wi_send,
    wo_send,
    wh_send,
    wm_send,
    packed_send,
    gains_send,
    packed_all,
    gains_all,
    before_ref,
    state_send,
    total_send,
    cut_ref,
    du_ref,
    bx_ref,
    amat_ref,
    spread_ref,
    gather_sem,
    cot_sem,
    edge_sem,
    state_sem,
    total_sem,
):
    rows = steps * CHUNKS
    width = DI // shards
    me = lax.axis_index("seq")
    shard, core, chip, partner, others = shard_peers(shards)
    far = len(others)
    ring = [lax.rem(me + by, spans) for by in range(1, spans)]
    greet([at_shard(partner)] + [at_shard(o) for o in others] + [at_seq(to) for to in ring])

    def copy(source, target, sems, at, to):
        return pltpu.make_async_remote_copy(
            src_ref=source, dst_ref=target, send_sem=sems.at[(0, *at)], recv_sem=sems.at[(1, *at)], **to
        )

    sources = (wi_send, packed_send, gains_send, wo_send, wh_send, wm_send)
    wholes = (wi_all, packed_all, gains_all, wo_all, wh_all, wm_all)

    def sent(k, i):
        to = partner if i == far else others[i]
        return copy(sources[k], wholes[k].at[shard], gather_sem, (k, i), at_shard(to))

    def passed(k, i):
        came = lax.rem(chip + far - i, far + 1) * 2 + core
        return copy(
            wholes[k].at[came], wholes[k].at[came], gather_sem, (k, far + 1 + i), at_shard(partner)
        )

    def spread(*which):
        for k in which:
            for i in range(far + 1):
                sent(k, i).start()
        for k in which:
            wholes[k][shard] = sources[k][...]

    def pass_on(*which):
        for i in range(far):
            for k in which:
                sent(k, i).wait_recv()
                passed(k, i).start()

    def finish(*which):
        for k in which:
            for i in range(far):
                sent(k, i).wait_send()
                passed(k, i).wait()
            sent(k, far).wait()

    wi_send[...] = wi_ref[...].astype(BF16)
    small_ref[...] = jnp.zeros_like(small_ref)
    for source, first, size in ((select_ref, SEL, STEP), (decay_ref, DEC, STATE)):
        eye = (
            lax.broadcasted_iota(jnp.int32, (size, size), 0)
            == lax.broadcasted_iota(jnp.int32, (size, size), 1)
        )
        small_ref[first : first + size, :] = dot_nt(
            eye.astype(F32).astype(BF16), source[...].astype(BF16)
        )
    for source, first in (
        (stepw_ref, STEP),
        (taps_ref, TAPS),
        (bias_ref, BIAS),
        (stepb_ref, STEPB),
        (skip_ref, SKIP),
    ):
        small_ref[first : first + source.shape[0], :] = source[...]
    packed_send[...] = small_ref[...].astype(BF16)
    lane = lax.broadcasted_iota(jnp.int32, (2 * CHUNKS, D // shards), 0)
    gains_send[...] = jnp.where(lane == 0, mixer_ref[...], attention_ref[...]).astype(BF16)
    spread(0, 1, 2)
    last = tokens_ref.at[pl.ds(rows - 2 * CHUNKS, 2 * CHUNKS)]
    edge = copy(last, before_ref, edge_sem, (), at_seq(ring[0]))
    edge.start()

    def cot_copy(by):
        return copy(
            cot_ref.at[ring[by - 1]], given_ref.at[me], cot_sem, (by,), at_seq(ring[by - 1])
        )

    for by in range(1, spans):
        cot_copy(by).start()
    given_ref[me] = cot_ref[me]
    wo_send[...] = wo_ref[...].astype(BF16)
    wh_send[...] = wh_ref[...].astype(BF16)
    wm_send[...] = wm_ref[...].astype(BF16)
    for part in range(D // LANES):
        lanes = slice(part * LANES, (part + 1) * LANES)
        row_ref[...] = tokens_ref[:, lanes].astype(F32)
        for step in range(steps):
            x_ref[step * CHUNKS : (step + 1) * CHUNKS, lanes] = row_ref[
                pl.ds(step, CHUNKS, stride=steps), :
            ]
    pass_on(0, 1, 2)
    spread(3, 4, 5)
    finish(0, 1, 2)
    edge.wait()

    starts = starts_of(lengths_ref, nseq)
    packed_ref[...] = jnp.concatenate([packed_all[s] for s in range(shards)], axis=1)
    gains = jnp.concatenate([gains_all[s].astype(F32) for s in range(shards)], axis=1)
    gains_ref[...] = gains[:CHUNKS]
    gain = gains[0:1]
    x = x_ref[...]
    xn1 = (x * norm(x) * gain).astype(BF16)
    before = before_ref[...].astype(F32)
    edge_n = (before * norm(before) * gain).astype(BF16)
    wide = 2 * DI // shards
    for s in range(shards):
        piece = dot_nn(xn1, wi_all[s])
        if s < shards // 2:
            ext_ref[EDGE:, s * wide : (s + 1) * wide] = piece
        else:
            at = (s - shards // 2) * wide
            zgate_ref[:, at : at + wide] = piece
    edge_x = jnp.concatenate([dot_nn(edge_n, wi_all[s]) for s in range(shards // 2)], axis=1)
    count = before_ref.shape[0]
    chunk = lax.broadcasted_iota(jnp.int32, (CHUNKS, DI), 0)
    for k in range(CONV - 1):
        late = (steps - CONV + 1 + k) * CHUNKS + EDGE
        moved = pltpu.roll(ext_ref[late : late + CHUNKS, :], 1, 0)
        at = count - CONV + 1 + k
        ext_ref[k * CHUNKS : (k + 1) * CHUNKS, :] = jnp.where(
            chunk == 0, jnp.broadcast_to(edge_x[at : at + 1, :], (CHUNKS, DI)), moved
        )
    small = packed_ref[DEC:PACK, :].astype(F32)
    taps = small[TAPS - DEC : TAPS - DEC + CONV, :]
    bias = small[BIAS - DEC : BIAS - DEC + 1, :]

    def conv_step(step, carry):
        places = lax.broadcasted_iota(jnp.int32, (CHUNKS, 1), 0) * steps + step + me * rows
        first = start_of(places, starts)
        total = jnp.broadcast_to(bias, (CHUNKS, DI))
        for k in range(CONV):
            at = pl.ds(pl.multiple_of((step + k) * CHUNKS, CHUNKS), CHUNKS)
            inside = places - (CONV - 1) + k >= first
            total = total + jnp.where(inside, taps[k : k + 1, :] * ext_ref[at, :], 0.0)
        conv_ref[tile(step), :] = total
        du_ref[tile(step), :] = total * jax.nn.sigmoid(total)
        return carry

    lax.fori_loop(0, steps, conv_step, 0)
    u = du_ref[...].astype(BF16)
    u_ref[...] = u
    xdbl = dot_nt(u, packed_ref[SEL : SEL + STEP, :])
    xdbl_ref[...] = xdbl
    delta_ref[...] = dot_nn(
        xdbl[:, :RANK].astype(BF16), packed_ref[STEP : STEP + RANK, :]
    )
    stepb = small[STEPB - DEC : STEPB - DEC + 1, :]

    def delta_step(step, total):
        places = lax.broadcasted_iota(jnp.int32, (CHUNKS, 1), 0) * steps + step + me * rows
        pre = delta_ref[tile(step), :] + stepb
        delta = jnp.maximum(pre, 0.0) + jnp.log1p(jnp.exp(-jnp.abs(pre)))
        delta_ref[tile(step), :] = delta
        cut = jnp.where(begin_of(places, starts), CUT, delta)
        cut_ref[tile(step), :] = cut
        du_ref[tile(step), :] = delta * du_ref[tile(step), :].astype(BF16).astype(F32)
        return total + cut

    totals = lax.fori_loop(0, steps, delta_step, jnp.zeros((CHUNKS, DI), F32))
    totals_ref[...] = totals
    total = jnp.sum(totals, axis=0, keepdims=True)
    for group in range(GROUPS_CH):
        total_send[group : group + 1, :] = total[:, group * LANES : (group + 1) * LANES]
    span_totals_ref[me] = total_send[...]

    def total_copy(by):
        return copy(
            total_send, span_totals_ref.at[me], total_sem, (by,), at_seq(ring[by - 1])
        )

    for by in range(1, spans):
        total_copy(by).start()
    pass_on(3)
    spread_decay(packed_ref, amat_ref, spread_ref)
    spread_columns(xdbl_ref, RANK, bx_ref, steps)

    def state_copy(by, at):
        return copy(
            state_send.at[at], states_ref.at[me, at], state_sem, (by, at), at_seq(ring[by - 1])
        )

    def pair_step(pair, carry):
        for odd in range(2):
            lanes = lanes_of(pair * 2 + odd)
            amat = [spread_ref[st * CHUNKS : (st + 1) * CHUNKS, lanes] for st in range(STATE)]

            def step_fn(step, states):
                cut = cut_ref[tile(step), lanes]
                drive = du_ref[tile(step), lanes]
                return tuple(
                    jnp.exp(cut * amat[st]) * states[st] + drive * bx_ref[state_at(step, st), :]
                    for st in range(STATE)
                )

            states = lax.fori_loop(
                0, steps, step_fn, (jnp.zeros((CHUNKS, LANES), F32),) * STATE
            )
            for st in range(STATE):
                ends_ref[st, :, lanes] = states[st]
        lanes = pl.ds(pl.multiple_of(pair * 2 * LANES, 2 * LANES), 2 * LANES)
        amat = amat_ref[:, lanes]
        state = jnp.zeros((STATE, 2 * LANES), F32)
        for k in range(CHUNKS):
            state = jnp.exp(amat * totals_ref[k : k + 1, lanes]) * state + ends_ref[:, k, lanes]
        state_send[pair] = state.astype(BF16)
        for by in range(1, spans):

            @pl.when(me + by < spans)
            def _():
                state_copy(by, pair).start()

        return carry

    lax.fori_loop(0, GROUPS_CH // 2, pair_step, 0)
    pass_on(4, 5)
    finish(3, 4, 5)
    for by in range(1, spans):
        cot_copy(by).wait()
        total_copy(by).wait()
        for pair in range(GROUPS_CH // 2):

            @pl.when(me + by < spans)
            def _():
                state_copy(by, pair).wait_send()

            @pl.when(me - by >= 0)
            def _():
                state_copy(by, pair).wait_recv()


def total_row(values):
    return jnp.concatenate([values[g : g + 1, :] for g in range(GROUPS_CH)], axis=1)


def lane_low(rows):
    return lax.broadcasted_iota(jnp.int32, (rows, LANES), 1) < HEAD_DIM


def pick_rows(index_ref, rows, steps):
    places = row_places(lax.broadcasted_iota(jnp.int32, (rows, 1), 0), steps)
    return (index_ref[...] == places).astype(F32).astype(BF16)


def second_kernel(
    steps,
    nseq,
    spans,
    lengths_ref,
    my_ref,
    tokens_ref,
    packed_ref,
    gains_ref,
    wo_ref,
    wh_ref,
    wm_ref,
    given_ref,
    index_ref,
    states_ref,
    span_totals_ref,
    ends_ref,
    totals_ref,
    delta_ref,
    u_ref,
    xdbl_ref,
    zgate_ref,
    yfull_ref,
    gated_ref,
    x1_ref,
    init_ref,
    dout_ref,
    parts_ref,
    cut_ref,
    du_ref,
    bx_ref,
    cx_ref,
    amat_ref,
    spread_ref,
):
    my = my_ref[0]
    rows = steps * CHUNKS
    spread_decay(packed_ref, amat_ref, spread_ref)
    exponent_steps(delta_ref, lengths_ref, my, nseq, cut_ref, steps)
    du_ref[...] = delta_ref[...] * u_ref[...].astype(F32)
    spread_columns(xdbl_ref, RANK, bx_ref, steps)
    spread_columns(xdbl_ref, RANK + STATE, cx_ref, steps)
    amat = amat_ref[...]

    def chain(k, state):
        decay = jnp.exp(amat * total_row(span_totals_ref[k]))
        came = jnp.concatenate([states_ref[k, g].astype(F32) for g in range(GROUPS_CH // 2)], axis=1)
        return decay * state + came

    state = lax.fori_loop(0, my, chain, jnp.zeros((STATE, DI), F32))
    for k in range(CHUNKS):
        init_ref[:, k, :] = state
        if k < CHUNKS - 1:
            state = jnp.exp(amat * totals_ref[k : k + 1, :]) * state + ends_ref[:, k, :]

    def group_step(group, carry):
        lanes = lanes_of(group)
        amat_g = [spread_ref[st * CHUNKS : (st + 1) * CHUNKS, lanes] for st in range(STATE)]

        def step_fn(step, states):
            cut = cut_ref[tile(step), lanes]
            drive = du_ref[tile(step), lanes]
            new = tuple(
                jnp.exp(cut * amat_g[st]) * states[st] + drive * bx_ref[state_at(step, st), :]
                for st in range(STATE)
            )
            terms = [new[st] * cx_ref[state_at(step, st), :] for st in range(STATE)]
            while len(terms) > 1:
                terms = [a + b for a, b in zip(terms[::2], terms[1::2])]
            yfull_ref[tile(step), lanes] = terms[0]
            return new

        lax.fori_loop(
            0, steps, step_fn, tuple(init_ref[st, :, lanes] for st in range(STATE))
        )
        return carry

    lax.fori_loop(0, GROUPS_CH, group_step, 0)
    skip = packed_ref[DEC:PACK, :].astype(F32)[SKIP - DEC : SKIP - DEC + 1, :]

    def gate_step(pair, carry):
        at = pl.ds(pl.multiple_of(pair * 2 * CHUNKS, 2 * CHUNKS), 2 * CHUNKS)
        yfull = yfull_ref[at, :] + skip * u_ref[at, :].astype(F32)
        yfull_ref[at, :] = yfull
        gate = zgate_ref[at, :]
        gated_ref[at, :] = (yfull * (gate * jax.nn.sigmoid(gate))).astype(BF16)
        return carry

    lax.fori_loop(0, steps // 2, gate_step, 0)
    x1 = tokens_ref[...] + dot_nn(gated_ref[...], wo_ref[...])
    x1_ref[...] = x1
    xn2 = (x1 * norm(x1) * gains_ref[1:2, :].astype(F32)).astype(BF16)
    dout = dot_nn(pick_rows(index_ref, rows, steps), given_ref[...]).astype(BF16)
    dout_ref[...] = dout
    dcontext = dot_nt(dout, wm_ref[...]).astype(BF16).astype(F32)
    qkv = jnp.concatenate([dot_nn(xn2, wh_ref[s]) for s in range(wh_ref.shape[0])], axis=1)
    qkv = qkv.astype(BF16).astype(F32)
    low = lane_low(rows)
    scale = 1.0 / math.sqrt(HEAD_DIM)
    ratio = spans // HEADS
    part = rows // ratio
    for pair in range(HEADS // 2):
        at = pair * LANES
        q = qkv[:, at : at + LANES] * scale
        k = qkv[:, D + at : D + at + LANES]
        v = qkv[:, 2 * D + at : 2 * D + at + LANES]
        d = dcontext[:, at : at + LANES]
        for odd in range(2):
            if odd:
                qd = jnp.where(low, pltpu.roll(q, HEAD_DIM, 1), d)
                kv = jnp.where(low, pltpu.roll(k, HEAD_DIM, 1), v)
            else:
                qd = jnp.where(low, q, pltpu.roll(d, HEAD_DIM, 1))
                kv = jnp.where(low, k, pltpu.roll(v, HEAD_DIM, 1))
            qd = qd.astype(BF16)
            kv = kv.astype(BF16)
            for sub in range(ratio):
                to = (2 * pair + odd) * ratio + sub
                parts_ref[to, 0:part, :] = qd[sub * part : (sub + 1) * part, :]
                parts_ref[to, part:, :] = kv


def attention_kernel(
    steps,
    nseq,
    ratio,
    lengths_ref,
    my_ref,
    parts_ref,
    out_ref,
    score_ref,
    dprob_ref,
    dkv_ref,
):
    block = pl.program_id(0)
    spans = pl.num_programs(0)
    rows = steps * CHUNKS
    part = rows // ratio
    sub = lax.rem(my_ref[0], ratio)
    starts = starts_of(lengths_ref, nseq)

    @pl.when(block == 0)
    def _():
        dkv_ref[...] = jnp.zeros_like(dkv_ref)

    qd = parts_ref[block, 0:part, :]
    low = lane_low(part)
    qd_float = qd.astype(F32)
    both = jnp.concatenate(
        [jnp.where(low, qd_float, 0.0), jnp.where(low, 0.0, qd_float)], axis=0
    ).astype(BF16)
    own = lax.broadcasted_iota(jnp.int32, (part, 1), 0) + sub * part
    query = row_places(own, steps) + block * rows
    first = start_of(query, starts)
    key_local = row_places(lax.broadcasted_iota(jnp.int32, (1, rows), 1), steps)

    def scores(at, top):
        kv = parts_ref[at, part:, :]
        joint = dot_nt(both, kv)
        key = key_local + at * rows
        allowed = (key <= query) & (key >= first)
        score = jnp.where(allowed, joint[:part], NEG)
        score_ref[at] = score
        dprob_ref[at] = joint[part:]
        return jnp.maximum(top, jnp.max(score, axis=1, keepdims=True))

    top = lax.fori_loop(0, block + 1, scores, jnp.full((part, 1), NEG, F32))

    def weigh(at, carry):
        total, context = carry
        prob = jnp.exp(score_ref[at] - top)
        score_ref[at] = prob
        context = context + dot_nn(prob.astype(BF16), parts_ref[at, part:, :])
        return (total + jnp.sum(prob, axis=1, keepdims=True), context)

    total, context = lax.fori_loop(
        0,
        block + 1,
        weigh,
        (jnp.zeros((part, 1), F32), jnp.zeros((part, LANES), F32)),
    )
    inverse = 1.0 / total
    context = context * inverse
    datt = jnp.sum(jnp.where(low, 0.0, context * qd_float), axis=1, keepdims=True)
    key_low = lane_low(rows)

    def back(at, dquery):
        prob = score_ref[at] * inverse
        dscore = (prob * (dprob_ref[at] - datt)).astype(BF16)
        dkv_ref[at] += jnp.where(key_low, dot_tn(dscore, qd), dot_tn(prob.astype(BF16), qd))
        return dquery + dot_nn(dscore, parts_ref[at, part:, :])

    dquery = lax.fori_loop(0, block + 1, back, jnp.zeros((part, LANES), F32))
    scale = 1.0 / math.sqrt(HEAD_DIM)
    out_ref[block, 0:part, :] = jnp.where(low, dquery * scale, context).astype(BF16)

    @pl.when(block == spans - 1)
    def _():
        out_ref[:, part:, :] = dkv_ref[...].astype(BF16)


def third_kernel(
    steps,
    nseq,
    spans,
    lengths_ref,
    my_ref,
    parts_ref,
    gains_ref,
    packed_ref,
    wo_ref,
    wh_ref,
    wm_ref,
    index_ref,
    dout_ref,
    x1_ref,
    gated_ref,
    yfull_ref,
    zgate_ref,
    u_ref,
    delta_ref,
    xdbl_ref,
    totals_ref,
    given_ref,
    merge_grad_ref,
    heads_grad_ref,
    output_grad_ref,
    gain_grad_ref,
    dx1_ref,
    dys_ref,
    dzgate_ref,
    skip_grad_ref,
    ends_ref,
    send_ref,
    cut_ref,
    cx_ref,
    amat_ref,
    spread_ref,
):
    my = my_ref[0]
    rows = steps * CHUNKS
    ratio = spans // HEADS
    part = rows // ratio
    low = lane_low(rows)
    contexts, dqs, dks, dvs = [], [], [], []
    for pair in range(HEADS // 2):
        dqc, dkv = [], []
        for odd in range(2):
            base = (2 * pair + odd) * ratio
            dqc.append(
                jnp.concatenate(
                    [parts_ref[base + sub, 0:part, :].astype(F32) for sub in range(ratio)], axis=0
                )
            )
            dkv.append(sum(parts_ref[base + sub, part:, :].astype(F32) for sub in range(ratio)))
        dqs.append(jnp.where(low, dqc[0], pltpu.roll(dqc[1], HEAD_DIM, 1)))
        contexts.append(jnp.where(low, pltpu.roll(dqc[0], HEAD_DIM, 1), dqc[1]))
        dks.append(jnp.where(low, dkv[0], pltpu.roll(dkv[1], HEAD_DIM, 1)))
        dvs.append(jnp.where(low, pltpu.roll(dkv[0], HEAD_DIM, 1), dkv[1]))
    context = jnp.concatenate(contexts, axis=1).astype(BF16)
    dqkv = jnp.concatenate(dqs + dks + dvs, axis=1).astype(BF16)
    x1 = x1_ref[...]
    dout = dout_ref[...]
    x2 = (x1 + dot_nn(context, wm_ref[...])).astype(BF16)
    given_ref[...] = dot_tn(pick_rows(index_ref, rows, steps), x2).astype(BF16)
    merge_grad_ref[...] = dot_tn(context, dout).astype(BF16)
    gain = gains_ref[1:2, :].astype(F32)
    inverse = norm(x1)
    normal = x1 * inverse
    xn2 = (normal * gain).astype(BF16)
    pieces = wh_ref.shape[0]
    wide = 3 * D // pieces
    dxn2 = jnp.zeros((rows, D), F32)
    for s in range(pieces):
        piece = dqkv[:, s * wide : (s + 1) * wide]
        heads_grad_ref[s] = dot_tn(xn2, piece).astype(BF16)
        dxn2 = dxn2 + dot_nt(piece, wh_ref[s])
    gain_grad_ref[...] = jnp.sum(dxn2 * normal, axis=0, keepdims=True)
    e2 = dxn2 * gain
    dx1 = dout.astype(F32) + inverse * (
        e2 - normal * jnp.mean(e2 * normal, axis=-1, keepdims=True)
    )
    dx1_ref[...] = dx1
    dmixed = dx1.astype(BF16)
    output_grad_ref[...] = dot_tn(gated_ref[...], dmixed).astype(BF16)
    dys_ref[...] = dot_nt(dmixed, wo_ref[...])

    def gate_step(pair, total):
        at = pl.ds(pl.multiple_of(pair * 2 * CHUNKS, 2 * CHUNKS), 2 * CHUNKS)
        dgated = dys_ref[at, :].astype(BF16).astype(F32)
        gate = zgate_ref[at, :]
        s = jax.nn.sigmoid(gate)
        dys = dgated * (gate * s)
        dys_ref[at, :] = dys
        dzgate_ref[at, :] = (dgated * yfull_ref[at, :] * (s * (1.0 + gate * (1.0 - s)))).astype(
            BF16
        )
        return total + dys * u_ref[at, :].astype(F32)

    total = lax.fori_loop(0, steps // 2, gate_step, jnp.zeros((2 * CHUNKS, DI), F32))
    skip_grad_ref[...] = jnp.sum(total, axis=0, keepdims=True)
    spread_decay(packed_ref, amat_ref, spread_ref)
    exponent_steps(delta_ref, lengths_ref, my, nseq, cut_ref, steps)
    spread_columns(xdbl_ref, RANK + STATE, cx_ref, steps)

    def group_step(group, carry):
        lanes = lanes_of(group)
        amat_g = [spread_ref[st * CHUNKS : (st + 1) * CHUNKS, lanes] for st in range(STATE)]

        def step_fn(turn, grads):
            step = steps - 1 - turn
            cut = cut_ref[tile(step), lanes]
            dys = dys_ref[tile(step), lanes]
            return tuple(
                jnp.exp(cut * amat_g[st]) * (grads[st] + dys * cx_ref[state_at(step, st), :])
                for st in range(STATE)
            )

        grads = lax.fori_loop(
            0, steps, step_fn, (jnp.zeros((CHUNKS, LANES), F32),) * STATE
        )
        for st in range(STATE):
            ends_ref[st, :, lanes] = grads[st]
        return carry

    lax.fori_loop(0, GROUPS_CH, group_step, 0)
    amat = amat_ref[...]
    state = jnp.zeros((STATE, DI), F32)
    for k in reversed(range(CHUNKS)):
        state = jnp.exp(amat * totals_ref[k : k + 1, :]) * state + ends_ref[:, k, :]
    send_ref[...] = state.astype(BF16)


def fourth_kernel(
    steps,
    nseq,
    spans,
    lengths_ref,
    my_ref,
    packed_ref,
    span_totals_ref,
    grads_ref,
    init_ref,
    ends_ref,
    totals_ref,
    delta_ref,
    u_ref,
    xdbl_ref,
    dys_ref,
    conv_ref,
    ext_ref,
    skip_grad_ref,
    dext_ref,
    spill_ref,
    small_ref,
    cut_ref,
    du_ref,
    bx_ref,
    cx_ref,
    db_ref,
    dc_ref,
    decay_ref,
    kept_ref,
    state_ref,
    bgrad_ref,
    adelta_ref,
    arrive_ref,
    dxdbl_ref,
    amat_ref,
    spread_ref,
):
    my = my_ref[0]
    rows = steps * CHUNKS
    starts = starts_of(lengths_ref, nseq)
    spread_decay(packed_ref, amat_ref, spread_ref)
    exponent_steps(delta_ref, lengths_ref, my, nseq, cut_ref, steps)
    du_ref[...] = delta_ref[...] * u_ref[...].astype(F32)
    spread_columns(xdbl_ref, RANK, bx_ref, steps)
    spread_columns(xdbl_ref, RANK + STATE, cx_ref, steps)
    amat = amat_ref[...]

    def chain(turn, state):
        k = spans - 1 - turn
        decay = jnp.exp(amat * total_row(span_totals_ref[k]))
        return decay * state + grads_ref[k].astype(F32)

    state = lax.fori_loop(0, spans - 1 - my, chain, jnp.zeros((STATE, DI), F32))
    for k in reversed(range(CHUNKS)):
        arrive_ref[:, k, :] = state
        if k:
            state = jnp.exp(amat * totals_ref[k : k + 1, :]) * state + ends_ref[:, k, :]
    db_ref[...] = jnp.zeros_like(db_ref)
    dc_ref[...] = jnp.zeros_like(dc_ref)
    half = STATE // 2

    def sum_of(terms):
        while len(terms) > 1:
            terms = [a + b for a, b in zip(terms[::2], terms[1::2])]
        return terms[0]

    def group_step(group, carry):
        lanes = lanes_of(group)
        for part in range(2):
            states = range(part * half, (part + 1) * half)
            amat_g = [spread_ref[st * CHUNKS : (st + 1) * CHUNKS, lanes] for st in states]

            def forward(step, held):
                cut = cut_ref[tile(step), lanes]
                drive = du_ref[tile(step), lanes]
                out = []
                for i, st in enumerate(states):
                    at = state_at(step, st)
                    decay = jnp.exp(cut * amat_g[i])
                    kept = decay * held[i]
                    new = kept + drive * bx_ref[at, :]
                    decay_ref[at, :] = decay
                    kept_ref[at, :] = kept
                    state_ref[at, :] = new
                    out.append(new)
                return tuple(out)

            lax.fori_loop(0, steps, forward, tuple(init_ref[st, :, lanes] for st in states))

            def backward(turn, held):
                grads, sums = held
                step = steps - 1 - turn
                delta = delta_ref[tile(step), lanes]
                drive = du_ref[tile(step), lanes]
                dys = dys_ref[tile(step), lanes]
                new, totals, by_b, by_a = [], [], [], []
                for i, st in enumerate(states):
                    at = state_at(step, st)
                    grad = grads[i] + dys * cx_ref[at, :]
                    new.append(decay_ref[at, :] * grad)
                    through = grad * kept_ref[at, :]
                    totals.append(sums[i] + through * delta)
                    by_a.append(amat_g[i] * through)
                    by_b.append(grad * bx_ref[at, :])
                    dc_ref[at, :] += state_ref[at, :] * dys
                    db_ref[at, :] += grad * drive
                if part:
                    bgrad_ref[tile(step), lanes] += sum_of(by_b)
                    adelta_ref[tile(step), lanes] += sum_of(by_a)
                else:
                    bgrad_ref[tile(step), lanes] = sum_of(by_b)
                    adelta_ref[tile(step), lanes] = sum_of(by_a)
                return (tuple(new), tuple(totals))

            _, sums = lax.fori_loop(
                0,
                steps,
                backward,
                (
                    tuple(arrive_ref[st, :, lanes] for st in states),
                    (jnp.zeros((CHUNKS, LANES), F32),) * half,
                ),
            )
            for i, st in enumerate(states):
                row = jnp.sum(sums[i], axis=0, keepdims=True)
                small_ref[DEC + st : DEC + st + 1, lanes] = row * amat_g[i][0:1, :]
        return carry

    lax.fori_loop(0, GROUPS_CH, group_step, 0)
    small = packed_ref[DEC:PACK, :].astype(F32)
    taps = small[TAPS - DEC : TAPS - DEC + CONV, :]
    skip = small[SKIP - DEC : SKIP - DEC + 1, :]

    def delta_step(step, total):
        at = tile(step)
        bgrad = bgrad_ref[at, :]
        delta = delta_ref[at, :]
        u = conv_ref[at, :]
        u = (u * jax.nn.sigmoid(u)).astype(BF16).astype(F32)
        ddelta = u * bgrad + adelta_ref[at, :]
        dtpre = (ddelta * (1.0 - jnp.exp(-delta))).astype(BF16).astype(F32)
        adelta_ref[at, :] = dtpre
        bgrad_ref[at, :] = dys_ref[at, :] * skip + delta * bgrad
        return total + dtpre

    total = lax.fori_loop(0, steps, delta_step, jnp.zeros((CHUNKS, DI), F32))
    small_ref[STEPB : STEPB + 1, :] = jnp.sum(total, axis=0, keepdims=True)
    small_ref[SKIP : SKIP + 1, :] = skip_grad_ref[...]
    small_ref[GAINS:, :] = jnp.zeros((PACK - GAINS, DI), F32)
    dtpre = adelta_ref[...].astype(BF16)
    steplow = xdbl_ref[:, 0:RANK].astype(BF16)
    small_ref[STEP : STEP + RANK, :] = dot_tn(steplow, dtpre)
    dxdbl_ref[:, 0:RANK] = dot_nt(dtpre, packed_ref[STEP : STEP + RANK, :])
    lane = lax.broadcasted_iota(jnp.int32, (CHUNKS, 2 * STATE), 1)

    def gather_step(step, carry):
        total = jnp.zeros((CHUNKS, 2 * STATE), F32)
        for st in range(STATE):
            at = state_at(step, st)
            total = jnp.where(lane == st, jnp.sum(db_ref[at, :], axis=1, keepdims=True), total)
            total = jnp.where(
                lane == STATE + st, jnp.sum(dc_ref[at, :], axis=1, keepdims=True), total
            )
        dxdbl_ref[tile(step), RANK:] = total
        return carry

    lax.fori_loop(0, steps, gather_step, 0)
    dxdbl = dxdbl_ref[...].astype(BF16)
    small_ref[SEL : SEL + STEP, :] = dot_tn(dxdbl, u_ref[...])
    bgrad_ref[...] += dot_nn(dxdbl, packed_ref[SEL : SEL + STEP, :])
    dext_ref[...] = jnp.zeros_like(dext_ref)
    zero = jnp.zeros((CHUNKS, DI), F32)

    def conv_step(step, totals):
        at = tile(step)
        dconv = bgrad_ref[at, :] * silu_slope(conv_ref[at, :])
        places = lax.broadcasted_iota(jnp.int32, (CHUNKS, 1), 0) * steps + step + my * rows
        first = start_of(places, starts)
        out = []
        for k in range(CONV):
            to = pl.ds(pl.multiple_of((step + k) * CHUNKS, CHUNKS), CHUNKS)
            inside = jnp.where(places - (CONV - 1) + k >= first, dconv, 0.0)
            out.append(totals[k] + inside * ext_ref[to, :])
            dext_ref[to, :] += taps[k : k + 1, :] * inside
        return tuple(out) + (totals[CONV] + dconv,)

    totals = lax.fori_loop(0, steps, conv_step, (zero,) * (CONV + 1))
    for k in range(CONV):
        small_ref[TAPS + k : TAPS + k + 1, :] = jnp.sum(totals[k], axis=0, keepdims=True)
    small_ref[BIAS : BIAS + 1, :] = jnp.sum(totals[CONV], axis=0, keepdims=True)
    chunk = lax.broadcasted_iota(jnp.int32, (CHUNKS, DI), 0)
    spill_ref[...] = jnp.zeros_like(spill_ref)
    for k in range(CONV - 1):
        block = dext_ref[k * CHUNKS : (k + 1) * CHUNKS, :]
        spill_ref[k : k + 1, :] = block[0:1, :]
        late = (steps - CONV + 1 + k) * CHUNKS + EDGE
        moved = pltpu.roll(block, CHUNKS - 1, 0)
        dext_ref[late : late + CHUNKS, :] += jnp.where(chunk < CHUNKS - 1, moved, 0.0)


def fifth_kernel(
    steps,
    tokens_ref,
    gains_ref,
    wi_ref,
    dext_ref,
    spill_ref,
    dzgate_ref,
    dx1_ref,
    token_grad_ref,
    input_grad_ref,
    gain_grad_ref,
    dxin_ref,
    dx_ref,
    row_ref,
):
    rows = steps * CHUNKS
    gain = gains_ref[0:1, :].astype(F32)
    x = tokens_ref[...]
    inverse = norm(x)
    normal = x * inverse
    xn1 = (normal * gain).astype(BF16)
    dxin_ref[...] = dext_ref[EDGE:, :]
    for k in range(CONV - 1):
        at = (steps - CONV + 2 + k) * CHUNKS - 1
        dxin_ref[at : at + 1, :] += spill_ref[k : k + 1, :]
    pieces = wi_ref.shape[0]
    wide = 2 * DI // pieces
    dxn1 = jnp.zeros((rows, D), F32)
    for s in range(pieces):
        at = s * wide % DI
        source = dxin_ref if s < pieces // 2 else dzgate_ref
        piece = source[:, at : at + wide].astype(BF16)
        input_grad_ref[s] = dot_tn(xn1, piece).astype(BF16)
        dxn1 = dxn1 + dot_nt(piece, wi_ref[s])
    gain_grad_ref[...] = jnp.sum(dxn1 * normal, axis=0, keepdims=True)
    e1 = dxn1 * gain
    dx_ref[...] = dx1_ref[...] + inverse * (
        e1 - normal * jnp.mean(e1 * normal, axis=-1, keepdims=True)
    )
    for part in range(D // LANES):
        lanes = slice(part * LANES, (part + 1) * LANES)
        for step in range(steps):
            row_ref[pl.ds(step, CHUNKS, stride=steps), :] = dx_ref[
                step * CHUNKS : (step + 1) * CHUNKS, lanes
            ]
        token_grad_ref[:, lanes] = row_ref[...]


def exchange_kernel(spans, count, *refs):
    mine, wholes = refs[:count], refs[count : 2 * count]
    send_sem, recv_sem, own_sem = refs[2 * count :]
    me = lax.axis_index("seq")
    greet([at_seq(lax.rem(me + by, spans)) for by in range(1, spans)])
    copies = []
    for by in range(1, spans):
        for k in range(count):
            copy = pltpu.make_async_remote_copy(
                src_ref=mine[k],
                dst_ref=wholes[k].at[me],
                send_sem=send_sem.at[k, by],
                recv_sem=recv_sem.at[k, by],
                **at_seq(lax.rem(me + by, spans)),
            )
            copy.start()
            copies.append(copy)
    for k in range(count):
        copy = pltpu.make_async_copy(mine[k], wholes[k].at[me], own_sem.at[k])
        copy.start()
        copies.append(copy)
    for copy in copies:
        copy.wait()


def reduce_kernel(count, shards, spans, *refs):
    grads, sums = refs[:count], refs[count : 2 * count]
    near, held, far, parts = (refs[(2 + i) * count : (3 + i) * count] for i in range(4))
    near_sem, far_sem, part_sem, last_sem = refs[6 * count :]
    me = lax.axis_index("seq")
    shard, core, chip, partner, others = shard_peers(shards)
    chips = shards // 2
    ring = [lax.rem(me + by, spans) for by in range(1, spans)]
    greet([at_shard(partner)] + [at_shard(o) for o in others] + [at_seq(to) for to in ring])

    def send(source, target, sems, at, to):
        copy = pltpu.make_async_remote_copy(
            src_ref=source, dst_ref=target, send_sem=sems.at[(0, *at)], recv_sem=sems.at[(1, *at)], **to
        )
        copy.start()
        return copy

    first = [
        [
            send(grads[k].at[x * 2 + 1 - core], near[k].at[x], near_sem, (k, x), at_shard(partner))
            for x in range(chips)
        ]
        for k in range(count)
    ]
    second = []
    for k in range(count):
        for x in range(chips):
            first[k][x].wait_recv()
            held[k][x] = (
                grads[k][x * 2 + core].astype(F32) + near[k][x].astype(F32)
            ).astype(BF16)
        second.append(
            [
                send(
                    held[k].at[lax.rem(chip + by, chips)],
                    far[k].at[by - 1],
                    far_sem,
                    (k, by),
                    at_shard(others[by - 1]),
                )
                for by in range(1, chips)
            ]
        )
    third = []
    for k in range(count):
        total = held[k][chip].astype(F32)
        for by in range(1, chips):
            second[k][by - 1].wait_recv()
            total = total + far[k][by - 1].astype(F32)
        near[k][0] = total.astype(BF16)
        third.append(
            [
                send(near[k].at[0, ring[by - 1]], parts[k].at[by], part_sem, (k, by), at_seq(ring[by - 1]))
                for by in range(1, spans)
            ]
        )
    fourth = []
    for k in range(count):
        total = near[k][0, me].astype(F32)
        for by in range(1, spans):
            third[k][by - 1].wait_recv()
            total = total + parts[k][by].astype(F32)
        sums[k][me] = total.astype(BF16)
        fourth.append(
            [
                send(sums[k].at[me], sums[k].at[me], last_sem, (k, by), at_seq(ring[by - 1]))
                for by in range(1, spans)
            ]
        )
    for group in first + second + third:
        for copy in group:
            copy.wait_send()
    for group in fourth:
        for copy in group:
            copy.wait()


def shape(*dims, kind=F32):
    return jax.ShapeDtypeStruct(dims, kind)


def vmem(*dims, kind=F32):
    return pltpu.VMEM(dims, kind)


def talk(kernel, name, number, outs, scratch, *args):
    return pl.pallas_call(
        kernel,
        out_shape=outs,
        in_specs=[VMEM] * len(args),
        out_specs=[VMEM] * len(outs),
        scratch_shapes=scratch,
        compiler_params=params(collective_id=number, has_side_effects=True),
        name=name,
    )(*args)


def exchanged(number, spans, *values):
    sems = [pltpu.SemaphoreType.DMA((len(values), spans))] * 2
    return talk(
        functools.partial(exchange_kernel, spans, len(values)),
        "exchange%d" % number,
        number,
        [shape(spans, *v.shape, kind=v.dtype) for v in values],
        sems + [pltpu.SemaphoreType.DMA((len(values),))],
        *values,
    )


def call(kernel, name, outs, scratch, scalars, *args, number=None):
    more = {} if number is None else {"collective_id": number, "has_side_effects": True}
    return pl.pallas_call(
        kernel,
        out_shape=outs,
        in_specs=[SMEM] * len(scalars) + [VMEM] * len(args),
        out_specs=jax.tree.map(lambda _: VMEM, outs),
        scratch_shapes=scratch,
        compiler_params=params(**more),
        name=name,
    )(*scalars, *args)


def step_apart(value, axis, by):
    count = lax.axis_size(axis)
    first, last = (max(0, -by), min(count, count - by))
    return lax.ppermute(value, axis, [(source, source + by) for source in range(first, last)])


def per_device(
    tokens,
    cotangent,
    positions,
    lengths,
    mixer_gain,
    input_weight,
    kernel_weight,
    kernel_bias,
    select_weight,
    step_weight,
    step_bias,
    decay_log,
    skip_scale,
    output_weight,
    attention_gain,
    heads_weight,
    merge_weight,
):
    spans = lax.axis_size("seq")
    shards = lax.axis_size("shard")
    my = lax.axis_index("seq")
    rows = tokens.shape[1]
    steps = rows // CHUNKS
    share = rows // spans
    nseq = lengths.shape[1]
    ratio = spans // HEADS
    part = rows // ratio
    width = DI // shards

    table = positions[0].reshape(spans, spans, share)
    index = (
        lax.dynamic_index_in_dim(table, my, axis=1, keepdims=False) - my * rows
    ).reshape(1, rows)
    scalars = (lengths[0], my.astype(jnp.int32).reshape(1))
    dma = pltpu.SemaphoreType.DMA
    spread = [vmem(STATE, DI), vmem(STATE * CHUNKS, DI)]
    columns = vmem(rows * STATE, LANES)
    plane = vmem(rows, DI)
    gain_len = D // shards
    halves = GROUPS_CH // 2
    weights = [(D, 2 * width), (width, D), (D, 3 * D // shards), (gain_len, D)]
    (
        x,
        wi,
        wo,
        wh,
        wm,
        packed_w,
        gains,
        given_cot,
        states,
        span_totals,
        ext,
        zgate,
        conv,
        u,
        delta,
        xdbl,
        ends,
        totals,
    ) = call(
        functools.partial(start_kernel, steps, nseq, shards, spans),
        "start",
        (
            [shape(rows, D)]
            + [shape(shards, *w, kind=BF16) for w in weights]
            + [
                shape(PACK, DI, kind=BF16),
                shape(CHUNKS, D),
                shape(spans, share, D, kind=BF16),
                shape(spans, halves, STATE, 2 * LANES, kind=BF16),
                shape(spans, GROUPS_CH, LANES),
                shape(EDGE + rows, DI),
                shape(rows, DI),
                shape(rows, DI),
                shape(rows, DI, kind=BF16),
                shape(rows, DI),
                shape(rows, STEP),
                shape(STATE, CHUNKS, DI),
                shape(CHUNKS, DI),
            ]
        ),
        [vmem(rows, LANES), vmem(PACK, width)]
        + [vmem(*w, kind=BF16) for w in weights]
        + [
            vmem(PACK, width, kind=BF16),
            vmem(2 * CHUNKS, gain_len, kind=BF16),
            vmem(shards, PACK, width, kind=BF16),
            vmem(shards, 2 * CHUNKS, gain_len, kind=BF16),
            vmem(2 * CHUNKS, D, kind=BF16),
            vmem(halves, STATE, 2 * LANES, kind=BF16),
            vmem(GROUPS_CH, LANES),
            plane,
            plane,
            columns,
        ]
        + spread
        + [
            dma((2, 6, shards - 1)),
            dma((2, spans)),
            dma((2,)),
            dma((2, spans, halves)),
            dma((2, spans)),
        ],
        scalars[:1],
        tokens[0],
        cotangent[0].reshape(spans, share, D),
        mixer_gain[None],
        attention_gain[None],
        select_weight,
        step_weight,
        decay_log,
        kernel_weight,
        kernel_bias[None],
        step_bias[None],
        skip_scale[None],
        input_weight,
        output_weight,
        heads_weight,
        merge_weight,
        number=0,
    )
    wo, wm = wo.reshape(DI, D), wm.reshape(D, D)
    given_cot = given_cot.reshape(rows, D)
    yfull, gated, x1, init, dout, parts = call(
        functools.partial(second_kernel, steps, nseq, spans),
        "second",
        (
            shape(rows, DI),
            shape(rows, DI, kind=BF16),
            shape(rows, D),
            shape(STATE, CHUNKS, DI),
            shape(rows, D, kind=BF16),
            shape(spans, part + rows, LANES, kind=BF16),
        ),
        [plane, plane, columns, columns] + spread,
        scalars,
        x,
        packed_w,
        gains,
        wo,
        wh,
        wm,
        given_cot,
        index,
        states,
        span_totals,
        ends,
        totals,
        delta,
        u,
        xdbl,
        zgate,
    )
    parts = lax.all_to_all(parts, "seq", split_axis=0, concat_axis=0, tiled=True)
    whole = pl.BlockSpec((spans, part + rows, LANES), lambda i: (0, 0, 0))
    parts = pl.pallas_call(
        functools.partial(attention_kernel, steps, nseq, ratio),
        grid=(spans,),
        out_shape=shape(spans, part + rows, LANES, kind=BF16),
        in_specs=[SMEM, SMEM, whole],
        out_specs=whole,
        scratch_shapes=[
            vmem(spans, part, rows),
            vmem(spans, part, rows),
            vmem(spans, rows, LANES),
        ],
        compiler_params=params(),
        name="attention",
    )(*scalars, parts)
    parts = lax.all_to_all(parts, "seq", split_axis=0, concat_axis=0, tiled=True)
    (
        given,
        merge_grad,
        heads_grad,
        output_grad,
        gain_two_grad,
        dx1,
        dys,
        dzgate,
        skip_grad,
        back_ends,
        back_send,
    ) = call(
        functools.partial(third_kernel, steps, nseq, spans),
        "third",
        (
            shape(rows, D, kind=BF16),
            shape(D, D, kind=BF16),
            shape(shards, D, 3 * D // shards, kind=BF16),
            shape(DI, D, kind=BF16),
            shape(1, D),
            shape(rows, D),
            shape(rows, DI),
            shape(rows, DI, kind=BF16),
            shape(1, DI),
            shape(STATE, CHUNKS, DI),
            shape(STATE, DI, kind=BF16),
        ),
        [plane, columns] + spread,
        scalars,
        parts,
        gains,
        packed_w,
        wo,
        wh,
        wm,
        index,
        dout,
        x1,
        gated,
        yfull,
        zgate,
        u,
        delta,
        xdbl,
        totals,
    )
    output = lax.all_to_all(
        given.reshape(spans, share, D), "seq", split_axis=0, concat_axis=0, tiled=True
    ).reshape(rows, D)
    (grads,) = exchanged(2, spans, back_send)
    dext, spill, small = call(
        functools.partial(fourth_kernel, steps, nseq, spans),
        "fourth",
        (shape(EDGE + rows, DI), shape(CHUNKS, DI), shape(PACK, DI)),
        [plane, plane]
        + [columns] * 7
        + [plane, plane, vmem(STATE, CHUNKS, DI), vmem(rows, STEP)]
        + spread,
        scalars,
        packed_w,
        span_totals,
        grads,
        init,
        back_ends,
        totals,
        delta,
        u,
        xdbl,
        dys,
        conv,
        ext,
        skip_grad,
    )
    spill = step_apart(spill, "seq", -1)
    token_grad, input_grad, gain_one_grad = call(
        functools.partial(fifth_kernel, steps),
        "fifth",
        (shape(rows, D), shape(shards, D, 2 * width, kind=BF16), shape(1, D)),
        [plane, vmem(rows, D), vmem(rows, LANES)],
        (),
        x,
        gains,
        wi,
        dext,
        spill,
        dzgate,
        dx1,
    )

    gain_grads = (
        jnp.concatenate([gain_one_grad, gain_two_grad], axis=0)
        .reshape(2, shards, D // shards)
        .transpose(1, 0, 2)
        .reshape(shards, 1, width)
    )
    small = small.reshape(PACK, shards, width).transpose(1, 0, 2)
    small = jnp.concatenate(
        [small[:, :GAINS], gain_grads, jnp.zeros((shards, PACK - GAINS - 1, width), F32)], axis=1
    )
    grads = [
        v.astype(BF16).reshape(shards, spans, -1, v.shape[-1])
        for v in (merge_grad, heads_grad, output_grad, input_grad, small)
    ]
    count, chips = len(grads), shards // 2
    sums = talk(
        functools.partial(reduce_kernel, count, shards, spans),
        "reduce",
        3,
        [shape(*v.shape[1:], kind=BF16) for v in grads],
        [vmem(chips, *v.shape[1:], kind=BF16) for v in grads]
        + [vmem(chips, *v.shape[1:], kind=BF16) for v in grads]
        + [vmem(max(chips - 1, 1), *v.shape[1:], kind=BF16) for v in grads]
        + [vmem(*v.shape[1:], kind=BF16) for v in grads]
        + [dma((2, count, chips))] * 2
        + [dma((2, count, spans))] * 2,
        *grads,
    )
    merge_grad, heads_grad, output_grad, input_grad, small = (
        v.reshape(-1, v.shape[-1]).astype(F32) for v in sums
    )
    return (
        output[None],
        token_grad[None],
        small[GAINS, :gain_len],
        input_grad,
        small[TAPS : TAPS + CONV],
        small[BIAS],
        small[SEL : SEL + STEP].T,
        small[STEP : STEP + RANK],
        small[STEPB],
        small[DEC : DEC + STATE].T,
        small[SKIP],
        output_grad,
        small[GAINS, gain_len:],
        heads_grad,
        merge_grad,
    )


def solution(mesh):
    return jax.shard_map(
        per_device,
        mesh=mesh,
        in_specs=(
            P("shard", "seq", None),
            P("shard", "seq", None),
            P("shard", None),
            P("shard", None),
            P("shard"),
            P(None, "shard"),
            P(None, "shard"),
            P("shard"),
            P("shard", None),
            P(None, "shard"),
            P("shard"),
            P("shard", None),
            P("shard"),
            P("shard", None),
            P("shard"),
            P(None, "shard"),
            P("shard", None),
        ),
        out_specs=(
            P("shard", "seq", None),
            P("shard", "seq", None),
            P("shard"),
            P(None, "shard"),
            P(None, "shard"),
            P("shard"),
            P("shard", None),
            P(None, "shard"),
            P("shard"),
            P("shard", None),
            P("shard"),
            P("shard", None),
            P("shard"),
            P(None, "shard"),
            P("shard", None),
        ),
        check_vma=False,
    )
```

```python
import functools
import math

import jax
import jax.numpy as jnp
from jax import lax
from jax.experimental import pallas as pl
from jax.experimental.pallas import tpu as pltpu
from jax.sharding import PartitionSpec as P

D = 512
DI = 1024
RANK = 32
HEADS = 8
STATE = 16
HEAD_DIM = 64
CONV = 4
CHUNKS = 8
LANES = 128
GROUPS_CH = DI // LANES
EDGE = (CONV - 1) * CHUNKS

SEL = 0
STEP = RANK + 2 * STATE
DEC = STEP + RANK
TAPS = DEC + STATE
BIAS = TAPS + CONV
STEPB = BIAS + 1
SKIP = STEPB + 1
GAINS = SKIP + 1
PACK = 128

EPS = 1e-05
NEG = -1e30
CUT = 1e30
F32 = jnp.float32
BF16 = jnp.bfloat16

VMEM = pl.BlockSpec(memory_space=pltpu.VMEM)
SMEM = pl.BlockSpec(memory_space=pltpu.SMEM)


def params(**more):
    return pltpu.CompilerParams(vmem_limit_bytes=60 << 20, **more)


def dot_nn(left, right):
    return lax.dot_general(left, right, (((1,), (0,)), ((), ())), preferred_element_type=F32)


def dot_nt(left, right):
    return lax.dot_general(left, right, (((1,), (1,)), ((), ())), preferred_element_type=F32)


def dot_tn(left, right):
    return lax.dot_general(left, right, (((0,), (0,)), ((), ())), preferred_element_type=F32)


def row_places(rows, steps):
    return (rows & (CHUNKS - 1)) * steps + (rows >> 3)


def starts_of(lengths_ref, nseq):
    starts = [jnp.int32(0)]
    for k in range(nseq - 1):
        starts.append(starts[-1] + lengths_ref[k])
    return starts


def start_of(places, starts):
    first = jnp.zeros_like(places)
    for start in starts[1:]:
        first = jnp.where(places >= start, start, first)
    return first


def begin_of(places, starts):
    found = places == starts[0]
    for start in starts[1:]:
        found = found | (places == start)
    return found


def norm(value):
    return lax.rsqrt(jnp.mean(value * value, axis=-1, keepdims=True) + EPS)


def silu_slope(value):
    s = jax.nn.sigmoid(value)
    return s * (1.0 + value * (1.0 - s))


def tile(step):
    return pl.ds(pl.multiple_of(step * CHUNKS, CHUNKS), CHUNKS)


def lanes_of(group):
    return pl.ds(pl.multiple_of(group * LANES, LANES), LANES)


def spread_decay(packed_ref, amat_ref, spread_ref):
    amat = -jnp.exp(packed_ref[DEC : DEC + STATE, :].astype(F32)) * math.log2(math.e)
    amat_ref[...] = amat
    for st in range(STATE):
        spread_ref[st * CHUNKS : (st + 1) * CHUNKS, :] = jnp.broadcast_to(
            amat[st : st + 1, :], (CHUNKS, DI)
        )


def spread_columns(source_ref, first, target_ref, steps):
    def one(step, carry):
        values = source_ref[tile(step), :]
        base = step * (STATE * CHUNKS)
        for st in range(STATE):
            at = pl.ds(pl.multiple_of(base + st * CHUNKS, CHUNKS), CHUNKS)
            column = values[:, first + st : first + st + 1]
            target_ref[at, :] = jnp.broadcast_to(column, (CHUNKS, LANES))
        return carry

    lax.fori_loop(0, steps, one, 0, unroll=2)


def state_at(step, st):
    return pl.ds(pl.multiple_of(step * (STATE * CHUNKS) + st * CHUNKS, CHUNKS), CHUNKS)


def at_seq(index):
    return {"device_id": {"seq": index}, "device_id_type": pl.DeviceIdType.MESH}


def at_shard(index):
    return {"device_id": {"shard": index}, "device_id_type": pl.DeviceIdType.MESH}


def greet(peers):
    barrier = pltpu.get_barrier_semaphore()
    for peer in peers:
        pl.semaphore_signal(barrier, inc=1, **peer)
    pl.semaphore_wait(barrier, len(peers))


def shard_peers(shards):
    shard = lax.axis_index("shard")
    core, chip = lax.rem(shard, 2), lax.div(shard, 2)
    partner = chip * 2 + 1 - core
    others = [lax.rem(chip + by, shards // 2) * 2 + core for by in range(1, shards // 2)]
    return shard, core, chip, partner, others


class Refs:
    def __init__(self, names, refs):
        for name, ref in zip(names, refs, strict=True):
            setattr(self, name, ref)


FORWARD_IN = (
    "lengths", "tokens", "cot", "index", "mixer", "attention", "select", "stepw", "decay", "taps", "bias",
    "stepb", "skip", "wi", "wo", "wh", "wm",
)
KEPT = (
    "x", "wi_all", "wo_all", "wh_all", "wm_all", "packed", "gains", "span_totals", "ext", "zgate", "conv",
    "u", "delta", "xdbl", "totals", "yfull", "gated", "x1", "init", "dout", "bx", "cx", "cut", "du",
    "context_send",
)
FORWARD_OUT = tuple(k + "_out" for k in KEPT) + ("dq_in", "dkv_in")
FORWARD_SCRATCH = KEPT + (
    "given", "states", "ends", "row", "small", "wi_send", "wo_send", "wh_send", "wm_send", "packed_send",
    "gains_send", "packed_all", "gains_all", "before", "state_send", "total_send", "amat", "spread", "q_send",
    "d_send", "kv_send", "q_in", "d_in", "kv_in", "kvt", "score", "dprob", "dkv", "dq_send", "dkv_send",
    "causal", "gather_sem", "cot_sem", "edge_sem", "state_sem", "total_sem", "q_sem", "d_sem", "kv_sem",
    "dq_sem", "dkv_sem", "keep_sem",
)


def forward_kernel(steps, nseq, shards, spans, *refs):
    r = Refs(FORWARD_IN + FORWARD_OUT + FORWARD_SCRATCH, refs)
    rows = steps * CHUNKS
    width = DI // shards
    me = lax.axis_index("seq")
    shard, core, chip, partner, others = shard_peers(shards)
    far = len(others)
    ring = [lax.rem(me + by, spans) for by in range(1, spans)]
    greet([at_shard(partner)] + [at_shard(o) for o in others] + [at_seq(to) for to in ring])

    def copy(source, target, sems, at, to):
        return pltpu.make_async_remote_copy(
            src_ref=source, dst_ref=target, send_sem=sems.at[(0, *at)], recv_sem=sems.at[(1, *at)], **to
        )

    sources = (r.wi_send, r.packed_send, r.gains_send, r.wo_send, r.wh_send, r.wm_send)
    wholes = (r.wi_all, r.packed_all, r.gains_all, r.wo_all, r.wh_all, r.wm_all)

    def sent(k, i):
        to = partner if i == far else others[i]
        return copy(sources[k], wholes[k].at[shard], r.gather_sem, (k, i), at_shard(to))

    def passed(k, i):
        came = lax.rem(chip + far - i, far + 1) * 2 + core
        return copy(
            wholes[k].at[came], wholes[k].at[came], r.gather_sem, (k, far + 1 + i), at_shard(partner)
        )

    def spread(*which):
        for k in which:
            for i in range(far + 1):
                sent(k, i).start()
        for k in which:
            wholes[k][shard] = sources[k][...]

    def pass_on(*which):
        for i in range(far):
            for k in which:
                sent(k, i).wait_recv()
                passed(k, i).start()

    def finish(*which):
        for k in which:
            for i in range(far):
                sent(k, i).wait_send()
                passed(k, i).wait()
            sent(k, far).wait()

    r.wi_send[...] = r.wi[...].astype(BF16)
    r.small[...] = jnp.zeros_like(r.small)
    for source, first in (
        (r.select, SEL),
        (r.decay, DEC),
        (r.stepw, STEP),
        (r.taps, TAPS),
        (r.bias, BIAS),
        (r.stepb, STEPB),
        (r.skip, SKIP),
    ):
        r.small[first : first + source.shape[0], :] = source[...]
    r.packed_send[...] = r.small[...].astype(BF16)
    lane = lax.broadcasted_iota(jnp.int32, (2 * CHUNKS, D // shards), 0)
    r.gains_send[...] = jnp.where(lane == 0, r.mixer[...], r.attention[...]).astype(BF16)
    spread(0, 1, 2)
    last = r.tokens.at[pl.ds(rows - 2 * CHUNKS, 2 * CHUNKS)]
    edge = copy(last, r.before, r.edge_sem, (), at_seq(ring[0]))
    edge.start()

    def cot_copy(by):
        return copy(
            r.cot.at[ring[by - 1]], r.given.at[me], r.cot_sem, (by,), at_seq(ring[by - 1])
        )

    for by in range(1, spans):
        cot_copy(by).start()
    r.given[me] = r.cot[me]
    r.wo_send[...] = r.wo[...].astype(BF16)
    r.wh_send[...] = r.wh[...].astype(BF16)
    r.wm_send[...] = r.wm[...].astype(BF16)
    for part in range(D // LANES):
        lanes = slice(part * LANES, (part + 1) * LANES)
        r.row[...] = r.tokens[:, lanes].astype(F32)
        for step in range(steps):
            r.x[step * CHUNKS : (step + 1) * CHUNKS, lanes] = r.row[
                pl.ds(step, CHUNKS, stride=steps), :
            ]
    pass_on(0, 1, 2)
    spread(3, 4, 5)
    finish(0, 1, 2)
    edge.wait()

    starts = starts_of(r.lengths, nseq)
    r.packed[...] = jnp.concatenate([r.packed_all[s] for s in range(shards)], axis=1)
    gains = jnp.concatenate([r.gains_all[s].astype(F32) for s in range(shards)], axis=1)
    r.gains[...] = gains[:CHUNKS]
    gain = gains[0:1]
    x = r.x[...]
    xn1 = (x * norm(x) * gain).astype(BF16)
    before = r.before[...].astype(F32)
    edge_n = (before * norm(before) * gain).astype(BF16)
    wide = 2 * DI // shards
    for s in range(shards):
        piece = dot_nn(xn1, r.wi_all[s])
        if s < shards // 2:
            r.ext[EDGE:, s * wide : (s + 1) * wide] = piece
        else:
            at = (s - shards // 2) * wide
            r.zgate[:, at : at + wide] = piece
    edge_x = jnp.concatenate([dot_nn(edge_n, r.wi_all[s]) for s in range(shards // 2)], axis=1)
    count = r.before.shape[0]
    chunk = lax.broadcasted_iota(jnp.int32, (CHUNKS, DI), 0)
    for k in range(CONV - 1):
        late = (steps - CONV + 1 + k) * CHUNKS + EDGE
        moved = pltpu.roll(r.ext[late : late + CHUNKS, :], 1, 0)
        at = count - CONV + 1 + k
        r.ext[k * CHUNKS : (k + 1) * CHUNKS, :] = jnp.where(
            chunk == 0, jnp.broadcast_to(edge_x[at : at + 1, :], (CHUNKS, DI)), moved
        )
    small = r.packed[DEC:PACK, :].astype(F32)
    taps = small[TAPS - DEC : TAPS - DEC + CONV, :]
    bias = small[BIAS - DEC : BIAS - DEC + 1, :]

    def conv_step(step, carry):
        places = lax.broadcasted_iota(jnp.int32, (CHUNKS, 1), 0) * steps + step + me * rows
        first = start_of(places, starts)
        total = jnp.broadcast_to(bias, (CHUNKS, DI))
        for k in range(CONV):
            at = pl.ds(pl.multiple_of((step + k) * CHUNKS, CHUNKS), CHUNKS)
            inside = places - (CONV - 1) + k >= first
            total = total + jnp.where(inside, taps[k : k + 1, :] * r.ext[at, :], 0.0)
        r.conv[tile(step), :] = total
        r.du[tile(step), :] = total * jax.nn.sigmoid(total)
        return carry

    lax.fori_loop(0, steps, conv_step, 0, unroll=2)
    u = r.du[...].astype(BF16)
    r.u[...] = u
    xdbl = dot_nt(u, r.packed[SEL : SEL + STEP, :])
    r.xdbl[...] = xdbl
    r.delta[...] = dot_nn(
        xdbl[:, :RANK].astype(BF16), r.packed[STEP : STEP + RANK, :]
    )
    stepb = small[STEPB - DEC : STEPB - DEC + 1, :]

    def delta_step(step, total):
        places = lax.broadcasted_iota(jnp.int32, (CHUNKS, 1), 0) * steps + step + me * rows
        pre = r.delta[tile(step), :] + stepb
        delta = jnp.maximum(pre, 0.0) + jnp.log1p(jnp.exp(-jnp.abs(pre)))
        r.delta[tile(step), :] = delta
        cut = jnp.where(begin_of(places, starts), CUT, delta)
        r.cut[tile(step), :] = cut
        r.du[tile(step), :] = delta * r.du[tile(step), :].astype(BF16).astype(F32)
        return total + cut

    totals = lax.fori_loop(0, steps, delta_step, jnp.zeros((CHUNKS, DI), F32), unroll=2)
    r.totals[...] = totals
    total = jnp.sum(totals, axis=0, keepdims=True)
    for group in range(GROUPS_CH):
        r.total_send[group : group + 1, :] = total[:, group * LANES : (group + 1) * LANES]
    r.span_totals[me] = r.total_send[...]

    def total_copy(by):
        return copy(
            r.total_send, r.span_totals.at[me], r.total_sem, (by,), at_seq(ring[by - 1])
        )

    for by in range(1, spans):
        total_copy(by).start()
    pass_on(3)
    spread_decay(r.packed, r.amat, r.spread)
    spread_columns(r.xdbl, RANK, r.bx, steps)

    def state_copy(by, at):
        return copy(
            r.state_send.at[at], r.states.at[me, at], r.state_sem, (by, at), at_seq(ring[by - 1])
        )

    def pair_step(pair, carry):
        for odd in range(2):
            lanes = lanes_of(pair * 2 + odd)
            amat = [r.spread[st * CHUNKS : (st + 1) * CHUNKS, lanes] for st in range(STATE)]

            def step_fn(step, states):
                cut = r.cut[tile(step), lanes]
                drive = r.du[tile(step), lanes]
                return tuple(
                    jnp.exp2(cut * amat[st]) * states[st] + drive * r.bx[state_at(step, st), :]
                    for st in range(STATE)
                )

            states = lax.fori_loop(
                0, steps, step_fn, (jnp.zeros((CHUNKS, LANES), F32),) * STATE, unroll=4
            )
            for st in range(STATE):
                r.ends[st, :, lanes] = states[st]
        lanes = pl.ds(pl.multiple_of(pair * 2 * LANES, 2 * LANES), 2 * LANES)
        amat = r.amat[:, lanes]
        state = jnp.zeros((STATE, 2 * LANES), F32)
        for k in range(CHUNKS):
            state = jnp.exp2(amat * r.totals[k : k + 1, lanes]) * state + r.ends[:, k, lanes]
        r.state_send[pair] = state.astype(BF16)
        for by in range(1, spans):

            @pl.when(me + by < spans)
            def _():
                state_copy(by, pair).start()

        return carry

    lax.fori_loop(0, GROUPS_CH // 2, pair_step, 0)
    pass_on(4, 5)
    for by in range(1, spans):
        cot_copy(by).wait()
    finish(3, 4, 5)

    ratio = spans // HEADS
    sub = lax.rem(me, ratio)
    head = lax.div(me, ratio)
    half = rows // 2
    given = jnp.concatenate([r.given[j] for j in range(spans)], axis=0)
    dout = dot_nn(pick_rows(r.index, me, rows, steps), given).astype(BF16)
    r.dout[...] = dout
    merge = jnp.concatenate([r.wm_all[s] for s in range(shards)], axis=0)
    dcontext = dot_nt(dout, merge).astype(BF16).astype(F32)
    low = lane_low(half)

    def packs(pair):
        above, below = pair[:half], pair[half:]
        yield jnp.where(low, above, pltpu.roll(below, HEAD_DIM, 1))
        yield jnp.where(low, pltpu.roll(above, HEAD_DIM, 1), below)

    for pair in range(HEADS // 2):
        at = pair * LANES
        for odd, pack in enumerate(packs(dcontext[:, at : at + LANES])):
            r.d_send[2 * pair + odd] = pack.astype(BF16)

    def rows_copy(source, target, sems, by):
        to = ring[by - 1]
        slot = lax.div(me, ratio)
        return copy(source.at[lax.div(to, ratio)], target.at[slot], sems, (by,), at_seq(to))

    def kv_copy(by):
        to = ring[by - 1]
        return copy(
            r.kv_send.at[lax.div(to, ratio)],
            r.kv_in.at[pl.ds(pl.multiple_of(me * rows, rows), rows)],
            r.kv_sem,
            (by,),
            at_seq(to),
        )

    def to_rows(source, target, sems, act):
        for by in range(1, spans):
            if ratio == 1:
                act(rows_copy(source, target, sems, by))
            else:
                pl.when(lax.rem(by, ratio) == 0)(lambda: act(rows_copy(source, target, sems, by)))

    to_rows(r.d_send, r.d_in, r.d_sem, lambda c: c.start())
    r.d_in[lax.div(me, ratio)] = r.d_send[head]
    spread_columns(r.xdbl, RANK + STATE, r.cx, steps)
    for by in range(1, spans):
        total_copy(by).wait()
        for pair in range(GROUPS_CH // 2):

            @pl.when(me + by < spans)
            def _():
                state_copy(by, pair).wait_send()

            @pl.when(me - by >= 0)
            def _():
                state_copy(by, pair).wait_recv()

    amat = r.amat[...]

    def chain(k, state):
        decay = jnp.exp2(amat * total_row(r.span_totals[k]))
        came = jnp.concatenate(
            [r.states[k, g].astype(F32) for g in range(GROUPS_CH // 2)], axis=1
        )
        return decay * state + came

    state = lax.fori_loop(0, me, chain, jnp.zeros((STATE, DI), F32))
    for k in range(CHUNKS):
        r.init[:, k, :] = state
        if k < CHUNKS - 1:
            state = jnp.exp2(amat * r.totals[k : k + 1, :]) * state + r.ends[:, k, :]

    def group_step(group, carry):
        lanes = lanes_of(group)
        amat_g = [r.spread[st * CHUNKS : (st + 1) * CHUNKS, lanes] for st in range(STATE)]

        def step_fn(step, states):
            cut = r.cut[tile(step), lanes]
            drive = r.du[tile(step), lanes]
            new = tuple(
                jnp.exp2(cut * amat_g[st]) * states[st] + drive * r.bx[state_at(step, st), :]
                for st in range(STATE)
            )
            terms = [new[st] * r.cx[state_at(step, st), :] for st in range(STATE)]
            while len(terms) > 1:
                terms = [a + b for a, b in zip(terms[::2], terms[1::2])]
            r.yfull[tile(step), lanes] = terms[0]
            return new

        lax.fori_loop(
            0, steps, step_fn, tuple(r.init[st, :, lanes] for st in range(STATE)), unroll=4
        )
        return carry

    lax.fori_loop(0, GROUPS_CH, group_step, 0)
    skip = small[SKIP - DEC : SKIP - DEC + 1, :]

    def gate_step(pair, carry):
        at = pl.ds(pl.multiple_of(pair * 2 * CHUNKS, 2 * CHUNKS), 2 * CHUNKS)
        yfull = r.yfull[at, :] + skip * r.u[at, :].astype(F32)
        r.yfull[at, :] = yfull
        gate = r.zgate[at, :]
        r.gated[at, :] = (yfull * (gate * jax.nn.sigmoid(gate))).astype(BF16)
        return carry

    lax.fori_loop(0, steps // 2, gate_step, 0)
    wo = jnp.concatenate([r.wo_all[s] for s in range(shards)], axis=0)
    x1 = r.x[...] + dot_nn(r.gated[...], wo)
    r.x1[...] = x1
    xn2 = (x1 * norm(x1) * gains[1:2, :]).astype(BF16)
    qkv = jnp.concatenate([dot_nn(xn2, r.wh_all[s]) for s in range(shards)], axis=1)
    qkv = qkv.astype(BF16).astype(F32)
    scale = 1.0 / math.sqrt(HEAD_DIM)
    full_low = lane_low(rows)
    for pair in range(HEADS // 2):
        at = pair * LANES
        for odd, pack in enumerate(packs(qkv[:, at : at + LANES] * scale)):
            r.q_send[2 * pair + odd] = pack.astype(BF16)
        k = qkv[:, D + at : D + at + LANES]
        v = qkv[:, 2 * D + at : 2 * D + at + LANES]
        r.kv_send[2 * pair] = jnp.where(full_low, k, pltpu.roll(v, HEAD_DIM, 1)).astype(BF16)
        r.kv_send[2 * pair + 1] = jnp.where(full_low, pltpu.roll(k, HEAD_DIM, 1), v).astype(BF16)
    to_rows(r.q_send, r.q_in, r.q_sem, lambda c: c.start())
    for by in range(1, spans):
        kv_copy(by).start()
    r.q_in[lax.div(me, ratio)] = r.q_send[head]
    r.kv_in[pl.ds(pl.multiple_of(me * rows, rows), rows), :] = r.kv_send[head]
    keeps = [
        pltpu.make_async_copy(getattr(r, name), getattr(r, name + "_out"), r.keep_sem.at[i])
        for i, name in enumerate(KEPT)
    ]
    for keep in keeps[:-1]:
        keep.start()
    query_local = row_places(lax.broadcasted_iota(jnp.int32, (1, rows), 1), steps)
    key_local = row_places(lax.broadcasted_iota(jnp.int32, (rows, 1), 0), steps)
    r.causal[...] = jnp.where(key_local <= query_local, 0.0, NEG)
    r.dkv[...] = jnp.zeros_like(r.dkv)
    to_rows(r.d_send, r.d_in, r.d_sem, lambda c: c.wait())
    to_rows(r.q_send, r.q_in, r.q_sem, lambda c: c.wait())
    for by in range(1, spans):
        kv_copy(by).wait()

    static = ratio == 1
    blocks = spans // ratio

    def each(count, fn, carry):
        if not static:
            return lax.fori_loop(0, count, fn, carry)
        for j in range(count):
            carry = fn(j, carry)
        return carry

    def key_rows(j):
        return pl.ds(j * rows if static else pl.multiple_of(j * rows, rows), rows)

    def turn(j, carry):
        r.kvt[j] = r.kv_in[key_rows(j), :].astype(F32).T.astype(BF16)
        return carry

    each(spans, turn, 0)
    folded = (rows // CHUNKS, CHUNKS, rows)

    def dq_copy(to, by, t):
        return copy(r.dq_send.at[t], r.dq_in.at[head], r.dq_sem, (by,), at_seq(to))

    def query_block(t, carry):
        i = t * ratio + sub
        slot = t % 2 if static else 0
        q = r.q_in[t].astype(F32)
        d = r.d_in[t].astype(F32)
        qt = q.T
        dt = d.T
        zero = jnp.zeros((HEAD_DIM, rows), F32)
        qt = jnp.concatenate([qt[:HEAD_DIM], qt[HEAD_DIM:]], axis=1)
        dt = jnp.concatenate([dt[:HEAD_DIM], dt[HEAD_DIM:]], axis=1)
        both = jnp.concatenate(
            [jnp.concatenate([qt, zero], axis=1), jnp.concatenate([zero, dt], axis=1)], axis=0
        ).astype(BF16)
        none = jnp.zeros((half, LANES), F32)
        natural = jnp.concatenate(
            [
                jnp.where(low, none, pltpu.roll(d, HEAD_DIM, 1)),
                jnp.where(low, none, d),
                jnp.where(low, q, none),
                jnp.where(low, pltpu.roll(q, HEAD_DIM, 1), none),
            ],
            axis=0,
        ).astype(BF16)
        first = start_of(query_local + i * rows, starts)

        def scores(j, top):
            joint = dot_nn(r.kv_in[key_rows(j), :], both)
            score = joint[:, :rows]
            if static:
                if j == t:
                    score = score + r.causal[...]
                if j in (0, t) or t == spans - 1:
                    score = jnp.where(key_local + j * rows >= first, score, NEG)
            else:
                query = query_local + i * rows
                key = key_local + j * rows
                score = jnp.where((key <= query) & (key >= first), score, NEG)
            r.score[slot, j] = score
            r.dprob[slot, j] = joint[:, rows:]
            return jnp.maximum(top, jnp.max(score.reshape(folded), axis=0))

        top = each(t + 1 if static else i + 1, scores, jnp.full((CHUNKS, rows), NEG, F32))
        top = jnp.max(top, axis=0, keepdims=True)

        def weigh(j, sums):
            total, dot = sums
            prob = jnp.exp(r.score[slot, j] - top)
            r.score[slot, j] = prob
            total = total + jnp.sum(prob.reshape(folded), axis=0)
            dot = dot + jnp.sum((prob * r.dprob[slot, j]).reshape(folded), axis=0)
            return total, dot

        zero = jnp.zeros((CHUNKS, rows), F32)
        total, dot = each(t + 1 if static else i + 1, weigh, (zero, zero))
        inverse = 1.0 / jnp.sum(total, axis=0, keepdims=True)
        datt = jnp.sum(dot, axis=0, keepdims=True) * inverse

        def back(j, sums):
            prob = r.score[slot, j] * inverse
            dscore = prob * (r.dprob[slot, j] - datt)
            joint = jnp.concatenate([prob.astype(BF16), dscore.astype(BF16)], axis=1)
            r.dkv[key_rows(j), :] += dot_nn(joint, natural)
            return sums + dot_nn(r.kvt[j], joint)

        sums = each(t + 1 if static else i + 1, back, jnp.zeros((LANES, 2 * rows), F32))
        dqt = sums[:HEAD_DIM, rows:] * scale
        ctx = sums[HEAD_DIM:, :rows]
        dqt = jnp.concatenate([dqt[:, :half], dqt[:, half:]], axis=0)
        ctx = jnp.concatenate([ctx[:, :half], ctx[:, half:]], axis=0)
        r.dq_send[t] = dqt.T.astype(BF16)
        r.context_send[t] = ctx.T.astype(BF16)
        by = lax.rem(i - me + spans, spans)

        @pl.when(i != me)
        def _():
            dq_copy(i, by, t).start()

        @pl.when(i == me)
        def _():
            r.dq_in[head] = r.dq_send[t]

        return carry

    if static:
        for t in range(blocks):
            query_block(t, 0)
    else:
        lax.fori_loop(0, blocks, query_block, 0)
    keeps[-1].start()

    def cast(j, carry):
        r.dkv_send[j] = r.dkv[key_rows(j), :].astype(BF16)
        return carry

    each(spans, cast, 0)

    def dkv_copy(by):
        to = ring[by - 1]
        return copy(r.dkv_send.at[to], r.dkv_in.at[me], r.dkv_sem, (by,), at_seq(to))

    for by in range(1, spans):
        dkv_copy(by).start()
    r.dkv_in[me] = r.dkv_send[me]
    for t in range(blocks):
        i = t * ratio + sub
        by = lax.rem(i - me + spans, spans)

        @pl.when(i != me)
        def _():
            dq_copy(i, by, t).wait_send()

    for h in range(HEADS):
        came = h * ratio + sub
        by = lax.rem(me - came + spans, spans)

        @pl.when(came != me)
        def _():
            dq_copy(came, by, 0).wait_recv()

    for by in range(1, spans):
        dkv_copy(by).wait()
    for keep in keeps:
        keep.wait()


def total_row(values):
    return jnp.concatenate([values[g : g + 1, :] for g in range(GROUPS_CH)], axis=1)


def lane_low(rows):
    return lax.broadcasted_iota(jnp.int32, (rows, LANES), 1) < HEAD_DIM


def pick_rows(table_ref, me, rows, steps):
    spans = table_ref.shape[0]
    share = rows // spans
    shift = lax.rem((spans - me) * share, rows)
    moved = pltpu.roll(table_ref[...], shift, 1)
    lane = lax.broadcasted_iota(jnp.int32, (1, rows), 1)
    index = moved[0:1]
    for j in range(1, spans):
        line = pltpu.roll(moved[j : j + 1], j * share, 1)
        index = jnp.where(lane >= j * share, line, index)
    places = row_places(lax.broadcasted_iota(jnp.int32, (rows, 1), 0), steps) + me * rows
    return (index == places.astype(F32)).astype(F32).astype(BF16)


GRADS = ("heads", "out", "merge", "late", "early", "small")
BACKWARD_IN = ("lengths", "index", "dq_in", "dkv_in") + tuple(k + "_kept" for k in KEPT)
BACKWARD_OUT = (
    "output", "token_grad", "last_heads", "last_out", "last_merge", "last_small", "pair_in",
)
FINAL_OUT = (
    "output", "token_grad", "mixer_grad", "input_grad", "taps_grad", "bias_grad", "select_grad", "stepw_grad",
    "stepb_grad", "decay_grad", "skip_grad", "output_grad", "attention_grad", "heads_grad", "merge_grad",
)
BACKWARD_SCRATCH = KEPT + (
    "context", "given", "dx1", "dys", "dzgate", "ends", "grad_send", "grads_in", "db", "dc", "decay", "held",
    "state", "bgrad", "adelta", "arrive", "dxdbl", "dext", "spill", "spill_in", "small", "row", "amat",
    "spread", "sub_late", "sub_early",
) + tuple(
    kind + name for kind in ("g_", "near_", "sum_", "far_", "part_") for name in GRADS
) + (
    "load_sem", "context_sem", "given_sem", "state_sem", "spill_sem", "near_sem", "far_sem", "part_sem",
    "last_sem", "pair_sem",
)


def backward_kernel(steps, nseq, shards, spans, *refs):
    r = Refs(BACKWARD_IN + BACKWARD_OUT + BACKWARD_SCRATCH, refs)
    rows = steps * CHUNKS
    width = DI // shards
    me = lax.axis_index("seq")
    shard, core, chip, partner, others = shard_peers(shards)
    chips = shards // 2
    ring = [lax.rem(me + by, spans) for by in range(1, spans)]
    every = [me] + ring
    ratio = spans // HEADS
    sub = lax.rem(me, ratio)
    half = rows // 2
    blocks = spans // ratio
    starts = starts_of(r.lengths, nseq)
    loads = {
        name: pltpu.make_async_copy(getattr(r, name + "_kept"), getattr(r, name), r.load_sem.at[i])
        for i, name in enumerate(KEPT)
    }
    early = ("context_send", "dout", "x1", "gains", "wh_all")
    middle = ("gated", "wo_all", "zgate", "yfull", "u", "x")
    late = ("wm_all", "packed", "cut", "cx", "totals", "span_totals", "init", "delta", "du", "bx", "xdbl")
    last = ("conv", "ext", "wi_all")
    for name in early + middle + late + last:
        loads[name].start()

    def loaded(*names):
        for name in names:
            loads[name].wait()

    targets = [lax.div(shard, 2), shards // 2 + lax.div(shard, 2)]
    mine = lax.div(shard, shards // 2)
    first_piece = 2 * lax.rem(shard, shards // 2)

    def anywhere(index, at):
        return {"device_id": {"seq": index, "shard": at}, "device_id_type": pl.DeviceIdType.MESH}

    barrier = pltpu.get_barrier_semaphore()

    def signal(to):
        pl.semaphore_signal(barrier, inc=1, **to)

    peers = [at_shard(partner)] + [at_shard(o) for o in others] + [at_seq(to) for to in ring]
    for peer in peers:
        signal(peer)
    selves = jnp.int32(0)
    for by in range(spans):
        for at in targets + [first_piece, first_piece + 1]:
            if by:
                signal(anywhere(every[by], at))
            else:
                pl.when(at != shard)(lambda: signal(anywhere(me, at)))
                selves = selves + (at == shard).astype(jnp.int32)
    pl.semaphore_wait(barrier, len(peers) + 4 * spans - selves)

    def copy(source, target, sems, at, to):
        return pltpu.make_async_remote_copy(
            src_ref=source, dst_ref=target, send_sem=sems.at[(0, *at)], recv_sem=sems.at[(1, *at)], **to
        )

    def ref(kind, k):
        return getattr(r, kind + "_" + GRADS[k])

    def near_copy(k, x):
        return copy(
            ref("g", k).at[x * 2 + 1 - core], ref("near", k).at[x], r.near_sem, (k, x), at_shard(partner)
        )

    def far_copy(k, by):
        source = ref("sum", k).at[lax.rem(chip + by, chips)]
        return copy(source, ref("far", k).at[by - 1], r.far_sem, (k, by), at_shard(others[by - 1]))

    def part_copy(k, by):
        to = ring[by - 1]
        return copy(
            ref("near", k).at[0, to], ref("part", k).at[by], r.part_sem, (k, by), at_seq(to)
        )

    def last_copy(k, by):
        held = ref("last", k).at[me]
        return copy(held, held, r.last_sem, (k, by), at_seq(ring[by - 1]))

    def pair_copy(k, by, parity, to):
        source = r.sub_early if GRADS[k] == "early" else r.sub_late
        return copy(
            source, r.pair_in.at[parity, me], r.pair_sem, (k - 3, parity, by), anywhere(every[by], to)
        )

    def near_send(k):
        for x in range(chips):
            near_copy(k, x).start()

    def far_send(k):
        for x in range(chips):
            near_copy(k, x).wait_recv()
            ref("sum", k)[x] = (
                ref("g", k)[x * 2 + core].astype(F32) + ref("near", k)[x].astype(F32)
            ).astype(BF16)
        for by in range(1, chips):
            far_copy(k, by).start()

    def part_send(k):
        total = ref("sum", k)[chip].astype(F32)
        for by in range(1, chips):
            far_copy(k, by).wait_recv()
            total = total + ref("far", k)[by - 1].astype(F32)
        ref("near", k)[0] = total.astype(BF16)
        for by in range(1, chips):
            far_copy(k, by).wait_send()
        for by in range(1, spans):
            part_copy(k, by).start()

    def last_send(k):
        total = ref("near", k)[0, me].astype(F32)
        for by in range(1, spans):
            part_copy(k, by).wait_recv()
            total = total + ref("part", k)[by].astype(F32)
        if k not in (3, 4):
            ref("last", k)[me] = total.astype(BF16)
            for by in range(1, spans):
                last_copy(k, by).start()
            return
        source = r.sub_early if GRADS[k] == "early" else r.sub_late
        source[...] = total.astype(BF16)
        to = targets[4 - k]
        parity = lax.rem(shard, 2)
        for by in range(spans):
            if by:
                pair_copy(k, by, parity, to).start()
            else:

                @pl.when(to != shard)
                def _():
                    pair_copy(k, 0, parity, to).start()

                @pl.when(to == shard)
                def _():
                    r.pair_in[parity, me] = source[...]

    def finish(k):
        for x in range(chips):
            near_copy(k, x).wait_send()
        for by in range(1, spans):
            part_copy(k, by).wait_send()
        if k not in (3, 4):
            for by in range(1, spans):
                last_copy(k, by).wait()
            return
        to = targets[4 - k]
        parity = lax.rem(shard, 2)
        for by in range(spans):
            if by:
                pair_copy(k, by, parity, to).wait_send()
            else:

                @pl.when(to != shard)
                def _():
                    pair_copy(k, 0, parity, to).wait_send()

        @pl.when(mine == 4 - k)
        def _():
            for parity in range(2):
                for by in range(spans):
                    if by:
                        pair_copy(k, by, parity, to).wait_recv()
                    else:

                        @pl.when(first_piece + parity != shard)
                        def _():
                            pair_copy(k, 0, parity, to).wait_recv()

    def put(k, piece, value):
        size = value.shape[0] // spans
        for j in range(spans):
            ref("g", k)[piece, j] = value[j * size : (j + 1) * size].astype(BF16)

    loaded("context_send")
    head = lax.div(me, ratio)

    def context_copy(t, by, to):
        return copy(r.context_send.at[t], r.context.at[head], r.context_sem, (by,), at_seq(to))

    for t in range(blocks):
        i = t * ratio + sub
        by = lax.rem(i - me + spans, spans)

        @pl.when(i != me)
        def _():
            context_copy(t, by, i).start()

        @pl.when(i == me)
        def _():
            r.context[head] = r.context_send[t]

    low = lane_low(rows)
    half_low = lane_low(half)

    def unpacked(source, pair):
        even, odd = source[2 * pair].astype(F32), source[2 * pair + 1].astype(F32)
        return jnp.concatenate(
            [
                jnp.where(half_low, even, pltpu.roll(odd, HEAD_DIM, 1)),
                jnp.where(half_low, pltpu.roll(even, HEAD_DIM, 1), odd),
            ],
            axis=0,
        )

    dqs, dks, dvs = [], [], []
    for pair in range(HEADS // 2):
        dkv = [
            sum(r.dkv_in[(2 * pair + odd) * ratio + part].astype(F32) for part in range(ratio))
            for odd in range(2)
        ]
        dqs.append(unpacked(r.dq_in, pair))
        dks.append(jnp.where(low, dkv[0], pltpu.roll(dkv[1], HEAD_DIM, 1)))
        dvs.append(jnp.where(low, pltpu.roll(dkv[0], HEAD_DIM, 1), dkv[1]))
    dqkv = jnp.concatenate(dqs + dks + dvs, axis=1).astype(BF16)
    loaded("x1", "gains", "wh_all", "dout")
    x1 = r.x1[...]
    inverse = norm(x1)
    normal = x1 * inverse
    gain = r.gains[1:2, :]
    xn2 = (normal * gain).astype(BF16)
    wide = 3 * D // shards
    dxn2 = jnp.zeros((rows, D), F32)
    for s in range(shards):
        piece = dqkv[:, s * wide : (s + 1) * wide]
        put(0, s, dot_tn(xn2, piece))
        dxn2 = dxn2 + dot_nt(piece, r.wh_all[s])
    near_send(0)
    attention_gain = jnp.sum(dxn2 * normal, axis=0, keepdims=True)
    e2 = dxn2 * gain
    dx1 = r.dout[...].astype(F32) + inverse * (
        e2 - normal * jnp.mean(e2 * normal, axis=-1, keepdims=True)
    )
    r.dx1[...] = dx1
    dmixed = dx1.astype(BF16)
    loaded("gated", "wo_all")
    for s in range(shards):
        put(1, s, dot_tn(r.gated[:, s * width : (s + 1) * width], dmixed))
        r.dys[:, s * width : (s + 1) * width] = dot_nt(dmixed, r.wo_all[s])
    near_send(1)
    far_send(0)
    loaded("zgate", "yfull", "u", "x")

    def gate_step(pair, total):
        at = pl.ds(pl.multiple_of(pair * 2 * CHUNKS, 2 * CHUNKS), 2 * CHUNKS)
        dgated = r.dys[at, :].astype(BF16).astype(F32)
        gate = r.zgate[at, :]
        s = jax.nn.sigmoid(gate)
        dys = dgated * (gate * s)
        r.dys[at, :] = dys
        r.dzgate[at, :] = (dgated * r.yfull[at, :] * (s * (1.0 + gate * (1.0 - s)))).astype(BF16)
        return total + dys * r.u[at, :].astype(F32)

    total = lax.fori_loop(0, steps // 2, gate_step, jnp.zeros((2 * CHUNKS, DI), F32))
    r.small[SKIP : SKIP + 1, :] = jnp.sum(total, axis=0, keepdims=True)
    far_send(1)
    x = r.x[...]
    inverse_one = norm(x)
    normal_one = x * inverse_one
    gain_one = r.gains[0:1, :]
    xn1 = (normal_one * gain_one).astype(BF16)
    for s in range(shards):
        put(3, s, dot_tn(xn1, r.dzgate[:, s * width : (s + 1) * width]))
    near_send(3)
    loaded("wm_all", "packed", "cut", "cx", "totals", "span_totals")
    for h in range(HEADS):
        came = h * ratio + sub
        by = lax.rem(me - came + spans, spans)

        @pl.when(came != me)
        def _():
            context_copy(0, by, came).wait_recv()

    context = jnp.concatenate([unpacked(r.context, p) for p in range(HEADS // 2)], axis=1)
    context = context.astype(BF16)
    short = D // shards
    x2 = x1
    for s in range(shards):
        part = context[:, s * short : (s + 1) * short]
        x2 = x2 + dot_nn(part, r.wm_all[s])
        put(2, s, dot_tn(part, r.dout[...]))
    near_send(2)
    given = dot_tn(pick_rows(r.index, me, rows, steps), x2.astype(BF16))
    share = rows // spans
    for j in range(spans):
        r.given[j] = given[j * share : (j + 1) * share].astype(BF16)

    def given_copy(by):
        to = ring[by - 1]
        return copy(r.given.at[to], r.output.at[me], r.given_sem, (by,), at_seq(to))

    for by in range(1, spans):
        given_copy(by).start()
    r.output[me] = r.given[me]

    spread_decay(r.packed, r.amat, r.spread)

    def state_copy(by, at):
        to = lax.rem(me - by + spans, spans)
        return copy(
            r.grad_send.at[at], r.grads_in.at[me, at], r.state_sem, (by, at), at_seq(to)
        )

    def pair_step(pair, carry):
        for odd in range(2):
            lanes = lanes_of(pair * 2 + odd)
            amat = [r.spread[st * CHUNKS : (st + 1) * CHUNKS, lanes] for st in range(STATE)]

            def step_fn(turn, grads):
                step = steps - 1 - turn
                cut = r.cut[tile(step), lanes]
                dys = r.dys[tile(step), lanes]
                return tuple(
                    jnp.exp2(cut * amat[st]) * (grads[st] + dys * r.cx[state_at(step, st), :])
                    for st in range(STATE)
                )

            grads = lax.fori_loop(
                0, steps, step_fn, (jnp.zeros((CHUNKS, LANES), F32),) * STATE, unroll=4
            )
            for st in range(STATE):
                r.ends[st, :, lanes] = grads[st]
        lanes = pl.ds(pl.multiple_of(pair * 2 * LANES, 2 * LANES), 2 * LANES)
        amat = r.amat[:, lanes]
        state = jnp.zeros((STATE, 2 * LANES), F32)
        for k in reversed(range(CHUNKS)):
            state = jnp.exp2(amat * r.totals[k : k + 1, lanes]) * state + r.ends[:, k, lanes]
        r.grad_send[pair] = state.astype(BF16)
        for by in range(1, spans):

            @pl.when(me - by >= 0)
            def _():
                state_copy(by, pair).start()

        @pl.when(pair == 0)
        def _():
            far_send(3)

        @pl.when(pair == 1)
        def _():
            far_send(2)

        @pl.when(pair == 2)
        def _():
            part_send(0)

        return carry

    lax.fori_loop(0, GROUPS_CH // 2, pair_step, 0)
    loaded("init", "delta", "du", "bx", "xdbl", *last)
    r.db[...] = jnp.zeros_like(r.db)
    r.dc[...] = jnp.zeros_like(r.dc)
    for by in range(1, spans):
        for pair in range(GROUPS_CH // 2):

            @pl.when(me - by >= 0)
            def _():
                state_copy(by, pair).wait_send()

            @pl.when(me + by < spans)
            def _():
                state_copy(by, pair).wait_recv()

    amat = r.amat[...]

    def chain(turn, state):
        k = spans - 1 - turn
        decay = jnp.exp2(amat * total_row(r.span_totals[k]))
        came = jnp.concatenate(
            [r.grads_in[k, g].astype(F32) for g in range(GROUPS_CH // 2)], axis=1
        )
        return decay * state + came

    state = lax.fori_loop(0, spans - 1 - me, chain, jnp.zeros((STATE, DI), F32))
    for k in reversed(range(CHUNKS)):
        r.arrive[:, k, :] = state
        if k:
            state = jnp.exp2(amat * r.totals[k : k + 1, :]) * state + r.ends[:, k, :]
    eight = STATE // 2

    def sum_of(terms):
        while len(terms) > 1:
            terms = [a + b for a, b in zip(terms[::2], terms[1::2])]
        return terms[0]

    def kept_at(step, i):
        return pl.ds(pl.multiple_of(step * (eight * CHUNKS) + i * CHUNKS, CHUNKS), CHUNKS)

    stages = [
        lambda: part_send(1),
        lambda: part_send(3),
        lambda: part_send(2),
        lambda: last_send(0),
        lambda: last_send(1),
        lambda: last_send(3),
        lambda: last_send(2),
    ]

    def group_step(group, carry):
        lanes = lanes_of(group)
        for part in range(2):
            states = range(part * eight, (part + 1) * eight)
            amat_g = [r.spread[st * CHUNKS : (st + 1) * CHUNKS, lanes] for st in states]

            def forward(step, held):
                cut = r.cut[tile(step), lanes]
                drive = r.du[tile(step), lanes]
                out = []
                for i, st in enumerate(states):
                    decay = jnp.exp2(cut * amat_g[i])
                    kept = decay * held[i]
                    new = kept + drive * r.bx[state_at(step, st), :]
                    r.decay[kept_at(step, i), :] = decay
                    r.held[kept_at(step, i), :] = kept
                    r.state[kept_at(step, i), :] = new
                    out.append(new)
                return tuple(out)

            lax.fori_loop(
                0, steps, forward, tuple(r.init[st, :, lanes] for st in states), unroll=4
            )

            def backward(turn, held):
                grads, sums = held
                step = steps - 1 - turn
                delta = r.delta[tile(step), lanes]
                drive = r.du[tile(step), lanes]
                dys = r.dys[tile(step), lanes]
                new, totals, by_b, by_a = [], [], [], []
                for i, st in enumerate(states):
                    at = state_at(step, st)
                    grad = grads[i] + dys * r.cx[at, :]
                    new.append(r.decay[kept_at(step, i), :] * grad)
                    through = grad * r.held[kept_at(step, i), :]
                    totals.append(sums[i] + through * delta)
                    by_a.append(amat_g[i] * through)
                    by_b.append(grad * r.bx[at, :])
                    r.dc[at, :] += r.state[kept_at(step, i), :] * dys
                    r.db[at, :] += grad * drive
                if part:
                    r.bgrad[tile(step), lanes] += sum_of(by_b)
                    r.adelta[tile(step), lanes] += sum_of(by_a)
                else:
                    r.bgrad[tile(step), lanes] = sum_of(by_b)
                    r.adelta[tile(step), lanes] = sum_of(by_a)
                return (tuple(new), tuple(totals))

            _, sums = lax.fori_loop(
                0,
                steps,
                backward,
                (
                    tuple(r.arrive[st, :, lanes] for st in states),
                    (jnp.zeros((CHUNKS, LANES), F32),) * eight,
                ),
                unroll=4,
            )
            for i, st in enumerate(states):
                row = jnp.sum(sums[i], axis=0, keepdims=True)
                amat_row = amat_g[i][0:1, :] * math.log(2.0)
                r.small[DEC + st : DEC + st + 1, lanes] = row * amat_row
        for k, stage in enumerate(stages):
            pl.when(group == k)(stage)
        return carry

    lax.fori_loop(0, GROUPS_CH, group_step, 0)
    small = r.packed[DEC:PACK, :].astype(F32)
    taps = small[TAPS - DEC : TAPS - DEC + CONV, :]
    skip = small[SKIP - DEC : SKIP - DEC + 1, :]

    def delta_step(step, total):
        at = tile(step)
        bgrad = r.bgrad[at, :]
        delta = r.delta[at, :]
        u = r.conv[at, :]
        u = (u * jax.nn.sigmoid(u)).astype(BF16).astype(F32)
        ddelta = u * bgrad + r.adelta[at, :] * math.log(2.0)
        dtpre = (ddelta * (1.0 - jnp.exp(-delta))).astype(BF16).astype(F32)
        r.adelta[at, :] = dtpre
        r.bgrad[at, :] = r.dys[at, :] * skip + delta * bgrad
        return total + dtpre

    total = lax.fori_loop(0, steps, delta_step, jnp.zeros((CHUNKS, DI), F32))
    r.small[STEPB : STEPB + 1, :] = jnp.sum(total, axis=0, keepdims=True)
    r.small[GAINS:, :] = jnp.zeros((PACK - GAINS, DI), F32)
    dtpre = r.adelta[...].astype(BF16)
    steplow = r.xdbl[:, 0:RANK].astype(BF16)
    r.small[STEP : STEP + RANK, :] = dot_tn(steplow, dtpre)
    r.dxdbl[:, 0:RANK] = dot_nt(dtpre, r.packed[STEP : STEP + RANK, :])
    lane = lax.broadcasted_iota(jnp.int32, (CHUNKS, 2 * STATE), 1)

    def gather_step(step, carry):
        total = jnp.zeros((CHUNKS, 2 * STATE), F32)
        for st in range(STATE):
            at = state_at(step, st)
            total = jnp.where(lane == st, jnp.sum(r.db[at, :], axis=1, keepdims=True), total)
            total = jnp.where(
                lane == STATE + st, jnp.sum(r.dc[at, :], axis=1, keepdims=True), total
            )
        r.dxdbl[tile(step), RANK:] = total
        return carry

    lax.fori_loop(0, steps, gather_step, 0, unroll=2)
    dxdbl = r.dxdbl[...].astype(BF16)
    r.small[SEL : SEL + STEP, :] = dot_tn(dxdbl, r.u[...])
    r.bgrad[...] += dot_nn(dxdbl, r.packed[SEL : SEL + STEP, :])
    r.dext[...] = jnp.zeros_like(r.dext)
    r.spill[...] = jnp.zeros_like(r.spill)

    @pl.when(me == spans - 1)
    def _():
        r.spill_in[...] = jnp.zeros_like(r.spill_in)

    zero = jnp.zeros((CHUNKS, DI), F32)

    def conv_step(step, totals):
        at = tile(step)
        dconv = r.bgrad[at, :] * silu_slope(r.conv[at, :])
        places = lax.broadcasted_iota(jnp.int32, (CHUNKS, 1), 0) * steps + step + me * rows
        first = start_of(places, starts)
        out = []
        for k in range(CONV):
            to = pl.ds(pl.multiple_of((step + k) * CHUNKS, CHUNKS), CHUNKS)
            inside = jnp.where(places - (CONV - 1) + k >= first, dconv, 0.0)
            out.append(totals[k] + inside * r.ext[to, :])
            r.dext[to, :] += taps[k : k + 1, :] * inside
        return tuple(out) + (totals[CONV] + dconv,)

    totals = lax.fori_loop(0, CONV - 1, conv_step, (zero,) * (CONV + 1))
    for k in range(CONV - 1):
        r.spill[k : k + 1, :] = r.dext[k * CHUNKS : k * CHUNKS + 1, :]
    behind = lax.rem(me + spans - 1, spans)
    spill = copy(r.spill, r.spill_in, r.spill_sem, (), at_seq(behind))

    @pl.when(me > 0)
    def _():
        spill.start()

    totals = lax.fori_loop(CONV - 1, steps, conv_step, totals)
    for k in range(CONV):
        r.small[TAPS + k : TAPS + k + 1, :] = jnp.sum(totals[k], axis=0, keepdims=True)
    r.small[BIAS : BIAS + 1, :] = jnp.sum(totals[CONV], axis=0, keepdims=True)

    @pl.when(me > 0)
    def _():
        spill.wait_send()

    @pl.when(me < spans - 1)
    def _():
        spill.wait_recv()

    chunk = lax.broadcasted_iota(jnp.int32, (CHUNKS, DI), 0)
    for k in range(CONV - 1):
        block = r.dext[k * CHUNKS : (k + 1) * CHUNKS, :]
        late = (steps - CONV + 1 + k) * CHUNKS + EDGE
        moved = pltpu.roll(block, CHUNKS - 1, 0)
        came = jnp.broadcast_to(r.spill_in[k : k + 1, :], (CHUNKS, DI))
        r.dext[late : late + CHUNKS, :] += jnp.where(chunk < CHUNKS - 1, moved, came)
    dxin = r.dext[EDGE:, :].astype(BF16)
    for s in range(shards):
        put(4, s, dot_tn(xn1, dxin[:, s * width : (s + 1) * width]))
    near_send(4)
    wide = 2 * width
    dxn1 = jnp.zeros((rows, D), F32)
    for s in range(shards):
        at = s * wide % DI
        if s < shards // 2:
            piece = dxin[:, at : at + wide]
        else:
            piece = r.dzgate[:, at : at + wide]
        dxn1 = dxn1 + dot_nt(piece, r.wi_all[s])
    mixer_gain = jnp.sum(dxn1 * normal_one, axis=0, keepdims=True)
    for s in range(shards):
        at = s * width
        gains = slice(s * short, (s + 1) * short)
        r.small[GAINS : GAINS + 1, at : at + short] = mixer_gain[:, gains]
        r.small[GAINS : GAINS + 1, at + short : at + 2 * short] = attention_gain[:, gains]
    for s in range(shards):
        put(5, s, r.small[:, s * width : (s + 1) * width])
    near_send(5)
    far_send(4)
    far_send(5)
    e1 = dxn1 * gain_one
    dx = r.dx1[...] + inverse_one * (
        e1 - normal_one * jnp.mean(e1 * normal_one, axis=-1, keepdims=True)
    )
    r.dx1[...] = dx
    for part in range(D // LANES):
        lanes = slice(part * LANES, (part + 1) * LANES)
        for step in range(steps):
            r.row[pl.ds(step, CHUNKS, stride=steps), :] = r.dx1[
                step * CHUNKS : (step + 1) * CHUNKS, lanes
            ]
        r.token_grad[:, lanes] = r.row[...]
    part_send(4)
    part_send(5)
    for k in (0, 1, 2, 3):
        finish(k)
    last_send(4)
    last_send(5)
    for by in range(1, spans):
        given_copy(by).wait()
    for t in range(blocks):
        i = t * ratio + sub
        by = lax.rem(i - me + spans, spans)

        @pl.when(i != me)
        def _():
            context_copy(t, by, i).wait_send()

    finish(5)
    finish(4)


def final_kernel(*refs):
    r = Refs(tuple(k + "_in" for k in BACKWARD_OUT) + FINAL_OUT, refs)

    def whole(source):
        return jnp.concatenate([source[j].astype(F32) for j in range(source.shape[0])], axis=0)

    r.output[...] = r.output_in[...]
    r.token_grad[...] = r.token_grad_in[...]
    r.heads_grad[...] = whole(r.last_heads_in)
    r.output_grad[...] = whole(r.last_out_in)
    r.merge_grad[...] = whole(r.last_merge_in)
    small = whole(r.last_small_in)
    short = r.mixer_grad.shape[1]
    width = r.taps_grad.shape[1]
    r.select_grad[...] = small[SEL : SEL + STEP]
    r.stepw_grad[...] = small[STEP : STEP + RANK]
    r.decay_grad[...] = small[DEC : DEC + STATE]
    r.taps_grad[...] = small[TAPS : TAPS + CONV]
    r.bias_grad[...] = small[BIAS : BIAS + 1]
    r.stepb_grad[...] = small[STEPB : STEPB + 1]
    r.skip_grad[...] = small[SKIP : SKIP + 1]
    r.mixer_grad[...] = small[GAINS : GAINS + 1, :short]
    r.attention_grad[...] = small[GAINS : GAINS + 1, short:]
    for parity in range(2):
        r.input_grad[:, parity * width : (parity + 1) * width] = whole(r.pair_in_in.at[parity])


def shape(*dims, kind=F32):
    return jax.ShapeDtypeStruct(dims, kind)


def vmem(*dims, kind=F32):
    return pltpu.VMEM(dims, kind)


def per_device(
    tokens,
    cotangent,
    positions,
    lengths,
    mixer_gain,
    input_weight,
    kernel_weight,
    kernel_bias,
    select_weight,
    step_weight,
    step_bias,
    decay_log,
    skip_scale,
    output_weight,
    attention_gain,
    heads_weight,
    merge_weight,
):
    spans = lax.axis_size("seq")
    shards = lax.axis_size("shard")
    rows = tokens.shape[1]
    steps = rows // CHUNKS
    share = rows // spans
    nseq = lengths.shape[1]
    ratio = spans // HEADS
    part = rows // ratio
    width = DI // shards

    index = positions[0].reshape(spans, rows).astype(F32)
    dma = pltpu.SemaphoreType.DMA
    spread = [vmem(STATE, DI), vmem(STATE * CHUNKS, DI)]
    columns = vmem(rows * STATE, LANES)
    plane = vmem(rows, DI)
    gain_len = D // shards
    halves = GROUPS_CH // 2
    weights = [(D, 2 * width), (width, D), (D, 3 * D // shards), (gain_len, D)]
    half = rows // 2
    blocks = spans // ratio
    slots = 2 if ratio == 1 else 1
    kept = (
        [shape(rows, D)]
        + [shape(shards, *w, kind=BF16) for w in weights]
        + [
            shape(PACK, DI, kind=BF16),
            shape(CHUNKS, D),
            shape(spans, GROUPS_CH, LANES),
            shape(EDGE + rows, DI),
            shape(rows, DI),
            shape(rows, DI),
            shape(rows, DI, kind=BF16),
            shape(rows, DI),
            shape(rows, STEP),
            shape(CHUNKS, DI),
            shape(rows, DI),
            shape(rows, DI, kind=BF16),
            shape(rows, D),
            shape(STATE, CHUNKS, DI),
            shape(rows, D, kind=BF16),
            shape(rows * STATE, LANES),
            shape(rows * STATE, LANES),
            shape(rows, DI),
            shape(rows, DI),
            shape(blocks, half, LANES, kind=BF16),
        ]
    )
    back = [shape(HEADS, half, LANES, kind=BF16), shape(spans, rows, LANES, kind=BF16)]
    inputs = [
        lengths[0],
        tokens[0],
        cotangent[0].reshape(spans, share, D),
        index,
        mixer_gain[None],
        attention_gain[None],
        select_weight.T,
        step_weight,
        decay_log.T,
        kernel_weight,
        kernel_bias[None],
        step_bias[None],
        skip_scale[None],
        input_weight,
        output_weight,
        heads_weight,
        merge_weight,
    ]
    outs = pl.pallas_call(
        functools.partial(forward_kernel, steps, nseq, shards, spans),
        out_shape=kept + back,
        in_specs=[SMEM] + [VMEM] * (len(inputs) - 1),
        out_specs=[pl.BlockSpec(memory_space=pl.ANY)] * len(kept) + [VMEM] * len(back),
        scratch_shapes=[vmem(*k.shape, kind=k.dtype) for k in kept]
        + [
            vmem(spans, share, D, kind=BF16),
            vmem(spans, halves, STATE, 2 * LANES, kind=BF16),
            vmem(STATE, CHUNKS, DI),
            vmem(rows, LANES),
            vmem(PACK, width),
        ]
        + [vmem(*w, kind=BF16) for w in weights]
        + [
            vmem(PACK, width, kind=BF16),
            vmem(2 * CHUNKS, gain_len, kind=BF16),
            vmem(shards, PACK, width, kind=BF16),
            vmem(shards, 2 * CHUNKS, gain_len, kind=BF16),
            vmem(2 * CHUNKS, D, kind=BF16),
            vmem(halves, STATE, 2 * LANES, kind=BF16),
            vmem(GROUPS_CH, LANES),
        ]
        + spread
        + [
            vmem(HEADS, half, LANES, kind=BF16),
            vmem(HEADS, half, LANES, kind=BF16),
            vmem(HEADS, rows, LANES, kind=BF16),
            vmem(blocks, half, LANES, kind=BF16),
            vmem(blocks, half, LANES, kind=BF16),
            vmem(spans * rows, LANES, kind=BF16),
            vmem(spans, LANES, rows, kind=BF16),
            vmem(slots, spans, rows, rows),
            vmem(slots, spans, rows, rows),
            vmem(spans * rows, LANES),
            vmem(blocks, half, LANES, kind=BF16),
            vmem(spans, rows, LANES, kind=BF16),
            vmem(rows, rows),
            dma((2, 6, shards - 1)),
            dma((2, spans)),
            dma((2,)),
            dma((2, spans, halves)),
        ]
        + [dma((2, spans))] * 6
        + [dma((len(kept),))],
        compiler_params=params(collective_id=0, has_side_effects=True),
        name="forward",
    )(*inputs)
    saved, back = outs[: len(kept)], outs[len(kept) :]
    parts = {
        "heads": (D // spans, 3 * D // shards),
        "out": (width // spans, D),
        "merge": (gain_len // spans, D),
        "late": (D // spans, width),
        "early": (D // spans, width),
        "small": (PACK // spans, width),
    }
    chips = shards // 2
    sizes = [(spans, *parts[k]) for k in GRADS]
    count = len(GRADS)
    anyspace = pl.BlockSpec(memory_space=pl.ANY)
    summed = [
        shape(spans, share, D, kind=BF16),
        shape(rows, D),
        shape(spans, *parts["heads"], kind=BF16),
        shape(spans, *parts["out"], kind=BF16),
        shape(spans, *parts["merge"], kind=BF16),
        shape(spans, *parts["small"], kind=BF16),
        shape(2, spans, *parts["late"], kind=BF16),
    ]
    few = vmem(rows * STATE // 2, LANES)
    state = vmem(STATE, CHUNKS, DI)
    summed = pl.pallas_call(
        functools.partial(backward_kernel, steps, nseq, shards, spans),
        out_shape=summed,
        in_specs=[SMEM] + [VMEM] * 3 + [anyspace] * len(kept),
        out_specs=[VMEM] * len(summed),
        scratch_shapes=[vmem(*k.shape, kind=k.dtype) for k in kept]
        + [
            vmem(HEADS, half, LANES, kind=BF16),
            vmem(spans, share, D, kind=BF16),
            vmem(rows, D),
            plane,
            vmem(rows, DI, kind=BF16),
            state,
            vmem(halves, STATE, 2 * LANES, kind=BF16),
            vmem(spans, halves, STATE, 2 * LANES, kind=BF16),
            columns,
            columns,
            few,
            few,
            few,
            plane,
            plane,
            state,
            vmem(rows, STEP),
            vmem(EDGE + rows, DI),
            vmem(CHUNKS, DI),
            vmem(CHUNKS, DI),
            vmem(PACK, DI),
            vmem(rows, LANES),
        ]
        + spread
        + [
            vmem(*parts["late"], kind=BF16),
            vmem(*parts["late"], kind=BF16),
        ]
        + [vmem(shards, *k, kind=BF16) for k in sizes]
        + [vmem(chips, *k, kind=BF16) for k in sizes] * 2
        + [vmem(max(chips - 1, 1), *k, kind=BF16) for k in sizes]
        + [vmem(*k, kind=BF16) for k in sizes]
        + [
            dma((len(kept),)),
            dma((2, spans)),
            dma((2, spans)),
            dma((2, spans, halves)),
            dma((2,)),
            dma((2, count, chips)),
            dma((2, count, chips)),
            dma((2, count, spans)),
            dma((2, count, spans)),
            dma((2, 2, 2, spans)),
        ],
        compiler_params=params(collective_id=1, has_side_effects=True),
        name="backward",
    )(lengths[0], index, *back, *saved)
    results = pl.pallas_call(
        final_kernel,
        out_shape=[
            shape(rows, D, kind=BF16),
            shape(rows, D),
            shape(1, gain_len),
            shape(D, 2 * width),
            shape(CONV, width),
            shape(1, width),
            shape(STEP, width),
            shape(RANK, width),
            shape(1, width),
            shape(STATE, width),
            shape(1, width),
            shape(width, D),
            shape(1, gain_len),
            shape(D, 3 * D // shards),
            shape(gain_len, D),
        ],
        in_specs=[VMEM] * len(summed),
        out_specs=[VMEM] * len(FINAL_OUT),
        compiler_params=params(),
        name="final",
    )(summed[0].reshape(rows, D), *summed[1:])
    flat, turned = {2, 5, 8, 10, 12}, {6, 9}
    return tuple(
        v[None] if i < 2 else v.reshape(-1) if i in flat else v.T if i in turned else v
        for i, v in enumerate(results)
    )


def solution(mesh):
    return jax.shard_map(
        per_device,
        mesh=mesh,
        in_specs=(
            P("shard", "seq", None),
            P("shard", "seq", None),
            P("shard", None),
            P("shard", None),
            P("shard"),
            P(None, "shard"),
            P(None, "shard"),
            P("shard"),
            P("shard", None),
            P(None, "shard"),
            P("shard"),
            P("shard", None),
            P("shard"),
            P("shard", None),
            P("shard"),
            P(None, "shard"),
            P("shard", None),
        ),
        out_specs=(
            P("shard", "seq", None),
            P("shard", "seq", None),
            P("shard"),
            P(None, "shard"),
            P(None, "shard"),
            P("shard"),
            P("shard", None),
            P(None, "shard"),
            P("shard"),
            P("shard", None),
            P("shard"),
            P("shard", None),
            P("shard"),
            P(None, "shard"),
            P("shard", None),
        ),
        check_vma=False,
    )
```

```python
import functools
import math
from typing import Any, NamedTuple

import jax
import jax.numpy as jnp
from jax import lax
from jax.experimental import pallas as pl
from jax.experimental.pallas import tpu as pltpu
from jax.sharding import PartitionSpec as P

D = 512
DI = 1024
RANK = 32
HEADS = 8
STATE = 16
HEAD_DIM = 64
CONV = 4
CHUNKS = 8
LANES = 128
GROUPS_CH = DI // LANES
EDGE = (CONV - 1) * CHUNKS
OUTER = 4

SEL = 0
STEP = RANK + 2 * STATE
DEC = STEP + RANK
TAPS = DEC + STATE
BIAS = TAPS + CONV
STEPB = BIAS + 1
SKIP = STEPB + 1
GAINS = SKIP + 1
PACK = 128

EPS = 1e-05
NEG = -1e30
CUT = 1e30
F32 = jnp.float32
BF16 = jnp.bfloat16

VMEM = pl.BlockSpec(memory_space=pltpu.VMEM)
SMEM = pl.BlockSpec(memory_space=pltpu.SMEM)


def params(**more):
    return pltpu.CompilerParams(vmem_limit_bytes=60 << 20, **more)


def dot_nn(left, right):
    return lax.dot_general(left, right, (((1,), (0,)), ((), ())), preferred_element_type=F32)


def dot_nt(left, right):
    return lax.dot_general(left, right, (((1,), (1,)), ((), ())), preferred_element_type=F32)


def dot_tn(left, right):
    return lax.dot_general(left, right, (((0,), (0,)), ((), ())), preferred_element_type=F32)


def row_places(rows, steps):
    return (rows & (CHUNKS - 1)) * steps + (rows >> 3)


def starts_of(lengths_ref, nseq):
    starts = [jnp.int32(0)]
    for k in range(nseq - 1):
        starts.append(starts[-1] + lengths_ref[k])
    return starts


def start_of(places, starts):
    first = jnp.zeros_like(places)
    for start in starts[1:]:
        first = jnp.where(places >= start, start, first)
    return first


def begin_of(places, starts):
    found = places == starts[0]
    for start in starts[1:]:
        found = found | (places == start)
    return found


def norm(value):
    return lax.rsqrt(jnp.mean(value * value, axis=-1, keepdims=True) + EPS)


def silu_slope(value):
    s = jax.nn.sigmoid(value)
    return s * (1.0 + value * (1.0 - s))


def tile(step):
    return pl.ds(pl.multiple_of(step * CHUNKS, CHUNKS), CHUNKS)


def lanes_of(group):
    return pl.ds(pl.multiple_of(group * LANES, LANES), LANES)


def spread_decay(packed_ref, amat_ref, spread_ref):
    amat = -jnp.exp(packed_ref[DEC : DEC + STATE, :].astype(F32)) * math.log2(math.e)
    amat_ref[...] = amat
    for st in range(STATE):
        spread_ref[st * CHUNKS : (st + 1) * CHUNKS, :] = jnp.broadcast_to(
            amat[st : st + 1, :], (CHUNKS, DI)
        )


def spread_columns(source_ref, first, target_ref, steps):
    def one(step, carry):
        values = source_ref[tile(step), :]
        base = step * (STATE * CHUNKS)
        for st in range(STATE):
            at = pl.ds(pl.multiple_of(base + st * CHUNKS, CHUNKS), CHUNKS)
            column = values[:, first + st : first + st + 1]
            target_ref[at, :] = jnp.broadcast_to(column, (CHUNKS, LANES))
        return carry

    lax.fori_loop(0, steps, one, 0, unroll=2)


def state_at(step, st):
    return pl.ds(pl.multiple_of(step * (STATE * CHUNKS) + st * CHUNKS, CHUNKS), CHUNKS)


def at_seq(index):
    return {"device_id": {"seq": index}, "device_id_type": pl.DeviceIdType.MESH}


def at_shard(index):
    return {"device_id": {"shard": index}, "device_id_type": pl.DeviceIdType.MESH}


def greet(peers):
    barrier = pltpu.get_barrier_semaphore()
    for peer in peers:
        pl.semaphore_signal(barrier, inc=1, **peer)
    pl.semaphore_wait(barrier, len(peers))


def shard_peers(shards):
    shard = lax.axis_index("shard")
    core, chip = lax.rem(shard, 2), lax.div(shard, 2)
    partner = chip * 2 + 1 - core
    others = [lax.rem(chip + by, shards // 2) * 2 + core for by in range(1, shards // 2)]
    return shard, core, chip, partner, others


class Refs:
    def __init__(self, names, refs):
        for name, ref in zip(names, refs, strict=True):
            setattr(self, name, ref)


class ForwardIn(NamedTuple):
    lengths: Any
    tokens: Any
    cot: Any
    index: Any
    mixer: Any
    attention: Any
    select: Any
    stepw: Any
    decay: Any
    taps: Any
    bias: Any
    stepb: Any
    skip: Any
    wi: Any
    wo: Any
    wh: Any
    wm: Any


FORWARD_IN = ForwardIn._fields
class Kept(NamedTuple):
    x: Any
    wi_all: Any
    wo_all: Any
    wh_all: Any
    wm_all: Any
    packed: Any
    gains: Any
    span_totals: Any
    ext: Any
    zgate: Any
    conv: Any
    u: Any
    delta: Any
    xdbl: Any
    totals: Any
    yfull: Any
    gated: Any
    x1: Any
    init: Any
    dout: Any
    bx: Any
    cx: Any
    cut: Any
    du: Any
    context_send: Any


KEPT = Kept._fields
FORWARD_OUT = tuple(k + "_out" for k in KEPT) + ("dq_in", "dkv_in")
class ForwardScratch(NamedTuple):
    given: Any
    states: Any
    ends: Any
    row: Any
    small: Any
    wi_send: Any
    wo_send: Any
    wh_send: Any
    wm_send: Any
    packed_send: Any
    gains_send: Any
    packed_all: Any
    gains_all: Any
    before: Any
    state_send: Any
    total_send: Any
    amat: Any
    spread: Any
    q_send: Any
    d_send: Any
    kv_send: Any
    q_in: Any
    d_in: Any
    kv_in: Any
    kvt: Any
    score: Any
    dprob: Any
    dkv: Any
    dq_send: Any
    dkv_send: Any
    causal: Any
    gather_sem: Any
    cot_sem: Any
    edge_sem: Any
    state_sem: Any
    total_sem: Any
    q_sem: Any
    d_sem: Any
    kv_sem: Any
    dq_sem: Any
    dkv_sem: Any
    keep_sem: Any


FORWARD_SCRATCH = KEPT + ForwardScratch._fields


def forward_kernel(steps, nseq, shards, spans, *refs):
    r = Refs(FORWARD_IN + FORWARD_OUT + FORWARD_SCRATCH, refs)
    rows = steps * CHUNKS
    width = DI // shards
    me = lax.axis_index("seq")
    shard, core, chip, partner, others = shard_peers(shards)
    far = len(others)
    ring = [lax.rem(me + by, spans) for by in range(1, spans)]
    greet([at_shard(partner)] + [at_shard(o) for o in others] + [at_seq(to) for to in ring])

    def copy(source, target, sems, at, to):
        return pltpu.make_async_remote_copy(
            src_ref=source, dst_ref=target, send_sem=sems.at[(0, *at)], recv_sem=sems.at[(1, *at)], **to
        )

    sources = (r.wi_send, r.packed_send, r.gains_send, r.wo_send, r.wh_send, r.wm_send)
    wholes = (r.wi_all, r.packed_all, r.gains_all, r.wo_all, r.wh_all, r.wm_all)

    def sent(k, i):
        to = partner if i == far else others[i]
        return copy(sources[k], wholes[k].at[shard], r.gather_sem, (k, i), at_shard(to))

    def passed(k, i):
        came = lax.rem(chip + far - i, far + 1) * 2 + core
        return copy(
            wholes[k].at[came], wholes[k].at[came], r.gather_sem, (k, far + 1 + i), at_shard(partner)
        )

    def spread(*which):
        for k in which:
            for i in range(far + 1):
                sent(k, i).start()
        for k in which:
            wholes[k][shard] = sources[k][...]

    def pass_on(*which):
        for i in range(far):
            for k in which:
                sent(k, i).wait_recv()
                passed(k, i).start()

    def finish(*which):
        for k in which:
            for i in range(far):
                sent(k, i).wait_send()
                passed(k, i).wait()
            sent(k, far).wait()

    r.wi_send[...] = r.wi[...].astype(BF16)
    r.small[...] = jnp.zeros_like(r.small)
    for source, first in (
        (r.select, SEL),
        (r.decay, DEC),
        (r.stepw, STEP),
        (r.taps, TAPS),
        (r.bias, BIAS),
        (r.stepb, STEPB),
        (r.skip, SKIP),
    ):
        r.small[first : first + source.shape[0], :] = source[...]
    r.packed_send[...] = r.small[...].astype(BF16)
    lane = lax.broadcasted_iota(jnp.int32, (2 * CHUNKS, D // shards), 0)
    r.gains_send[...] = jnp.where(lane == 0, r.mixer[...], r.attention[...]).astype(BF16)
    spread(0, 1, 2)
    last = r.tokens.at[pl.ds(rows - 2 * CHUNKS, 2 * CHUNKS)]
    edge = copy(last, r.before, r.edge_sem, (), at_seq(ring[0]))
    edge.start()

    def cot_copy(by):
        return copy(
            r.cot.at[ring[by - 1]], r.given.at[me], r.cot_sem, (by,), at_seq(ring[by - 1])
        )

    for by in range(1, spans):
        cot_copy(by).start()
    r.given[me] = r.cot[me]
    r.wo_send[...] = r.wo[...].astype(BF16)
    r.wh_send[...] = r.wh[...].astype(BF16)
    r.wm_send[...] = r.wm[...].astype(BF16)
    for part in range(D // LANES):
        lanes = slice(part * LANES, (part + 1) * LANES)
        r.row[...] = r.tokens[:, lanes].astype(F32)
        for step in range(steps):
            r.x[step * CHUNKS : (step + 1) * CHUNKS, lanes] = r.row[
                pl.ds(step, CHUNKS, stride=steps), :
            ]
    pass_on(0, 1, 2)
    spread(3, 4, 5)
    finish(0, 1, 2)
    edge.wait()

    starts = starts_of(r.lengths, nseq)
    r.packed[...] = jnp.concatenate([r.packed_all[s] for s in range(shards)], axis=1)
    gains = jnp.concatenate([r.gains_all[s].astype(F32) for s in range(shards)], axis=1)
    r.gains[...] = gains[:CHUNKS]
    gain = gains[0:1]
    x = r.x[...]
    xn1 = (x * norm(x) * gain).astype(BF16)
    before = r.before[...].astype(F32)
    edge_n = (before * norm(before) * gain).astype(BF16)
    wide = 2 * DI // shards
    for s in range(shards):
        piece = dot_nn(xn1, r.wi_all[s])
        if s < shards // 2:
            r.ext[EDGE:, s * wide : (s + 1) * wide] = piece
        else:
            at = (s - shards // 2) * wide
            r.zgate[:, at : at + wide] = piece
    edge_x = jnp.concatenate([dot_nn(edge_n, r.wi_all[s]) for s in range(shards // 2)], axis=1)
    count = r.before.shape[0]
    chunk = lax.broadcasted_iota(jnp.int32, (CHUNKS, DI), 0)
    for k in range(CONV - 1):
        late = (steps - CONV + 1 + k) * CHUNKS + EDGE
        moved = pltpu.roll(r.ext[late : late + CHUNKS, :], 1, 0)
        at = count - CONV + 1 + k
        r.ext[k * CHUNKS : (k + 1) * CHUNKS, :] = jnp.where(
            chunk == 0, jnp.broadcast_to(edge_x[at : at + 1, :], (CHUNKS, DI)), moved
        )
    small = r.packed[DEC:PACK, :].astype(F32)
    taps = small[TAPS - DEC : TAPS - DEC + CONV, :]
    bias = small[BIAS - DEC : BIAS - DEC + 1, :]

    def conv_step(step, carry):
        places = lax.broadcasted_iota(jnp.int32, (CHUNKS, 1), 0) * steps + step + me * rows
        first = start_of(places, starts)
        total = jnp.broadcast_to(bias, (CHUNKS, DI))
        for k in range(CONV):
            at = pl.ds(pl.multiple_of((step + k) * CHUNKS, CHUNKS), CHUNKS)
            inside = places - (CONV - 1) + k >= first
            total = total + jnp.where(inside, taps[k : k + 1, :] * r.ext[at, :], 0.0)
        r.conv[tile(step), :] = total
        r.du[tile(step), :] = total * jax.nn.sigmoid(total)
        return carry

    lax.fori_loop(0, steps, conv_step, 0, unroll=2)
    u = r.du[...].astype(BF16)
    r.u[...] = u
    xdbl = dot_nt(u, r.packed[SEL : SEL + STEP, :])
    r.xdbl[...] = xdbl
    r.delta[...] = dot_nn(
        xdbl[:, :RANK].astype(BF16), r.packed[STEP : STEP + RANK, :]
    )
    stepb = small[STEPB - DEC : STEPB - DEC + 1, :]

    def delta_step(step, total):
        places = lax.broadcasted_iota(jnp.int32, (CHUNKS, 1), 0) * steps + step + me * rows
        pre = r.delta[tile(step), :] + stepb
        delta = jnp.maximum(pre, 0.0) + jnp.log1p(jnp.exp(-jnp.abs(pre)))
        r.delta[tile(step), :] = delta
        cut = jnp.where(begin_of(places, starts), CUT, delta)
        r.cut[tile(step), :] = cut
        r.du[tile(step), :] = delta * r.du[tile(step), :].astype(BF16).astype(F32)
        return total + cut

    totals = lax.fori_loop(0, steps, delta_step, jnp.zeros((CHUNKS, DI), F32), unroll=2)
    r.totals[...] = totals
    total = jnp.sum(totals, axis=0, keepdims=True)
    for group in range(GROUPS_CH):
        r.total_send[group : group + 1, :] = total[:, group * LANES : (group + 1) * LANES]
    r.span_totals[me] = r.total_send[...]

    def total_copy(by):
        return copy(
            r.total_send, r.span_totals.at[me], r.total_sem, (by,), at_seq(ring[by - 1])
        )

    for by in range(1, spans):
        total_copy(by).start()
    pass_on(3)
    spread_decay(r.packed, r.amat, r.spread)
    spread_columns(r.xdbl, RANK, r.bx, steps)

    def state_copy(by, at):
        return copy(
            r.state_send.at[at], r.states.at[me, at], r.state_sem, (by, at), at_seq(ring[by - 1])
        )

    def pair_step(pair, carry):
        for odd in range(2):
            lanes = lanes_of(pair * 2 + odd)
            amat = [r.spread[st * CHUNKS : (st + 1) * CHUNKS, lanes] for st in range(STATE)]

            def step_fn(step, states):
                cut = r.cut[tile(step), lanes]
                drive = r.du[tile(step), lanes]
                return tuple(
                    jnp.exp2(cut * amat[st]) * states[st] + drive * r.bx[state_at(step, st), :]
                    for st in range(STATE)
                )

            states = lax.fori_loop(
                0, steps, step_fn, (jnp.zeros((CHUNKS, LANES), F32),) * STATE, unroll=4
            )
            for st in range(STATE):
                r.ends[st, :, lanes] = states[st]
        lanes = pl.ds(pl.multiple_of(pair * 2 * LANES, 2 * LANES), 2 * LANES)
        amat = r.amat[:, lanes]
        state = jnp.zeros((STATE, 2 * LANES), F32)
        for k in range(CHUNKS):
            state = jnp.exp2(amat * r.totals[k : k + 1, lanes]) * state + r.ends[:, k, lanes]
        r.state_send[pair] = state.astype(BF16)
        for by in range(1, spans):

            @pl.when(me + by < spans)
            def _():
                state_copy(by, pair).start()

        return carry

    lax.fori_loop(0, GROUPS_CH // 2, pair_step, 0)
    pass_on(4, 5)
    for by in range(1, spans):
        cot_copy(by).wait()
    finish(3, 4, 5)

    ratio = spans // HEADS
    sub = lax.rem(me, ratio)
    head = lax.div(me, ratio)
    half = rows // 2
    given = jnp.concatenate([r.given[j] for j in range(spans)], axis=0)
    dout = dot_nn(pick_rows(r.index, me, rows, steps), given).astype(BF16)
    r.dout[...] = dout
    merge = jnp.concatenate([r.wm_all[s] for s in range(shards)], axis=0)
    dcontext = dot_nt(dout, merge).astype(BF16).astype(F32)
    low = lane_low(half)

    def packs(pair):
        above, below = pair[:half], pair[half:]
        yield jnp.where(low, above, pltpu.roll(below, HEAD_DIM, 1))
        yield jnp.where(low, pltpu.roll(above, HEAD_DIM, 1), below)

    for pair in range(HEADS // 2):
        at = pair * LANES
        for odd, pack in enumerate(packs(dcontext[:, at : at + LANES])):
            r.d_send[2 * pair + odd] = pack.astype(BF16)

    def rows_copy(source, target, sems, by):
        to = ring[by - 1]
        slot = lax.div(me, ratio)
        return copy(source.at[lax.div(to, ratio)], target.at[slot], sems, (by,), at_seq(to))

    def kv_copy(by):
        to = ring[by - 1]
        return copy(
            r.kv_send.at[lax.div(to, ratio)],
            r.kv_in.at[pl.ds(pl.multiple_of(me * rows, rows), rows)],
            r.kv_sem,
            (by,),
            at_seq(to),
        )

    def to_rows(source, target, sems, act):
        for by in range(1, spans):
            if ratio == 1:
                act(rows_copy(source, target, sems, by))
            else:
                pl.when(lax.rem(by, ratio) == 0)(lambda: act(rows_copy(source, target, sems, by)))

    to_rows(r.d_send, r.d_in, r.d_sem, lambda c: c.start())
    r.d_in[lax.div(me, ratio)] = r.d_send[head]
    spread_columns(r.xdbl, RANK + STATE, r.cx, steps)
    for by in range(1, spans):
        total_copy(by).wait()
        for pair in range(GROUPS_CH // 2):

            @pl.when(me + by < spans)
            def _():
                state_copy(by, pair).wait_send()

            @pl.when(me - by >= 0)
            def _():
                state_copy(by, pair).wait_recv()

    amat = r.amat[...]

    def chain(k, state):
        decay = jnp.exp2(amat * total_row(r.span_totals[k]))
        came = jnp.concatenate(
            [r.states[k, g].astype(F32) for g in range(GROUPS_CH // 2)], axis=1
        )
        return decay * state + came

    state = lax.fori_loop(0, me, chain, jnp.zeros((STATE, DI), F32))
    for k in range(CHUNKS):
        r.init[:, k, :] = state
        if k < CHUNKS - 1:
            state = jnp.exp2(amat * r.totals[k : k + 1, :]) * state + r.ends[:, k, :]

    def group_step(group, carry):
        lanes = lanes_of(group)
        amat_g = [r.spread[st * CHUNKS : (st + 1) * CHUNKS, lanes] for st in range(STATE)]

        def step_fn(step, states):
            cut = r.cut[tile(step), lanes]
            drive = r.du[tile(step), lanes]
            new = tuple(
                jnp.exp2(cut * amat_g[st]) * states[st] + drive * r.bx[state_at(step, st), :]
                for st in range(STATE)
            )
            terms = [new[st] * r.cx[state_at(step, st), :] for st in range(STATE)]
            while len(terms) > 1:
                terms = [a + b for a, b in zip(terms[::2], terms[1::2])]
            r.yfull[tile(step), lanes] = terms[0]
            return new

        lax.fori_loop(
            0, steps, step_fn, tuple(r.init[st, :, lanes] for st in range(STATE)), unroll=4
        )
        return carry

    lax.fori_loop(0, GROUPS_CH, group_step, 0)
    skip = small[SKIP - DEC : SKIP - DEC + 1, :]

    def gate_step(pair, carry):
        at = pl.ds(pl.multiple_of(pair * 2 * CHUNKS, 2 * CHUNKS), 2 * CHUNKS)
        yfull = r.yfull[at, :] + skip * r.u[at, :].astype(F32)
        r.yfull[at, :] = yfull
        gate = r.zgate[at, :]
        r.gated[at, :] = (yfull * (gate * jax.nn.sigmoid(gate))).astype(BF16)
        return carry

    lax.fori_loop(0, steps // 2, gate_step, 0)
    wo = jnp.concatenate([r.wo_all[s] for s in range(shards)], axis=0)
    x1 = r.x[...] + dot_nn(r.gated[...], wo)
    r.x1[...] = x1
    xn2 = (x1 * norm(x1) * gains[1:2, :]).astype(BF16)
    qkv = jnp.concatenate([dot_nn(xn2, r.wh_all[s]) for s in range(shards)], axis=1)
    qkv = qkv.astype(BF16).astype(F32)
    scale = 1.0 / math.sqrt(HEAD_DIM)
    full_low = lane_low(rows)
    for pair in range(HEADS // 2):
        at = pair * LANES
        for odd, pack in enumerate(packs(qkv[:, at : at + LANES] * scale)):
            r.q_send[2 * pair + odd] = pack.astype(BF16)
        k = qkv[:, D + at : D + at + LANES]
        v = qkv[:, 2 * D + at : 2 * D + at + LANES]
        r.kv_send[2 * pair] = jnp.where(full_low, k, pltpu.roll(v, HEAD_DIM, 1)).astype(BF16)
        r.kv_send[2 * pair + 1] = jnp.where(full_low, pltpu.roll(k, HEAD_DIM, 1), v).astype(BF16)
    to_rows(r.q_send, r.q_in, r.q_sem, lambda c: c.start())
    for by in range(1, spans):
        kv_copy(by).start()
    r.q_in[lax.div(me, ratio)] = r.q_send[head]
    r.kv_in[pl.ds(pl.multiple_of(me * rows, rows), rows), :] = r.kv_send[head]
    keeps = [
        pltpu.make_async_copy(getattr(r, name), getattr(r, name + "_out"), r.keep_sem.at[i])
        for i, name in enumerate(KEPT)
    ]
    for keep in keeps[:-1]:
        keep.start()
    query_local = row_places(lax.broadcasted_iota(jnp.int32, (1, rows), 1), steps)
    key_local = row_places(lax.broadcasted_iota(jnp.int32, (rows, 1), 0), steps)
    r.causal[...] = jnp.where(key_local <= query_local, 0.0, NEG)
    r.dkv[...] = jnp.zeros_like(r.dkv)
    to_rows(r.d_send, r.d_in, r.d_sem, lambda c: c.wait())
    to_rows(r.q_send, r.q_in, r.q_sem, lambda c: c.wait())
    for by in range(1, spans):
        kv_copy(by).wait()

    static = ratio == 1
    blocks = spans // ratio

    def each(count, fn, carry):
        if not static:
            return lax.fori_loop(0, count, fn, carry)
        for j in range(count):
            carry = fn(j, carry)
        return carry

    def key_rows(j):
        return pl.ds(j * rows if static else pl.multiple_of(j * rows, rows), rows)

    def turn(j, carry):
        r.kvt[j] = r.kv_in[key_rows(j), :].astype(F32).T.astype(BF16)
        return carry

    each(spans, turn, 0)
    folded = (rows // CHUNKS, CHUNKS, rows)

    def dq_copy(to, by, t):
        return copy(r.dq_send.at[t], r.dq_in.at[head], r.dq_sem, (by,), at_seq(to))

    def query_block(t, carry):
        i = t * ratio + sub
        slot = t % 2 if static else 0
        q = r.q_in[t].astype(F32)
        d = r.d_in[t].astype(F32)
        qt = q.T
        dt = d.T
        zero = jnp.zeros((HEAD_DIM, rows), F32)
        qt = jnp.concatenate([qt[:HEAD_DIM], qt[HEAD_DIM:]], axis=1)
        dt = jnp.concatenate([dt[:HEAD_DIM], dt[HEAD_DIM:]], axis=1)
        both = jnp.concatenate(
            [jnp.concatenate([qt, zero], axis=1), jnp.concatenate([zero, dt], axis=1)], axis=0
        ).astype(BF16)
        none = jnp.zeros((half, LANES), F32)
        natural = jnp.concatenate(
            [
                jnp.where(low, none, pltpu.roll(d, HEAD_DIM, 1)),
                jnp.where(low, none, d),
                jnp.where(low, q, none),
                jnp.where(low, pltpu.roll(q, HEAD_DIM, 1), none),
            ],
            axis=0,
        ).astype(BF16)
        first = start_of(query_local + i * rows, starts)

        def scores(j, top):
            joint = dot_nn(r.kv_in[key_rows(j), :], both)
            score = joint[:, :rows]
            if static:
                if j == t:
                    score = score + r.causal[...]
                if j in (0, t) or t == spans - 1:
                    score = jnp.where(key_local + j * rows >= first, score, NEG)
            else:
                query = query_local + i * rows
                key = key_local + j * rows
                score = jnp.where((key <= query) & (key >= first), score, NEG)
            r.score[slot, j] = score
            r.dprob[slot, j] = joint[:, rows:]
            return jnp.maximum(top, jnp.max(score.reshape(folded), axis=0))

        top = each(t + 1 if static else i + 1, scores, jnp.full((CHUNKS, rows), NEG, F32))
        top = jnp.max(top, axis=0, keepdims=True)

        def weigh(j, sums):
            total, dot = sums
            prob = jnp.exp(r.score[slot, j] - top)
            r.score[slot, j] = prob
            total = total + jnp.sum(prob.reshape(folded), axis=0)
            dot = dot + jnp.sum((prob * r.dprob[slot, j]).reshape(folded), axis=0)
            return total, dot

        zero = jnp.zeros((CHUNKS, rows), F32)
        total, dot = each(t + 1 if static else i + 1, weigh, (zero, zero))
        inverse = 1.0 / jnp.sum(total, axis=0, keepdims=True)
        datt = jnp.sum(dot, axis=0, keepdims=True) * inverse

        def back(j, sums):
            prob = r.score[slot, j] * inverse
            dscore = prob * (r.dprob[slot, j] - datt)
            joint = jnp.concatenate([prob.astype(BF16), dscore.astype(BF16)], axis=1)
            r.dkv[key_rows(j), :] += dot_nn(joint, natural)
            return sums + dot_nn(r.kvt[j], joint)

        sums = each(t + 1 if static else i + 1, back, jnp.zeros((LANES, 2 * rows), F32))
        dqt = sums[:HEAD_DIM, rows:] * scale
        ctx = sums[HEAD_DIM:, :rows]
        dqt = jnp.concatenate([dqt[:, :half], dqt[:, half:]], axis=0)
        ctx = jnp.concatenate([ctx[:, :half], ctx[:, half:]], axis=0)
        r.dq_send[t] = dqt.T.astype(BF16)
        r.context_send[t] = ctx.T.astype(BF16)
        by = lax.rem(i - me + spans, spans)

        @pl.when(i != me)
        def _():
            dq_copy(i, by, t).start()

        @pl.when(i == me)
        def _():
            r.dq_in[head] = r.dq_send[t]

        return carry

    if static:
        for t in range(blocks):
            query_block(t, 0)
    else:
        lax.fori_loop(0, blocks, query_block, 0)
    keeps[-1].start()

    def cast(j, carry):
        r.dkv_send[j] = r.dkv[key_rows(j), :].astype(BF16)
        return carry

    each(spans, cast, 0)

    def dkv_copy(by):
        to = ring[by - 1]
        return copy(r.dkv_send.at[to], r.dkv_in.at[me], r.dkv_sem, (by,), at_seq(to))

    for by in range(1, spans):
        dkv_copy(by).start()
    r.dkv_in[me] = r.dkv_send[me]
    for t in range(blocks):
        i = t * ratio + sub
        by = lax.rem(i - me + spans, spans)

        @pl.when(i != me)
        def _():
            dq_copy(i, by, t).wait_send()

    for h in range(HEADS):
        came = h * ratio + sub
        by = lax.rem(me - came + spans, spans)

        @pl.when(came != me)
        def _():
            dq_copy(came, by, 0).wait_recv()

    for by in range(1, spans):
        dkv_copy(by).wait()
    for keep in keeps:
        keep.wait()


def total_row(values):
    return jnp.concatenate([values[g : g + 1, :] for g in range(GROUPS_CH)], axis=1)


def lane_low(rows):
    return lax.broadcasted_iota(jnp.int32, (rows, LANES), 1) < HEAD_DIM


def pick_rows(table_ref, me, rows, steps):
    spans = table_ref.shape[0]
    share = rows // spans
    shift = lax.rem((spans - me) * share, rows)
    moved = pltpu.roll(table_ref[...], shift, 1)
    lane = lax.broadcasted_iota(jnp.int32, (1, rows), 1)
    index = moved[0:1]
    for j in range(1, spans):
        line = pltpu.roll(moved[j : j + 1], j * share, 1)
        index = jnp.where(lane >= j * share, line, index)
    places = row_places(lax.broadcasted_iota(jnp.int32, (rows, 1), 0), steps) + me * rows
    return (index == places.astype(F32)).astype(F32).astype(BF16)


GRADS = ("heads", "out", "merge", "late", "early", "small")
BACKWARD_IN = ("lengths", "index", "dq_in", "dkv_in") + tuple(k + "_kept" for k in KEPT)
class BackwardOut(NamedTuple):
    output: Any
    token_grad: Any
    last_heads: Any
    last_out: Any
    last_merge: Any
    last_small: Any
    pair_in: Any


BACKWARD_OUT = BackwardOut._fields
class FinalOut(NamedTuple):
    output: Any
    token_grad: Any
    mixer_grad: Any
    input_grad: Any
    taps_grad: Any
    bias_grad: Any
    select_grad: Any
    stepw_grad: Any
    stepb_grad: Any
    decay_grad: Any
    skip_grad: Any
    output_grad: Any
    attention_grad: Any
    heads_grad: Any
    merge_grad: Any


FINAL_OUT = FinalOut._fields
class BackwardScratch(NamedTuple):
    context: Any
    given: Any
    dx1: Any
    dys: Any
    dzgate: Any
    ends: Any
    grad_send: Any
    grads_in: Any
    db: Any
    dc: Any
    decay: Any
    held: Any
    state: Any
    bgrad: Any
    adelta: Any
    arrive: Any
    dxdbl: Any
    dext: Any
    spill: Any
    spill_in: Any
    small: Any
    row: Any
    amat: Any
    spread: Any
    sub_late: Any
    sub_early: Any


class BackwardSems(NamedTuple):
    load_sem: Any
    context_sem: Any
    given_sem: Any
    state_sem: Any
    spill_sem: Any
    near_sem: Any
    far_sem: Any
    part_sem: Any
    last_sem: Any
    pair_sem: Any
    inner_sem: Any
    outer_sem: Any
    late_outer_sem: Any
    late_inner_sem: Any


BACKWARD_SCRATCH = (
    KEPT
    + BackwardScratch._fields
    + tuple(kind + name for kind in ("g_", "near_", "sum_", "far_", "part_") for name in GRADS)
    + BackwardSems._fields
)


def backward_kernel(steps, nseq, shards, spans, *refs):
    r = Refs(BACKWARD_IN + BACKWARD_OUT + BACKWARD_SCRATCH, refs)
    rows = steps * CHUNKS
    width = DI // shards
    me = lax.axis_index("seq")
    shard, core, chip, partner, others = shard_peers(shards)
    chips = shards // 2
    ring = [lax.rem(me + by, spans) for by in range(1, spans)]
    every = [me] + ring
    ratio = spans // HEADS
    sub = lax.rem(me, ratio)
    half = rows // 2
    blocks = spans // ratio
    starts = starts_of(r.lengths, nseq)
    loads = {
        name: pltpu.make_async_copy(getattr(r, name + "_kept"), getattr(r, name), r.load_sem.at[i])
        for i, name in enumerate(KEPT)
    }
    early = ("context_send", "dout", "x1", "gains", "wh_all")
    middle = ("gated", "wo_all", "zgate", "yfull", "u", "x")
    late = ("wm_all", "packed", "cut", "cx", "totals", "span_totals", "init", "delta", "du", "bx", "xdbl")
    last = ("conv", "ext", "wi_all")
    for name in early + middle + late + last:
        loads[name].start()

    def loaded(*names):
        for name in names:
            loads[name].wait()

    targets = [lax.div(shard, 2), shards // 2 + lax.div(shard, 2)]
    mine = lax.div(shard, shards // 2)
    first_piece = 2 * lax.rem(shard, shards // 2)

    def anywhere(index, at):
        return {"device_id": {"seq": index, "shard": at}, "device_id_type": pl.DeviceIdType.MESH}

    barrier = pltpu.get_barrier_semaphore()

    def signal(to):
        pl.semaphore_signal(barrier, inc=1, **to)

    peers = [at_shard(partner)] + [at_shard(o) for o in others] + [at_seq(to) for to in ring]
    for peer in peers:
        signal(peer)
    selves = jnp.int32(0)
    for by in range(spans):
        for at in targets + [first_piece, first_piece + 1]:
            if by:
                signal(anywhere(every[by], at))
            else:
                pl.when(at != shard)(lambda: signal(anywhere(me, at)))
                selves = selves + (at == shard).astype(jnp.int32)
    pl.semaphore_wait(barrier, len(peers) + 4 * spans - selves)

    def copy(source, target, sems, at, to):
        return pltpu.make_async_remote_copy(
            src_ref=source, dst_ref=target, send_sem=sems.at[(0, *at)], recv_sem=sems.at[(1, *at)], **to
        )

    def ref(kind, k):
        return getattr(r, kind + "_" + GRADS[k])

    def near_copy(k, x):
        return copy(
            ref("g", k).at[x * 2 + 1 - core], ref("near", k).at[x], r.near_sem, (k, x), at_shard(partner)
        )

    def far_copy(k, by):
        source = ref("sum", k).at[lax.rem(chip + by, chips)]
        return copy(source, ref("far", k).at[by - 1], r.far_sem, (k, by), at_shard(others[by - 1]))

    def part_copy(k, by):
        to = ring[by - 1]
        return copy(
            ref("near", k).at[0, to], ref("part", k).at[by], r.part_sem, (k, by), at_seq(to)
        )

    def last_copy(k, by):
        held = ref("last", k).at[me]
        return copy(held, held, r.last_sem, (k, by), at_seq(ring[by - 1]))

    def pair_copy(by, at):
        return copy(
            r.sub_early, r.pair_in.at[at, me], r.pair_sem, (at, by), anywhere(every[by], targets[0])
        )

    def near_send(k):
        for x in range(chips):
            near_copy(k, x).start()

    def far_send(k):
        for x in range(chips):
            near_copy(k, x).wait_recv()
            ref("sum", k)[x] = (
                ref("g", k)[x * 2 + core].astype(F32) + ref("near", k)[x].astype(F32)
            ).astype(BF16)
        for by in range(1, chips):
            far_copy(k, by).start()

    def part_send(k):
        total = ref("sum", k)[chip].astype(F32)
        for by in range(1, chips):
            far_copy(k, by).wait_recv()
            total = total + ref("far", k)[by - 1].astype(F32)
        ref("near", k)[0] = total.astype(BF16)
        for by in range(1, chips):
            far_copy(k, by).wait_send()
        for by in range(1, spans):
            part_copy(k, by).start()

    def last_send(k):
        total = ref("near", k)[0, me].astype(F32)
        for by in range(1, spans):
            part_copy(k, by).wait_recv()
            total = total + ref("part", k)[by].astype(F32)
        if k == 5:
            ref("last", k)[me] = total.astype(BF16)
            for by in range(1, spans):
                last_copy(k, by).start()
            return
        r.sub_early[...] = total.astype(BF16)
        for by in range(spans):
            to_owner(by == 0, targets[0], pair_copy(by, parity), lambda c: c.start())

        @pl.when(targets[0] == shard)
        def _():
            r.pair_in[parity, me] = r.sub_early[...]

    def to_owner(same, to, made, act):
        if same:
            pl.when(to != shard)(lambda: act(made))
        else:
            act(made)

    inner = spans // OUTER
    low_me, high_me = lax.rem(me, inner), lax.div(me, inner)
    lows = [lax.rem(low_me + by, inner) for by in range(inner)]
    highs = [lax.rem(high_me + by, OUTER) for by in range(OUTER)]
    own_part = low_me * OUTER + high_me
    middle_at = (inner - 1) * OUTER
    parity = lax.rem(shard, 2)

    def inner_copy(k, by):
        return copy(
            ref("near", k).at[0, pl.ds(lows[by] * OUTER, OUTER)],
            ref("part", k).at[pl.ds((by - 1) * OUTER, OUTER)],
            r.inner_sem,
            (k, 0, by),
            at_seq(high_me * inner + lows[by]),
        )

    def outer_copy(k, by):
        return copy(
            ref("part", k).at[middle_at + highs[by]],
            ref("part", k).at[spans + by - 1],
            r.outer_sem,
            (k, 0, by),
            at_seq(highs[by] * inner + low_me),
        )

    def outer_last(k, by):
        held = ref("last", k).at[own_part]
        return copy(held, held, r.outer_sem, (k, 1, by), at_seq(highs[by] * inner + low_me))

    def inner_last(k, by):
        held = ref("last", k).at[pl.ds(low_me * OUTER, OUTER)]
        return copy(held, held, r.inner_sem, (k, 1, by), at_seq(high_me * inner + lows[by]))

    def late_outer(by, at):
        return copy(
            r.sub_late,
            r.pair_in.at[at, own_part],
            r.late_outer_sem,
            (at, by),
            anywhere(highs[by] * inner + low_me, targets[1]),
        )

    def late_inner(by, at):
        held = r.pair_in.at[at, pl.ds(low_me * OUTER, OUTER)]
        to = at_seq(high_me * inner + lows[by])
        return copy(held, held, r.late_inner_sem, (at, by), to)

    def inner_send(k):
        total = ref("sum", k)[chip].astype(F32)
        for by in range(1, chips):
            far_copy(k, by).wait_recv()
            total = total + ref("far", k)[by - 1].astype(F32)
        ref("near", k)[0] = total.astype(BF16)
        for by in range(1, inner):
            inner_copy(k, by).start()

    def outer_send(k):
        total = ref("near", k)[0, pl.ds(low_me * OUTER, OUTER)].astype(F32)
        for by in range(1, inner):
            inner_copy(k, by).wait_recv()
            total = total + ref("part", k)[(by - 1) * OUTER : by * OUTER].astype(F32)
        ref("part", k)[middle_at : middle_at + OUTER] = total.astype(BF16)
        for by in range(1, OUTER):
            outer_copy(k, by).start()

    def outer_back(k):
        total = ref("part", k)[middle_at + high_me].astype(F32)
        for by in range(1, OUTER):
            outer_copy(k, by).wait_recv()
            total = total + ref("part", k)[spans + by - 1].astype(F32)
        if k != 3:
            ref("last", k)[own_part] = total.astype(BF16)
            for by in range(1, OUTER):
                outer_last(k, by).start()
            return
        r.sub_late[...] = total.astype(BF16)
        for by in range(OUTER):
            to_owner(by == 0, targets[1], late_outer(by, parity), lambda c: c.start())

        @pl.when(targets[1] == shard)
        def _():
            r.pair_in[parity, own_part] = r.sub_late[...]

    def inner_back(k):
        if k != 3:
            for by in range(1, OUTER):
                outer_last(k, by).wait_recv()
            for by in range(1, inner):
                inner_last(k, by).start()
            return

        @pl.when(mine == 1)
        def _():
            for at in range(2):
                for by in range(OUTER):
                    to_owner(by == 0, first_piece + at, late_outer(by, at), lambda c: c.wait_recv())
                for by in range(1, inner):
                    late_inner(by, at).start()

    def finish(k):
        for x in range(chips):
            near_copy(k, x).wait_send()
        if k < 4:
            for by in range(1, chips):
                far_copy(k, by).wait_send()
            for by in range(1, inner):
                inner_copy(k, by).wait_send()
            for by in range(1, OUTER):
                outer_copy(k, by).wait_send()
        else:
            for by in range(1, spans):
                part_copy(k, by).wait_send()
        if k < 3:
            for by in range(1, OUTER):
                outer_last(k, by).wait_send()
            for by in range(1, inner):
                inner_last(k, by).wait()
        elif k == 3:
            for by in range(OUTER):
                to_owner(by == 0, targets[1], late_outer(by, parity), lambda c: c.wait_send())

            @pl.when(mine == 1)
            def _():
                for at in range(2):
                    for by in range(1, inner):
                        late_inner(by, at).wait()

        elif k == 5:
            for by in range(1, spans):
                last_copy(k, by).wait()
        else:
            for by in range(spans):
                to_owner(by == 0, targets[0], pair_copy(by, parity), lambda c: c.wait_send())

            @pl.when(mine == 0)
            def _():
                for at in range(2):
                    for by in range(spans):
                        to_owner(by == 0, first_piece + at, pair_copy(by, at), lambda c: c.wait_recv())

    def put(k, piece, value):
        size = value.shape[0] // spans
        for j in range(spans):
            ref("g", k)[piece, j] = value[j * size : (j + 1) * size].astype(BF16)

    loaded("context_send")
    head = lax.div(me, ratio)

    def context_copy(t, by, to):
        return copy(r.context_send.at[t], r.context.at[head], r.context_sem, (by,), at_seq(to))

    for t in range(blocks):
        i = t * ratio + sub
        by = lax.rem(i - me + spans, spans)

        @pl.when(i != me)
        def _():
            context_copy(t, by, i).start()

        @pl.when(i == me)
        def _():
            r.context[head] = r.context_send[t]

    low = lane_low(rows)
    half_low = lane_low(half)

    def unpacked(source, pair):
        even, odd = source[2 * pair].astype(F32), source[2 * pair + 1].astype(F32)
        return jnp.concatenate(
            [
                jnp.where(half_low, even, pltpu.roll(odd, HEAD_DIM, 1)),
                jnp.where(half_low, pltpu.roll(even, HEAD_DIM, 1), odd),
            ],
            axis=0,
        )

    dqs, dks, dvs = [], [], []
    for pair in range(HEADS // 2):
        dkv = [
            sum(r.dkv_in[(2 * pair + odd) * ratio + part].astype(F32) for part in range(ratio))
            for odd in range(2)
        ]
        dqs.append(unpacked(r.dq_in, pair))
        dks.append(jnp.where(low, dkv[0], pltpu.roll(dkv[1], HEAD_DIM, 1)))
        dvs.append(jnp.where(low, pltpu.roll(dkv[0], HEAD_DIM, 1), dkv[1]))
    dqkv = jnp.concatenate(dqs + dks + dvs, axis=1).astype(BF16)
    loaded("x1", "gains", "wh_all", "dout")
    x1 = r.x1[...]
    inverse = norm(x1)
    normal = x1 * inverse
    gain = r.gains[1:2, :]
    xn2 = (normal * gain).astype(BF16)
    wide = 3 * D // shards
    dxn2 = jnp.zeros((rows, D), F32)
    for s in range(shards):
        piece = dqkv[:, s * wide : (s + 1) * wide]
        put(0, s, dot_tn(xn2, piece))
        dxn2 = dxn2 + dot_nt(piece, r.wh_all[s])
    near_send(0)
    attention_gain = jnp.sum(dxn2 * normal, axis=0, keepdims=True)
    e2 = dxn2 * gain
    dx1 = r.dout[...].astype(F32) + inverse * (
        e2 - normal * jnp.mean(e2 * normal, axis=-1, keepdims=True)
    )
    r.dx1[...] = dx1
    dmixed = dx1.astype(BF16)
    loaded("gated", "wo_all")
    for s in range(shards):
        put(1, s, dot_tn(r.gated[:, s * width : (s + 1) * width], dmixed))
        r.dys[:, s * width : (s + 1) * width] = dot_nt(dmixed, r.wo_all[s])
    near_send(1)
    far_send(0)
    loaded("zgate", "yfull", "u", "x")

    def gate_step(pair, total):
        at = pl.ds(pl.multiple_of(pair * 2 * CHUNKS, 2 * CHUNKS), 2 * CHUNKS)
        dgated = r.dys[at, :].astype(BF16).astype(F32)
        gate = r.zgate[at, :]
        s = jax.nn.sigmoid(gate)
        dys = dgated * (gate * s)
        r.dys[at, :] = dys
        r.dzgate[at, :] = (dgated * r.yfull[at, :] * (s * (1.0 + gate * (1.0 - s)))).astype(BF16)
        return total + dys * r.u[at, :].astype(F32)

    total = lax.fori_loop(0, steps // 2, gate_step, jnp.zeros((2 * CHUNKS, DI), F32))
    r.small[SKIP : SKIP + 1, :] = jnp.sum(total, axis=0, keepdims=True)
    far_send(1)
    x = r.x[...]
    inverse_one = norm(x)
    normal_one = x * inverse_one
    gain_one = r.gains[0:1, :]
    xn1 = (normal_one * gain_one).astype(BF16)
    for s in range(shards):
        put(3, s, dot_tn(xn1, r.dzgate[:, s * width : (s + 1) * width]))
    near_send(3)
    loaded("wm_all", "packed", "cut", "cx", "totals", "span_totals")
    spread_decay(r.packed, r.amat, r.spread)

    def state_copy(by, at):
        to = lax.rem(me - by + spans, spans)
        return copy(
            r.grad_send.at[at], r.grads_in.at[me, at], r.state_sem, (by, at), at_seq(to)
        )

    def pair_step(pair, carry):
        for odd in range(2):
            lanes = lanes_of(pair * 2 + odd)
            amat = [r.spread[st * CHUNKS : (st + 1) * CHUNKS, lanes] for st in range(STATE)]

            def step_fn(turn, grads):
                step = steps - 1 - turn
                cut = r.cut[tile(step), lanes]
                dys = r.dys[tile(step), lanes]
                return tuple(
                    jnp.exp2(cut * amat[st]) * (grads[st] + dys * r.cx[state_at(step, st), :])
                    for st in range(STATE)
                )

            grads = lax.fori_loop(
                0, steps, step_fn, (jnp.zeros((CHUNKS, LANES), F32),) * STATE, unroll=4
            )
            for st in range(STATE):
                r.ends[st, :, lanes] = grads[st]
        lanes = pl.ds(pl.multiple_of(pair * 2 * LANES, 2 * LANES), 2 * LANES)
        amat = r.amat[:, lanes]
        state = jnp.zeros((STATE, 2 * LANES), F32)
        for k in reversed(range(CHUNKS)):
            state = jnp.exp2(amat * r.totals[k : k + 1, lanes]) * state + r.ends[:, k, lanes]
        r.grad_send[pair] = state.astype(BF16)
        for by in range(1, spans):

            @pl.when(me - by >= 0)
            def _():
                state_copy(by, pair).start()

        pl.when(pair == 0)(lambda: far_send(3))
        return carry

    lax.fori_loop(0, GROUPS_CH // 2, pair_step, 0)
    for h in range(HEADS):
        came = h * ratio + sub
        by = lax.rem(me - came + spans, spans)

        @pl.when(came != me)
        def _():
            context_copy(0, by, came).wait_recv()

    context = jnp.concatenate([unpacked(r.context, p) for p in range(HEADS // 2)], axis=1)
    context = context.astype(BF16)
    short = D // shards
    x2 = x1
    for s in range(shards):
        part = context[:, s * short : (s + 1) * short]
        x2 = x2 + dot_nn(part, r.wm_all[s])
        put(2, s, dot_tn(part, r.dout[...]))
    near_send(2)
    given = dot_tn(pick_rows(r.index, me, rows, steps), x2.astype(BF16))
    share = rows // spans
    for j in range(spans):
        r.given[j] = given[j * share : (j + 1) * share].astype(BF16)

    def given_copy(by):
        to = ring[by - 1]
        return copy(r.given.at[to], r.output.at[me], r.given_sem, (by,), at_seq(to))

    for by in range(1, spans):
        given_copy(by).start()
    r.output[me] = r.given[me]

    loaded("init", "delta", "du", "bx", "xdbl", *last)
    r.db[...] = jnp.zeros_like(r.db)
    r.dc[...] = jnp.zeros_like(r.dc)
    for by in range(1, spans):
        for pair in range(GROUPS_CH // 2):

            @pl.when(me - by >= 0)
            def _():
                state_copy(by, pair).wait_send()

            @pl.when(me + by < spans)
            def _():
                state_copy(by, pair).wait_recv()

    amat = r.amat[...]

    def chain(turn, state):
        k = spans - 1 - turn
        decay = jnp.exp2(amat * total_row(r.span_totals[k]))
        came = jnp.concatenate(
            [r.grads_in[k, g].astype(F32) for g in range(GROUPS_CH // 2)], axis=1
        )
        return decay * state + came

    state = lax.fori_loop(0, spans - 1 - me, chain, jnp.zeros((STATE, DI), F32))
    for k in reversed(range(CHUNKS)):
        r.arrive[:, k, :] = state
        if k:
            state = jnp.exp2(amat * r.totals[k : k + 1, :]) * state + r.ends[:, k, :]
    eight = STATE // 2

    def sum_of(terms):
        while len(terms) > 1:
            terms = [a + b for a, b in zip(terms[::2], terms[1::2])]
        return terms[0]

    def kept_at(step, i):
        return pl.ds(pl.multiple_of(step * (eight * CHUNKS) + i * CHUNKS, CHUNKS), CHUNKS)

    stages = {
        0: ((far_send, 2), (inner_send, 0)),
        1: ((inner_send, 1),),
        2: ((outer_send, 0),),
        3: ((outer_send, 1),),
        4: ((outer_back, 0),),
        5: ((inner_send, 3),),
        6: ((outer_back, 1), (inner_send, 2)),
        7: ((inner_back, 0), (outer_send, 3)),
    }

    def run(todo):
        for stage, k in todo:
            stage(k)

    def group_step(group, carry):
        lanes = lanes_of(group)
        for part in range(2):
            states = range(part * eight, (part + 1) * eight)
            amat_g = [r.spread[st * CHUNKS : (st + 1) * CHUNKS, lanes] for st in states]

            def forward(step, held):
                cut = r.cut[tile(step), lanes]
                drive = r.du[tile(step), lanes]
                out = []
                for i, st in enumerate(states):
                    decay = jnp.exp2(cut * amat_g[i])
                    kept = decay * held[i]
                    new = kept + drive * r.bx[state_at(step, st), :]
                    r.decay[kept_at(step, i), :] = decay
                    r.held[kept_at(step, i), :] = kept
                    r.state[kept_at(step, i), :] = new
                    out.append(new)
                return tuple(out)

            lax.fori_loop(
                0, steps, forward, tuple(r.init[st, :, lanes] for st in states), unroll=4
            )

            def backward(turn, held):
                grads, sums = held
                step = steps - 1 - turn
                delta = r.delta[tile(step), lanes]
                drive = r.du[tile(step), lanes]
                dys = r.dys[tile(step), lanes]
                new, totals, by_b, by_a = [], [], [], []
                for i, st in enumerate(states):
                    at = state_at(step, st)
                    grad = grads[i] + dys * r.cx[at, :]
                    new.append(r.decay[kept_at(step, i), :] * grad)
                    through = grad * r.held[kept_at(step, i), :]
                    totals.append(sums[i] + through * delta)
                    by_a.append(amat_g[i] * through)
                    by_b.append(grad * r.bx[at, :])
                    r.dc[at, :] += r.state[kept_at(step, i), :] * dys
                    r.db[at, :] += grad * drive
                if part:
                    r.bgrad[tile(step), lanes] += sum_of(by_b)
                    r.adelta[tile(step), lanes] += sum_of(by_a)
                else:
                    r.bgrad[tile(step), lanes] = sum_of(by_b)
                    r.adelta[tile(step), lanes] = sum_of(by_a)
                return (tuple(new), tuple(totals))

            _, sums = lax.fori_loop(
                0,
                steps,
                backward,
                (
                    tuple(r.arrive[st, :, lanes] for st in states),
                    (jnp.zeros((CHUNKS, LANES), F32),) * eight,
                ),
                unroll=4,
            )
            for i, st in enumerate(states):
                row = jnp.sum(sums[i], axis=0, keepdims=True)
                amat_row = amat_g[i][0:1, :] * math.log(2.0)
                r.small[DEC + st : DEC + st + 1, lanes] = row * amat_row
        for at, todo in stages.items():
            pl.when(group == at)(functools.partial(run, todo))
        return carry

    lax.fori_loop(0, GROUPS_CH, group_step, 0)
    small = r.packed[DEC:PACK, :].astype(F32)
    taps = small[TAPS - DEC : TAPS - DEC + CONV, :]
    skip = small[SKIP - DEC : SKIP - DEC + 1, :]

    def delta_step(step, total):
        at = tile(step)
        bgrad = r.bgrad[at, :]
        delta = r.delta[at, :]
        u = r.conv[at, :]
        u = (u * jax.nn.sigmoid(u)).astype(BF16).astype(F32)
        ddelta = u * bgrad + r.adelta[at, :] * math.log(2.0)
        dtpre = (ddelta * (1.0 - jnp.exp(-delta))).astype(BF16).astype(F32)
        r.adelta[at, :] = dtpre
        r.bgrad[at, :] = r.dys[at, :] * skip + delta * bgrad
        return total + dtpre

    total = lax.fori_loop(0, steps, delta_step, jnp.zeros((CHUNKS, DI), F32))
    run(((inner_back, 1), (outer_send, 2)))
    r.small[STEPB : STEPB + 1, :] = jnp.sum(total, axis=0, keepdims=True)
    r.small[GAINS:, :] = jnp.zeros((PACK - GAINS, DI), F32)
    dtpre = r.adelta[...].astype(BF16)
    steplow = r.xdbl[:, 0:RANK].astype(BF16)
    r.small[STEP : STEP + RANK, :] = dot_tn(steplow, dtpre)
    r.dxdbl[:, 0:RANK] = dot_nt(dtpre, r.packed[STEP : STEP + RANK, :])
    lane = lax.broadcasted_iota(jnp.int32, (CHUNKS, 2 * STATE), 1)

    def gather_step(step, carry):
        total = jnp.zeros((CHUNKS, 2 * STATE), F32)
        for st in range(STATE):
            at = state_at(step, st)
            total = jnp.where(lane == st, jnp.sum(r.db[at, :], axis=1, keepdims=True), total)
            total = jnp.where(
                lane == STATE + st, jnp.sum(r.dc[at, :], axis=1, keepdims=True), total
            )
        r.dxdbl[tile(step), RANK:] = total
        return carry

    lax.fori_loop(0, steps, gather_step, 0, unroll=2)
    run(((outer_back, 3),))
    dxdbl = r.dxdbl[...].astype(BF16)
    r.small[SEL : SEL + STEP, :] = dot_tn(dxdbl, r.u[...])
    r.bgrad[...] += dot_nn(dxdbl, r.packed[SEL : SEL + STEP, :])
    r.dext[...] = jnp.zeros_like(r.dext)
    r.spill[...] = jnp.zeros_like(r.spill)

    @pl.when(me == spans - 1)
    def _():
        r.spill_in[...] = jnp.zeros_like(r.spill_in)

    zero = jnp.zeros((CHUNKS, DI), F32)

    def conv_step(step, totals):
        at = tile(step)
        dconv = r.bgrad[at, :] * silu_slope(r.conv[at, :])
        places = lax.broadcasted_iota(jnp.int32, (CHUNKS, 1), 0) * steps + step + me * rows
        first = start_of(places, starts)
        out = []
        for k in range(CONV):
            to = pl.ds(pl.multiple_of((step + k) * CHUNKS, CHUNKS), CHUNKS)
            inside = jnp.where(places - (CONV - 1) + k >= first, dconv, 0.0)
            out.append(totals[k] + inside * r.ext[to, :])
            r.dext[to, :] += taps[k : k + 1, :] * inside
        return tuple(out) + (totals[CONV] + dconv,)

    totals = lax.fori_loop(0, CONV - 1, conv_step, (zero,) * (CONV + 1))
    for k in range(CONV - 1):
        r.spill[k : k + 1, :] = r.dext[k * CHUNKS : k * CHUNKS + 1, :]
    behind = lax.rem(me + spans - 1, spans)
    spill = copy(r.spill, r.spill_in, r.spill_sem, (), at_seq(behind))

    @pl.when(me > 0)
    def _():
        spill.start()

    totals = lax.fori_loop(CONV - 1, steps, conv_step, totals)
    run(((outer_back, 2),))
    for k in range(CONV):
        r.small[TAPS + k : TAPS + k + 1, :] = jnp.sum(totals[k], axis=0, keepdims=True)
    r.small[BIAS : BIAS + 1, :] = jnp.sum(totals[CONV], axis=0, keepdims=True)

    @pl.when(me > 0)
    def _():
        spill.wait_send()

    @pl.when(me < spans - 1)
    def _():
        spill.wait_recv()

    chunk = lax.broadcasted_iota(jnp.int32, (CHUNKS, DI), 0)
    for k in range(CONV - 1):
        block = r.dext[k * CHUNKS : (k + 1) * CHUNKS, :]
        late = (steps - CONV + 1 + k) * CHUNKS + EDGE
        moved = pltpu.roll(block, CHUNKS - 1, 0)
        came = jnp.broadcast_to(r.spill_in[k : k + 1, :], (CHUNKS, DI))
        r.dext[late : late + CHUNKS, :] += jnp.where(chunk < CHUNKS - 1, moved, came)
    dxin = r.dext[EDGE:, :].astype(BF16)
    for s in range(shards):
        put(4, s, dot_tn(xn1, dxin[:, s * width : (s + 1) * width]))
    near_send(4)
    run(((inner_back, 3), (inner_back, 2)))
    wide = 2 * width
    dxn1 = jnp.zeros((rows, D), F32)
    for s in range(shards):
        at = s * wide % DI
        if s < shards // 2:
            piece = dxin[:, at : at + wide]
        else:
            piece = r.dzgate[:, at : at + wide]
        dxn1 = dxn1 + dot_nt(piece, r.wi_all[s])
    mixer_gain = jnp.sum(dxn1 * normal_one, axis=0, keepdims=True)
    for s in range(shards):
        at = s * width
        gains = slice(s * short, (s + 1) * short)
        r.small[GAINS : GAINS + 1, at : at + short] = mixer_gain[:, gains]
        r.small[GAINS : GAINS + 1, at + short : at + 2 * short] = attention_gain[:, gains]
    for s in range(shards):
        put(5, s, r.small[:, s * width : (s + 1) * width])
    near_send(5)
    far_send(4)
    far_send(5)
    e1 = dxn1 * gain_one
    dx = r.dx1[...] + inverse_one * (
        e1 - normal_one * jnp.mean(e1 * normal_one, axis=-1, keepdims=True)
    )
    r.dx1[...] = dx
    for part in range(D // LANES):
        lanes = slice(part * LANES, (part + 1) * LANES)
        for step in range(steps):
            r.row[pl.ds(step, CHUNKS, stride=steps), :] = r.dx1[
                step * CHUNKS : (step + 1) * CHUNKS, lanes
            ]
        r.token_grad[:, lanes] = r.row[...]
    part_send(4)
    part_send(5)
    for k in (0, 1, 2, 3):
        finish(k)
    last_send(4)
    last_send(5)
    for by in range(1, spans):
        given_copy(by).wait()
    for t in range(blocks):
        i = t * ratio + sub
        by = lax.rem(i - me + spans, spans)

        @pl.when(i != me)
        def _():
            context_copy(t, by, i).wait_send()

    finish(5)
    finish(4)


def final_kernel(*refs):
    r = Refs(tuple(k + "_in" for k in BACKWARD_OUT) + FINAL_OUT, refs)

    def whole(source):
        return jnp.concatenate([source[j].astype(F32) for j in range(source.shape[0])], axis=0)

    r.output[...] = r.output_in[...]
    r.token_grad[...] = r.token_grad_in[...]
    r.heads_grad[...] = whole(r.last_heads_in)
    r.output_grad[...] = whole(r.last_out_in)
    r.merge_grad[...] = whole(r.last_merge_in)
    small = whole(r.last_small_in)
    short = r.mixer_grad.shape[1]
    width = r.taps_grad.shape[1]
    r.select_grad[...] = small[SEL : SEL + STEP]
    r.stepw_grad[...] = small[STEP : STEP + RANK]
    r.decay_grad[...] = small[DEC : DEC + STATE]
    r.taps_grad[...] = small[TAPS : TAPS + CONV]
    r.bias_grad[...] = small[BIAS : BIAS + 1]
    r.stepb_grad[...] = small[STEPB : STEPB + 1]
    r.skip_grad[...] = small[SKIP : SKIP + 1]
    r.mixer_grad[...] = small[GAINS : GAINS + 1, :short]
    r.attention_grad[...] = small[GAINS : GAINS + 1, short:]
    for parity in range(2):
        r.input_grad[:, parity * width : (parity + 1) * width] = whole(r.pair_in_in.at[parity])


def shape(*dims, kind=F32):
    return jax.ShapeDtypeStruct(dims, kind)


def vmem(*dims, kind=F32):
    return pltpu.VMEM(dims, kind)


def per_device(
    tokens,
    cotangent,
    positions,
    lengths,
    mixer_gain,
    input_weight,
    kernel_weight,
    kernel_bias,
    select_weight,
    step_weight,
    step_bias,
    decay_log,
    skip_scale,
    output_weight,
    attention_gain,
    heads_weight,
    merge_weight,
):
    spans = lax.axis_size("seq")
    shards = lax.axis_size("shard")
    rows = tokens.shape[1]
    steps = rows // CHUNKS
    share = rows // spans
    nseq = lengths.shape[1]
    ratio = spans // HEADS
    part = rows // ratio
    width = DI // shards

    index = positions[0].reshape(spans, rows).astype(F32)
    dma = pltpu.SemaphoreType.DMA
    spread = [vmem(STATE, DI), vmem(STATE * CHUNKS, DI)]
    columns = vmem(rows * STATE, LANES)
    plane = vmem(rows, DI)
    gain_len = D // shards
    halves = GROUPS_CH // 2
    weights = [(D, 2 * width), (width, D), (D, 3 * D // shards), (gain_len, D)]
    half = rows // 2
    blocks = spans // ratio
    slots = 2 if ratio == 1 else 1
    kept = (
        [shape(rows, D)]
        + [shape(shards, *w, kind=BF16) for w in weights]
        + [
            shape(PACK, DI, kind=BF16),
            shape(CHUNKS, D),
            shape(spans, GROUPS_CH, LANES),
            shape(EDGE + rows, DI),
            shape(rows, DI),
            shape(rows, DI),
            shape(rows, DI, kind=BF16),
            shape(rows, DI),
            shape(rows, STEP),
            shape(CHUNKS, DI),
            shape(rows, DI),
            shape(rows, DI, kind=BF16),
            shape(rows, D),
            shape(STATE, CHUNKS, DI),
            shape(rows, D, kind=BF16),
            shape(rows * STATE, LANES),
            shape(rows * STATE, LANES),
            shape(rows, DI),
            shape(rows, DI),
            shape(blocks, half, LANES, kind=BF16),
        ]
    )
    back = [shape(HEADS, half, LANES, kind=BF16), shape(spans, rows, LANES, kind=BF16)]
    inputs = [
        lengths[0],
        tokens[0],
        cotangent[0].reshape(spans, share, D),
        index,
        mixer_gain[None],
        attention_gain[None],
        select_weight.T,
        step_weight,
        decay_log.T,
        kernel_weight,
        kernel_bias[None],
        step_bias[None],
        skip_scale[None],
        input_weight,
        output_weight,
        heads_weight,
        merge_weight,
    ]
    outs = pl.pallas_call(
        functools.partial(forward_kernel, steps, nseq, shards, spans),
        out_shape=kept + back,
        in_specs=[SMEM] + [VMEM] * (len(inputs) - 1),
        out_specs=[pl.BlockSpec(memory_space=pl.ANY)] * len(kept) + [VMEM] * len(back),
        scratch_shapes=[vmem(*k.shape, kind=k.dtype) for k in kept]
        + [
            vmem(spans, share, D, kind=BF16),
            vmem(spans, halves, STATE, 2 * LANES, kind=BF16),
            vmem(STATE, CHUNKS, DI),
            vmem(rows, LANES),
            vmem(PACK, width),
        ]
        + [vmem(*w, kind=BF16) for w in weights]
        + [
            vmem(PACK, width, kind=BF16),
            vmem(2 * CHUNKS, gain_len, kind=BF16),
            vmem(shards, PACK, width, kind=BF16),
            vmem(shards, 2 * CHUNKS, gain_len, kind=BF16),
            vmem(2 * CHUNKS, D, kind=BF16),
            vmem(halves, STATE, 2 * LANES, kind=BF16),
            vmem(GROUPS_CH, LANES),
        ]
        + spread
        + [
            vmem(HEADS, half, LANES, kind=BF16),
            vmem(HEADS, half, LANES, kind=BF16),
            vmem(HEADS, rows, LANES, kind=BF16),
            vmem(blocks, half, LANES, kind=BF16),
            vmem(blocks, half, LANES, kind=BF16),
            vmem(spans * rows, LANES, kind=BF16),
            vmem(spans, LANES, rows, kind=BF16),
            vmem(slots, spans, rows, rows),
            vmem(slots, spans, rows, rows),
            vmem(spans * rows, LANES),
            vmem(blocks, half, LANES, kind=BF16),
            vmem(spans, rows, LANES, kind=BF16),
            vmem(rows, rows),
            dma((2, 6, shards - 1)),
            dma((2, spans)),
            dma((2,)),
            dma((2, spans, halves)),
        ]
        + [dma((2, spans))] * 6
        + [dma((len(kept),))],
        compiler_params=params(collective_id=0, has_side_effects=True),
        name="forward",
    )(*inputs)
    saved, back = outs[: len(kept)], outs[len(kept) :]
    parts = {
        "heads": (D // spans, 3 * D // shards),
        "out": (width // spans, D),
        "merge": (gain_len // spans, D),
        "late": (D // spans, width),
        "early": (D // spans, width),
        "small": (PACK // spans, width),
    }
    chips = shards // 2
    sizes = [(spans, *parts[k]) for k in GRADS]
    count = len(GRADS)
    anyspace = pl.BlockSpec(memory_space=pl.ANY)
    summed = [
        shape(spans, share, D, kind=BF16),
        shape(rows, D),
        shape(spans, *parts["heads"], kind=BF16),
        shape(spans, *parts["out"], kind=BF16),
        shape(spans, *parts["merge"], kind=BF16),
        shape(spans, *parts["small"], kind=BF16),
        shape(2, spans, *parts["late"], kind=BF16),
    ]
    few = vmem(rows * STATE // 2, LANES)
    state = vmem(STATE, CHUNKS, DI)
    summed = pl.pallas_call(
        functools.partial(backward_kernel, steps, nseq, shards, spans),
        out_shape=summed,
        in_specs=[SMEM] + [VMEM] * 3 + [anyspace] * len(kept),
        out_specs=[VMEM] * len(summed),
        scratch_shapes=[vmem(*k.shape, kind=k.dtype) for k in kept]
        + [
            vmem(HEADS, half, LANES, kind=BF16),
            vmem(spans, share, D, kind=BF16),
            vmem(rows, D),
            plane,
            vmem(rows, DI, kind=BF16),
            state,
            vmem(halves, STATE, 2 * LANES, kind=BF16),
            vmem(spans, halves, STATE, 2 * LANES, kind=BF16),
            columns,
            columns,
            few,
            few,
            few,
            plane,
            plane,
            state,
            vmem(rows, STEP),
            vmem(EDGE + rows, DI),
            vmem(CHUNKS, DI),
            vmem(CHUNKS, DI),
            vmem(PACK, DI),
            vmem(rows, LANES),
        ]
        + spread
        + [
            vmem(*parts["late"], kind=BF16),
            vmem(*parts["late"], kind=BF16),
        ]
        + [vmem(shards, *k, kind=BF16) for k in sizes]
        + [vmem(chips, *k, kind=BF16) for k in sizes] * 2
        + [vmem(max(chips - 1, 1), *k, kind=BF16) for k in sizes]
        + [vmem(spans + OUTER - 1, *k[1:], kind=BF16) for k in sizes]
        + [
            dma((len(kept),)),
            dma((2, spans)),
            dma((2, spans)),
            dma((2, spans, halves)),
            dma((2,)),
            dma((2, count, chips)),
            dma((2, count, chips)),
            dma((2, count, spans)),
            dma((2, count, spans)),
            dma((2, 2, spans)),
            dma((2, 4, 2, spans // OUTER)),
            dma((2, 4, 2, OUTER)),
            dma((2, 2, OUTER)),
            dma((2, 2, spans // OUTER)),
        ],
        compiler_params=params(collective_id=1, has_side_effects=True),
        name="backward",
    )(lengths[0], index, *back, *saved)
    results = pl.pallas_call(
        final_kernel,
        out_shape=[
            shape(rows, D, kind=BF16),
            shape(rows, D),
            shape(1, gain_len),
            shape(D, 2 * width),
            shape(CONV, width),
            shape(1, width),
            shape(STEP, width),
            shape(RANK, width),
            shape(1, width),
            shape(STATE, width),
            shape(1, width),
            shape(width, D),
            shape(1, gain_len),
            shape(D, 3 * D // shards),
            shape(gain_len, D),
        ],
        in_specs=[VMEM] * len(summed),
        out_specs=[VMEM] * len(FINAL_OUT),
        compiler_params=params(),
        name="final",
    )(summed[0].reshape(rows, D), *summed[1:])
    flat, turned = {2, 5, 8, 10, 12}, {6, 9}
    return tuple(
        v[None] if i < 2 else v.reshape(-1) if i in flat else v.T if i in turned else v
        for i, v in enumerate(results)
    )


def solution(mesh):
    return jax.shard_map(
        per_device,
        mesh=mesh,
        in_specs=(
            P("shard", "seq", None),
            P("shard", "seq", None),
            P("shard", None),
            P("shard", None),
            P("shard"),
            P(None, "shard"),
            P(None, "shard"),
            P("shard"),
            P("shard", None),
            P(None, "shard"),
            P("shard"),
            P("shard", None),
            P("shard"),
            P("shard", None),
            P("shard"),
            P(None, "shard"),
            P("shard", None),
        ),
        out_specs=(
            P("shard", "seq", None),
            P("shard", "seq", None),
            P("shard"),
            P(None, "shard"),
            P(None, "shard"),
            P("shard"),
            P("shard", None),
            P(None, "shard"),
            P("shard"),
            P("shard", None),
            P("shard"),
            P("shard", None),
            P("shard"),
            P(None, "shard"),
            P("shard", None),
        ),
        check_vma=False,
    )
```

```python
import functools
import math
from typing import Any, NamedTuple

import jax
import jax.numpy as jnp
from jax import lax
from jax.experimental import pallas as pl
from jax.experimental.pallas import tpu as pltpu
from jax.sharding import PartitionSpec as P

D = 512
DI = 1024
RANK = 32
HEADS = 8
STATE = 16
HEAD_DIM = 64
CONV = 4
CHUNKS = 8
LANES = 128
GROUPS_CH = DI // LANES
EDGE = (CONV - 1) * CHUNKS
OUTER = 4

SEL = 0
STEP = RANK + 2 * STATE
DEC = STEP + RANK
TAPS = DEC + STATE
BIAS = TAPS + CONV
STEPB = BIAS + 1
SKIP = STEPB + 1
GAINS = SKIP + 1
PACK = 128

EPS = 1e-05
NEG = -1e30
CUT = 1e30
F32 = jnp.float32
BF16 = jnp.bfloat16

VMEM = pl.BlockSpec(memory_space=pltpu.VMEM)
SMEM = pl.BlockSpec(memory_space=pltpu.SMEM)


def params(**more):
    return pltpu.CompilerParams(vmem_limit_bytes=62 << 20, **more)


def dot_nn(left, right):
    return lax.dot_general(left, right, (((1,), (0,)), ((), ())), preferred_element_type=F32)


def dot_nt(left, right):
    return lax.dot_general(left, right, (((1,), (1,)), ((), ())), preferred_element_type=F32)


def dot_tn(left, right):
    return lax.dot_general(left, right, (((0,), (0,)), ((), ())), preferred_element_type=F32)


def row_places(rows, steps):
    return (rows & (CHUNKS - 1)) * steps + (rows >> 3)


def starts_of(lengths_ref, nseq):
    starts = [jnp.int32(0)]
    for k in range(nseq - 1):
        starts.append(starts[-1] + lengths_ref[k])
    return starts


def start_of(places, starts):
    first = jnp.zeros_like(places)
    for start in starts[1:]:
        first = jnp.where(places >= start, start, first)
    return first


def begin_of(places, starts):
    found = places == starts[0]
    for start in starts[1:]:
        found = found | (places == start)
    return found


def norm(value):
    return lax.rsqrt(jnp.mean(value * value, axis=-1, keepdims=True) + EPS)


def silu_slope(value):
    s = jax.nn.sigmoid(value)
    return s * (1.0 + value * (1.0 - s))


def tile(step):
    return pl.ds(pl.multiple_of(step * CHUNKS, CHUNKS), CHUNKS)


def lanes_of(group):
    return pl.ds(pl.multiple_of(group * LANES, LANES), LANES)


def spread_decay(packed_ref, amat_ref, spread_ref):
    amat = -jnp.exp(packed_ref[DEC : DEC + STATE, :].astype(F32)) * math.log2(math.e)
    amat_ref[...] = amat
    for st in range(STATE):
        spread_ref[st * CHUNKS : (st + 1) * CHUNKS, :] = jnp.broadcast_to(
            amat[st : st + 1, :], (CHUNKS, DI)
        )


def column(st):
    return slice(st * LANES, (st + 1) * LANES)


def thirds(value):
    high = value.astype(BF16)
    rest = value - high.astype(F32)
    middle = rest.astype(BF16)
    return high, middle, (rest - middle.astype(F32)).astype(BF16)


def spread_columns(values):
    terms = jnp.concatenate([t.astype(F32) for t in thirds(values)], axis=1).astype(BF16)
    count = terms.shape[1]
    line = lax.broadcasted_iota(jnp.int32, (count, STATE * LANES), 0)
    lane = lax.broadcasted_iota(jnp.int32, (count, STATE * LANES), 1)
    chosen = (line & (STATE - 1)) == lax.div(lane, LANES)
    return dot_nn(terms, chosen.astype(F32).astype(BF16))


def gather_columns(value):
    line = lax.broadcasted_iota(jnp.int32, (STATE * LANES, STATE), 0)
    lane = lax.broadcasted_iota(jnp.int32, (STATE * LANES, STATE), 1)
    chosen = (lax.div(line, LANES) == lane).astype(F32).astype(BF16)
    return sum(dot_nn(term, chosen) for term in thirds(value)[:2])


def at_seq(index):
    return {"device_id": {"seq": index}, "device_id_type": pl.DeviceIdType.MESH}


def at_shard(index):
    return {"device_id": {"shard": index}, "device_id_type": pl.DeviceIdType.MESH}


def greet(peers):
    barrier = pltpu.get_barrier_semaphore()
    for peer in peers:
        pl.semaphore_signal(barrier, inc=1, **peer)
    pl.semaphore_wait(barrier, len(peers))


def shard_peers(shards):
    shard = lax.axis_index("shard")
    core, chip = lax.rem(shard, 2), lax.div(shard, 2)
    partner = chip * 2 + 1 - core
    others = [lax.rem(chip + by, shards // 2) * 2 + core for by in range(1, shards // 2)]
    return shard, core, chip, partner, others


class Refs:
    def __init__(self, names, refs):
        for name, ref in zip(names, refs, strict=True):
            setattr(self, name, ref)


class ForwardIn(NamedTuple):
    lengths: Any
    tokens: Any
    cot: Any
    index: Any
    mixer: Any
    attention: Any
    select: Any
    stepw: Any
    decay: Any
    taps: Any
    bias: Any
    stepb: Any
    skip: Any
    wi: Any
    wo: Any
    wh: Any
    wm: Any


FORWARD_IN = ForwardIn._fields
class Kept(NamedTuple):
    x: Any
    wi_all: Any
    wo_all: Any
    wh_all: Any
    wm_all: Any
    packed: Any
    gains: Any
    span_totals: Any
    ext: Any
    zgate: Any
    conv: Any
    u: Any
    delta: Any
    xdbl: Any
    totals: Any
    yfull: Any
    gated: Any
    x1: Any
    init: Any
    dout: Any
    bx: Any
    cx: Any
    cut: Any
    du: Any
    context_send: Any


KEPT = Kept._fields
FORWARD_OUT = tuple(k + "_out" for k in KEPT) + ("dq_in", "dkv_in")
class ForwardScratch(NamedTuple):
    given: Any
    states: Any
    ends: Any
    row: Any
    small: Any
    wi_send: Any
    wo_send: Any
    wh_send: Any
    wm_send: Any
    packed_send: Any
    gains_send: Any
    packed_all: Any
    gains_all: Any
    before: Any
    state_send: Any
    total_send: Any
    amat: Any
    spread: Any
    q_send: Any
    d_send: Any
    kv_send: Any
    q_in: Any
    d_in: Any
    kv_in: Any
    kvt: Any
    score: Any
    dprob: Any
    dkv: Any
    dq_send: Any
    dkv_send: Any
    causal: Any
    gather_sem: Any
    share_sem: Any
    cot_sem: Any
    edge_sem: Any
    state_sem: Any
    total_sem: Any
    q_sem: Any
    d_sem: Any
    kv_sem: Any
    dq_sem: Any
    dkv_sem: Any
    keep_sem: Any


FORWARD_SCRATCH = KEPT + ForwardScratch._fields


def forward_kernel(steps, nseq, shards, spans, *refs):
    r = Refs(FORWARD_IN + FORWARD_OUT + FORWARD_SCRATCH, refs)
    rows = steps * CHUNKS
    width = DI // shards
    me = lax.axis_index("seq")
    shard, core, chip, partner, others = shard_peers(shards)
    far = len(others)
    ring = [lax.rem(me + by, spans) for by in range(1, spans)]
    greet([at_shard(partner)] + [at_shard(o) for o in others] + [at_seq(to) for to in ring])

    def copy(source, target, sems, at, to):
        return pltpu.make_async_remote_copy(
            src_ref=source, dst_ref=target, send_sem=sems.at[(0, *at)], recv_sem=sems.at[(1, *at)], **to
        )

    sources = (r.wi_send, r.packed_send, r.gains_send, r.wo_send, r.wh_send, r.wm_send)
    wholes = (r.wi_all, r.packed_all, r.gains_all, r.wo_all, r.wh_all, r.wm_all)

    share = D // 2 // spans
    straight = D - share * spans

    def own_share(index):
        return pl.ds(pl.multiple_of(straight + index * share, share), share)

    def sent(k, i):
        if i == far:
            return copy(sources[k], wholes[k].at[shard], r.gather_sem, (k, i), at_shard(partner))
        source, target = sources[k], wholes[k].at[shard]
        if k == 0:
            source, target = source.at[0:straight], wholes[k].at[shard, 0:straight]
        return copy(source, target, r.gather_sem, (k, i), at_shard(others[i]))

    def shared(i):
        return copy(
            r.wi_send.at[own_share(me)],
            r.wi_all.at[shard, own_share(me)],
            r.share_sem,
            (i, 0),
            at_shard(others[i]),
        )

    def fanned(i, by):
        came = lax.rem(chip + far - i, far + 1) * 2 + core
        held = r.wi_all.at[came, own_share(me)]
        return copy(held, held, r.share_sem, (i, by), at_seq(ring[by - 1]))

    def passed(k, i):
        came = lax.rem(chip + far - i, far + 1) * 2 + core
        return copy(
            wholes[k].at[came], wholes[k].at[came], r.gather_sem, (k, far + 1 + i), at_shard(partner)
        )

    def spread(*which):
        for k in which:
            for i in range(far + 1):
                sent(k, i).start()
        for k in which:
            wholes[k][shard] = sources[k][...]

    def pass_on(*which):
        for i in range(far):
            for k in which:
                sent(k, i).wait_recv()
                passed(k, i).start()

    def finish(*which):
        for k in which:
            for i in range(far):
                sent(k, i).wait_send()
                passed(k, i).wait()
            sent(k, far).wait()

    r.wi_send[...] = r.wi[...].astype(BF16)
    r.small[...] = jnp.zeros_like(r.small)
    for source, first in (
        (r.select, SEL),
        (r.decay, DEC),
        (r.stepw, STEP),
        (r.taps, TAPS),
        (r.bias, BIAS),
        (r.stepb, STEPB),
        (r.skip, SKIP),
    ):
        r.small[first : first + source.shape[0], :] = source[...]
    r.packed_send[...] = r.small[...].astype(BF16)
    lane = lax.broadcasted_iota(jnp.int32, (2 * CHUNKS, D // shards), 0)
    r.gains_send[...] = jnp.where(lane == 0, r.mixer[...], r.attention[...]).astype(BF16)
    for i in range(far):
        shared(i).start()
    spread(0, 1, 2)
    last = r.tokens.at[pl.ds(rows - 2 * CHUNKS, 2 * CHUNKS)]
    edge = copy(last, r.before, r.edge_sem, (), at_seq(ring[0]))
    edge.start()

    def cot_copy(by):
        return copy(
            r.cot.at[ring[by - 1]], r.given.at[me], r.cot_sem, (by,), at_seq(ring[by - 1])
        )

    for i in range(far):
        shared(i).wait_recv()
        for by in range(1, spans):
            fanned(i, by).start()
    r.wo_send[...] = r.wo[...].astype(BF16)
    r.wh_send[...] = r.wh[...].astype(BF16)
    r.wm_send[...] = r.wm[...].astype(BF16)
    for part in range(D // LANES):
        lanes = slice(part * LANES, (part + 1) * LANES)
        r.row[...] = r.tokens[:, lanes].astype(F32)
        for step in range(steps):
            r.x[step * CHUNKS : (step + 1) * CHUNKS, lanes] = r.row[
                pl.ds(step, CHUNKS, stride=steps), :
            ]
    for i in range(far):
        shared(i).wait_send()
        for by in range(1, spans):
            fanned(i, by).wait()
    pass_on(0, 1, 2)
    for by in range(1, spans):
        cot_copy(by).start()
    r.given[me] = r.cot[me]
    spread(5, 3, 4)
    finish(0, 1, 2)
    edge.wait()

    starts = starts_of(r.lengths, nseq)
    r.packed[...] = jnp.concatenate([r.packed_all[s] for s in range(shards)], axis=1)
    gains = jnp.concatenate([r.gains_all[s].astype(F32) for s in range(shards)], axis=1)
    r.gains[...] = gains[:CHUNKS]
    gain = gains[0:1]
    x = r.x[...]
    xn1 = (x * norm(x) * gain).astype(BF16)
    before = r.before[...].astype(F32)
    edge_n = (before * norm(before) * gain).astype(BF16)
    wide = 2 * DI // shards
    for s in range(shards):
        piece = dot_nn(xn1, r.wi_all[s])
        if s < shards // 2:
            r.ext[EDGE:, s * wide : (s + 1) * wide] = piece
        else:
            at = (s - shards // 2) * wide
            r.zgate[:, at : at + wide] = piece
    edge_x = jnp.concatenate([dot_nn(edge_n, r.wi_all[s]) for s in range(shards // 2)], axis=1)
    count = r.before.shape[0]
    chunk = lax.broadcasted_iota(jnp.int32, (CHUNKS, DI), 0)
    for k in range(CONV - 1):
        late = (steps - CONV + 1 + k) * CHUNKS + EDGE
        moved = pltpu.roll(r.ext[late : late + CHUNKS, :], 1, 0)
        at = count - CONV + 1 + k
        r.ext[k * CHUNKS : (k + 1) * CHUNKS, :] = jnp.where(
            chunk == 0, jnp.broadcast_to(edge_x[at : at + 1, :], (CHUNKS, DI)), moved
        )
    small = r.packed[DEC:PACK, :].astype(F32)
    taps = small[TAPS - DEC : TAPS - DEC + CONV, :]
    bias = small[BIAS - DEC : BIAS - DEC + 1, :]

    def conv_step(step, carry):
        places = lax.broadcasted_iota(jnp.int32, (CHUNKS, 1), 0) * steps + step + me * rows
        first = start_of(places, starts)
        total = jnp.broadcast_to(bias, (CHUNKS, DI))
        for k in range(CONV):
            at = pl.ds(pl.multiple_of((step + k) * CHUNKS, CHUNKS), CHUNKS)
            inside = places - (CONV - 1) + k >= first
            total = total + jnp.where(inside, taps[k : k + 1, :] * r.ext[at, :], 0.0)
        r.conv[tile(step), :] = total
        r.du[tile(step), :] = total * jax.nn.sigmoid(total)
        return carry

    lax.fori_loop(0, steps, conv_step, 0, unroll=2)
    u = r.du[...].astype(BF16)
    r.u[...] = u
    xdbl = dot_nt(u, r.packed[SEL : SEL + STEP, :])
    r.xdbl[...] = xdbl
    r.delta[...] = dot_nn(
        xdbl[:, :RANK].astype(BF16), r.packed[STEP : STEP + RANK, :]
    )
    stepb = small[STEPB - DEC : STEPB - DEC + 1, :]

    def delta_step(step, total):
        places = lax.broadcasted_iota(jnp.int32, (CHUNKS, 1), 0) * steps + step + me * rows
        pre = r.delta[tile(step), :] + stepb
        delta = jnp.maximum(pre, 0.0) + jnp.log(1.0 + jnp.exp(-jnp.abs(pre)))
        r.delta[tile(step), :] = delta
        cut = jnp.where(begin_of(places, starts), CUT, delta)
        r.cut[tile(step), :] = cut
        r.du[tile(step), :] = delta * r.du[tile(step), :].astype(BF16).astype(F32)
        return total + cut

    totals = lax.fori_loop(0, steps, delta_step, jnp.zeros((CHUNKS, DI), F32), unroll=2)
    r.totals[...] = totals
    total = jnp.sum(totals, axis=0, keepdims=True)
    for group in range(GROUPS_CH):
        r.total_send[group : group + 1, :] = total[:, group * LANES : (group + 1) * LANES]
    r.span_totals[me] = r.total_send[...]

    def total_copy(by):
        return copy(
            r.total_send, r.span_totals.at[me], r.total_sem, (by,), at_seq(ring[by - 1])
        )

    for by in range(1, spans):
        total_copy(by).start()
    pass_on(5)
    spread_decay(r.packed, r.amat, r.spread)
    r.bx[...] = spread_columns(xdbl[:, RANK : RANK + STATE])

    def state_copy(by, at):
        return copy(
            r.state_send.at[at], r.states.at[me, at], r.state_sem, (by, at), at_seq(ring[by - 1])
        )

    def pair_step(pair, carry):
        for odd in range(2):
            lanes = lanes_of(pair * 2 + odd)
            amat = [r.spread[st * CHUNKS : (st + 1) * CHUNKS, lanes] for st in range(STATE)]

            def step_fn(step, states):
                cut = r.cut[tile(step), lanes]
                drive = r.du[tile(step), lanes]
                return tuple(
                    jnp.exp2(cut * amat[st]) * states[st] + drive * r.bx[tile(step), column(st)]
                    for st in range(STATE)
                )

            states = lax.fori_loop(
                0, steps, step_fn, (jnp.zeros((CHUNKS, LANES), F32),) * STATE, unroll=8
            )
            for st in range(STATE):
                r.ends[st, :, lanes] = states[st]
        lanes = pl.ds(pl.multiple_of(pair * 2 * LANES, 2 * LANES), 2 * LANES)
        amat = r.amat[:, lanes]
        state = jnp.zeros((STATE, 2 * LANES), F32)
        for k in range(CHUNKS):
            state = jnp.exp2(amat * r.totals[k : k + 1, lanes]) * state + r.ends[:, k, lanes]
        r.state_send[pair] = state.astype(BF16)
        for by in range(1, spans):

            @pl.when(me + by < spans)
            def _():
                state_copy(by, pair).start()

        return carry

    lax.fori_loop(0, GROUPS_CH // 2, pair_step, 0)
    pass_on(3)
    for by in range(1, spans):
        cot_copy(by).wait()
    finish(5)

    ratio = spans // HEADS
    sub = lax.rem(me, ratio)
    head = lax.div(me, ratio)
    half = rows // 2
    given = jnp.concatenate([r.given[j] for j in range(spans)], axis=0)
    dout = dot_nn(pick_rows(r.index, me, rows, steps), given).astype(BF16)
    r.dout[...] = dout
    merge = jnp.concatenate([r.wm_all[s] for s in range(shards)], axis=0)
    dcontext = dot_nt(dout, merge).astype(BF16).astype(F32)
    low = lane_low(half)

    def packs(pair):
        above, below = pair[:half], pair[half:]
        yield jnp.where(low, above, pltpu.roll(below, HEAD_DIM, 1))
        yield jnp.where(low, pltpu.roll(above, HEAD_DIM, 1), below)

    for pair in range(HEADS // 2):
        at = pair * LANES
        for odd, pack in enumerate(packs(dcontext[:, at : at + LANES])):
            r.d_send[2 * pair + odd] = pack.astype(BF16)

    def rows_copy(source, target, sems, by):
        to = ring[by - 1]
        slot = lax.div(me, ratio)
        return copy(source.at[lax.div(to, ratio)], target.at[slot], sems, (by,), at_seq(to))

    def kv_copy(by):
        to = ring[by - 1]
        return copy(
            r.kv_send.at[lax.div(to, ratio)],
            r.kv_in.at[pl.ds(pl.multiple_of(me * rows, rows), rows)],
            r.kv_sem,
            (by,),
            at_seq(to),
        )

    def to_rows(source, target, sems, act):
        for by in range(1, spans):
            if ratio == 1:
                act(rows_copy(source, target, sems, by))
            else:
                pl.when(lax.rem(by, ratio) == 0)(lambda: act(rows_copy(source, target, sems, by)))

    to_rows(r.d_send, r.d_in, r.d_sem, lambda c: c.start())
    r.d_in[lax.div(me, ratio)] = r.d_send[head]
    r.cx[...] = spread_columns(xdbl[:, RANK + STATE :])
    for by in range(1, spans):
        total_copy(by).wait()
        for pair in range(GROUPS_CH // 2):

            @pl.when(me + by < spans)
            def _():
                state_copy(by, pair).wait_send()

            @pl.when(me - by >= 0)
            def _():
                state_copy(by, pair).wait_recv()

    amat = r.amat[...]

    def chain(k, state):
        decay = jnp.exp2(amat * total_row(r.span_totals[k]))
        came = jnp.concatenate(
            [r.states[k, g].astype(F32) for g in range(GROUPS_CH // 2)], axis=1
        )
        return decay * state + came

    state = lax.fori_loop(0, me, chain, jnp.zeros((STATE, DI), F32))
    for k in range(CHUNKS):
        r.init[:, k, :] = state
        if k < CHUNKS - 1:
            state = jnp.exp2(amat * r.totals[k : k + 1, :]) * state + r.ends[:, k, :]

    def group_step(group, carry):
        lanes = lanes_of(group)
        amat_g = [r.spread[st * CHUNKS : (st + 1) * CHUNKS, lanes] for st in range(STATE)]

        def step_fn(step, states):
            cut = r.cut[tile(step), lanes]
            drive = r.du[tile(step), lanes]
            new = tuple(
                jnp.exp2(cut * amat_g[st]) * states[st] + drive * r.bx[tile(step), column(st)]
                for st in range(STATE)
            )
            terms = [new[st] * r.cx[tile(step), column(st)] for st in range(STATE)]
            while len(terms) > 1:
                terms = [a + b for a, b in zip(terms[::2], terms[1::2])]
            r.yfull[tile(step), lanes] = terms[0]
            return new

        lax.fori_loop(
            0, steps, step_fn, tuple(r.init[st, :, lanes] for st in range(STATE)), unroll=8
        )
        return carry

    lax.fori_loop(0, GROUPS_CH, group_step, 0)
    skip = small[SKIP - DEC : SKIP - DEC + 1, :]

    def gate_step(pair, carry):
        at = pl.ds(pl.multiple_of(pair * 2 * CHUNKS, 2 * CHUNKS), 2 * CHUNKS)
        yfull = r.yfull[at, :] + skip * r.u[at, :].astype(F32)
        r.yfull[at, :] = yfull
        gate = r.zgate[at, :]
        r.gated[at, :] = (yfull * (gate * jax.nn.sigmoid(gate))).astype(BF16)
        return carry

    lax.fori_loop(0, steps // 2, gate_step, 0)
    pass_on(4)
    finish(3)
    wo = jnp.concatenate([r.wo_all[s] for s in range(shards)], axis=0)
    x1 = r.x[...] + dot_nn(r.gated[...], wo)
    r.x1[...] = x1
    xn2 = (x1 * norm(x1) * gains[1:2, :]).astype(BF16)
    finish(4)
    qkv = jnp.concatenate([dot_nn(xn2, r.wh_all[s]) for s in range(shards)], axis=1)
    qkv = qkv.astype(BF16).astype(F32)
    scale = 1.0 / math.sqrt(HEAD_DIM)
    full_low = lane_low(rows)
    for pair in range(HEADS // 2):
        at = pair * LANES
        for odd, pack in enumerate(packs(qkv[:, at : at + LANES] * scale)):
            r.q_send[2 * pair + odd] = pack.astype(BF16)
        k = qkv[:, D + at : D + at + LANES]
        v = qkv[:, 2 * D + at : 2 * D + at + LANES]
        r.kv_send[2 * pair] = jnp.where(full_low, k, pltpu.roll(v, HEAD_DIM, 1)).astype(BF16)
        r.kv_send[2 * pair + 1] = jnp.where(full_low, pltpu.roll(k, HEAD_DIM, 1), v).astype(BF16)
    to_rows(r.q_send, r.q_in, r.q_sem, lambda c: c.start())
    for by in range(1, spans):
        kv_copy(by).start()
    r.q_in[lax.div(me, ratio)] = r.q_send[head]
    r.kv_in[pl.ds(pl.multiple_of(me * rows, rows), rows), :] = r.kv_send[head]
    keeps = [
        pltpu.make_async_copy(getattr(r, name), getattr(r, name + "_out"), r.keep_sem.at[i])
        for i, name in enumerate(KEPT)
    ]
    for keep in keeps[:-1]:
        keep.start()
    query_local = row_places(lax.broadcasted_iota(jnp.int32, (1, rows), 1), steps)
    key_local = row_places(lax.broadcasted_iota(jnp.int32, (rows, 1), 0), steps)
    r.causal[...] = jnp.where(key_local <= query_local, 0.0, NEG)
    r.dkv[...] = jnp.zeros_like(r.dkv)
    to_rows(r.d_send, r.d_in, r.d_sem, lambda c: c.wait())
    to_rows(r.q_send, r.q_in, r.q_sem, lambda c: c.wait())
    for by in range(1, spans):
        kv_copy(by).wait()

    static = ratio == 1
    blocks = spans // ratio

    def each(count, fn, carry):
        if not static:
            return lax.fori_loop(0, count, fn, carry)
        for j in range(count):
            carry = fn(j, carry)
        return carry

    def key_rows(j):
        return pl.ds(j * rows if static else pl.multiple_of(j * rows, rows), rows)

    def turn(j, carry):
        r.kvt[j] = r.kv_in[key_rows(j), :].astype(F32).T.astype(BF16)
        return carry

    each(spans, turn, 0)
    folded = (rows // CHUNKS, CHUNKS, rows)

    def dq_copy(to, by, t):
        return copy(r.dq_send.at[t], r.dq_in.at[head], r.dq_sem, (by,), at_seq(to))

    def query_block(t, carry):
        i = t * ratio + sub
        slot = t % 2 if static else 0
        q = r.q_in[t].astype(F32)
        d = r.d_in[t].astype(F32)
        qt = q.T
        dt = d.T
        zero = jnp.zeros((HEAD_DIM, rows), F32)
        qt = jnp.concatenate([qt[:HEAD_DIM], qt[HEAD_DIM:]], axis=1)
        dt = jnp.concatenate([dt[:HEAD_DIM], dt[HEAD_DIM:]], axis=1)
        both = jnp.concatenate(
            [jnp.concatenate([qt, zero], axis=1), jnp.concatenate([zero, dt], axis=1)], axis=0
        ).astype(BF16)
        none = jnp.zeros((half, LANES), F32)
        natural = jnp.concatenate(
            [
                jnp.where(low, none, pltpu.roll(d, HEAD_DIM, 1)),
                jnp.where(low, none, d),
                jnp.where(low, q, none),
                jnp.where(low, pltpu.roll(q, HEAD_DIM, 1), none),
            ],
            axis=0,
        ).astype(BF16)
        first = start_of(query_local + i * rows, starts)

        def scores(j, top):
            joint = dot_nn(r.kv_in[key_rows(j), :], both)
            score = joint[:, :rows]
            if static:
                if j == t:
                    score = score + r.causal[...]
                if j in (0, t) or t == spans - 1:
                    score = jnp.where(key_local + j * rows >= first, score, NEG)
            else:
                query = query_local + i * rows
                key = key_local + j * rows
                score = jnp.where((key <= query) & (key >= first), score, NEG)
            r.score[slot, j] = score
            r.dprob[slot, j] = joint[:, rows:]
            return jnp.maximum(top, jnp.max(score.reshape(folded), axis=0))

        top = each(t + 1 if static else i + 1, scores, jnp.full((CHUNKS, rows), NEG, F32))
        top = jnp.max(top, axis=0, keepdims=True)

        def weigh(j, sums):
            total, dot = sums
            prob = jnp.exp(r.score[slot, j] - top)
            r.score[slot, j] = prob
            total = total + jnp.sum(prob.reshape(folded), axis=0)
            dot = dot + jnp.sum((prob * r.dprob[slot, j]).reshape(folded), axis=0)
            return total, dot

        zero = jnp.zeros((CHUNKS, rows), F32)
        total, dot = each(t + 1 if static else i + 1, weigh, (zero, zero))
        inverse = 1.0 / jnp.sum(total, axis=0, keepdims=True)
        datt = jnp.sum(dot, axis=0, keepdims=True) * inverse

        def back(j, sums):
            prob = r.score[slot, j] * inverse
            dscore = prob * (r.dprob[slot, j] - datt)
            joint = jnp.concatenate([prob.astype(BF16), dscore.astype(BF16)], axis=1)
            r.dkv[key_rows(j), :] += dot_nn(joint, natural)
            return sums + dot_nn(r.kvt[j], joint)

        sums = each(t + 1 if static else i + 1, back, jnp.zeros((LANES, 2 * rows), F32))
        dqt = sums[:HEAD_DIM, rows:] * scale
        ctx = sums[HEAD_DIM:, :rows]
        dqt = jnp.concatenate([dqt[:, :half], dqt[:, half:]], axis=0)
        ctx = jnp.concatenate([ctx[:, :half], ctx[:, half:]], axis=0)
        r.dq_send[t] = dqt.T.astype(BF16)
        r.context_send[t] = ctx.T.astype(BF16)
        by = lax.rem(i - me + spans, spans)

        @pl.when(i != me)
        def _():
            dq_copy(i, by, t).start()

        @pl.when(i == me)
        def _():
            r.dq_in[head] = r.dq_send[t]

        return carry

    if static:
        for t in range(blocks):
            query_block(t, 0)
    else:
        lax.fori_loop(0, blocks, query_block, 0)
    keeps[-1].start()

    def cast(j, carry):
        r.dkv_send[j] = r.dkv[key_rows(j), :].astype(BF16)
        return carry

    each(spans, cast, 0)

    def dkv_copy(by):
        to = ring[by - 1]
        return copy(r.dkv_send.at[to], r.dkv_in.at[me], r.dkv_sem, (by,), at_seq(to))

    for by in range(1, spans):
        dkv_copy(by).start()
    r.dkv_in[me] = r.dkv_send[me]
    for t in range(blocks):
        i = t * ratio + sub
        by = lax.rem(i - me + spans, spans)

        @pl.when(i != me)
        def _():
            dq_copy(i, by, t).wait_send()

    for h in range(HEADS):
        came = h * ratio + sub
        by = lax.rem(me - came + spans, spans)

        @pl.when(came != me)
        def _():
            dq_copy(came, by, 0).wait_recv()

    for by in range(1, spans):
        dkv_copy(by).wait()
    for keep in keeps:
        keep.wait()


def total_row(values):
    return jnp.concatenate([values[g : g + 1, :] for g in range(GROUPS_CH)], axis=1)


def lane_low(rows):
    return lax.broadcasted_iota(jnp.int32, (rows, LANES), 1) < HEAD_DIM


def pick_rows(table_ref, me, rows, steps):
    spans = table_ref.shape[0]
    share = rows // spans
    shift = lax.rem((spans - me) * share, rows)
    moved = pltpu.roll(table_ref[...], shift, 1)
    lane = lax.broadcasted_iota(jnp.int32, (1, rows), 1)
    index = moved[0:1]
    for j in range(1, spans):
        line = pltpu.roll(moved[j : j + 1], j * share, 1)
        index = jnp.where(lane >= j * share, line, index)
    places = row_places(lax.broadcasted_iota(jnp.int32, (rows, 1), 0), steps) + me * rows
    return (index == places.astype(F32)).astype(F32).astype(BF16)


GRADS = ("heads", "out", "merge", "late", "early", "other", "small")
SMALL = 6
BACKWARD_IN = ("lengths", "index", "dq_in", "dkv_in") + tuple(k + "_kept" for k in KEPT)
class BackwardOut(NamedTuple):
    output: Any
    token_grad: Any
    last_heads: Any
    last_out: Any
    last_merge: Any
    last_small: Any
    pair_in: Any
    early_in: Any
    other_in: Any


BACKWARD_OUT = BackwardOut._fields
class FinalOut(NamedTuple):
    output: Any
    token_grad: Any
    mixer_grad: Any
    input_grad: Any
    taps_grad: Any
    bias_grad: Any
    select_grad: Any
    stepw_grad: Any
    stepb_grad: Any
    decay_grad: Any
    skip_grad: Any
    output_grad: Any
    attention_grad: Any
    heads_grad: Any
    merge_grad: Any


FINAL_OUT = FinalOut._fields
class BackwardScratch(NamedTuple):
    context: Any
    given: Any
    dx1: Any
    dys: Any
    dzgate: Any
    ends: Any
    grad_send: Any
    grads_in: Any
    db: Any
    dc: Any
    decay: Any
    held: Any
    state: Any
    bgrad: Any
    adelta: Any
    arrive: Any
    dxdbl: Any
    dext: Any
    spill: Any
    spill_in: Any
    small: Any
    row: Any
    amat: Any
    spread: Any
    sub_late: Any
    sub_early: Any
    sub_other: Any


class BackwardSems(NamedTuple):
    load_sem: Any
    context_sem: Any
    given_sem: Any
    state_sem: Any
    spill_sem: Any
    near_sem: Any
    far_sem: Any
    part_sem: Any
    last_sem: Any
    pair_sem: Any
    inner_sem: Any
    outer_sem: Any
    late_outer_sem: Any
    late_inner_sem: Any


BACKWARD_SCRATCH = (
    KEPT
    + BackwardScratch._fields
    + tuple(kind + name for kind in ("g_", "near_", "sum_", "far_", "part_") for name in GRADS)
    + BackwardSems._fields
)


def backward_kernel(steps, nseq, shards, spans, *refs):
    r = Refs(BACKWARD_IN + BACKWARD_OUT + BACKWARD_SCRATCH, refs)
    rows = steps * CHUNKS
    width = DI // shards
    me = lax.axis_index("seq")
    shard, core, chip, partner, others = shard_peers(shards)
    chips = shards // 2
    ring = [lax.rem(me + by, spans) for by in range(1, spans)]
    every = [me] + ring
    ratio = spans // HEADS
    sub = lax.rem(me, ratio)
    half = rows // 2
    blocks = spans // ratio
    starts = starts_of(r.lengths, nseq)
    loads = {
        name: pltpu.make_async_copy(getattr(r, name + "_kept"), getattr(r, name), r.load_sem.at[i])
        for i, name in enumerate(KEPT)
    }
    early = ("context_send", "dout", "x1", "gains", "wh_all")
    middle = ("gated", "wo_all", "zgate", "yfull", "u", "x")
    late = ("wm_all", "packed", "cut", "cx", "totals", "span_totals", "init", "delta", "du", "bx", "xdbl")
    last = ("conv", "ext", "wi_all")
    for name in early + middle:
        loads[name].start()

    def loaded(*names):
        for name in names:
            loads[name].wait()

    targets = [lax.div(shard, 2), shards // 2 + lax.div(shard, 2)]
    mine = lax.div(shard, shards // 2)
    first_piece = 2 * lax.rem(shard, shards // 2)

    def anywhere(index, at):
        return {"device_id": {"seq": index, "shard": at}, "device_id_type": pl.DeviceIdType.MESH}

    barrier = pltpu.get_barrier_semaphore()

    def signal(to):
        pl.semaphore_signal(barrier, inc=1, **to)

    peers = [at_shard(partner)] + [at_shard(o) for o in others] + [at_seq(to) for to in ring]
    for peer in peers:
        signal(peer)
    selves = jnp.int32(0)
    for by in range(spans):
        for at in targets + [first_piece, first_piece + 1]:
            if by:
                signal(anywhere(every[by], at))
            else:
                pl.when(at != shard)(lambda: signal(anywhere(me, at)))
                selves = selves + (at == shard).astype(jnp.int32)
    pl.semaphore_wait(barrier, len(peers) + 4 * spans - selves)

    def copy(source, target, sems, at, to):
        return pltpu.make_async_remote_copy(
            src_ref=source, dst_ref=target, send_sem=sems.at[(0, *at)], recv_sem=sems.at[(1, *at)], **to
        )

    def ref(kind, k):
        return getattr(r, kind + "_" + GRADS[k])

    def near_copy(k, x):
        return copy(
            ref("g", k).at[x * 2 + 1 - core], ref("near", k).at[x], r.near_sem, (k, x), at_shard(partner)
        )

    def far_copy(k, by):
        source = ref("sum", k).at[lax.rem(chip + by, chips)]
        return copy(source, ref("far", k).at[by - 1], r.far_sem, (k, by), at_shard(others[by - 1]))

    def part_copy(k, by):
        to = ring[by - 1]
        return copy(
            ref("near", k).at[0, to], ref("part", k).at[by], r.part_sem, (k, by), at_seq(to)
        )

    def last_copy(k, by):
        held = ref("last", k).at[me]
        return copy(held, held, r.last_sem, (k, by), at_seq(ring[by - 1]))

    def pair_refs(k):
        return (r.sub_early, r.early_in) if GRADS[k] == "early" else (r.sub_other, r.other_in)

    def pair_copy(k, by, at):
        source, target = pair_refs(k)
        to = anywhere(every[by], targets[0])
        return copy(source, target.at[at, me], r.pair_sem, (k - 4, at, by), to)

    def near_send(k):
        for x in range(chips):
            near_copy(k, x).start()

    def far_send(k):
        for x in range(chips):
            near_copy(k, x).wait_recv()
            ref("sum", k)[x] = (
                ref("g", k)[x * 2 + core].astype(F32) + ref("near", k)[x].astype(F32)
            ).astype(BF16)
        for by in range(1, chips):
            far_copy(k, by).start()

    def part_send(k):
        total = ref("sum", k)[chip].astype(F32)
        for by in range(1, chips):
            far_copy(k, by).wait_recv()
            total = total + ref("far", k)[by - 1].astype(F32)
        ref("near", k)[0] = total.astype(BF16)
        for by in range(1, chips):
            far_copy(k, by).wait_send()
        for by in range(1, spans):
            part_copy(k, by).start()

    def last_send(k):
        total = ref("near", k)[0, me].astype(F32)
        for by in range(1, spans):
            part_copy(k, by).wait_recv()
            total = total + ref("part", k)[by].astype(F32)
        if k == SMALL:
            ref("last", k)[me] = total.astype(BF16)
            for by in range(1, spans):
                last_copy(k, by).start()
            return
        source, target = pair_refs(k)
        source[...] = total.astype(BF16)
        for by in range(spans):
            to_owner(by == 0, targets[0], pair_copy(k, by, parity), lambda c: c.start())

        @pl.when(targets[0] == shard)
        def _():
            target[parity, me] = source[...]

    def to_owner(same, to, made, act):
        if same:
            pl.when(to != shard)(lambda: act(made))
        else:
            act(made)

    inner = spans // OUTER
    low_me, high_me = lax.rem(me, inner), lax.div(me, inner)
    lows = [lax.rem(low_me + by, inner) for by in range(inner)]
    highs = [lax.rem(high_me + by, OUTER) for by in range(OUTER)]
    own_part = low_me * OUTER + high_me
    middle_at = (inner - 1) * OUTER
    parity = lax.rem(shard, 2)

    def inner_copy(k, by):
        return copy(
            ref("near", k).at[0, pl.ds(lows[by] * OUTER, OUTER)],
            ref("part", k).at[pl.ds((by - 1) * OUTER, OUTER)],
            r.inner_sem,
            (k, 0, by),
            at_seq(high_me * inner + lows[by]),
        )

    def outer_copy(k, by):
        return copy(
            ref("part", k).at[middle_at + highs[by]],
            ref("part", k).at[spans + by - 1],
            r.outer_sem,
            (k, 0, by),
            at_seq(highs[by] * inner + low_me),
        )

    def outer_last(k, by):
        held = ref("last", k).at[own_part]
        return copy(held, held, r.outer_sem, (k, 1, by), at_seq(highs[by] * inner + low_me))

    def inner_last(k, by):
        held = ref("last", k).at[pl.ds(low_me * OUTER, OUTER)]
        return copy(held, held, r.inner_sem, (k, 1, by), at_seq(high_me * inner + lows[by]))

    def late_outer(by, at):
        return copy(
            r.sub_late,
            r.pair_in.at[at, own_part],
            r.late_outer_sem,
            (at, by),
            anywhere(highs[by] * inner + low_me, targets[1]),
        )

    def late_inner(by, at):
        held = r.pair_in.at[at, pl.ds(low_me * OUTER, OUTER)]
        to = at_seq(high_me * inner + lows[by])
        return copy(held, held, r.late_inner_sem, (at, by), to)

    def inner_send(k):
        total = ref("sum", k)[chip].astype(F32)
        for by in range(1, chips):
            far_copy(k, by).wait_recv()
            total = total + ref("far", k)[by - 1].astype(F32)
        ref("near", k)[0] = total.astype(BF16)
        for by in range(1, inner):
            inner_copy(k, by).start()

    def outer_send(k):
        total = ref("near", k)[0, pl.ds(low_me * OUTER, OUTER)].astype(F32)
        for by in range(1, inner):
            inner_copy(k, by).wait_recv()
            total = total + ref("part", k)[(by - 1) * OUTER : by * OUTER].astype(F32)
        ref("part", k)[middle_at : middle_at + OUTER] = total.astype(BF16)
        for by in range(1, OUTER):
            outer_copy(k, by).start()

    def outer_back(k):
        total = ref("part", k)[middle_at + high_me].astype(F32)
        for by in range(1, OUTER):
            outer_copy(k, by).wait_recv()
            total = total + ref("part", k)[spans + by - 1].astype(F32)
        if k != 3:
            ref("last", k)[own_part] = total.astype(BF16)
            for by in range(1, OUTER):
                outer_last(k, by).start()
            return
        r.sub_late[...] = total.astype(BF16)
        for by in range(OUTER):
            to_owner(by == 0, targets[1], late_outer(by, parity), lambda c: c.start())

        @pl.when(targets[1] == shard)
        def _():
            r.pair_in[parity, own_part] = r.sub_late[...]

    def inner_back(k):
        if k != 3:
            for by in range(1, OUTER):
                outer_last(k, by).wait_recv()
            for by in range(1, inner):
                inner_last(k, by).start()
            return

        @pl.when(mine == 1)
        def _():
            for at in range(2):
                for by in range(OUTER):
                    to_owner(by == 0, first_piece + at, late_outer(by, at), lambda c: c.wait_recv())
                for by in range(1, inner):
                    late_inner(by, at).start()

    def finish(k):
        for x in range(chips):
            near_copy(k, x).wait_send()
        if k < 4:
            for by in range(1, chips):
                far_copy(k, by).wait_send()
            for by in range(1, inner):
                inner_copy(k, by).wait_send()
            for by in range(1, OUTER):
                outer_copy(k, by).wait_send()
        else:
            for by in range(1, spans):
                part_copy(k, by).wait_send()
        if k < 3:
            for by in range(1, OUTER):
                outer_last(k, by).wait_send()
            for by in range(1, inner):
                inner_last(k, by).wait()
        elif k == 3:
            for by in range(OUTER):
                to_owner(by == 0, targets[1], late_outer(by, parity), lambda c: c.wait_send())

            @pl.when(mine == 1)
            def _():
                for at in range(2):
                    for by in range(1, inner):
                        late_inner(by, at).wait()

        elif k == SMALL:
            for by in range(1, spans):
                last_copy(k, by).wait()
        else:
            for by in range(spans):
                to_owner(by == 0, targets[0], pair_copy(k, by, parity), lambda c: c.wait_send())

            @pl.when(mine == 0)
            def _():
                for at in range(2):
                    for by in range(spans):
                        made = pair_copy(k, by, at)
                        to_owner(by == 0, first_piece + at, made, lambda c: c.wait_recv())

    def put(k, piece, value):
        size = value.shape[0] // spans
        for j in range(spans):
            ref("g", k)[piece, j] = value[j * size : (j + 1) * size].astype(BF16)

    loaded("context_send")
    head = lax.div(me, ratio)

    def context_copy(t, by, to):
        return copy(r.context_send.at[t], r.context.at[head], r.context_sem, (by,), at_seq(to))

    for t in range(blocks):
        i = t * ratio + sub
        by = lax.rem(i - me + spans, spans)

        @pl.when(i != me)
        def _():
            context_copy(t, by, i).start()

        @pl.when(i == me)
        def _():
            r.context[head] = r.context_send[t]

    low = lane_low(rows)
    half_low = lane_low(half)

    def unpacked(source, pair):
        even, odd = source[2 * pair].astype(F32), source[2 * pair + 1].astype(F32)
        return jnp.concatenate(
            [
                jnp.where(half_low, even, pltpu.roll(odd, HEAD_DIM, 1)),
                jnp.where(half_low, pltpu.roll(even, HEAD_DIM, 1), odd),
            ],
            axis=0,
        )

    dqs, dks, dvs = [], [], []
    for pair in range(HEADS // 2):
        dkv = [
            sum(r.dkv_in[(2 * pair + odd) * ratio + part].astype(F32) for part in range(ratio))
            for odd in range(2)
        ]
        dqs.append(unpacked(r.dq_in, pair))
        dks.append(jnp.where(low, dkv[0], pltpu.roll(dkv[1], HEAD_DIM, 1)))
        dvs.append(jnp.where(low, pltpu.roll(dkv[0], HEAD_DIM, 1), dkv[1]))
    dqkv = jnp.concatenate(dqs + dks + dvs, axis=1).astype(BF16)
    loaded("x1", "gains", "wh_all", "dout")
    for name in late + last:
        loads[name].start()
    x1 = r.x1[...]
    inverse = norm(x1)
    normal = x1 * inverse
    gain = r.gains[1:2, :]
    xn2 = (normal * gain).astype(BF16)
    wide = 3 * D // shards
    dxn2 = jnp.zeros((rows, D), F32)
    for s in range(shards):
        piece = dqkv[:, s * wide : (s + 1) * wide]
        put(0, s, dot_tn(xn2, piece))
        dxn2 = dxn2 + dot_nt(piece, r.wh_all[s])
    near_send(0)
    attention_gain = jnp.sum(dxn2 * normal, axis=0, keepdims=True)
    e2 = dxn2 * gain
    dx1 = r.dout[...].astype(F32) + inverse * (
        e2 - normal * jnp.mean(e2 * normal, axis=-1, keepdims=True)
    )
    r.dx1[...] = dx1
    dmixed = dx1.astype(BF16)
    loaded("gated", "wo_all")
    for s in range(shards):
        put(1, s, dot_tn(r.gated[:, s * width : (s + 1) * width], dmixed))
        r.dys[:, s * width : (s + 1) * width] = dot_nt(dmixed, r.wo_all[s])
    near_send(1)
    far_send(0)
    loaded("zgate", "yfull", "u", "x")

    def gate_step(pair, total):
        at = pl.ds(pl.multiple_of(pair * 2 * CHUNKS, 2 * CHUNKS), 2 * CHUNKS)
        dgated = r.dys[at, :].astype(BF16).astype(F32)
        gate = r.zgate[at, :]
        s = jax.nn.sigmoid(gate)
        dys = dgated * (gate * s)
        r.dys[at, :] = dys
        r.dzgate[at, :] = (dgated * r.yfull[at, :] * (s * (1.0 + gate * (1.0 - s)))).astype(BF16)
        return total + dys * r.u[at, :].astype(F32)

    total = lax.fori_loop(0, steps // 2, gate_step, jnp.zeros((2 * CHUNKS, DI), F32))
    r.small[SKIP : SKIP + 1, :] = jnp.sum(total, axis=0, keepdims=True)
    far_send(1)
    x = r.x[...]
    inverse_one = norm(x)
    normal_one = x * inverse_one
    gain_one = r.gains[0:1, :]
    xn1 = (normal_one * gain_one).astype(BF16)
    for s in range(shards):
        put(3, s, dot_tn(xn1, r.dzgate[:, s * width : (s + 1) * width]))
    near_send(3)
    loaded("wm_all", "packed", "cut", "cx", "totals", "span_totals")
    spread_decay(r.packed, r.amat, r.spread)

    def state_copy(by, at):
        to = lax.rem(me - by + spans, spans)
        return copy(
            r.grad_send.at[at], r.grads_in.at[me, at], r.state_sem, (by, at), at_seq(to)
        )

    def pair_step(pair, carry):
        for odd in range(2):
            lanes = lanes_of(pair * 2 + odd)
            amat = [r.spread[st * CHUNKS : (st + 1) * CHUNKS, lanes] for st in range(STATE)]

            def step_fn(turn, grads):
                step = steps - 1 - turn
                cut = r.cut[tile(step), lanes]
                dys = r.dys[tile(step), lanes]
                return tuple(
                    jnp.exp2(cut * amat[st]) * (grads[st] + dys * r.cx[tile(step), column(st)])
                    for st in range(STATE)
                )

            grads = lax.fori_loop(
                0, steps, step_fn, (jnp.zeros((CHUNKS, LANES), F32),) * STATE, unroll=8
            )
            for st in range(STATE):
                r.ends[st, :, lanes] = grads[st]
        lanes = pl.ds(pl.multiple_of(pair * 2 * LANES, 2 * LANES), 2 * LANES)
        amat = r.amat[:, lanes]
        state = jnp.zeros((STATE, 2 * LANES), F32)
        for k in reversed(range(CHUNKS)):
            state = jnp.exp2(amat * r.totals[k : k + 1, lanes]) * state + r.ends[:, k, lanes]
        r.grad_send[pair] = state.astype(BF16)
        for by in range(1, spans):

            @pl.when(me - by >= 0)
            def _():
                state_copy(by, pair).start()

        pl.when(pair == 0)(lambda: far_send(3))
        return carry

    lax.fori_loop(0, GROUPS_CH // 2, pair_step, 0)
    for h in range(HEADS):
        came = h * ratio + sub
        by = lax.rem(me - came + spans, spans)

        @pl.when(came != me)
        def _():
            context_copy(0, by, came).wait_recv()

    context = jnp.concatenate([unpacked(r.context, p) for p in range(HEADS // 2)], axis=1)
    context = context.astype(BF16)
    short = D // shards
    x2 = x1
    for s in range(shards):
        part = context[:, s * short : (s + 1) * short]
        x2 = x2 + dot_nn(part, r.wm_all[s])
        put(2, s, dot_tn(part, r.dout[...]))
    near_send(2)
    given = dot_tn(pick_rows(r.index, me, rows, steps), x2.astype(BF16))
    share = rows // spans
    for j in range(spans):
        r.given[j] = given[j * share : (j + 1) * share].astype(BF16)

    def given_copy(by):
        to = ring[by - 1]
        return copy(r.given.at[to], r.output.at[me], r.given_sem, (by,), at_seq(to))

    r.output[me] = r.given[me]

    loaded("init", "delta", "du", "bx", "xdbl", *last)
    r.db[...] = jnp.zeros_like(r.db)
    r.dc[...] = jnp.zeros_like(r.dc)
    for by in range(1, spans):
        for pair in range(GROUPS_CH // 2):

            @pl.when(me - by >= 0)
            def _():
                state_copy(by, pair).wait_send()

            @pl.when(me + by < spans)
            def _():
                state_copy(by, pair).wait_recv()

    for by in range(1, spans):
        given_copy(by).start()
    amat = r.amat[...]

    def chain(turn, state):
        k = spans - 1 - turn
        decay = jnp.exp2(amat * total_row(r.span_totals[k]))
        came = jnp.concatenate(
            [r.grads_in[k, g].astype(F32) for g in range(GROUPS_CH // 2)], axis=1
        )
        return decay * state + came

    state = lax.fori_loop(0, spans - 1 - me, chain, jnp.zeros((STATE, DI), F32))
    for k in reversed(range(CHUNKS)):
        r.arrive[:, k, :] = state
        if k:
            state = jnp.exp2(amat * r.totals[k : k + 1, :]) * state + r.ends[:, k, :]
    eight = STATE // 2

    def sum_of(terms):
        while len(terms) > 1:
            terms = [a + b for a, b in zip(terms[::2], terms[1::2])]
        return terms[0]

    def kept_at(step, i):
        return pl.ds(pl.multiple_of(step * (eight * CHUNKS) + i * CHUNKS, CHUNKS), CHUNKS)

    stages = {
        0: ((far_send, 2), (inner_send, 0)),
        1: ((inner_send, 1),),
        2: ((outer_send, 0),),
        3: ((outer_send, 1),),
        4: ((outer_back, 0),),
        5: ((inner_send, 3),),
        6: ((outer_back, 1), (inner_send, 2)),
        7: ((inner_back, 0), (outer_send, 3)),
    }

    def run(todo):
        for stage, k in todo:
            stage(k)

    def group_step(group, carry):
        lanes = lanes_of(group)
        for part in range(2):
            states = range(part * eight, (part + 1) * eight)
            amat_g = [r.spread[st * CHUNKS : (st + 1) * CHUNKS, lanes] for st in states]

            def forward(step, held):
                cut = r.cut[tile(step), lanes]
                drive = r.du[tile(step), lanes]
                out = []
                for i, st in enumerate(states):
                    decay = jnp.exp2(cut * amat_g[i])
                    kept = decay * held[i]
                    new = kept + drive * r.bx[tile(step), column(st)]
                    r.decay[kept_at(step, i), :] = decay
                    r.held[kept_at(step, i), :] = kept
                    r.state[kept_at(step, i), :] = new
                    out.append(new)
                return tuple(out)

            lax.fori_loop(
                0, steps, forward, tuple(r.init[st, :, lanes] for st in states), unroll=8
            )

            def backward(turn, held):
                grads, sums = held
                step = steps - 1 - turn
                delta = r.delta[tile(step), lanes]
                drive = r.du[tile(step), lanes]
                dys = r.dys[tile(step), lanes]
                new, totals, by_b, by_a = [], [], [], []
                for i, st in enumerate(states):
                    at = tile(step)
                    grad = grads[i] + dys * r.cx[at, column(st)]
                    new.append(r.decay[kept_at(step, i), :] * grad)
                    through = grad * r.held[kept_at(step, i), :]
                    totals.append(sums[i] + through * delta)
                    by_a.append(amat_g[i] * through)
                    by_b.append(grad * r.bx[at, column(st)])
                    r.dc[at, column(st)] += r.state[kept_at(step, i), :] * dys
                    r.db[at, column(st)] += grad * drive
                if part:
                    r.bgrad[tile(step), lanes] += sum_of(by_b)
                    r.adelta[tile(step), lanes] += sum_of(by_a)
                else:
                    r.bgrad[tile(step), lanes] = sum_of(by_b)
                    r.adelta[tile(step), lanes] = sum_of(by_a)
                return (tuple(new), tuple(totals))

            _, sums = lax.fori_loop(
                0,
                steps,
                backward,
                (
                    tuple(r.arrive[st, :, lanes] for st in states),
                    (jnp.zeros((CHUNKS, LANES), F32),) * eight,
                ),
                unroll=8,
            )
            for i, st in enumerate(states):
                row = jnp.sum(sums[i], axis=0, keepdims=True)
                amat_row = amat_g[i][0:1, :] * math.log(2.0)
                r.small[DEC + st : DEC + st + 1, lanes] = row * amat_row
        for at, todo in stages.items():
            pl.when(group == at)(functools.partial(run, todo))
        return carry

    lax.fori_loop(0, GROUPS_CH, group_step, 0)
    small = r.packed[DEC:PACK, :].astype(F32)
    taps = small[TAPS - DEC : TAPS - DEC + CONV, :]
    skip = small[SKIP - DEC : SKIP - DEC + 1, :]

    def delta_step(step, total):
        at = tile(step)
        bgrad = r.bgrad[at, :]
        delta = r.delta[at, :]
        u = r.conv[at, :]
        u = (u * jax.nn.sigmoid(u)).astype(BF16).astype(F32)
        ddelta = u * bgrad + r.adelta[at, :] * math.log(2.0)
        dtpre = (ddelta * (1.0 - jnp.exp(-delta))).astype(BF16).astype(F32)
        r.adelta[at, :] = dtpre
        r.bgrad[at, :] = r.dys[at, :] * skip + delta * bgrad
        return total + dtpre

    total = lax.fori_loop(0, steps, delta_step, jnp.zeros((CHUNKS, DI), F32))
    run(((inner_back, 1), (outer_send, 2)))
    r.small[STEPB : STEPB + 1, :] = jnp.sum(total, axis=0, keepdims=True)
    r.small[GAINS:, :] = jnp.zeros((PACK - GAINS, DI), F32)
    dtpre = r.adelta[...].astype(BF16)
    steplow = r.xdbl[:, 0:RANK].astype(BF16)
    r.small[STEP : STEP + RANK, :] = dot_tn(steplow, dtpre)
    r.dxdbl[:, 0:RANK] = dot_nt(dtpre, r.packed[STEP : STEP + RANK, :])
    for part in range(4):
        at = slice(part * rows // 4, (part + 1) * rows // 4)
        r.dxdbl[at, RANK : RANK + STATE] = gather_columns(r.db[at, :])
        r.dxdbl[at, RANK + STATE :] = gather_columns(r.dc[at, :])
    run(((outer_back, 3),))
    dxdbl = r.dxdbl[...].astype(BF16)
    r.small[SEL : SEL + STEP, :] = dot_tn(dxdbl, r.u[...])
    r.bgrad[...] += dot_nn(dxdbl, r.packed[SEL : SEL + STEP, :])
    r.dext[...] = jnp.zeros_like(r.dext)
    r.spill[...] = jnp.zeros_like(r.spill)

    @pl.when(me == spans - 1)
    def _():
        r.spill_in[...] = jnp.zeros_like(r.spill_in)

    def conv_steps(first_step, last_step, ranges, totals):
        def one(step, totals):
            at = tile(step)
            places = lax.broadcasted_iota(jnp.int32, (CHUNKS, 1), 0) * steps + step + me * rows
            first = start_of(places, starts)
            inside = [places - (CONV - 1) + k >= first for k in range(CONV)]
            out = []
            for lanes, sums in zip(ranges, totals):
                dconv = r.bgrad[at, lanes] * silu_slope(r.conv[at, lanes])
                new = []
                for k in range(CONV):
                    to = pl.ds(pl.multiple_of((step + k) * CHUNKS, CHUNKS), CHUNKS)
                    counted = jnp.where(inside[k], dconv, 0.0)
                    new.append(sums[k] + counted * r.ext[to, lanes])
                    r.dext[to, lanes] += taps[k : k + 1, lanes] * counted
                out.append(tuple(new) + (sums[CONV] + dconv,))
            return tuple(out)

        return lax.fori_loop(first_step, last_step, one, totals)

    quarter = width // 2
    halves = [
        [slice((2 * o + part) * width, (2 * o + part + 1) * width) for o in range(chips)]
        for part in range(2)
    ]
    zero = jnp.zeros((CHUNKS, width), F32)
    firsts = [
        conv_steps(0, CONV - 1, ranges, tuple((zero,) * (CONV + 1) for _ in ranges))
        for ranges in halves
    ]
    for k in range(CONV - 1):
        r.spill[k : k + 1, :] = r.dext[k * CHUNKS : k * CHUNKS + 1, :]
    behind = lax.rem(me + spans - 1, spans)
    spill = copy(r.spill, r.spill_in, r.spill_sem, (), at_seq(behind))

    @pl.when(me > 0)
    def _():
        spill.start()

    chunk = lax.broadcasted_iota(jnp.int32, (CHUNKS, width), 0)
    dxin = []
    for part, ranges in enumerate(halves):
        totals = conv_steps(CONV - 1, steps, ranges, firsts[part])
        if part:
            far_send(4)
            run(((outer_back, 2),))
        else:

            @pl.when(me > 0)
            def _():
                spill.wait_send()

            @pl.when(me < spans - 1)
            def _():
                spill.wait_recv()

        for o, lanes in enumerate(ranges):
            for k in range(CONV):
                r.small[TAPS + k : TAPS + k + 1, lanes] = jnp.sum(
                    totals[o][k], axis=0, keepdims=True
                )
            r.small[BIAS : BIAS + 1, lanes] = jnp.sum(totals[o][CONV], axis=0, keepdims=True)
            for k in range(CONV - 1):
                block = r.dext[k * CHUNKS : (k + 1) * CHUNKS, lanes]
                edge = (steps - CONV + 1 + k) * CHUNKS + EDGE
                moved = pltpu.roll(block, CHUNKS - 1, 0)
                came = jnp.broadcast_to(r.spill_in[k : k + 1, lanes], (CHUNKS, width))
                r.dext[edge : edge + CHUNKS, lanes] += jnp.where(
                    chunk < CHUNKS - 1, moved, came
                )
            piece = r.dext[EDGE:, lanes].astype(BF16)
            dxin.append(piece)
            grad = dot_tn(xn1, piece)
            for parity_at in range(2):
                put(4 + part, 2 * o + parity_at, grad[:, parity_at * quarter : (parity_at + 1) * quarter])
        near_send(4 + part)
    run(((inner_back, 3), (inner_back, 2)))
    wide = 2 * width
    dxn1 = jnp.zeros((rows, D), F32)
    for s in range(shards):
        if s < chips:
            piece = jnp.concatenate([dxin[s], dxin[chips + s]], axis=1)
        else:
            at = (s - chips) * wide
            piece = r.dzgate[:, at : at + wide]
        dxn1 = dxn1 + dot_nt(piece, r.wi_all[s])
    mixer_gain = jnp.sum(dxn1 * normal_one, axis=0, keepdims=True)
    for s in range(shards):
        at = s * width
        gains = slice(s * short, (s + 1) * short)
        r.small[GAINS : GAINS + 1, at : at + short] = mixer_gain[:, gains]
        r.small[GAINS : GAINS + 1, at + short : at + 2 * short] = attention_gain[:, gains]
    for s in range(shards):
        put(SMALL, s, r.small[:, s * width : (s + 1) * width])
    near_send(SMALL)
    far_send(5)
    far_send(SMALL)
    part_send(4)
    e1 = dxn1 * gain_one
    dx = r.dx1[...] + inverse_one * (
        e1 - normal_one * jnp.mean(e1 * normal_one, axis=-1, keepdims=True)
    )
    r.dx1[...] = dx
    for part in range(D // LANES):
        lanes = slice(part * LANES, (part + 1) * LANES)
        for step in range(steps):
            r.row[pl.ds(step, CHUNKS, stride=steps), :] = r.dx1[
                step * CHUNKS : (step + 1) * CHUNKS, lanes
            ]
        r.token_grad[:, lanes] = r.row[...]
    part_send(5)
    part_send(SMALL)
    for k in (0, 1, 2, 3):
        finish(k)
    last_send(4)
    last_send(5)
    last_send(SMALL)
    for by in range(1, spans):
        given_copy(by).wait()
    for t in range(blocks):
        i = t * ratio + sub
        by = lax.rem(i - me + spans, spans)

        @pl.when(i != me)
        def _():
            context_copy(t, by, i).wait_send()

    finish(SMALL)
    finish(4)
    finish(5)


def final_kernel(*refs):
    r = Refs(tuple(k + "_in" for k in BACKWARD_OUT) + FINAL_OUT, refs)

    def whole(source):
        return jnp.concatenate([source[j].astype(F32) for j in range(source.shape[0])], axis=0)

    r.output[...] = r.output_in[...]
    r.token_grad[...] = r.token_grad_in[...]
    r.heads_grad[...] = whole(r.last_heads_in)
    r.output_grad[...] = whole(r.last_out_in)
    r.merge_grad[...] = whole(r.last_merge_in)
    small = whole(r.last_small_in)
    short = r.mixer_grad.shape[1]
    width = r.taps_grad.shape[1]
    r.select_grad[...] = small[SEL : SEL + STEP]
    r.stepw_grad[...] = small[STEP : STEP + RANK]
    r.decay_grad[...] = small[DEC : DEC + STATE]
    r.taps_grad[...] = small[TAPS : TAPS + CONV]
    r.bias_grad[...] = small[BIAS : BIAS + 1]
    r.stepb_grad[...] = small[STEPB : STEPB + 1]
    r.skip_grad[...] = small[SKIP : SKIP + 1]
    r.mixer_grad[...] = small[GAINS : GAINS + 1, :short]
    r.attention_grad[...] = small[GAINS : GAINS + 1, short:]
    late = jnp.concatenate([whole(r.pair_in_in.at[at]) for at in range(2)], axis=1)
    early = jnp.concatenate(
        [whole(source.at[at]) for source in (r.early_in_in, r.other_in_in) for at in range(2)], axis=1
    )
    inner_half = lax.axis_index("shard") < lax.axis_size("shard") // 2
    r.input_grad[...] = jnp.where(inner_half, early, late)


def shape(*dims, kind=F32):
    return jax.ShapeDtypeStruct(dims, kind)


def vmem(*dims, kind=F32):
    return pltpu.VMEM(dims, kind)


def per_device(
    tokens,
    cotangent,
    positions,
    lengths,
    mixer_gain,
    input_weight,
    kernel_weight,
    kernel_bias,
    select_weight,
    step_weight,
    step_bias,
    decay_log,
    skip_scale,
    output_weight,
    attention_gain,
    heads_weight,
    merge_weight,
):
    spans = lax.axis_size("seq")
    shards = lax.axis_size("shard")
    rows = tokens.shape[1]
    steps = rows // CHUNKS
    share = rows // spans
    nseq = lengths.shape[1]
    ratio = spans // HEADS
    part = rows // ratio
    width = DI // shards

    index = positions[0].reshape(spans, rows).astype(F32)
    dma = pltpu.SemaphoreType.DMA
    spread = [vmem(STATE, DI), vmem(STATE * CHUNKS, DI)]
    columns = vmem(rows, STATE * LANES)
    plane = vmem(rows, DI)
    gain_len = D // shards
    halves = GROUPS_CH // 2
    weights = [(D, 2 * width), (width, D), (D, 3 * D // shards), (gain_len, D)]
    half = rows // 2
    blocks = spans // ratio
    slots = 2 if ratio == 1 else 1
    kept = (
        [shape(rows, D)]
        + [shape(shards, *w, kind=BF16) for w in weights]
        + [
            shape(PACK, DI, kind=BF16),
            shape(CHUNKS, D),
            shape(spans, GROUPS_CH, LANES),
            shape(EDGE + rows, DI),
            shape(rows, DI),
            shape(rows, DI),
            shape(rows, DI, kind=BF16),
            shape(rows, DI),
            shape(rows, STEP),
            shape(CHUNKS, DI),
            shape(rows, DI),
            shape(rows, DI, kind=BF16),
            shape(rows, D),
            shape(STATE, CHUNKS, DI),
            shape(rows, D, kind=BF16),
            shape(rows, STATE * LANES),
            shape(rows, STATE * LANES),
            shape(rows, DI),
            shape(rows, DI),
            shape(blocks, half, LANES, kind=BF16),
        ]
    )
    back = [shape(HEADS, half, LANES, kind=BF16), shape(spans, rows, LANES, kind=BF16)]
    inputs = [
        lengths[0],
        tokens[0],
        cotangent[0].reshape(spans, share, D),
        index,
        mixer_gain[None],
        attention_gain[None],
        select_weight.T,
        step_weight,
        decay_log.T,
        kernel_weight,
        kernel_bias[None],
        step_bias[None],
        skip_scale[None],
        input_weight,
        output_weight,
        heads_weight,
        merge_weight,
    ]
    outs = pl.pallas_call(
        functools.partial(forward_kernel, steps, nseq, shards, spans),
        out_shape=kept + back,
        in_specs=[SMEM] + [VMEM] * (len(inputs) - 1),
        out_specs=[pl.BlockSpec(memory_space=pl.ANY)] * len(kept) + [VMEM] * len(back),
        scratch_shapes=[vmem(*k.shape, kind=k.dtype) for k in kept]
        + [
            vmem(spans, share, D, kind=BF16),
            vmem(spans, halves, STATE, 2 * LANES, kind=BF16),
            vmem(STATE, CHUNKS, DI),
            vmem(rows, LANES),
            vmem(PACK, width),
        ]
        + [vmem(*w, kind=BF16) for w in weights]
        + [
            vmem(PACK, width, kind=BF16),
            vmem(2 * CHUNKS, gain_len, kind=BF16),
            vmem(shards, PACK, width, kind=BF16),
            vmem(shards, 2 * CHUNKS, gain_len, kind=BF16),
            vmem(2 * CHUNKS, D, kind=BF16),
            vmem(halves, STATE, 2 * LANES, kind=BF16),
            vmem(GROUPS_CH, LANES),
        ]
        + spread
        + [
            vmem(HEADS, half, LANES, kind=BF16),
            vmem(HEADS, half, LANES, kind=BF16),
            vmem(HEADS, rows, LANES, kind=BF16),
            vmem(blocks, half, LANES, kind=BF16),
            vmem(blocks, half, LANES, kind=BF16),
            vmem(spans * rows, LANES, kind=BF16),
            vmem(spans, LANES, rows, kind=BF16),
            vmem(slots, spans, rows, rows),
            vmem(slots, spans, rows, rows),
            vmem(spans * rows, LANES),
            vmem(blocks, half, LANES, kind=BF16),
            vmem(spans, rows, LANES, kind=BF16),
            vmem(rows, rows),
            dma((2, 6, shards - 1)),
            dma((2, max(shards // 2 - 1, 1), spans)),
            dma((2, spans)),
            dma((2,)),
            dma((2, spans, halves)),
        ]
        + [dma((2, spans))] * 6
        + [dma((len(kept),))],
        compiler_params=params(collective_id=0, has_side_effects=True),
        name="forward",
    )(*inputs)
    saved, back = outs[: len(kept)], outs[len(kept) :]
    parts = {
        "heads": (D // spans, 3 * D // shards),
        "out": (width // spans, D),
        "merge": (gain_len // spans, D),
        "late": (D // spans, width),
        "early": (D // spans, width // 2),
        "other": (D // spans, width // 2),
        "small": (PACK // spans, width),
    }
    chips = shards // 2
    sizes = [(spans, *parts[k]) for k in GRADS]
    count = len(GRADS)
    anyspace = pl.BlockSpec(memory_space=pl.ANY)
    summed = [
        shape(spans, share, D, kind=BF16),
        shape(rows, D),
        shape(spans, *parts["heads"], kind=BF16),
        shape(spans, *parts["out"], kind=BF16),
        shape(spans, *parts["merge"], kind=BF16),
        shape(spans, *parts["small"], kind=BF16),
        shape(2, spans, *parts["late"], kind=BF16),
        shape(2, spans, *parts["early"], kind=BF16),
        shape(2, spans, *parts["other"], kind=BF16),
    ]
    few = vmem(rows * STATE // 2, LANES)
    state = vmem(STATE, CHUNKS, DI)
    summed = pl.pallas_call(
        functools.partial(backward_kernel, steps, nseq, shards, spans),
        out_shape=summed,
        in_specs=[SMEM] + [VMEM] * 3 + [anyspace] * len(kept),
        out_specs=[VMEM] * len(summed),
        scratch_shapes=[vmem(*k.shape, kind=k.dtype) for k in kept]
        + [
            vmem(HEADS, half, LANES, kind=BF16),
            vmem(spans, share, D, kind=BF16),
            vmem(rows, D),
            plane,
            vmem(rows, DI, kind=BF16),
            state,
            vmem(halves, STATE, 2 * LANES, kind=BF16),
            vmem(spans, halves, STATE, 2 * LANES, kind=BF16),
            columns,
            columns,
            few,
            few,
            few,
            plane,
            plane,
            state,
            vmem(rows, STEP),
            vmem(EDGE + rows, DI),
            vmem(CHUNKS, DI),
            vmem(CHUNKS, DI),
            vmem(PACK, DI),
            vmem(rows, LANES),
        ]
        + spread
        + [
            vmem(*parts["late"], kind=BF16),
            vmem(*parts["early"], kind=BF16),
            vmem(*parts["other"], kind=BF16),
        ]
        + [vmem(shards, *k, kind=BF16) for k in sizes]
        + [vmem(chips, *k, kind=BF16) for k in sizes] * 2
        + [vmem(max(chips - 1, 1), *k, kind=BF16) for k in sizes]
        + [vmem(spans + OUTER - 1, *k[1:], kind=BF16) for k in sizes]
        + [
            dma((len(kept),)),
            dma((2, spans)),
            dma((2, spans)),
            dma((2, spans, halves)),
            dma((2,)),
            dma((2, count, chips)),
            dma((2, count, chips)),
            dma((2, count, spans)),
            dma((2, count, spans)),
            dma((2, 2, 2, spans)),
            dma((2, 4, 2, spans // OUTER)),
            dma((2, 4, 2, OUTER)),
            dma((2, 2, OUTER)),
            dma((2, 2, spans // OUTER)),
        ],
        compiler_params=params(collective_id=1, has_side_effects=True),
        name="backward",
    )(lengths[0], index, *back, *saved)
    results = pl.pallas_call(
        final_kernel,
        out_shape=[
            shape(rows, D, kind=BF16),
            shape(rows, D),
            shape(1, gain_len),
            shape(D, 2 * width),
            shape(CONV, width),
            shape(1, width),
            shape(STEP, width),
            shape(RANK, width),
            shape(1, width),
            shape(STATE, width),
            shape(1, width),
            shape(width, D),
            shape(1, gain_len),
            shape(D, 3 * D // shards),
            shape(gain_len, D),
        ],
        in_specs=[VMEM] * len(summed),
        out_specs=[VMEM] * len(FINAL_OUT),
        compiler_params=params(),
        name="final",
    )(summed[0].reshape(rows, D), *summed[1:])
    flat, turned = {2, 5, 8, 10, 12}, {6, 9}
    return tuple(
        v[None] if i < 2 else v.reshape(-1) if i in flat else v.T if i in turned else v
        for i, v in enumerate(results)
    )


def solution(mesh):
    return jax.shard_map(
        per_device,
        mesh=mesh,
        in_specs=(
            P("shard", "seq", None),
            P("shard", "seq", None),
            P("shard", None),
            P("shard", None),
            P("shard"),
            P(None, "shard"),
            P(None, "shard"),
            P("shard"),
            P("shard", None),
            P(None, "shard"),
            P("shard"),
            P("shard", None),
            P("shard"),
            P("shard", None),
            P("shard"),
            P(None, "shard"),
            P("shard", None),
        ),
        out_specs=(
            P("shard", "seq", None),
            P("shard", "seq", None),
            P("shard"),
            P(None, "shard"),
            P(None, "shard"),
            P("shard"),
            P("shard", None),
            P(None, "shard"),
            P("shard"),
            P("shard", None),
            P("shard"),
            P("shard", None),
            P("shard"),
            P(None, "shard"),
            P("shard", None),
        ),
        check_vma=False,
    )
```

```python
import functools
import math
from typing import Any, NamedTuple

import jax
import jax.numpy as jnp
from jax import lax
from jax.experimental import pallas as pl
from jax.experimental.pallas import tpu as pltpu
from jax.sharding import PartitionSpec as P

D = 512
DI = 1024
RANK = 32
HEADS = 8
STATE = 16
HEAD_DIM = 64
CONV = 4
CHUNKS = 8
LANES = 128
GROUPS_CH = DI // LANES
EDGE = (CONV - 1) * CHUNKS
OUTER = 4

SEL = 0
STEP = RANK + 2 * STATE
DEC = STEP + RANK
TAPS = DEC + STATE
BIAS = TAPS + CONV
STEPB = BIAS + 1
SKIP = STEPB + 1
GAINS = SKIP + 1
PACK = 128

EPS = 1e-05
NEG = -1e30
CUT = 1e30
F32 = jnp.float32
BF16 = jnp.bfloat16

VMEM = pl.BlockSpec(memory_space=pltpu.VMEM)
SMEM = pl.BlockSpec(memory_space=pltpu.SMEM)


def params(**more):
    return pltpu.CompilerParams(vmem_limit_bytes=62 << 20, **more)


def dot_nn(left, right):
    return lax.dot_general(left, right, (((1,), (0,)), ((), ())), preferred_element_type=F32)


def dot_nt(left, right):
    return lax.dot_general(left, right, (((1,), (1,)), ((), ())), preferred_element_type=F32)


def dot_tn(left, right):
    return lax.dot_general(left, right, (((0,), (0,)), ((), ())), preferred_element_type=F32)


def row_places(rows, steps):
    return (rows & (CHUNKS - 1)) * steps + (rows >> 3)


def starts_of(lengths_ref, nseq):
    starts = [jnp.int32(0)]
    for k in range(nseq - 1):
        starts.append(starts[-1] + lengths_ref[k])
    return starts


def start_of(places, starts):
    first = jnp.zeros_like(places)
    for start in starts[1:]:
        first = jnp.where(places >= start, start, first)
    return first


def begin_of(places, starts):
    found = places == starts[0]
    for start in starts[1:]:
        found = found | (places == start)
    return found


def norm(value):
    return lax.rsqrt(jnp.mean(value * value, axis=-1, keepdims=True) + EPS)


def silu_slope(value):
    s = jax.nn.sigmoid(value)
    return s * (1.0 + value * (1.0 - s))


def tile(step):
    return pl.ds(pl.multiple_of(step * CHUNKS, CHUNKS), CHUNKS)


def lanes_of(group):
    return pl.ds(pl.multiple_of(group * LANES, LANES), LANES)


def spread_decay(packed_ref, amat_ref, spread_ref):
    amat = -jnp.exp(packed_ref[DEC : DEC + STATE, :].astype(F32)) * math.log2(math.e)
    amat_ref[...] = amat
    for st in range(STATE):
        spread_ref[st * CHUNKS : (st + 1) * CHUNKS, :] = jnp.broadcast_to(
            amat[st : st + 1, :], (CHUNKS, DI)
        )


def column(st):
    return slice(st * LANES, (st + 1) * LANES)


def thirds(value):
    high = value.astype(BF16)
    rest = value - high.astype(F32)
    middle = rest.astype(BF16)
    return high, middle, (rest - middle.astype(F32)).astype(BF16)


def spread_columns(values):
    terms = jnp.concatenate([t.astype(F32) for t in thirds(values)], axis=1).astype(BF16)
    count = terms.shape[1]
    line = lax.broadcasted_iota(jnp.int32, (count, STATE * LANES), 0)
    lane = lax.broadcasted_iota(jnp.int32, (count, STATE * LANES), 1)
    chosen = (line & (STATE - 1)) == lax.div(lane, LANES)
    return dot_nn(terms, chosen.astype(F32).astype(BF16))


def gather_columns(value):
    line = lax.broadcasted_iota(jnp.int32, (STATE * LANES, STATE), 0)
    lane = lax.broadcasted_iota(jnp.int32, (STATE * LANES, STATE), 1)
    chosen = (lax.div(line, LANES) == lane).astype(F32).astype(BF16)
    return sum(dot_nn(term, chosen) for term in thirds(value)[:2])


def at_seq(index):
    return {"device_id": {"seq": index}, "device_id_type": pl.DeviceIdType.MESH}


def at_shard(index):
    return {"device_id": {"shard": index}, "device_id_type": pl.DeviceIdType.MESH}


def greet(peers):
    barrier = pltpu.get_barrier_semaphore()
    for peer in peers:
        pl.semaphore_signal(barrier, inc=1, **peer)
    pl.semaphore_wait(barrier, len(peers))


def shard_peers(shards):
    shard = lax.axis_index("shard")
    core, chip = lax.rem(shard, 2), lax.div(shard, 2)
    partner = chip * 2 + 1 - core
    others = [lax.rem(chip + by, shards // 2) * 2 + core for by in range(1, shards // 2)]
    return shard, core, chip, partner, others


class Refs:
    def __init__(self, names, refs):
        for name, ref in zip(names, refs, strict=True):
            setattr(self, name, ref)


class ForwardIn(NamedTuple):
    lengths: Any
    tokens: Any
    cot: Any
    index: Any
    mixer: Any
    attention: Any
    select: Any
    stepw: Any
    decay: Any
    taps: Any
    bias: Any
    stepb: Any
    skip: Any
    wi: Any
    wo: Any
    wh: Any
    wm: Any


FORWARD_IN = ForwardIn._fields
class Kept(NamedTuple):
    x: Any
    wi_all: Any
    wo_all: Any
    wh_all: Any
    wm_all: Any
    packed: Any
    gains: Any
    span_totals: Any
    ext: Any
    zgate: Any
    conv: Any
    u: Any
    delta: Any
    xdbl: Any
    totals: Any
    yfull: Any
    gated: Any
    x1: Any
    init: Any
    dout: Any
    bx: Any
    cx: Any
    cut: Any
    du: Any
    context_send: Any


KEPT = Kept._fields
FORWARD_OUT = tuple(k + "_out" for k in KEPT) + ("dq_in", "dkv_in")
class ForwardScratch(NamedTuple):
    given: Any
    states: Any
    ends: Any
    row: Any
    small: Any
    wi_send: Any
    wo_send: Any
    wh_send: Any
    wm_send: Any
    packed_send: Any
    gains_send: Any
    packed_all: Any
    gains_all: Any
    before: Any
    state_send: Any
    total_send: Any
    amat: Any
    spread: Any
    q_send: Any
    d_send: Any
    kv_send: Any
    q_in: Any
    d_in: Any
    kv_in: Any
    kvt: Any
    score: Any
    dprob: Any
    dkv: Any
    dq_send: Any
    dkv_send: Any
    causal: Any
    gather_sem: Any
    share_sem: Any
    cot_sem: Any
    edge_sem: Any
    state_sem: Any
    total_sem: Any
    q_sem: Any
    d_sem: Any
    kv_sem: Any
    dq_sem: Any
    dkv_sem: Any
    keep_sem: Any


FORWARD_SCRATCH = KEPT + ForwardScratch._fields


def forward_kernel(steps, nseq, shards, spans, *refs):
    r = Refs(FORWARD_IN + FORWARD_OUT + FORWARD_SCRATCH, refs)
    rows = steps * CHUNKS
    width = DI // shards
    me = lax.axis_index("seq")
    shard, core, chip, partner, others = shard_peers(shards)
    far = len(others)
    ring = [lax.rem(me + by, spans) for by in range(1, spans)]
    greet([at_shard(partner)] + [at_shard(o) for o in others] + [at_seq(to) for to in ring])

    def copy(source, target, sems, at, to):
        return pltpu.make_async_remote_copy(
            src_ref=source, dst_ref=target, send_sem=sems.at[(0, *at)], recv_sem=sems.at[(1, *at)], **to
        )

    sources = (r.wi_send, r.packed_send, r.gains_send, r.wo_send, r.wh_send, r.wm_send)
    wholes = (r.wi_all, r.packed_all, r.gains_all, r.wo_all, r.wh_all, r.wm_all)

    share = D // 2 // spans
    straight = D - share * spans

    def own_share(index):
        return pl.ds(pl.multiple_of(straight + index * share, share), share)

    def sent(k, i):
        if i == far:
            return copy(sources[k], wholes[k].at[shard], r.gather_sem, (k, i), at_shard(partner))
        source, target = sources[k], wholes[k].at[shard]
        if k == 0:
            source, target = source.at[0:straight], wholes[k].at[shard, 0:straight]
        return copy(source, target, r.gather_sem, (k, i), at_shard(others[i]))

    def shared(i):
        return copy(
            r.wi_send.at[own_share(me)],
            r.wi_all.at[shard, own_share(me)],
            r.share_sem,
            (i, 0),
            at_shard(others[i]),
        )

    def fanned(i, by):
        came = lax.rem(chip + far - i, far + 1) * 2 + core
        held = r.wi_all.at[came, own_share(me)]
        return copy(held, held, r.share_sem, (i, by), at_seq(ring[by - 1]))

    def passed(k, i):
        came = lax.rem(chip + far - i, far + 1) * 2 + core
        return copy(
            wholes[k].at[came], wholes[k].at[came], r.gather_sem, (k, far + 1 + i), at_shard(partner)
        )

    def spread(*which):
        for k in which:
            for i in range(far + 1):
                sent(k, i).start()
        for k in which:
            wholes[k][shard] = sources[k][...]

    def pass_on(*which):
        for i in range(far):
            for k in which:
                sent(k, i).wait_recv()
                passed(k, i).start()

    def finish(*which):
        for k in which:
            for i in range(far):
                sent(k, i).wait_send()
                passed(k, i).wait()
            sent(k, far).wait()

    r.wi_send[...] = r.wi[...].astype(BF16)
    r.small[...] = jnp.zeros_like(r.small)
    for source, first in (
        (r.select, SEL),
        (r.decay, DEC),
        (r.stepw, STEP),
        (r.taps, TAPS),
        (r.bias, BIAS),
        (r.stepb, STEPB),
        (r.skip, SKIP),
    ):
        r.small[first : first + source.shape[0], :] = source[...]
    r.packed_send[...] = r.small[...].astype(BF16)
    lane = lax.broadcasted_iota(jnp.int32, (2 * CHUNKS, D // shards), 0)
    r.gains_send[...] = jnp.where(lane == 0, r.mixer[...], r.attention[...]).astype(BF16)
    for i in range(far):
        shared(i).start()
    spread(0, 1, 2)
    last = r.tokens.at[pl.ds(rows - 2 * CHUNKS, 2 * CHUNKS)]
    edge = copy(last, r.before, r.edge_sem, (), at_seq(ring[0]))
    edge.start()

    def cot_copy(by):
        return copy(
            r.cot.at[ring[by - 1]], r.given.at[me], r.cot_sem, (by,), at_seq(ring[by - 1])
        )

    for i in range(far):
        shared(i).wait_recv()
        for by in range(1, spans):
            fanned(i, by).start()
    r.wo_send[...] = r.wo[...].astype(BF16)
    r.wh_send[...] = r.wh[...].astype(BF16)
    r.wm_send[...] = r.wm[...].astype(BF16)
    for part in range(D // LANES):
        lanes = slice(part * LANES, (part + 1) * LANES)
        r.row[...] = r.tokens[:, lanes].astype(F32)
        for step in range(steps):
            r.x[step * CHUNKS : (step + 1) * CHUNKS, lanes] = r.row[
                pl.ds(step, CHUNKS, stride=steps), :
            ]
    for i in range(far):
        shared(i).wait_send()
        for by in range(1, spans):
            fanned(i, by).wait()
    pass_on(0, 1, 2)
    for by in range(1, spans):
        cot_copy(by).start()
    r.given[me] = r.cot[me]
    spread(5, 3, 4)
    finish(0, 1, 2)
    edge.wait()

    starts = starts_of(r.lengths, nseq)
    r.packed[...] = jnp.concatenate([r.packed_all[s] for s in range(shards)], axis=1)
    gains = jnp.concatenate([r.gains_all[s].astype(F32) for s in range(shards)], axis=1)
    r.gains[...] = gains[:CHUNKS]
    gain = gains[0:1]
    x = r.x[...]
    xn1 = (x * norm(x) * gain).astype(BF16)
    before = r.before[...].astype(F32)
    edge_n = (before * norm(before) * gain).astype(BF16)
    wide = 2 * DI // shards
    for s in range(shards):
        piece = dot_nn(xn1, r.wi_all[s])
        if s < shards // 2:
            r.ext[EDGE:, s * wide : (s + 1) * wide] = piece
        else:
            at = (s - shards // 2) * wide
            r.zgate[:, at : at + wide] = piece
    edge_x = jnp.concatenate([dot_nn(edge_n, r.wi_all[s]) for s in range(shards // 2)], axis=1)
    count = r.before.shape[0]
    chunk = lax.broadcasted_iota(jnp.int32, (CHUNKS, DI), 0)
    for k in range(CONV - 1):
        late = (steps - CONV + 1 + k) * CHUNKS + EDGE
        moved = pltpu.roll(r.ext[late : late + CHUNKS, :], 1, 0)
        at = count - CONV + 1 + k
        r.ext[k * CHUNKS : (k + 1) * CHUNKS, :] = jnp.where(
            chunk == 0, jnp.broadcast_to(edge_x[at : at + 1, :], (CHUNKS, DI)), moved
        )
    small = r.packed[DEC:PACK, :].astype(F32)
    taps = small[TAPS - DEC : TAPS - DEC + CONV, :]
    bias = small[BIAS - DEC : BIAS - DEC + 1, :]

    def conv_step(step, carry):
        places = lax.broadcasted_iota(jnp.int32, (CHUNKS, 1), 0) * steps + step + me * rows
        first = start_of(places, starts)
        total = jnp.broadcast_to(bias, (CHUNKS, DI))
        for k in range(CONV):
            at = pl.ds(pl.multiple_of((step + k) * CHUNKS, CHUNKS), CHUNKS)
            inside = places - (CONV - 1) + k >= first
            total = total + jnp.where(inside, taps[k : k + 1, :] * r.ext[at, :], 0.0)
        r.conv[tile(step), :] = total
        r.du[tile(step), :] = total * jax.nn.sigmoid(total)
        return carry

    lax.fori_loop(0, steps, conv_step, 0, unroll=2)
    u = r.du[...].astype(BF16)
    r.u[...] = u
    xdbl = dot_nt(u, r.packed[SEL : SEL + STEP, :])
    r.xdbl[...] = xdbl
    r.delta[...] = dot_nn(
        xdbl[:, :RANK].astype(BF16), r.packed[STEP : STEP + RANK, :]
    )
    stepb = small[STEPB - DEC : STEPB - DEC + 1, :]

    def delta_step(step, total):
        places = lax.broadcasted_iota(jnp.int32, (CHUNKS, 1), 0) * steps + step + me * rows
        pre = r.delta[tile(step), :] + stepb
        delta = jnp.maximum(pre, 0.0) + jnp.log(1.0 + jnp.exp(-jnp.abs(pre)))
        r.delta[tile(step), :] = delta
        cut = jnp.where(begin_of(places, starts), CUT, delta)
        r.cut[tile(step), :] = cut
        r.du[tile(step), :] = delta * r.du[tile(step), :].astype(BF16).astype(F32)
        return total + cut

    totals = lax.fori_loop(0, steps, delta_step, jnp.zeros((CHUNKS, DI), F32), unroll=2)
    r.totals[...] = totals
    total = jnp.sum(totals, axis=0, keepdims=True)
    for group in range(GROUPS_CH):
        r.total_send[group : group + 1, :] = total[:, group * LANES : (group + 1) * LANES]
    r.span_totals[me] = r.total_send[...]

    def total_copy(by):
        return copy(
            r.total_send, r.span_totals.at[me], r.total_sem, (by,), at_seq(ring[by - 1])
        )

    for by in range(1, spans):
        total_copy(by).start()
    pass_on(5)
    spread_decay(r.packed, r.amat, r.spread)
    r.bx[...] = spread_columns(xdbl[:, RANK : RANK + STATE])

    def state_copy(by, at):
        return copy(
            r.state_send.at[at], r.states.at[me, at], r.state_sem, (by, at), at_seq(ring[by - 1])
        )

    def pair_step(pair, carry):
        for odd in range(2):
            lanes = lanes_of(pair * 2 + odd)
            amat = [r.spread[st * CHUNKS : (st + 1) * CHUNKS, lanes] for st in range(STATE)]

            def step_fn(step, states):
                cut = r.cut[tile(step), lanes]
                drive = r.du[tile(step), lanes]
                return tuple(
                    jnp.exp2(cut * amat[st]) * states[st] + drive * r.bx[tile(step), column(st)]
                    for st in range(STATE)
                )

            states = lax.fori_loop(
                0, steps, step_fn, (jnp.zeros((CHUNKS, LANES), F32),) * STATE, unroll=8
            )
            for st in range(STATE):
                r.ends[st, :, lanes] = states[st]
        lanes = pl.ds(pl.multiple_of(pair * 2 * LANES, 2 * LANES), 2 * LANES)
        amat = r.amat[:, lanes]
        state = jnp.zeros((STATE, 2 * LANES), F32)
        for k in range(CHUNKS):
            state = jnp.exp2(amat * r.totals[k : k + 1, lanes]) * state + r.ends[:, k, lanes]
        r.state_send[pair] = state.astype(BF16)
        for by in range(1, spans):

            @pl.when(me + by < spans)
            def _():
                state_copy(by, pair).start()

        return carry

    lax.fori_loop(0, GROUPS_CH // 2, pair_step, 0)
    pass_on(3)
    for by in range(1, spans):
        cot_copy(by).wait()
    finish(5)

    ratio = spans // HEADS
    sub = lax.rem(me, ratio)
    head = lax.div(me, ratio)
    half = rows // 2
    given = jnp.concatenate([r.given[j] for j in range(spans)], axis=0)
    dout = dot_nn(pick_rows(r.index, me, rows, steps), given).astype(BF16)
    r.dout[...] = dout
    merge = jnp.concatenate([r.wm_all[s] for s in range(shards)], axis=0)
    dcontext = dot_nt(dout, merge).astype(BF16).astype(F32)
    low = lane_low(half)

    quarter = half // 2
    quarter_low = lane_low(quarter)

    def packs(pair, target, first, part):
        above, below = pair[:quarter], pair[quarter:]
        at = slice(part * quarter, (part + 1) * quarter)
        even = jnp.where(quarter_low, above, pltpu.roll(below, HEAD_DIM, 1))
        odd = jnp.where(quarter_low, pltpu.roll(above, HEAD_DIM, 1), below)
        target[first, at] = even.astype(BF16)
        target[first + 1, at] = odd.astype(BF16)

    def half_rows(part):
        return slice(part * half, (part + 1) * half)

    for pair in range(HEADS // 2):
        for part in range(2):
            packs(dcontext[half_rows(part), pair * LANES : (pair + 1) * LANES], r.d_send, 2 * pair, part)

    def d_copy(by):
        to = ring[by - 1]
        slot = lax.div(me, ratio)
        return copy(r.d_send.at[lax.div(to, ratio)], r.d_in.at[slot], r.d_sem, (by,), at_seq(to))

    def q_copy(by, part):
        to = ring[by - 1]
        at = pl.ds(part * quarter, quarter)
        source, target = r.q_send.at[lax.div(to, ratio), at], r.q_in.at[lax.div(me, ratio), at]
        return copy(source, target, r.q_sem, (by, part), at_seq(to))

    def kv_copy(by, part):
        to = ring[by - 1]
        return copy(
            r.kv_send.at[lax.div(to, ratio), pl.ds(part * half, half)],
            r.kv_in.at[pl.ds(pl.multiple_of(me * rows + part * half, half), half)],
            r.kv_sem,
            (by, part),
            at_seq(to),
        )

    def to_rows(made, act):
        for by in range(1, spans):
            if ratio == 1:
                act(made(by))
            else:
                pl.when(lax.rem(by, ratio) == 0)(lambda: act(made(by)))

    to_rows(d_copy, lambda c: c.start())
    r.d_in[lax.div(me, ratio)] = r.d_send[head]
    r.cx[...] = spread_columns(xdbl[:, RANK + STATE :])
    for by in range(1, spans):
        total_copy(by).wait()
        for pair in range(GROUPS_CH // 2):

            @pl.when(me + by < spans)
            def _():
                state_copy(by, pair).wait_send()

            @pl.when(me - by >= 0)
            def _():
                state_copy(by, pair).wait_recv()

    amat = r.amat[...]

    def chain(k, state):
        decay = jnp.exp2(amat * total_row(r.span_totals[k]))
        came = jnp.concatenate(
            [r.states[k, g].astype(F32) for g in range(GROUPS_CH // 2)], axis=1
        )
        return decay * state + came

    state = lax.fori_loop(0, me, chain, jnp.zeros((STATE, DI), F32))
    for k in range(CHUNKS):
        r.init[:, k, :] = state
        if k < CHUNKS - 1:
            state = jnp.exp2(amat * r.totals[k : k + 1, :]) * state + r.ends[:, k, :]

    skip = small[SKIP - DEC : SKIP - DEC + 1, :]
    wo = None
    scale = 1.0 / math.sqrt(HEAD_DIM)

    for part in range(2):
        entering, leaving = (r.init, r.ends) if part == 0 else (r.ends, None)

        def group_step(group, carry):
            lanes = lanes_of(group)
            amat_g = [r.spread[st * CHUNKS : (st + 1) * CHUNKS, lanes] for st in range(STATE)]

            def step_fn(step, states):
                cut = r.cut[tile(step), lanes]
                drive = r.du[tile(step), lanes]
                new = tuple(
                    jnp.exp2(cut * amat_g[st]) * states[st] + drive * r.bx[tile(step), column(st)]
                    for st in range(STATE)
                )
                terms = [new[st] * r.cx[tile(step), column(st)] for st in range(STATE)]
                while len(terms) > 1:
                    terms = [a + b for a, b in zip(terms[::2], terms[1::2])]
                r.yfull[tile(step), lanes] = terms[0]
                return new

            states = lax.fori_loop(
                part * steps // 2,
                (part + 1) * steps // 2,
                step_fn,
                tuple(entering[st, :, lanes] for st in range(STATE)),
                unroll=8,
            )
            if leaving is not None:
                for st in range(STATE):
                    leaving[st, :, lanes] = states[st]
            return carry

        lax.fori_loop(0, GROUPS_CH, group_step, 0)

        def gate_step(pair, carry):
            at = pl.ds(pl.multiple_of(pair * 2 * CHUNKS, 2 * CHUNKS), 2 * CHUNKS)
            yfull = r.yfull[at, :] + skip * r.u[at, :].astype(F32)
            r.yfull[at, :] = yfull
            gate = r.zgate[at, :]
            r.gated[at, :] = (yfull * (gate * jax.nn.sigmoid(gate))).astype(BF16)
            return carry

        lax.fori_loop(part * steps // 4, (part + 1) * steps // 4, gate_step, 0)
        if part == 0:
            pass_on(4)
            finish(3)
            wo = jnp.concatenate([r.wo_all[s] for s in range(shards)], axis=0)
        ours = half_rows(part)
        x1 = r.x[ours, :] + dot_nn(r.gated[ours, :], wo)
        r.x1[ours, :] = x1
        xn2 = (x1 * norm(x1) * gains[1:2, :]).astype(BF16)
        if part == 0:
            finish(4)
        qkv = jnp.concatenate([dot_nn(xn2, r.wh_all[s]) for s in range(shards)], axis=1)
        qkv = qkv.astype(BF16).astype(F32)
        for pair in range(HEADS // 2):
            at = pair * LANES
            packs(qkv[:, at : at + LANES] * scale, r.q_send, 2 * pair, part)
            k = qkv[:, D + at : D + at + LANES]
            v = qkv[:, 2 * D + at : 2 * D + at + LANES]
            even = jnp.where(low, k, pltpu.roll(v, HEAD_DIM, 1))
            odd = jnp.where(low, pltpu.roll(k, HEAD_DIM, 1), v)
            r.kv_send[2 * pair, ours] = even.astype(BF16)
            r.kv_send[2 * pair + 1, ours] = odd.astype(BF16)
        to_rows(functools.partial(q_copy, part=part), lambda c: c.start())
        for by in range(1, spans):
            kv_copy(by, part).start()
    r.q_in[lax.div(me, ratio)] = r.q_send[head]
    r.kv_in[pl.ds(pl.multiple_of(me * rows, rows), rows), :] = r.kv_send[head]
    keeps = [
        pltpu.make_async_copy(getattr(r, name), getattr(r, name + "_out"), r.keep_sem.at[i])
        for i, name in enumerate(KEPT)
    ]
    for keep in keeps[:-1]:
        keep.start()
    at = lax.broadcasted_iota(jnp.int32, (1, rows), 1)
    turn_at = lax.rem(lax.div(at, quarter), 2) * half + lax.div(at, half) * quarter + lax.rem(at, quarter)
    query_local = row_places(turn_at, steps)
    key_local = row_places(lax.broadcasted_iota(jnp.int32, (rows, 1), 0), steps)
    r.causal[...] = jnp.where(key_local <= query_local, 0.0, NEG)
    r.dkv[...] = jnp.zeros_like(r.dkv)
    to_rows(d_copy, lambda c: c.wait())
    for part in range(2):
        to_rows(functools.partial(q_copy, part=part), lambda c: c.wait())
        for by in range(1, spans):
            kv_copy(by, part).wait()

    static = ratio == 1
    blocks = spans // ratio

    def each(count, fn, carry):
        if not static:
            return lax.fori_loop(0, count, fn, carry)
        for j in range(count):
            carry = fn(j, carry)
        return carry

    def key_rows(j):
        return pl.ds(j * rows if static else pl.multiple_of(j * rows, rows), rows)

    def turn(j, carry):
        r.kvt[j] = r.kv_in[key_rows(j), :].astype(F32).T.astype(BF16)
        return carry

    each(spans, turn, 0)
    folded = (rows // CHUNKS, CHUNKS, rows)

    def dq_copy(to, by, t):
        return copy(r.dq_send.at[t], r.dq_in.at[head], r.dq_sem, (by,), at_seq(to))

    def query_block(t, carry):
        i = t * ratio + sub
        slot = t % 2 if static else 0
        q = r.q_in[t].astype(F32)
        d = r.d_in[t].astype(F32)
        qt = q.T
        dt = d.T
        zero = jnp.zeros((HEAD_DIM, rows), F32)
        qt = jnp.concatenate([qt[:HEAD_DIM], qt[HEAD_DIM:]], axis=1)
        dt = jnp.concatenate([dt[:HEAD_DIM], dt[HEAD_DIM:]], axis=1)
        both = jnp.concatenate(
            [jnp.concatenate([qt, zero], axis=1), jnp.concatenate([zero, dt], axis=1)], axis=0
        ).astype(BF16)
        none = jnp.zeros((half, LANES), F32)
        natural = jnp.concatenate(
            [
                jnp.where(low, none, pltpu.roll(d, HEAD_DIM, 1)),
                jnp.where(low, none, d),
                jnp.where(low, q, none),
                jnp.where(low, pltpu.roll(q, HEAD_DIM, 1), none),
            ],
            axis=0,
        ).astype(BF16)
        first = start_of(query_local + i * rows, starts)

        def scores(j, top):
            joint = dot_nn(r.kv_in[key_rows(j), :], both)
            score = joint[:, :rows]
            if static:
                if j == t:
                    score = score + r.causal[...]
                if j in (0, t) or t == spans - 1:
                    score = jnp.where(key_local + j * rows >= first, score, NEG)
            else:
                query = query_local + i * rows
                key = key_local + j * rows
                score = jnp.where((key <= query) & (key >= first), score, NEG)
            r.score[slot, j] = score
            r.dprob[slot, j] = joint[:, rows:]
            return jnp.maximum(top, jnp.max(score.reshape(folded), axis=0))

        top = each(t + 1 if static else i + 1, scores, jnp.full((CHUNKS, rows), NEG, F32))
        top = jnp.max(top, axis=0, keepdims=True)

        def weigh(j, sums):
            total, dot = sums
            prob = jnp.exp(r.score[slot, j] - top)
            r.score[slot, j] = prob
            total = total + jnp.sum(prob.reshape(folded), axis=0)
            dot = dot + jnp.sum((prob * r.dprob[slot, j]).reshape(folded), axis=0)
            return total, dot

        zero = jnp.zeros((CHUNKS, rows), F32)
        total, dot = each(t + 1 if static else i + 1, weigh, (zero, zero))
        inverse = 1.0 / jnp.sum(total, axis=0, keepdims=True)
        datt = jnp.sum(dot, axis=0, keepdims=True) * inverse

        def back(j, sums):
            prob = r.score[slot, j] * inverse
            dscore = prob * (r.dprob[slot, j] - datt)
            joint = jnp.concatenate([prob.astype(BF16), dscore.astype(BF16)], axis=1)
            r.dkv[key_rows(j), :] += dot_nn(joint, natural)
            return sums + dot_nn(r.kvt[j], joint)

        sums = each(t + 1 if static else i + 1, back, jnp.zeros((LANES, 2 * rows), F32))
        dqt = sums[:HEAD_DIM, rows:] * scale
        ctx = sums[HEAD_DIM:, :rows]
        dqt = jnp.concatenate([dqt[:, :half], dqt[:, half:]], axis=0)
        ctx = jnp.concatenate([ctx[:, :half], ctx[:, half:]], axis=0)
        r.dq_send[t] = dqt.T.astype(BF16)
        r.context_send[t] = ctx.T.astype(BF16)
        by = lax.rem(i - me + spans, spans)

        @pl.when(i != me)
        def _():
            dq_copy(i, by, t).start()

        @pl.when(i == me)
        def _():
            r.dq_in[head] = r.dq_send[t]

        return carry

    if static:
        for t in range(blocks):
            query_block(t, 0)
    else:
        lax.fori_loop(0, blocks, query_block, 0)
    keeps[-1].start()

    def cast(j, carry):
        r.dkv_send[j] = r.dkv[key_rows(j), :].astype(BF16)
        return carry

    each(spans, cast, 0)

    def dkv_copy(by):
        to = ring[by - 1]
        return copy(r.dkv_send.at[to], r.dkv_in.at[me], r.dkv_sem, (by,), at_seq(to))

    for by in range(1, spans):
        dkv_copy(by).start()
    r.dkv_in[me] = r.dkv_send[me]
    for t in range(blocks):
        i = t * ratio + sub
        by = lax.rem(i - me + spans, spans)

        @pl.when(i != me)
        def _():
            dq_copy(i, by, t).wait_send()

    for h in range(HEADS):
        came = h * ratio + sub
        by = lax.rem(me - came + spans, spans)

        @pl.when(came != me)
        def _():
            dq_copy(came, by, 0).wait_recv()

    for by in range(1, spans):
        dkv_copy(by).wait()
    for keep in keeps:
        keep.wait()


def total_row(values):
    return jnp.concatenate([values[g : g + 1, :] for g in range(GROUPS_CH)], axis=1)


def lane_low(rows):
    return lax.broadcasted_iota(jnp.int32, (rows, LANES), 1) < HEAD_DIM


def pick_rows(table_ref, me, rows, steps):
    spans = table_ref.shape[1] // rows
    share = rows // spans
    lane = lax.broadcasted_iota(jnp.int32, (1, rows), 1)
    index = jnp.zeros((1, rows), F32)
    for j in range(spans):
        line = table_ref[:, j * rows : (j + 1) * rows].astype(F32)
        line = pltpu.roll(line, lax.rem((j + spans - me) * share, rows), 1)
        index = jnp.where(lane >= j * share, line, index)
    places = row_places(lax.broadcasted_iota(jnp.int32, (rows, 1), 0), steps) + me * rows
    return (index == places.astype(F32)).astype(F32).astype(BF16)


GRADS = ("heads", "out", "merge", "late", "early", "other", "small")
SMALL = 6
BACKWARD_IN = ("lengths", "index", "dq_in", "dkv_in") + tuple(k + "_kept" for k in KEPT)
class BackwardOut(NamedTuple):
    output: Any
    token_grad: Any
    last_heads: Any
    last_out: Any
    last_merge: Any
    last_small: Any
    pair_in: Any
    early_in: Any
    other_in: Any


BACKWARD_OUT = BackwardOut._fields
class FinalOut(NamedTuple):
    output: Any
    token_grad: Any
    mixer_grad: Any
    input_grad: Any
    taps_grad: Any
    bias_grad: Any
    select_grad: Any
    stepw_grad: Any
    stepb_grad: Any
    decay_grad: Any
    skip_grad: Any
    output_grad: Any
    attention_grad: Any
    heads_grad: Any
    merge_grad: Any


FINAL_OUT = FinalOut._fields
class BackwardScratch(NamedTuple):
    context: Any
    given: Any
    dx1: Any
    dys: Any
    dzgate: Any
    ends: Any
    grad_send: Any
    grads_in: Any
    db: Any
    dc: Any
    decay: Any
    held: Any
    state: Any
    bgrad: Any
    adelta: Any
    arrive: Any
    dxdbl: Any
    dext: Any
    spill: Any
    spill_in: Any
    small: Any
    row: Any
    amat: Any
    spread: Any
    sub_late: Any
    sub_early: Any
    sub_other: Any


class BackwardSems(NamedTuple):
    load_sem: Any
    context_sem: Any
    given_sem: Any
    state_sem: Any
    spill_sem: Any
    near_sem: Any
    far_sem: Any
    part_sem: Any
    last_sem: Any
    pair_sem: Any
    inner_sem: Any
    outer_sem: Any
    late_outer_sem: Any
    late_inner_sem: Any


BACKWARD_SCRATCH = (
    KEPT
    + BackwardScratch._fields
    + tuple(kind + name for kind in ("g_", "near_", "sum_", "far_", "part_") for name in GRADS)
    + BackwardSems._fields
)


def backward_kernel(steps, nseq, shards, spans, *refs):
    r = Refs(BACKWARD_IN + BACKWARD_OUT + BACKWARD_SCRATCH, refs)
    rows = steps * CHUNKS
    width = DI // shards
    me = lax.axis_index("seq")
    shard, core, chip, partner, others = shard_peers(shards)
    chips = shards // 2
    ring = [lax.rem(me + by, spans) for by in range(1, spans)]
    every = [me] + ring
    ratio = spans // HEADS
    sub = lax.rem(me, ratio)
    half = rows // 2
    blocks = spans // ratio
    starts = starts_of(r.lengths, nseq)
    loads = {
        name: pltpu.make_async_copy(getattr(r, name + "_kept"), getattr(r, name), r.load_sem.at[i])
        for i, name in enumerate(KEPT)
    }
    early = ("context_send", "dout", "x1", "gains", "wh_all")
    middle = ("gated", "wo_all", "zgate", "yfull", "u", "x")
    late = ("wm_all", "packed", "cut", "cx", "totals", "span_totals", "init", "delta", "du", "bx", "xdbl")
    last = ("conv", "ext", "wi_all")
    for name in early + middle:
        loads[name].start()

    def loaded(*names):
        for name in names:
            loads[name].wait()

    targets = [lax.div(shard, 2), shards // 2 + lax.div(shard, 2)]
    mine = lax.div(shard, shards // 2)
    first_piece = 2 * lax.rem(shard, shards // 2)

    def anywhere(index, at):
        return {"device_id": {"seq": index, "shard": at}, "device_id_type": pl.DeviceIdType.MESH}

    barrier = pltpu.get_barrier_semaphore()

    def signal(to):
        pl.semaphore_signal(barrier, inc=1, **to)

    peers = [at_shard(partner)] + [at_shard(o) for o in others] + [at_seq(to) for to in ring]
    for peer in peers:
        signal(peer)
    selves = jnp.int32(0)
    for by in range(spans):
        for at in targets + [first_piece, first_piece + 1]:
            if by:
                signal(anywhere(every[by], at))
            else:
                pl.when(at != shard)(lambda: signal(anywhere(me, at)))
                selves = selves + (at == shard).astype(jnp.int32)
    pl.semaphore_wait(barrier, len(peers) + 4 * spans - selves)

    def copy(source, target, sems, at, to):
        return pltpu.make_async_remote_copy(
            src_ref=source, dst_ref=target, send_sem=sems.at[(0, *at)], recv_sem=sems.at[(1, *at)], **to
        )

    def ref(kind, k):
        return getattr(r, kind + "_" + GRADS[k])

    def near_copy(k, x):
        return copy(
            ref("g", k).at[x * 2 + 1 - core], ref("near", k).at[x], r.near_sem, (k, x), at_shard(partner)
        )

    def far_copy(k, by):
        source = ref("sum", k).at[lax.rem(chip + by, chips)]
        return copy(source, ref("far", k).at[by - 1], r.far_sem, (k, by), at_shard(others[by - 1]))

    def part_copy(k, by):
        to = ring[by - 1]
        return copy(
            ref("near", k).at[0, to], ref("part", k).at[by], r.part_sem, (k, by), at_seq(to)
        )

    def last_copy(k, by):
        held = ref("last", k).at[me]
        return copy(held, held, r.last_sem, (k, by), at_seq(ring[by - 1]))

    def pair_refs(k):
        return (r.sub_early, r.early_in) if GRADS[k] == "early" else (r.sub_other, r.other_in)

    def pair_copy(k, by, at):
        source, target = pair_refs(k)
        to = anywhere(every[by], targets[0])
        return copy(source, target.at[at, me], r.pair_sem, (k - 4, at, by), to)

    def near_send(k):
        for x in range(chips):
            near_copy(k, x).start()

    def far_send(k):
        for x in range(chips):
            near_copy(k, x).wait_recv()
            ref("sum", k)[x] = (
                ref("g", k)[x * 2 + core].astype(F32) + ref("near", k)[x].astype(F32)
            ).astype(BF16)
        for by in range(1, chips):
            far_copy(k, by).start()

    def part_send(k):
        total = ref("sum", k)[chip].astype(F32)
        for by in range(1, chips):
            far_copy(k, by).wait_recv()
            total = total + ref("far", k)[by - 1].astype(F32)
        ref("near", k)[0] = total.astype(BF16)
        for by in range(1, chips):
            far_copy(k, by).wait_send()
        for by in range(1, spans):
            part_copy(k, by).start()

    def last_send(k):
        total = ref("near", k)[0, me].astype(F32)
        for by in range(1, spans):
            part_copy(k, by).wait_recv()
            total = total + ref("part", k)[by].astype(F32)
        if k == SMALL:
            ref("last", k)[me] = total.astype(BF16)
            for by in range(1, spans):
                last_copy(k, by).start()
            return
        source, target = pair_refs(k)
        source[...] = total.astype(BF16)
        for by in range(spans):
            to_owner(by == 0, targets[0], pair_copy(k, by, parity), lambda c: c.start())

        @pl.when(targets[0] == shard)
        def _():
            target[parity, me] = source[...]

    def to_owner(same, to, made, act):
        if same:
            pl.when(to != shard)(lambda: act(made))
        else:
            act(made)

    inner = spans // OUTER
    low_me, high_me = lax.rem(me, inner), lax.div(me, inner)
    lows = [lax.rem(low_me + by, inner) for by in range(inner)]
    highs = [lax.rem(high_me + by, OUTER) for by in range(OUTER)]
    own_part = low_me * OUTER + high_me
    middle_at = (inner - 1) * OUTER
    parity = lax.rem(shard, 2)

    def inner_copy(k, by):
        return copy(
            ref("near", k).at[0, pl.ds(lows[by] * OUTER, OUTER)],
            ref("part", k).at[pl.ds((by - 1) * OUTER, OUTER)],
            r.inner_sem,
            (k, 0, by),
            at_seq(high_me * inner + lows[by]),
        )

    def outer_copy(k, by):
        return copy(
            ref("part", k).at[middle_at + highs[by]],
            ref("part", k).at[spans + by - 1],
            r.outer_sem,
            (k, 0, by),
            at_seq(highs[by] * inner + low_me),
        )

    def outer_last(k, by):
        held = ref("last", k).at[own_part]
        return copy(held, held, r.outer_sem, (k, 1, by), at_seq(highs[by] * inner + low_me))

    def inner_last(k, by):
        held = ref("last", k).at[pl.ds(low_me * OUTER, OUTER)]
        return copy(held, held, r.inner_sem, (k, 1, by), at_seq(high_me * inner + lows[by]))

    def late_outer(by, at):
        return copy(
            r.sub_late,
            r.pair_in.at[at, own_part],
            r.late_outer_sem,
            (at, by),
            anywhere(highs[by] * inner + low_me, targets[1]),
        )

    def late_inner(by, at):
        held = r.pair_in.at[at, pl.ds(low_me * OUTER, OUTER)]
        to = at_seq(high_me * inner + lows[by])
        return copy(held, held, r.late_inner_sem, (at, by), to)

    def inner_send(k):
        total = ref("sum", k)[chip].astype(F32)
        for by in range(1, chips):
            far_copy(k, by).wait_recv()
            total = total + ref("far", k)[by - 1].astype(F32)
        ref("near", k)[0] = total.astype(BF16)
        for by in range(1, inner):
            inner_copy(k, by).start()

    def outer_send(k):
        total = ref("near", k)[0, pl.ds(low_me * OUTER, OUTER)].astype(F32)
        for by in range(1, inner):
            inner_copy(k, by).wait_recv()
            total = total + ref("part", k)[(by - 1) * OUTER : by * OUTER].astype(F32)
        ref("part", k)[middle_at : middle_at + OUTER] = total.astype(BF16)
        for by in range(1, OUTER):
            outer_copy(k, by).start()

    def outer_back(k):
        total = ref("part", k)[middle_at + high_me].astype(F32)
        for by in range(1, OUTER):
            outer_copy(k, by).wait_recv()
            total = total + ref("part", k)[spans + by - 1].astype(F32)
        if k != 3:
            ref("last", k)[own_part] = total.astype(BF16)
            for by in range(1, OUTER):
                outer_last(k, by).start()
            return
        r.sub_late[...] = total.astype(BF16)
        for by in range(OUTER):
            to_owner(by == 0, targets[1], late_outer(by, parity), lambda c: c.start())

        @pl.when(targets[1] == shard)
        def _():
            r.pair_in[parity, own_part] = r.sub_late[...]

    def inner_back(k):
        if k != 3:
            for by in range(1, OUTER):
                outer_last(k, by).wait_recv()
            for by in range(1, inner):
                inner_last(k, by).start()
            return

        @pl.when(mine == 1)
        def _():
            for at in range(2):
                for by in range(OUTER):
                    to_owner(by == 0, first_piece + at, late_outer(by, at), lambda c: c.wait_recv())
                for by in range(1, inner):
                    late_inner(by, at).start()

    def finish(k):
        for x in range(chips):
            near_copy(k, x).wait_send()
        if k < 4:
            for by in range(1, chips):
                far_copy(k, by).wait_send()
            for by in range(1, inner):
                inner_copy(k, by).wait_send()
            for by in range(1, OUTER):
                outer_copy(k, by).wait_send()
        else:
            for by in range(1, spans):
                part_copy(k, by).wait_send()
        if k < 3:
            for by in range(1, OUTER):
                outer_last(k, by).wait_send()
            for by in range(1, inner):
                inner_last(k, by).wait()
        elif k == 3:
            for by in range(OUTER):
                to_owner(by == 0, targets[1], late_outer(by, parity), lambda c: c.wait_send())

            @pl.when(mine == 1)
            def _():
                for at in range(2):
                    for by in range(1, inner):
                        late_inner(by, at).wait()

        elif k == SMALL:
            for by in range(1, spans):
                last_copy(k, by).wait()
        else:
            for by in range(spans):
                to_owner(by == 0, targets[0], pair_copy(k, by, parity), lambda c: c.wait_send())

            @pl.when(mine == 0)
            def _():
                for at in range(2):
                    for by in range(spans):
                        made = pair_copy(k, by, at)
                        to_owner(by == 0, first_piece + at, made, lambda c: c.wait_recv())

    def put(k, piece, value):
        size = value.shape[0] // spans
        for j in range(spans):
            ref("g", k)[piece, j] = value[j * size : (j + 1) * size].astype(BF16)

    loaded("context_send")
    head = lax.div(me, ratio)

    def context_copy(t, by, to):
        return copy(r.context_send.at[t], r.context.at[head], r.context_sem, (by,), at_seq(to))

    for t in range(blocks):
        i = t * ratio + sub
        by = lax.rem(i - me + spans, spans)

        @pl.when(i != me)
        def _():
            context_copy(t, by, i).start()

        @pl.when(i == me)
        def _():
            r.context[head] = r.context_send[t]

    low = lane_low(rows)
    half_low = lane_low(half)

    def unpacked(source, pair):
        even, odd = source[2 * pair].astype(F32), source[2 * pair + 1].astype(F32)
        first = jnp.where(half_low, even, pltpu.roll(odd, HEAD_DIM, 1))
        second = jnp.where(half_low, pltpu.roll(even, HEAD_DIM, 1), odd)
        quarter = half // 2
        return jnp.concatenate(
            [first[:quarter], second[:quarter], first[quarter:], second[quarter:]], axis=0
        )

    dqs, dks, dvs = [], [], []
    for pair in range(HEADS // 2):
        dkv = [
            sum(r.dkv_in[(2 * pair + odd) * ratio + part].astype(F32) for part in range(ratio))
            for odd in range(2)
        ]
        dqs.append(unpacked(r.dq_in, pair))
        dks.append(jnp.where(low, dkv[0], pltpu.roll(dkv[1], HEAD_DIM, 1)))
        dvs.append(jnp.where(low, pltpu.roll(dkv[0], HEAD_DIM, 1), dkv[1]))
    dqkv = jnp.concatenate(dqs + dks + dvs, axis=1).astype(BF16)
    loaded("x1", "gains", "wh_all", "dout")
    for name in late + last:
        loads[name].start()
    x1 = r.x1[...]
    inverse = norm(x1)
    normal = x1 * inverse
    gain = r.gains[1:2, :]
    xn2 = (normal * gain).astype(BF16)
    wide = 3 * D // shards
    dxn2 = jnp.zeros((rows, D), F32)
    for s in range(shards):
        piece = dqkv[:, s * wide : (s + 1) * wide]
        put(0, s, dot_tn(xn2, piece))
        dxn2 = dxn2 + dot_nt(piece, r.wh_all[s])
    near_send(0)
    attention_gain = jnp.sum(dxn2 * normal, axis=0, keepdims=True)
    e2 = dxn2 * gain
    dx1 = r.dout[...].astype(F32) + inverse * (
        e2 - normal * jnp.mean(e2 * normal, axis=-1, keepdims=True)
    )
    r.dx1[...] = dx1
    dmixed = dx1.astype(BF16)
    loaded("gated", "wo_all")
    for s in range(shards):
        put(1, s, dot_tn(r.gated[:, s * width : (s + 1) * width], dmixed))
        r.dys[:, s * width : (s + 1) * width] = dot_nt(dmixed, r.wo_all[s])
    near_send(1)
    far_send(0)
    loaded("zgate", "yfull", "u", "x")

    def gate_step(pair, total):
        at = pl.ds(pl.multiple_of(pair * 2 * CHUNKS, 2 * CHUNKS), 2 * CHUNKS)
        dgated = r.dys[at, :].astype(BF16).astype(F32)
        gate = r.zgate[at, :]
        s = jax.nn.sigmoid(gate)
        dys = dgated * (gate * s)
        r.dys[at, :] = dys
        r.dzgate[at, :] = (dgated * r.yfull[at, :] * (s * (1.0 + gate * (1.0 - s)))).astype(BF16)
        return total + dys * r.u[at, :].astype(F32)

    total = lax.fori_loop(0, steps // 2, gate_step, jnp.zeros((2 * CHUNKS, DI), F32))
    r.small[SKIP : SKIP + 1, :] = jnp.sum(total, axis=0, keepdims=True)
    far_send(1)
    x = r.x[...]
    inverse_one = norm(x)
    normal_one = x * inverse_one
    gain_one = r.gains[0:1, :]
    xn1 = (normal_one * gain_one).astype(BF16)
    for s in range(shards):
        put(3, s, dot_tn(xn1, r.dzgate[:, s * width : (s + 1) * width]))
    near_send(3)
    loaded("wm_all", "packed", "cut", "cx", "totals", "span_totals")
    spread_decay(r.packed, r.amat, r.spread)

    def state_copy(by, at):
        to = lax.rem(me - by + spans, spans)
        return copy(
            r.grad_send.at[at], r.grads_in.at[me, at], r.state_sem, (by, at), at_seq(to)
        )

    def pair_step(pair, carry):
        for odd in range(2):
            lanes = lanes_of(pair * 2 + odd)
            amat = [r.spread[st * CHUNKS : (st + 1) * CHUNKS, lanes] for st in range(STATE)]

            def step_fn(turn, grads):
                step = steps - 1 - turn
                cut = r.cut[tile(step), lanes]
                dys = r.dys[tile(step), lanes]
                return tuple(
                    jnp.exp2(cut * amat[st]) * (grads[st] + dys * r.cx[tile(step), column(st)])
                    for st in range(STATE)
                )

            grads = lax.fori_loop(
                0, steps, step_fn, (jnp.zeros((CHUNKS, LANES), F32),) * STATE, unroll=8
            )
            for st in range(STATE):
                r.ends[st, :, lanes] = grads[st]
        lanes = pl.ds(pl.multiple_of(pair * 2 * LANES, 2 * LANES), 2 * LANES)
        amat = r.amat[:, lanes]
        state = jnp.zeros((STATE, 2 * LANES), F32)
        for k in reversed(range(CHUNKS)):
            state = jnp.exp2(amat * r.totals[k : k + 1, lanes]) * state + r.ends[:, k, lanes]
        r.grad_send[pair] = state.astype(BF16)
        for by in range(1, spans):

            @pl.when(me - by >= 0)
            def _():
                state_copy(by, pair).start()

        pl.when(pair == 0)(lambda: far_send(3))
        return carry

    lax.fori_loop(0, GROUPS_CH // 2, pair_step, 0)
    for h in range(HEADS):
        came = h * ratio + sub
        by = lax.rem(me - came + spans, spans)

        @pl.when(came != me)
        def _():
            context_copy(0, by, came).wait_recv()

    context = jnp.concatenate([unpacked(r.context, p) for p in range(HEADS // 2)], axis=1)
    context = context.astype(BF16)
    short = D // shards
    x2 = x1
    for s in range(shards):
        part = context[:, s * short : (s + 1) * short]
        x2 = x2 + dot_nn(part, r.wm_all[s])
        put(2, s, dot_tn(part, r.dout[...]))
    near_send(2)
    given = dot_tn(pick_rows(r.index, me, rows, steps), x2.astype(BF16))
    share = rows // spans
    for j in range(spans):
        r.given[j] = given[j * share : (j + 1) * share].astype(BF16)

    def given_copy(by):
        to = ring[by - 1]
        return copy(r.given.at[to], r.output.at[me], r.given_sem, (by,), at_seq(to))

    r.output[me] = r.given[me]

    loaded("init", "delta", "du", "bx", "xdbl", *last)
    r.db[...] = jnp.zeros_like(r.db)
    r.dc[...] = jnp.zeros_like(r.dc)
    for by in range(1, spans):
        for pair in range(GROUPS_CH // 2):

            @pl.when(me - by >= 0)
            def _():
                state_copy(by, pair).wait_send()

            @pl.when(me + by < spans)
            def _():
                state_copy(by, pair).wait_recv()

    for by in range(1, spans):
        given_copy(by).start()
    amat = r.amat[...]

    def chain(turn, state):
        k = spans - 1 - turn
        decay = jnp.exp2(amat * total_row(r.span_totals[k]))
        came = jnp.concatenate(
            [r.grads_in[k, g].astype(F32) for g in range(GROUPS_CH // 2)], axis=1
        )
        return decay * state + came

    state = lax.fori_loop(0, spans - 1 - me, chain, jnp.zeros((STATE, DI), F32))
    for k in reversed(range(CHUNKS)):
        r.arrive[:, k, :] = state
        if k:
            state = jnp.exp2(amat * r.totals[k : k + 1, :]) * state + r.ends[:, k, :]
    eight = STATE // 2

    def sum_of(terms):
        while len(terms) > 1:
            terms = [a + b for a, b in zip(terms[::2], terms[1::2])]
        return terms[0]

    def kept_at(step, i):
        return pl.ds(pl.multiple_of(step * (eight * CHUNKS) + i * CHUNKS, CHUNKS), CHUNKS)

    stages = {
        0: ((far_send, 2), (inner_send, 0)),
        1: ((inner_send, 1),),
        2: ((outer_send, 0),),
        3: ((outer_send, 1),),
        4: ((outer_back, 0),),
        5: ((inner_send, 3),),
        6: ((outer_back, 1), (inner_send, 2)),
        7: ((inner_back, 0), (outer_send, 3)),
    }

    def run(todo):
        for stage, k in todo:
            stage(k)

    def group_step(group, carry):
        lanes = lanes_of(group)
        for part in range(2):
            states = range(part * eight, (part + 1) * eight)
            amat_g = [r.spread[st * CHUNKS : (st + 1) * CHUNKS, lanes] for st in states]

            def forward(step, held):
                cut = r.cut[tile(step), lanes]
                drive = r.du[tile(step), lanes]
                out = []
                for i, st in enumerate(states):
                    decay = jnp.exp2(cut * amat_g[i])
                    kept = decay * held[i]
                    new = kept + drive * r.bx[tile(step), column(st)]
                    r.decay[kept_at(step, i), :] = decay
                    r.held[kept_at(step, i), :] = kept
                    r.state[kept_at(step, i), :] = new
                    out.append(new)
                return tuple(out)

            lax.fori_loop(
                0, steps, forward, tuple(r.init[st, :, lanes] for st in states), unroll=8
            )

            def backward(turn, held):
                grads, sums = held
                step = steps - 1 - turn
                delta = r.delta[tile(step), lanes]
                drive = r.du[tile(step), lanes]
                dys = r.dys[tile(step), lanes]
                new, totals, by_b, by_a = [], [], [], []
                for i, st in enumerate(states):
                    at = tile(step)
                    grad = grads[i] + dys * r.cx[at, column(st)]
                    new.append(r.decay[kept_at(step, i), :] * grad)
                    through = grad * r.held[kept_at(step, i), :]
                    totals.append(sums[i] + through * delta)
                    by_a.append(amat_g[i] * through)
                    by_b.append(grad * r.bx[at, column(st)])
                    r.dc[at, column(st)] += r.state[kept_at(step, i), :] * dys
                    r.db[at, column(st)] += grad * drive
                if part:
                    r.bgrad[tile(step), lanes] += sum_of(by_b)
                    r.adelta[tile(step), lanes] += sum_of(by_a)
                else:
                    r.bgrad[tile(step), lanes] = sum_of(by_b)
                    r.adelta[tile(step), lanes] = sum_of(by_a)
                return (tuple(new), tuple(totals))

            _, sums = lax.fori_loop(
                0,
                steps,
                backward,
                (
                    tuple(r.arrive[st, :, lanes] for st in states),
                    (jnp.zeros((CHUNKS, LANES), F32),) * eight,
                ),
                unroll=8,
            )
            for i, st in enumerate(states):
                row = jnp.sum(sums[i], axis=0, keepdims=True)
                amat_row = amat_g[i][0:1, :] * math.log(2.0)
                r.small[DEC + st : DEC + st + 1, lanes] = row * amat_row
        for at, todo in stages.items():
            pl.when(group == at)(functools.partial(run, todo))
        return carry

    lax.fori_loop(0, GROUPS_CH, group_step, 0)
    small = r.packed[DEC:PACK, :].astype(F32)
    taps = small[TAPS - DEC : TAPS - DEC + CONV, :]
    skip = small[SKIP - DEC : SKIP - DEC + 1, :]

    def delta_step(step, total):
        at = tile(step)
        bgrad = r.bgrad[at, :]
        delta = r.delta[at, :]
        u = r.conv[at, :]
        u = (u * jax.nn.sigmoid(u)).astype(BF16).astype(F32)
        ddelta = u * bgrad + r.adelta[at, :] * math.log(2.0)
        dtpre = (ddelta * (1.0 - jnp.exp(-delta))).astype(BF16).astype(F32)
        r.adelta[at, :] = dtpre
        r.bgrad[at, :] = r.dys[at, :] * skip + delta * bgrad
        return total + dtpre

    total = lax.fori_loop(0, steps, delta_step, jnp.zeros((CHUNKS, DI), F32))
    run(((inner_back, 1), (outer_send, 2)))
    r.small[STEPB : STEPB + 1, :] = jnp.sum(total, axis=0, keepdims=True)
    r.small[GAINS:, :] = jnp.zeros((PACK - GAINS, DI), F32)
    dtpre = r.adelta[...].astype(BF16)
    steplow = r.xdbl[:, 0:RANK].astype(BF16)
    r.small[STEP : STEP + RANK, :] = dot_tn(steplow, dtpre)
    r.dxdbl[:, 0:RANK] = dot_nt(dtpre, r.packed[STEP : STEP + RANK, :])
    for part in range(4):
        at = slice(part * rows // 4, (part + 1) * rows // 4)
        r.dxdbl[at, RANK : RANK + STATE] = gather_columns(r.db[at, :])
        r.dxdbl[at, RANK + STATE :] = gather_columns(r.dc[at, :])
    run(((outer_back, 3),))
    dxdbl = r.dxdbl[...].astype(BF16)
    r.small[SEL : SEL + STEP, :] = dot_tn(dxdbl, r.u[...])
    r.bgrad[...] += dot_nn(dxdbl, r.packed[SEL : SEL + STEP, :])
    r.dext[...] = jnp.zeros_like(r.dext)
    r.spill[...] = jnp.zeros_like(r.spill)

    @pl.when(me == spans - 1)
    def _():
        r.spill_in[...] = jnp.zeros_like(r.spill_in)

    def conv_steps(first_step, last_step, ranges, totals):
        def one(step, totals):
            at = tile(step)
            places = lax.broadcasted_iota(jnp.int32, (CHUNKS, 1), 0) * steps + step + me * rows
            first = start_of(places, starts)
            inside = [places - (CONV - 1) + k >= first for k in range(CONV)]
            out = []
            for lanes, sums in zip(ranges, totals):
                dconv = r.bgrad[at, lanes] * silu_slope(r.conv[at, lanes])
                new = []
                for k in range(CONV):
                    to = pl.ds(pl.multiple_of((step + k) * CHUNKS, CHUNKS), CHUNKS)
                    counted = jnp.where(inside[k], dconv, 0.0)
                    new.append(sums[k] + counted * r.ext[to, lanes])
                    r.dext[to, lanes] += taps[k : k + 1, lanes] * counted
                out.append(tuple(new) + (sums[CONV] + dconv,))
            return tuple(out)

        return lax.fori_loop(first_step, last_step, one, totals)

    quarter = width // 2
    halves = [
        [slice((2 * o + part) * width, (2 * o + part + 1) * width) for o in range(chips)]
        for part in range(2)
    ]
    zero = jnp.zeros((CHUNKS, width), F32)
    firsts = [
        conv_steps(0, CONV - 1, ranges, tuple((zero,) * (CONV + 1) for _ in ranges))
        for ranges in halves
    ]
    for k in range(CONV - 1):
        r.spill[k : k + 1, :] = r.dext[k * CHUNKS : k * CHUNKS + 1, :]
    behind = lax.rem(me + spans - 1, spans)
    spill = copy(r.spill, r.spill_in, r.spill_sem, (), at_seq(behind))

    @pl.when(me > 0)
    def _():
        spill.start()

    chunk = lax.broadcasted_iota(jnp.int32, (CHUNKS, width), 0)
    dxin = []
    for part, ranges in enumerate(halves):
        totals = conv_steps(CONV - 1, steps, ranges, firsts[part])
        if part:
            far_send(4)
            run(((outer_back, 2),))
        else:

            @pl.when(me > 0)
            def _():
                spill.wait_send()

            @pl.when(me < spans - 1)
            def _():
                spill.wait_recv()

        for o, lanes in enumerate(ranges):
            for k in range(CONV):
                r.small[TAPS + k : TAPS + k + 1, lanes] = jnp.sum(
                    totals[o][k], axis=0, keepdims=True
                )
            r.small[BIAS : BIAS + 1, lanes] = jnp.sum(totals[o][CONV], axis=0, keepdims=True)
            for k in range(CONV - 1):
                block = r.dext[k * CHUNKS : (k + 1) * CHUNKS, lanes]
                edge = (steps - CONV + 1 + k) * CHUNKS + EDGE
                moved = pltpu.roll(block, CHUNKS - 1, 0)
                came = jnp.broadcast_to(r.spill_in[k : k + 1, lanes], (CHUNKS, width))
                r.dext[edge : edge + CHUNKS, lanes] += jnp.where(
                    chunk < CHUNKS - 1, moved, came
                )
            piece = r.dext[EDGE:, lanes].astype(BF16)
            dxin.append(piece)
            grad = dot_tn(xn1, piece)
            for parity_at in range(2):
                put(4 + part, 2 * o + parity_at, grad[:, parity_at * quarter : (parity_at + 1) * quarter])
        near_send(4 + part)
    run(((inner_back, 3), (inner_back, 2)))
    wide = 2 * width
    dxn1 = jnp.zeros((rows, D), F32)
    for s in range(shards):
        if s < chips:
            piece = jnp.concatenate([dxin[s], dxin[chips + s]], axis=1)
        else:
            at = (s - chips) * wide
            piece = r.dzgate[:, at : at + wide]
        dxn1 = dxn1 + dot_nt(piece, r.wi_all[s])
    mixer_gain = jnp.sum(dxn1 * normal_one, axis=0, keepdims=True)
    for s in range(shards):
        at = s * width
        gains = slice(s * short, (s + 1) * short)
        r.small[GAINS : GAINS + 1, at : at + short] = mixer_gain[:, gains]
        r.small[GAINS : GAINS + 1, at + short : at + 2 * short] = attention_gain[:, gains]
    for s in range(shards):
        put(SMALL, s, r.small[:, s * width : (s + 1) * width])
    near_send(SMALL)
    far_send(5)
    far_send(SMALL)
    part_send(4)
    e1 = dxn1 * gain_one
    dx = r.dx1[...] + inverse_one * (
        e1 - normal_one * jnp.mean(e1 * normal_one, axis=-1, keepdims=True)
    )
    r.dx1[...] = dx
    for part in range(D // LANES):
        lanes = slice(part * LANES, (part + 1) * LANES)
        for step in range(steps):
            r.row[pl.ds(step, CHUNKS, stride=steps), :] = r.dx1[
                step * CHUNKS : (step + 1) * CHUNKS, lanes
            ]
        r.token_grad[:, lanes] = r.row[...]
    part_send(5)
    part_send(SMALL)
    for k in (0, 1, 2, 3):
        finish(k)
    last_send(4)
    last_send(5)
    last_send(SMALL)
    for by in range(1, spans):
        given_copy(by).wait()
    for t in range(blocks):
        i = t * ratio + sub
        by = lax.rem(i - me + spans, spans)

        @pl.when(i != me)
        def _():
            context_copy(t, by, i).wait_send()

    finish(SMALL)
    finish(4)
    finish(5)


def final_kernel(*refs):
    r = Refs(tuple(k + "_in" for k in BACKWARD_OUT) + FINAL_OUT, refs)

    def whole(source):
        return jnp.concatenate([source[j].astype(F32) for j in range(source.shape[0])], axis=0)

    r.output[...] = r.output_in[...]
    r.token_grad[...] = r.token_grad_in[...]
    r.heads_grad[...] = whole(r.last_heads_in)
    r.output_grad[...] = whole(r.last_out_in)
    r.merge_grad[...] = whole(r.last_merge_in)
    small = whole(r.last_small_in)
    short = r.mixer_grad.shape[1]
    width = r.taps_grad.shape[1]
    r.select_grad[...] = small[SEL : SEL + STEP]
    r.stepw_grad[...] = small[STEP : STEP + RANK]
    r.decay_grad[...] = small[DEC : DEC + STATE]
    r.taps_grad[...] = small[TAPS : TAPS + CONV]
    r.bias_grad[...] = small[BIAS : BIAS + 1]
    r.stepb_grad[...] = small[STEPB : STEPB + 1]
    r.skip_grad[...] = small[SKIP : SKIP + 1]
    r.mixer_grad[...] = small[GAINS : GAINS + 1, :short]
    r.attention_grad[...] = small[GAINS : GAINS + 1, short:]
    late = jnp.concatenate([whole(r.pair_in_in.at[at]) for at in range(2)], axis=1)
    early = jnp.concatenate(
        [whole(source.at[at]) for source in (r.early_in_in, r.other_in_in) for at in range(2)], axis=1
    )
    inner_half = lax.axis_index("shard") < lax.axis_size("shard") // 2
    r.input_grad[...] = jnp.where(inner_half, early, late)


def shape(*dims, kind=F32):
    return jax.ShapeDtypeStruct(dims, kind)


def vmem(*dims, kind=F32):
    return pltpu.VMEM(dims, kind)


def per_device(
    tokens,
    cotangent,
    positions,
    lengths,
    mixer_gain,
    input_weight,
    kernel_weight,
    kernel_bias,
    select_weight,
    step_weight,
    step_bias,
    decay_log,
    skip_scale,
    output_weight,
    attention_gain,
    heads_weight,
    merge_weight,
):
    spans = lax.axis_size("seq")
    shards = lax.axis_size("shard")
    rows = tokens.shape[1]
    steps = rows // CHUNKS
    share = rows // spans
    nseq = lengths.shape[1]
    ratio = spans // HEADS
    part = rows // ratio
    width = DI // shards

    index = positions
    dma = pltpu.SemaphoreType.DMA
    spread = [vmem(STATE, DI), vmem(STATE * CHUNKS, DI)]
    columns = vmem(rows, STATE * LANES)
    plane = vmem(rows, DI)
    gain_len = D // shards
    halves = GROUPS_CH // 2
    weights = [(D, 2 * width), (width, D), (D, 3 * D // shards), (gain_len, D)]
    half = rows // 2
    blocks = spans // ratio
    slots = 2 if ratio == 1 else 1
    kept = (
        [shape(rows, D)]
        + [shape(shards, *w, kind=BF16) for w in weights]
        + [
            shape(PACK, DI, kind=BF16),
            shape(CHUNKS, D),
            shape(spans, GROUPS_CH, LANES),
            shape(EDGE + rows, DI),
            shape(rows, DI),
            shape(rows, DI),
            shape(rows, DI, kind=BF16),
            shape(rows, DI),
            shape(rows, STEP),
            shape(CHUNKS, DI),
            shape(rows, DI),
            shape(rows, DI, kind=BF16),
            shape(rows, D),
            shape(STATE, CHUNKS, DI),
            shape(rows, D, kind=BF16),
            shape(rows, STATE * LANES),
            shape(rows, STATE * LANES),
            shape(rows, DI),
            shape(rows, DI),
            shape(blocks, half, LANES, kind=BF16),
        ]
    )
    back = [shape(HEADS, half, LANES, kind=BF16), shape(spans, rows, LANES, kind=BF16)]
    inputs = [
        lengths[0],
        tokens[0],
        cotangent[0].reshape(spans, share, D),
        index,
        mixer_gain[None],
        attention_gain[None],
        select_weight.T,
        step_weight,
        decay_log.T,
        kernel_weight,
        kernel_bias[None],
        step_bias[None],
        skip_scale[None],
        input_weight,
        output_weight,
        heads_weight,
        merge_weight,
    ]
    outs = pl.pallas_call(
        functools.partial(forward_kernel, steps, nseq, shards, spans),
        out_shape=kept + back,
        in_specs=[SMEM] + [VMEM] * (len(inputs) - 1),
        out_specs=[pl.BlockSpec(memory_space=pl.ANY)] * len(kept) + [VMEM] * len(back),
        scratch_shapes=[vmem(*k.shape, kind=k.dtype) for k in kept]
        + [
            vmem(spans, share, D, kind=BF16),
            vmem(spans, halves, STATE, 2 * LANES, kind=BF16),
            vmem(STATE, CHUNKS, DI),
            vmem(rows, LANES),
            vmem(PACK, width),
        ]
        + [vmem(*w, kind=BF16) for w in weights]
        + [
            vmem(PACK, width, kind=BF16),
            vmem(2 * CHUNKS, gain_len, kind=BF16),
            vmem(shards, PACK, width, kind=BF16),
            vmem(shards, 2 * CHUNKS, gain_len, kind=BF16),
            vmem(2 * CHUNKS, D, kind=BF16),
            vmem(halves, STATE, 2 * LANES, kind=BF16),
            vmem(GROUPS_CH, LANES),
        ]
        + spread
        + [
            vmem(HEADS, half, LANES, kind=BF16),
            vmem(HEADS, half, LANES, kind=BF16),
            vmem(HEADS, rows, LANES, kind=BF16),
            vmem(blocks, half, LANES, kind=BF16),
            vmem(blocks, half, LANES, kind=BF16),
            vmem(spans * rows, LANES, kind=BF16),
            vmem(spans, LANES, rows, kind=BF16),
            vmem(slots, spans, rows, rows),
            vmem(slots, spans, rows, rows),
            vmem(spans * rows, LANES),
            vmem(blocks, half, LANES, kind=BF16),
            vmem(spans, rows, LANES, kind=BF16),
            vmem(rows, rows),
            dma((2, 6, shards - 1)),
            dma((2, max(shards // 2 - 1, 1), spans)),
            dma((2, spans)),
            dma((2,)),
            dma((2, spans, halves)),
        ]
        + [dma((2, spans)), dma((2, spans, 2)), dma((2, spans)), dma((2, spans, 2))]
        + [dma((2, spans))] * 2
        + [dma((len(kept),))],
        compiler_params=params(collective_id=0, has_side_effects=True),
        name="forward",
    )(*inputs)
    saved, back = outs[: len(kept)], outs[len(kept) :]
    parts = {
        "heads": (D // spans, 3 * D // shards),
        "out": (width // spans, D),
        "merge": (gain_len // spans, D),
        "late": (D // spans, width),
        "early": (D // spans, width // 2),
        "other": (D // spans, width // 2),
        "small": (PACK // spans, width),
    }
    chips = shards // 2
    sizes = [(spans, *parts[k]) for k in GRADS]
    count = len(GRADS)
    anyspace = pl.BlockSpec(memory_space=pl.ANY)
    summed = [
        shape(spans, share, D, kind=BF16),
        shape(rows, D),
        shape(spans, *parts["heads"], kind=BF16),
        shape(spans, *parts["out"], kind=BF16),
        shape(spans, *parts["merge"], kind=BF16),
        shape(spans, *parts["small"], kind=BF16),
        shape(2, spans, *parts["late"], kind=BF16),
        shape(2, spans, *parts["early"], kind=BF16),
        shape(2, spans, *parts["other"], kind=BF16),
    ]
    few = vmem(rows * STATE // 2, LANES)
    state = vmem(STATE, CHUNKS, DI)
    summed = pl.pallas_call(
        functools.partial(backward_kernel, steps, nseq, shards, spans),
        out_shape=summed,
        in_specs=[SMEM] + [VMEM] * 3 + [anyspace] * len(kept),
        out_specs=[VMEM] * len(summed),
        scratch_shapes=[vmem(*k.shape, kind=k.dtype) for k in kept]
        + [
            vmem(HEADS, half, LANES, kind=BF16),
            vmem(spans, share, D, kind=BF16),
            vmem(rows, D),
            plane,
            vmem(rows, DI, kind=BF16),
            state,
            vmem(halves, STATE, 2 * LANES, kind=BF16),
            vmem(spans, halves, STATE, 2 * LANES, kind=BF16),
            columns,
            columns,
            few,
            few,
            few,
            plane,
            plane,
            state,
            vmem(rows, STEP),
            vmem(EDGE + rows, DI),
            vmem(CHUNKS, DI),
            vmem(CHUNKS, DI),
            vmem(PACK, DI),
            vmem(rows, LANES),
        ]
        + spread
        + [
            vmem(*parts["late"], kind=BF16),
            vmem(*parts["early"], kind=BF16),
            vmem(*parts["other"], kind=BF16),
        ]
        + [vmem(shards, *k, kind=BF16) for k in sizes]
        + [vmem(chips, *k, kind=BF16) for k in sizes] * 2
        + [vmem(max(chips - 1, 1), *k, kind=BF16) for k in sizes]
        + [vmem(spans + OUTER - 1, *k[1:], kind=BF16) for k in sizes]
        + [
            dma((len(kept),)),
            dma((2, spans)),
            dma((2, spans)),
            dma((2, spans, halves)),
            dma((2,)),
            dma((2, count, chips)),
            dma((2, count, chips)),
            dma((2, count, spans)),
            dma((2, count, spans)),
            dma((2, 2, 2, spans)),
            dma((2, 4, 2, spans // OUTER)),
            dma((2, 4, 2, OUTER)),
            dma((2, 2, OUTER)),
            dma((2, 2, spans // OUTER)),
        ],
        compiler_params=params(collective_id=1, has_side_effects=True),
        name="backward",
    )(lengths[0], index, *back, *saved)
    results = pl.pallas_call(
        final_kernel,
        out_shape=[
            shape(rows, D, kind=BF16),
            shape(rows, D),
            shape(1, gain_len),
            shape(D, 2 * width),
            shape(CONV, width),
            shape(1, width),
            shape(STEP, width),
            shape(RANK, width),
            shape(1, width),
            shape(STATE, width),
            shape(1, width),
            shape(width, D),
            shape(1, gain_len),
            shape(D, 3 * D // shards),
            shape(gain_len, D),
        ],
        in_specs=[VMEM] * len(summed),
        out_specs=[VMEM] * len(FINAL_OUT),
        compiler_params=params(),
        name="final",
    )(summed[0].reshape(rows, D), *summed[1:])
    flat, turned = {2, 5, 8, 10, 12}, {6, 9}
    return tuple(
        v[None] if i < 2 else v.reshape(-1) if i in flat else v.T if i in turned else v
        for i, v in enumerate(results)
    )


def solution(mesh):
    return jax.shard_map(
        per_device,
        mesh=mesh,
        in_specs=(
            P("shard", "seq", None),
            P("shard", "seq", None),
            P("shard", None),
            P("shard", None),
            P("shard"),
            P(None, "shard"),
            P(None, "shard"),
            P("shard"),
            P("shard", None),
            P(None, "shard"),
            P("shard"),
            P("shard", None),
            P("shard"),
            P("shard", None),
            P("shard"),
            P(None, "shard"),
            P("shard", None),
        ),
        out_specs=(
            P("shard", "seq", None),
            P("shard", "seq", None),
            P("shard"),
            P(None, "shard"),
            P(None, "shard"),
            P("shard"),
            P("shard", None),
            P(None, "shard"),
            P("shard"),
            P("shard", None),
            P("shard"),
            P("shard", None),
            P("shard"),
            P(None, "shard"),
            P("shard", None),
        ),
        check_vma=False,
    )
```

```python
import functools
import math
from typing import Any, NamedTuple

import jax
import jax.numpy as jnp
from jax import lax
from jax.experimental import pallas as pl
from jax.experimental.pallas import tpu as pltpu
from jax.sharding import PartitionSpec as P

D = 512
DI = 1024
RANK = 32
HEADS = 8
STATE = 16
HEAD_DIM = 64
CONV = 4
CHUNKS = 8
LANES = 128
GROUPS_CH = DI // LANES
EDGE = (CONV - 1) * CHUNKS
OUTER = 4

SEL = 0
STEP = RANK + 2 * STATE
DEC = STEP + RANK
TAPS = DEC + STATE
BIAS = TAPS + CONV
STEPB = BIAS + 1
SKIP = STEPB + 1
GAINS = SKIP + 1
PACK = 128

EPS = 1e-05
NEG = -1e30
CUT = 1e30
F32 = jnp.float32
BF16 = jnp.bfloat16

VMEM = pl.BlockSpec(memory_space=pltpu.VMEM)
SMEM = pl.BlockSpec(memory_space=pltpu.SMEM)


def params(**more):
    return pltpu.CompilerParams(vmem_limit_bytes=62 << 20, **more)


def dot_nn(left, right):
    return lax.dot_general(left, right, (((1,), (0,)), ((), ())), preferred_element_type=F32)


def dot_nt(left, right):
    return lax.dot_general(left, right, (((1,), (1,)), ((), ())), preferred_element_type=F32)


def dot_tn(left, right):
    return lax.dot_general(left, right, (((0,), (0,)), ((), ())), preferred_element_type=F32)


def row_places(rows, steps):
    return (rows & (CHUNKS - 1)) * steps + (rows >> 3)


def starts_of(lengths_ref, nseq):
    starts = [jnp.int32(0)]
    for k in range(nseq - 1):
        starts.append(starts[-1] + lengths_ref[k])
    return starts


def start_of(places, starts):
    first = jnp.zeros_like(places)
    for start in starts[1:]:
        first = jnp.where(places >= start, start, first)
    return first


def begin_of(places, starts):
    found = places == starts[0]
    for start in starts[1:]:
        found = found | (places == start)
    return found


def norm(value):
    return lax.rsqrt(jnp.mean(value * value, axis=-1, keepdims=True) + EPS)


def silu_slope(value):
    s = jax.nn.sigmoid(value)
    return s * (1.0 + value * (1.0 - s))


def tile(step):
    return pl.ds(pl.multiple_of(step * CHUNKS, CHUNKS), CHUNKS)


def lanes_of(group):
    return pl.ds(pl.multiple_of(group * LANES, LANES), LANES)


def spread_decay(packed_ref, amat_ref, spread_ref):
    amat = -jnp.exp(packed_ref[DEC : DEC + STATE, :].astype(F32)) * math.log2(math.e)
    amat_ref[...] = amat
    for st in range(STATE):
        spread_ref[st * CHUNKS : (st + 1) * CHUNKS, :] = jnp.broadcast_to(
            amat[st : st + 1, :], (CHUNKS, DI)
        )


def column(st):
    return slice(st * LANES, (st + 1) * LANES)


def thirds(value):
    high = value.astype(BF16)
    rest = value - high.astype(F32)
    middle = rest.astype(BF16)
    return high, middle, (rest - middle.astype(F32)).astype(BF16)


def spread_columns(values):
    terms = jnp.concatenate([t.astype(F32) for t in thirds(values)], axis=1).astype(BF16)
    count = terms.shape[1]
    line = lax.broadcasted_iota(jnp.int32, (count, STATE * LANES), 0)
    lane = lax.broadcasted_iota(jnp.int32, (count, STATE * LANES), 1)
    chosen = (line & (STATE - 1)) == lax.div(lane, LANES)
    return dot_nn(terms, chosen.astype(F32).astype(BF16))


def gather_columns(value):
    line = lax.broadcasted_iota(jnp.int32, (STATE * LANES, STATE), 0)
    lane = lax.broadcasted_iota(jnp.int32, (STATE * LANES, STATE), 1)
    chosen = (lax.div(line, LANES) == lane).astype(F32).astype(BF16)
    return sum(dot_nn(term, chosen) for term in thirds(value)[:2])


def at_seq(index):
    return {"device_id": {"seq": index}, "device_id_type": pl.DeviceIdType.MESH}


def at_shard(index):
    return {"device_id": {"shard": index}, "device_id_type": pl.DeviceIdType.MESH}


def greet(peers):
    barrier = pltpu.get_barrier_semaphore()
    for peer in peers:
        pl.semaphore_signal(barrier, inc=1, **peer)
    pl.semaphore_wait(barrier, len(peers))


def shard_peers(shards):
    shard = lax.axis_index("shard")
    core, chip = lax.rem(shard, 2), lax.div(shard, 2)
    partner = chip * 2 + 1 - core
    others = [lax.rem(chip + by, shards // 2) * 2 + core for by in range(1, shards // 2)]
    return shard, core, chip, partner, others


class Refs:
    def __init__(self, names, refs):
        for name, ref in zip(names, refs, strict=True):
            setattr(self, name, ref)


class ForwardIn(NamedTuple):
    lengths: Any
    tokens: Any
    cot: Any
    index: Any
    mixer: Any
    attention: Any
    select: Any
    stepw: Any
    decay: Any
    taps: Any
    bias: Any
    stepb: Any
    skip: Any
    wi_arg: Any
    wo_arg: Any
    wh_arg: Any
    wm_arg: Any


FORWARD_IN = ForwardIn._fields
class Kept(NamedTuple):
    x: Any
    wi_all: Any
    wo_all: Any
    wh_all: Any
    wm_all: Any
    packed: Any
    gains: Any
    span_totals: Any
    ext: Any
    zgate: Any
    conv: Any
    u: Any
    delta: Any
    xdbl: Any
    totals: Any
    yfull: Any
    gated: Any
    x1: Any
    init: Any
    dout: Any
    bx: Any
    cx: Any
    cut: Any
    du: Any
    context_send: Any


KEPT = Kept._fields
FORWARD_OUT = tuple(k + "_out" for k in KEPT) + ("dq_in", "dkv_in")
class ForwardScratch(NamedTuple):
    given: Any
    states: Any
    ends: Any
    row: Any
    small: Any
    wi_send: Any
    wo_send: Any
    wh_send: Any
    wm_send: Any
    packed_send: Any
    gains_send: Any
    packed_all: Any
    gains_all: Any
    before: Any
    state_send: Any
    total_send: Any
    amat: Any
    spread: Any
    q_send: Any
    d_send: Any
    kv_send: Any
    q_in: Any
    d_in: Any
    kv_in: Any
    kvt: Any
    score: Any
    dprob: Any
    dkv: Any
    dq_send: Any
    dkv_send: Any
    causal: Any
    gather_sem: Any
    share_sem: Any
    cot_sem: Any
    edge_sem: Any
    state_sem: Any
    total_sem: Any
    q_sem: Any
    d_sem: Any
    kv_sem: Any
    dq_sem: Any
    dkv_sem: Any
    keep_sem: Any
    wi: Any
    wo: Any
    wh: Any
    wm: Any
    arg_sem: Any


FORWARD_SCRATCH = KEPT + ForwardScratch._fields


def forward_kernel(steps, nseq, shards, spans, *refs):
    r = Refs(FORWARD_IN + FORWARD_OUT + FORWARD_SCRATCH, refs)
    rows = steps * CHUNKS
    width = DI // shards
    me = lax.axis_index("seq")
    shard, core, chip, partner, others = shard_peers(shards)
    far = len(others)
    ring = [lax.rem(me + by, spans) for by in range(1, spans)]
    arguments = [
        pltpu.make_async_copy(source, target, r.arg_sem.at[i])
        for i, (source, target) in enumerate(
            ((r.wi_arg, r.wi), (r.wo_arg, r.wo), (r.wh_arg, r.wh), (r.wm_arg, r.wm))
        )
    ]
    for argument in arguments:
        argument.start()
    greet([at_shard(partner)] + [at_shard(o) for o in others] + [at_seq(to) for to in ring])

    def copy(source, target, sems, at, to):
        return pltpu.make_async_remote_copy(
            src_ref=source, dst_ref=target, send_sem=sems.at[(0, *at)], recv_sem=sems.at[(1, *at)], **to
        )

    sources = (r.wi_send, r.packed_send, r.gains_send, r.wo_send, r.wh_send, r.wm_send)
    wholes = (r.wi_all, r.packed_all, r.gains_all, r.wo_all, r.wh_all, r.wm_all)

    share = D // 2 // spans
    straight = D - share * spans

    def own_share(index):
        return pl.ds(pl.multiple_of(straight + index * share, share), share)

    def sent(k, i):
        if i == far:
            return copy(sources[k], wholes[k].at[shard], r.gather_sem, (k, i), at_shard(partner))
        source, target = sources[k], wholes[k].at[shard]
        if k == 0:
            source, target = source.at[0:straight], wholes[k].at[shard, 0:straight]
        return copy(source, target, r.gather_sem, (k, i), at_shard(others[i]))

    def shared(i):
        return copy(
            r.wi_send.at[own_share(me)],
            r.wi_all.at[shard, own_share(me)],
            r.share_sem,
            (i, 0),
            at_shard(others[i]),
        )

    def fanned(i, by):
        came = lax.rem(chip + far - i, far + 1) * 2 + core
        held = r.wi_all.at[came, own_share(me)]
        return copy(held, held, r.share_sem, (i, by), at_seq(ring[by - 1]))

    def passed(k, i):
        came = lax.rem(chip + far - i, far + 1) * 2 + core
        return copy(
            wholes[k].at[came], wholes[k].at[came], r.gather_sem, (k, far + 1 + i), at_shard(partner)
        )

    def spread(*which):
        for k in which:
            for i in range(far + 1):
                sent(k, i).start()
        for k in which:
            wholes[k][shard] = sources[k][...]

    def pass_on(*which):
        for i in range(far):
            for k in which:
                sent(k, i).wait_recv()
                passed(k, i).start()

    def finish(*which):
        for k in which:
            for i in range(far):
                sent(k, i).wait_send()
                passed(k, i).wait()
            sent(k, far).wait()

    arguments[0].wait()
    r.wi_send[...] = r.wi[...].astype(BF16)
    r.small[...] = jnp.zeros_like(r.small)
    for source, first in (
        (r.select, SEL),
        (r.decay, DEC),
        (r.stepw, STEP),
        (r.taps, TAPS),
        (r.bias, BIAS),
        (r.stepb, STEPB),
        (r.skip, SKIP),
    ):
        r.small[first : first + source.shape[0], :] = source[...]
    r.packed_send[...] = r.small[...].astype(BF16)
    lane = lax.broadcasted_iota(jnp.int32, (2 * CHUNKS, D // shards), 0)
    r.gains_send[...] = jnp.where(lane == 0, r.mixer[...], r.attention[...]).astype(BF16)
    for i in range(far):
        shared(i).start()
    spread(0, 1, 2)
    last = r.tokens.at[pl.ds(rows - 2 * CHUNKS, 2 * CHUNKS)]
    edge = copy(last, r.before, r.edge_sem, (), at_seq(ring[0]))
    edge.start()

    def cot_copy(by):
        return copy(
            r.cot.at[ring[by - 1]], r.given.at[me], r.cot_sem, (by,), at_seq(ring[by - 1])
        )

    for i in range(far):
        shared(i).wait_recv()
        for by in range(1, spans):
            fanned(i, by).start()
    for argument in arguments[1:]:
        argument.wait()
    r.wo_send[...] = r.wo[...].astype(BF16)
    r.wh_send[...] = r.wh[...].astype(BF16)
    r.wm_send[...] = r.wm[...].astype(BF16)
    for part in range(D // LANES):
        lanes = slice(part * LANES, (part + 1) * LANES)
        r.row[...] = r.tokens[:, lanes].astype(F32)
        for step in range(steps):
            r.x[step * CHUNKS : (step + 1) * CHUNKS, lanes] = r.row[
                pl.ds(step, CHUNKS, stride=steps), :
            ]
    for i in range(far):
        shared(i).wait_send()
        for by in range(1, spans):
            fanned(i, by).wait()
    pass_on(0, 1, 2)
    for by in range(1, spans):
        cot_copy(by).start()
    r.given[me] = r.cot[me]
    spread(5, 3, 4)
    finish(0, 1, 2)
    edge.wait()

    starts = starts_of(r.lengths, nseq)
    r.packed[...] = jnp.concatenate([r.packed_all[s] for s in range(shards)], axis=1)
    gains = jnp.concatenate([r.gains_all[s].astype(F32) for s in range(shards)], axis=1)
    r.gains[...] = gains[:CHUNKS]
    gain = gains[0:1]
    x = r.x[...]
    xn1 = (x * norm(x) * gain).astype(BF16)
    before = r.before[...].astype(F32)
    edge_n = (before * norm(before) * gain).astype(BF16)
    wide = 2 * DI // shards
    for s in range(shards):
        piece = dot_nn(xn1, r.wi_all[s])
        if s < shards // 2:
            r.ext[EDGE:, s * wide : (s + 1) * wide] = piece
        else:
            at = (s - shards // 2) * wide
            r.zgate[:, at : at + wide] = piece
    edge_x = jnp.concatenate([dot_nn(edge_n, r.wi_all[s]) for s in range(shards // 2)], axis=1)
    count = r.before.shape[0]
    chunk = lax.broadcasted_iota(jnp.int32, (CHUNKS, DI), 0)
    for k in range(CONV - 1):
        late = (steps - CONV + 1 + k) * CHUNKS + EDGE
        moved = pltpu.roll(r.ext[late : late + CHUNKS, :], 1, 0)
        at = count - CONV + 1 + k
        r.ext[k * CHUNKS : (k + 1) * CHUNKS, :] = jnp.where(
            chunk == 0, jnp.broadcast_to(edge_x[at : at + 1, :], (CHUNKS, DI)), moved
        )
    small = r.packed[DEC:PACK, :].astype(F32)
    taps = small[TAPS - DEC : TAPS - DEC + CONV, :]
    bias = small[BIAS - DEC : BIAS - DEC + 1, :]

    def conv_step(step, carry):
        places = lax.broadcasted_iota(jnp.int32, (CHUNKS, 1), 0) * steps + step + me * rows
        first = start_of(places, starts)
        total = jnp.broadcast_to(bias, (CHUNKS, DI))
        for k in range(CONV):
            at = pl.ds(pl.multiple_of((step + k) * CHUNKS, CHUNKS), CHUNKS)
            inside = places - (CONV - 1) + k >= first
            total = total + jnp.where(inside, taps[k : k + 1, :] * r.ext[at, :], 0.0)
        r.conv[tile(step), :] = total
        r.du[tile(step), :] = total * jax.nn.sigmoid(total)
        return carry

    lax.fori_loop(0, steps, conv_step, 0, unroll=2)
    u = r.du[...].astype(BF16)
    r.u[...] = u
    xdbl = dot_nt(u, r.packed[SEL : SEL + STEP, :])
    r.xdbl[...] = xdbl
    r.delta[...] = dot_nn(
        xdbl[:, :RANK].astype(BF16), r.packed[STEP : STEP + RANK, :]
    )
    stepb = small[STEPB - DEC : STEPB - DEC + 1, :]

    def delta_step(step, total):
        places = lax.broadcasted_iota(jnp.int32, (CHUNKS, 1), 0) * steps + step + me * rows
        pre = r.delta[tile(step), :] + stepb
        delta = jnp.maximum(pre, 0.0) + jnp.log(1.0 + jnp.exp(-jnp.abs(pre)))
        r.delta[tile(step), :] = delta
        cut = jnp.where(begin_of(places, starts), CUT, delta)
        r.cut[tile(step), :] = cut
        r.du[tile(step), :] = delta * r.du[tile(step), :].astype(BF16).astype(F32)
        return total + cut

    totals = lax.fori_loop(0, steps, delta_step, jnp.zeros((CHUNKS, DI), F32), unroll=2)
    r.totals[...] = totals
    total = jnp.sum(totals, axis=0, keepdims=True)
    for group in range(GROUPS_CH):
        r.total_send[group : group + 1, :] = total[:, group * LANES : (group + 1) * LANES]
    r.span_totals[me] = r.total_send[...]

    def total_copy(by):
        return copy(
            r.total_send, r.span_totals.at[me], r.total_sem, (by,), at_seq(ring[by - 1])
        )

    for by in range(1, spans):
        total_copy(by).start()
    pass_on(5)
    spread_decay(r.packed, r.amat, r.spread)
    r.bx[...] = spread_columns(xdbl[:, RANK : RANK + STATE])

    def state_copy(by, at):
        return copy(
            r.state_send.at[at], r.states.at[me, at], r.state_sem, (by, at), at_seq(ring[by - 1])
        )

    def pair_step(pair, carry):
        for odd in range(2):
            lanes = lanes_of(pair * 2 + odd)
            amat = [r.spread[st * CHUNKS : (st + 1) * CHUNKS, lanes] for st in range(STATE)]

            def step_fn(step, states):
                cut = r.cut[tile(step), lanes]
                drive = r.du[tile(step), lanes]
                return tuple(
                    jnp.exp2(cut * amat[st]) * states[st] + drive * r.bx[tile(step), column(st)]
                    for st in range(STATE)
                )

            states = lax.fori_loop(
                0, steps, step_fn, (jnp.zeros((CHUNKS, LANES), F32),) * STATE, unroll=8
            )
            for st in range(STATE):
                r.ends[st, :, lanes] = states[st]
        lanes = pl.ds(pl.multiple_of(pair * 2 * LANES, 2 * LANES), 2 * LANES)
        amat = r.amat[:, lanes]
        state = jnp.zeros((STATE, 2 * LANES), F32)
        for k in range(CHUNKS):
            state = jnp.exp2(amat * r.totals[k : k + 1, lanes]) * state + r.ends[:, k, lanes]
        r.state_send[pair] = state.astype(BF16)
        for by in range(1, spans):

            @pl.when(me + by < spans)
            def _():
                state_copy(by, pair).start()

        return carry

    lax.fori_loop(0, GROUPS_CH // 2, pair_step, 0)
    pass_on(3)
    for by in range(1, spans):
        cot_copy(by).wait()
    finish(5)

    ratio = spans // HEADS
    sub = lax.rem(me, ratio)
    head = lax.div(me, ratio)
    half = rows // 2
    given = jnp.concatenate([r.given[j] for j in range(spans)], axis=0)
    dout = dot_nn(pick_rows(r.index, me, rows, steps), given).astype(BF16)
    r.dout[...] = dout
    merge = jnp.concatenate([r.wm_all[s] for s in range(shards)], axis=0)
    dcontext = dot_nt(dout, merge).astype(BF16).astype(F32)
    low = lane_low(half)

    quarter = half // 2
    quarter_low = lane_low(quarter)

    def packs(pair, target, first, part):
        above, below = pair[:quarter], pair[quarter:]
        at = slice(part * quarter, (part + 1) * quarter)
        even = jnp.where(quarter_low, above, pltpu.roll(below, HEAD_DIM, 1))
        odd = jnp.where(quarter_low, pltpu.roll(above, HEAD_DIM, 1), below)
        target[first, at] = even.astype(BF16)
        target[first + 1, at] = odd.astype(BF16)

    def half_rows(part):
        return slice(part * half, (part + 1) * half)

    for pair in range(HEADS // 2):
        for part in range(2):
            packs(dcontext[half_rows(part), pair * LANES : (pair + 1) * LANES], r.d_send, 2 * pair, part)

    def d_copy(by):
        to = ring[by - 1]
        slot = lax.div(me, ratio)
        return copy(r.d_send.at[lax.div(to, ratio)], r.d_in.at[slot], r.d_sem, (by,), at_seq(to))

    def q_copy(by, part):
        to = ring[by - 1]
        at = pl.ds(part * quarter, quarter)
        source, target = r.q_send.at[lax.div(to, ratio), at], r.q_in.at[lax.div(me, ratio), at]
        return copy(source, target, r.q_sem, (by, part), at_seq(to))

    def kv_copy(by, part):
        to = ring[by - 1]
        return copy(
            r.kv_send.at[lax.div(to, ratio), pl.ds(part * half, half)],
            r.kv_in.at[pl.ds(pl.multiple_of(me * rows + part * half, half), half)],
            r.kv_sem,
            (by, part),
            at_seq(to),
        )

    def to_rows(made, act):
        for by in range(1, spans):
            if ratio == 1:
                act(made(by))
            else:
                pl.when(lax.rem(by, ratio) == 0)(lambda: act(made(by)))

    to_rows(d_copy, lambda c: c.start())
    r.d_in[lax.div(me, ratio)] = r.d_send[head]
    r.cx[...] = spread_columns(xdbl[:, RANK + STATE :])
    for by in range(1, spans):
        total_copy(by).wait()
        for pair in range(GROUPS_CH // 2):

            @pl.when(me + by < spans)
            def _():
                state_copy(by, pair).wait_send()

            @pl.when(me - by >= 0)
            def _():
                state_copy(by, pair).wait_recv()

    amat = r.amat[...]

    def chain(k, state):
        decay = jnp.exp2(amat * total_row(r.span_totals[k]))
        came = jnp.concatenate(
            [r.states[k, g].astype(F32) for g in range(GROUPS_CH // 2)], axis=1
        )
        return decay * state + came

    state = lax.fori_loop(0, me, chain, jnp.zeros((STATE, DI), F32))
    for k in range(CHUNKS):
        r.init[:, k, :] = state
        if k < CHUNKS - 1:
            state = jnp.exp2(amat * r.totals[k : k + 1, :]) * state + r.ends[:, k, :]

    skip = small[SKIP - DEC : SKIP - DEC + 1, :]
    wo = None
    scale = 1.0 / math.sqrt(HEAD_DIM)

    for part in range(2):
        entering, leaving = (r.init, r.ends) if part == 0 else (r.ends, None)

        def group_step(group, carry):
            lanes = lanes_of(group)
            amat_g = [r.spread[st * CHUNKS : (st + 1) * CHUNKS, lanes] for st in range(STATE)]

            def step_fn(step, states):
                cut = r.cut[tile(step), lanes]
                drive = r.du[tile(step), lanes]
                new = tuple(
                    jnp.exp2(cut * amat_g[st]) * states[st] + drive * r.bx[tile(step), column(st)]
                    for st in range(STATE)
                )
                terms = [new[st] * r.cx[tile(step), column(st)] for st in range(STATE)]
                while len(terms) > 1:
                    terms = [a + b for a, b in zip(terms[::2], terms[1::2])]
                r.yfull[tile(step), lanes] = terms[0]
                return new

            states = lax.fori_loop(
                part * steps // 2,
                (part + 1) * steps // 2,
                step_fn,
                tuple(entering[st, :, lanes] for st in range(STATE)),
                unroll=8,
            )
            if leaving is not None:
                for st in range(STATE):
                    leaving[st, :, lanes] = states[st]
            return carry

        lax.fori_loop(0, GROUPS_CH, group_step, 0)

        def gate_step(pair, carry):
            at = pl.ds(pl.multiple_of(pair * 2 * CHUNKS, 2 * CHUNKS), 2 * CHUNKS)
            yfull = r.yfull[at, :] + skip * r.u[at, :].astype(F32)
            r.yfull[at, :] = yfull
            gate = r.zgate[at, :]
            r.gated[at, :] = (yfull * (gate * jax.nn.sigmoid(gate))).astype(BF16)
            return carry

        lax.fori_loop(part * steps // 4, (part + 1) * steps // 4, gate_step, 0)
        if part == 0:
            pass_on(4)
            finish(3)
            wo = jnp.concatenate([r.wo_all[s] for s in range(shards)], axis=0)
        ours = half_rows(part)
        x1 = r.x[ours, :] + dot_nn(r.gated[ours, :], wo)
        r.x1[ours, :] = x1
        xn2 = (x1 * norm(x1) * gains[1:2, :]).astype(BF16)
        if part == 0:
            finish(4)
        qkv = jnp.concatenate([dot_nn(xn2, r.wh_all[s]) for s in range(shards)], axis=1)
        qkv = qkv.astype(BF16).astype(F32)
        for pair in range(HEADS // 2):
            at = pair * LANES
            packs(qkv[:, at : at + LANES] * scale, r.q_send, 2 * pair, part)
            k = qkv[:, D + at : D + at + LANES]
            v = qkv[:, 2 * D + at : 2 * D + at + LANES]
            even = jnp.where(low, k, pltpu.roll(v, HEAD_DIM, 1))
            odd = jnp.where(low, pltpu.roll(k, HEAD_DIM, 1), v)
            r.kv_send[2 * pair, ours] = even.astype(BF16)
            r.kv_send[2 * pair + 1, ours] = odd.astype(BF16)
        to_rows(functools.partial(q_copy, part=part), lambda c: c.start())
        for by in range(1, spans):
            kv_copy(by, part).start()
    r.q_in[lax.div(me, ratio)] = r.q_send[head]
    r.kv_in[pl.ds(pl.multiple_of(me * rows, rows), rows), :] = r.kv_send[head]
    keeps = [
        pltpu.make_async_copy(getattr(r, name), getattr(r, name + "_out"), r.keep_sem.at[i])
        for i, name in enumerate(KEPT)
    ]
    for keep in keeps[:-1]:
        keep.start()
    at = lax.broadcasted_iota(jnp.int32, (1, rows), 1)
    turn_at = lax.rem(lax.div(at, quarter), 2) * half + lax.div(at, half) * quarter + lax.rem(at, quarter)
    query_local = row_places(turn_at, steps)
    key_local = row_places(lax.broadcasted_iota(jnp.int32, (rows, 1), 0), steps)
    r.causal[...] = jnp.where(key_local <= query_local, 0.0, NEG)
    r.dkv[...] = jnp.zeros_like(r.dkv)
    to_rows(d_copy, lambda c: c.wait())
    for part in range(2):
        to_rows(functools.partial(q_copy, part=part), lambda c: c.wait())
        for by in range(1, spans):
            kv_copy(by, part).wait()

    static = ratio == 1
    blocks = spans // ratio

    def each(count, fn, carry):
        if not static:
            return lax.fori_loop(0, count, fn, carry)
        for j in range(count):
            carry = fn(j, carry)
        return carry

    def key_rows(j):
        return pl.ds(j * rows if static else pl.multiple_of(j * rows, rows), rows)

    def turn(j, carry):
        r.kvt[j] = r.kv_in[key_rows(j), :].astype(F32).T.astype(BF16)
        return carry

    each(spans, turn, 0)
    folded = (rows // CHUNKS, CHUNKS, rows)

    def dq_copy(to, by, t):
        return copy(r.dq_send.at[t], r.dq_in.at[head], r.dq_sem, (by,), at_seq(to))

    def query_block(t, carry):
        i = t * ratio + sub
        slot = t % 2 if static else 0
        q = r.q_in[t].astype(F32)
        d = r.d_in[t].astype(F32)
        qt = q.T
        dt = d.T
        zero = jnp.zeros((HEAD_DIM, rows), F32)
        qt = jnp.concatenate([qt[:HEAD_DIM], qt[HEAD_DIM:]], axis=1)
        dt = jnp.concatenate([dt[:HEAD_DIM], dt[HEAD_DIM:]], axis=1)
        both = jnp.concatenate(
            [jnp.concatenate([qt, zero], axis=1), jnp.concatenate([zero, dt], axis=1)], axis=0
        ).astype(BF16)
        none = jnp.zeros((half, LANES), F32)
        natural = jnp.concatenate(
            [
                jnp.where(low, none, pltpu.roll(d, HEAD_DIM, 1)),
                jnp.where(low, none, d),
                jnp.where(low, q, none),
                jnp.where(low, pltpu.roll(q, HEAD_DIM, 1), none),
            ],
            axis=0,
        ).astype(BF16)
        first = start_of(query_local + i * rows, starts)

        def scores(j, top):
            joint = dot_nn(r.kv_in[key_rows(j), :], both)
            score = joint[:, :rows]
            if static:
                if j == t:
                    score = score + r.causal[...]
                if j in (0, t) or t == spans - 1:
                    score = jnp.where(key_local + j * rows >= first, score, NEG)
            else:
                query = query_local + i * rows
                key = key_local + j * rows
                score = jnp.where((key <= query) & (key >= first), score, NEG)
            r.score[slot, j] = score
            r.dprob[slot, j] = joint[:, rows:]
            return jnp.maximum(top, jnp.max(score.reshape(folded), axis=0))

        top = each(t + 1 if static else i + 1, scores, jnp.full((CHUNKS, rows), NEG, F32))
        top = jnp.max(top, axis=0, keepdims=True)

        def weigh(j, sums):
            total, dot = sums
            prob = jnp.exp(r.score[slot, j] - top)
            r.score[slot, j] = prob
            total = total + jnp.sum(prob.reshape(folded), axis=0)
            dot = dot + jnp.sum((prob * r.dprob[slot, j]).reshape(folded), axis=0)
            return total, dot

        zero = jnp.zeros((CHUNKS, rows), F32)
        total, dot = each(t + 1 if static else i + 1, weigh, (zero, zero))
        inverse = 1.0 / jnp.sum(total, axis=0, keepdims=True)
        datt = jnp.sum(dot, axis=0, keepdims=True) * inverse

        def back(j, sums):
            prob = r.score[slot, j] * inverse
            dscore = prob * (r.dprob[slot, j] - datt)
            joint = jnp.concatenate([prob.astype(BF16), dscore.astype(BF16)], axis=1)
            r.dkv[key_rows(j), :] += dot_nn(joint, natural)
            return sums + dot_nn(r.kvt[j], joint)

        sums = each(t + 1 if static else i + 1, back, jnp.zeros((LANES, 2 * rows), F32))
        dqt = sums[:HEAD_DIM, rows:] * scale
        ctx = sums[HEAD_DIM:, :rows]
        dqt = jnp.concatenate([dqt[:, :half], dqt[:, half:]], axis=0)
        ctx = jnp.concatenate([ctx[:, :half], ctx[:, half:]], axis=0)
        r.dq_send[t] = dqt.T.astype(BF16)
        r.context_send[t] = ctx.T.astype(BF16)
        by = lax.rem(i - me + spans, spans)

        @pl.when(i != me)
        def _():
            dq_copy(i, by, t).start()

        @pl.when(i == me)
        def _():
            r.dq_in[head] = r.dq_send[t]

        return carry

    if static:
        for t in range(blocks):
            query_block(t, 0)
    else:
        lax.fori_loop(0, blocks, query_block, 0)
    keeps[-1].start()

    def cast(j, carry):
        r.dkv_send[j] = r.dkv[key_rows(j), :].astype(BF16)
        return carry

    each(spans, cast, 0)

    def dkv_copy(by):
        to = ring[by - 1]
        return copy(r.dkv_send.at[to], r.dkv_in.at[me], r.dkv_sem, (by,), at_seq(to))

    for by in range(1, spans):
        dkv_copy(by).start()
    r.dkv_in[me] = r.dkv_send[me]
    for t in range(blocks):
        i = t * ratio + sub
        by = lax.rem(i - me + spans, spans)

        @pl.when(i != me)
        def _():
            dq_copy(i, by, t).wait_send()

    for h in range(HEADS):
        came = h * ratio + sub
        by = lax.rem(me - came + spans, spans)

        @pl.when(came != me)
        def _():
            dq_copy(came, by, 0).wait_recv()

    for by in range(1, spans):
        dkv_copy(by).wait()
    for keep in keeps:
        keep.wait()


def total_row(values):
    return jnp.concatenate([values[g : g + 1, :] for g in range(GROUPS_CH)], axis=1)


def lane_low(rows):
    return lax.broadcasted_iota(jnp.int32, (rows, LANES), 1) < HEAD_DIM


def pick_rows(table_ref, me, rows, steps):
    spans = table_ref.shape[1] // rows
    share = rows // spans
    lane = lax.broadcasted_iota(jnp.int32, (1, rows), 1)
    index = jnp.zeros((1, rows), F32)
    for j in range(spans):
        line = table_ref[:, j * rows : (j + 1) * rows].astype(F32)
        line = pltpu.roll(line, lax.rem((j + spans - me) * share, rows), 1)
        index = jnp.where(lane >= j * share, line, index)
    places = row_places(lax.broadcasted_iota(jnp.int32, (rows, 1), 0), steps) + me * rows
    return (index == places.astype(F32)).astype(F32).astype(BF16)


GRADS = ("heads", "out", "merge", "late", "early", "other", "small")
SMALL = 6
BACKWARD_IN = ("lengths", "index", "dq_in", "dkv_in") + tuple(k + "_kept" for k in KEPT)
class BackwardOut(NamedTuple):
    output: Any
    token_grad: Any
    last_heads: Any
    last_out: Any
    last_merge: Any
    last_small: Any
    pair_in: Any
    early_in: Any
    other_in: Any


BACKWARD_OUT = BackwardOut._fields
class FinalOut(NamedTuple):
    output: Any
    token_grad: Any
    mixer_grad: Any
    input_grad: Any
    taps_grad: Any
    bias_grad: Any
    select_grad: Any
    stepw_grad: Any
    stepb_grad: Any
    decay_grad: Any
    skip_grad: Any
    output_grad: Any
    attention_grad: Any
    heads_grad: Any
    merge_grad: Any


FINAL_OUT = FinalOut._fields
class BackwardScratch(NamedTuple):
    context: Any
    given: Any
    dx1: Any
    dys: Any
    dzgate: Any
    ends: Any
    grad_send: Any
    grads_in: Any
    db: Any
    dc: Any
    decay: Any
    held: Any
    state: Any
    bgrad: Any
    adelta: Any
    arrive: Any
    dxdbl: Any
    dext: Any
    spill: Any
    spill_in: Any
    small: Any
    row: Any
    amat: Any
    spread: Any
    sub_late: Any
    sub_early: Any
    sub_other: Any


class BackwardSems(NamedTuple):
    load_sem: Any
    context_sem: Any
    given_sem: Any
    state_sem: Any
    spill_sem: Any
    near_sem: Any
    far_sem: Any
    part_sem: Any
    last_sem: Any
    pair_sem: Any
    inner_sem: Any
    outer_sem: Any
    late_outer_sem: Any
    late_inner_sem: Any


BACKWARD_SCRATCH = (
    KEPT
    + BackwardScratch._fields
    + tuple(kind + name for kind in ("g_", "near_", "sum_", "far_", "part_") for name in GRADS)
    + BackwardSems._fields
)


def backward_kernel(steps, nseq, shards, spans, *refs):
    r = Refs(BACKWARD_IN + BACKWARD_OUT + BACKWARD_SCRATCH, refs)
    rows = steps * CHUNKS
    width = DI // shards
    me = lax.axis_index("seq")
    shard, core, chip, partner, others = shard_peers(shards)
    chips = shards // 2
    ring = [lax.rem(me + by, spans) for by in range(1, spans)]
    every = [me] + ring
    ratio = spans // HEADS
    sub = lax.rem(me, ratio)
    half = rows // 2
    blocks = spans // ratio
    starts = starts_of(r.lengths, nseq)
    loads = {
        name: pltpu.make_async_copy(getattr(r, name + "_kept"), getattr(r, name), r.load_sem.at[i])
        for i, name in enumerate(KEPT)
    }
    early = ("context_send", "dout", "x1", "gains", "wh_all")
    middle = ("gated", "wo_all", "zgate", "yfull", "u", "x")
    late = ("wm_all", "packed", "cut", "cx", "totals", "span_totals", "init", "delta", "du", "bx", "xdbl")
    last = ("conv", "ext", "wi_all")
    for name in early + middle:
        loads[name].start()

    def loaded(*names):
        for name in names:
            loads[name].wait()

    targets = [lax.div(shard, 2), shards // 2 + lax.div(shard, 2)]
    mine = lax.div(shard, shards // 2)
    first_piece = 2 * lax.rem(shard, shards // 2)

    def anywhere(index, at):
        return {"device_id": {"seq": index, "shard": at}, "device_id_type": pl.DeviceIdType.MESH}

    barrier = pltpu.get_barrier_semaphore()

    def signal(to):
        pl.semaphore_signal(barrier, inc=1, **to)

    peers = [at_shard(partner)] + [at_shard(o) for o in others] + [at_seq(to) for to in ring]
    for peer in peers:
        signal(peer)
    selves = jnp.int32(0)
    for by in range(spans):
        for at in targets + [first_piece, first_piece + 1]:
            if by:
                signal(anywhere(every[by], at))
            else:
                pl.when(at != shard)(lambda: signal(anywhere(me, at)))
                selves = selves + (at == shard).astype(jnp.int32)
    pl.semaphore_wait(barrier, len(peers) + 4 * spans - selves)

    def copy(source, target, sems, at, to):
        return pltpu.make_async_remote_copy(
            src_ref=source, dst_ref=target, send_sem=sems.at[(0, *at)], recv_sem=sems.at[(1, *at)], **to
        )

    def ref(kind, k):
        return getattr(r, kind + "_" + GRADS[k])

    def near_copy(k, x):
        return copy(
            ref("g", k).at[x * 2 + 1 - core], ref("near", k).at[x], r.near_sem, (k, x), at_shard(partner)
        )

    def far_copy(k, by):
        source = ref("sum", k).at[lax.rem(chip + by, chips)]
        return copy(source, ref("far", k).at[by - 1], r.far_sem, (k, by), at_shard(others[by - 1]))

    def part_copy(k, by):
        to = ring[by - 1]
        return copy(
            ref("near", k).at[0, to], ref("part", k).at[by], r.part_sem, (k, by), at_seq(to)
        )

    def last_copy(k, by):
        held = ref("last", k).at[me]
        return copy(held, held, r.last_sem, (k, by), at_seq(ring[by - 1]))

    def pair_refs(k):
        return (r.sub_early, r.early_in) if GRADS[k] == "early" else (r.sub_other, r.other_in)

    def pair_copy(k, by, at):
        source, target = pair_refs(k)
        to = anywhere(every[by], targets[0])
        return copy(source, target.at[at, me], r.pair_sem, (k - 4, at, by), to)

    def near_send(k):
        for x in range(chips):
            near_copy(k, x).start()

    def far_send(k):
        for x in range(chips):
            near_copy(k, x).wait_recv()
        for by in [*range(1, chips), 0]:
            x = lax.rem(chip + by, chips)
            ref("sum", k)[x] = (
                ref("g", k)[x * 2 + core].astype(F32) + ref("near", k)[x].astype(F32)
            ).astype(BF16)
            if by:
                far_copy(k, by).start()

    def part_send(k):
        total = ref("sum", k)[chip].astype(F32)
        for by in range(1, chips):
            far_copy(k, by).wait_recv()
            total = total + ref("far", k)[by - 1].astype(F32)
        ref("near", k)[0] = total.astype(BF16)
        for by in range(1, chips):
            far_copy(k, by).wait_send()
        for by in range(1, spans):
            part_copy(k, by).start()

    def last_send(k):
        total = ref("near", k)[0, me].astype(F32)
        for by in range(1, spans):
            part_copy(k, by).wait_recv()
            total = total + ref("part", k)[by].astype(F32)
        if k == SMALL:
            ref("last", k)[me] = total.astype(BF16)
            for by in range(1, spans):
                last_copy(k, by).start()
            return
        source, target = pair_refs(k)
        source[...] = total.astype(BF16)
        for by in range(spans):
            to_owner(by == 0, targets[0], pair_copy(k, by, parity), lambda c: c.start())

        @pl.when(targets[0] == shard)
        def _():
            target[parity, me] = source[...]

    def to_owner(same, to, made, act):
        if same:
            pl.when(to != shard)(lambda: act(made))
        else:
            act(made)

    inner = spans // OUTER
    low_me, high_me = lax.rem(me, inner), lax.div(me, inner)
    lows = [lax.rem(low_me + by, inner) for by in range(inner)]
    highs = [lax.rem(high_me + by, OUTER) for by in range(OUTER)]
    own_part = low_me * OUTER + high_me
    middle_at = (inner - 1) * OUTER
    parity = lax.rem(shard, 2)

    def inner_copy(k, by):
        return copy(
            ref("near", k).at[0, pl.ds(lows[by] * OUTER, OUTER)],
            ref("part", k).at[pl.ds((by - 1) * OUTER, OUTER)],
            r.inner_sem,
            (k, 0, by),
            at_seq(high_me * inner + lows[by]),
        )

    def outer_copy(k, by):
        return copy(
            ref("part", k).at[middle_at + highs[by]],
            ref("part", k).at[spans + by - 1],
            r.outer_sem,
            (k, 0, by),
            at_seq(highs[by] * inner + low_me),
        )

    def outer_last(k, by):
        held = ref("last", k).at[own_part]
        return copy(held, held, r.outer_sem, (k, 1, by), at_seq(highs[by] * inner + low_me))

    def inner_last(k, by):
        held = ref("last", k).at[pl.ds(low_me * OUTER, OUTER)]
        return copy(held, held, r.inner_sem, (k, 1, by), at_seq(high_me * inner + lows[by]))

    def late_outer(by, at):
        return copy(
            r.sub_late,
            r.pair_in.at[at, own_part],
            r.late_outer_sem,
            (at, by),
            anywhere(highs[by] * inner + low_me, targets[1]),
        )

    def late_inner(by, at):
        held = r.pair_in.at[at, pl.ds(low_me * OUTER, OUTER)]
        to = at_seq(high_me * inner + lows[by])
        return copy(held, held, r.late_inner_sem, (at, by), to)

    def inner_send(k):
        total = ref("sum", k)[chip].astype(F32)
        for by in range(1, chips):
            far_copy(k, by).wait_recv()
            total = total + ref("far", k)[by - 1].astype(F32)
        ref("near", k)[0] = total.astype(BF16)
        for by in range(1, inner):
            inner_copy(k, by).start()

    def outer_send(k):
        total = ref("near", k)[0, pl.ds(low_me * OUTER, OUTER)].astype(F32)
        for by in range(1, inner):
            inner_copy(k, by).wait_recv()
            total = total + ref("part", k)[(by - 1) * OUTER : by * OUTER].astype(F32)
        ref("part", k)[middle_at : middle_at + OUTER] = total.astype(BF16)
        for by in range(1, OUTER):
            outer_copy(k, by).start()

    def outer_back(k):
        total = ref("part", k)[middle_at + high_me].astype(F32)
        for by in range(1, OUTER):
            outer_copy(k, by).wait_recv()
            total = total + ref("part", k)[spans + by - 1].astype(F32)
        if k != 3:
            ref("last", k)[own_part] = total.astype(BF16)
            for by in range(1, OUTER):
                outer_last(k, by).start()
            return
        r.sub_late[...] = total.astype(BF16)
        for by in range(OUTER):
            to_owner(by == 0, targets[1], late_outer(by, parity), lambda c: c.start())

        @pl.when(targets[1] == shard)
        def _():
            r.pair_in[parity, own_part] = r.sub_late[...]

    def inner_back(k):
        if k != 3:
            for by in range(1, OUTER):
                outer_last(k, by).wait_recv()
            for by in range(1, inner):
                inner_last(k, by).start()
            return

        @pl.when(mine == 1)
        def _():
            for at in range(2):
                for by in range(OUTER):
                    to_owner(by == 0, first_piece + at, late_outer(by, at), lambda c: c.wait_recv())
                for by in range(1, inner):
                    late_inner(by, at).start()

    def finish(k):
        for x in range(chips):
            near_copy(k, x).wait_send()
        if k < 4:
            for by in range(1, chips):
                far_copy(k, by).wait_send()
            for by in range(1, inner):
                inner_copy(k, by).wait_send()
            for by in range(1, OUTER):
                outer_copy(k, by).wait_send()
        else:
            for by in range(1, spans):
                part_copy(k, by).wait_send()
        if k < 3:
            for by in range(1, OUTER):
                outer_last(k, by).wait_send()
            for by in range(1, inner):
                inner_last(k, by).wait()
        elif k == 3:
            for by in range(OUTER):
                to_owner(by == 0, targets[1], late_outer(by, parity), lambda c: c.wait_send())

            @pl.when(mine == 1)
            def _():
                for at in range(2):
                    for by in range(1, inner):
                        late_inner(by, at).wait()

        elif k == SMALL:
            for by in range(1, spans):
                last_copy(k, by).wait()
        else:
            for by in range(spans):
                to_owner(by == 0, targets[0], pair_copy(k, by, parity), lambda c: c.wait_send())

            @pl.when(mine == 0)
            def _():
                for at in range(2):
                    for by in range(spans):
                        made = pair_copy(k, by, at)
                        to_owner(by == 0, first_piece + at, made, lambda c: c.wait_recv())

    def put(k, piece, value):
        size = value.shape[0] // spans
        for j in range(spans):
            ref("g", k)[piece, j] = value[j * size : (j + 1) * size].astype(BF16)

    loaded("context_send")
    head = lax.div(me, ratio)

    def context_copy(t, by, to):
        return copy(r.context_send.at[t], r.context.at[head], r.context_sem, (by,), at_seq(to))

    for t in range(blocks):
        i = t * ratio + sub
        by = lax.rem(i - me + spans, spans)

        @pl.when(i != me)
        def _():
            context_copy(t, by, i).start()

        @pl.when(i == me)
        def _():
            r.context[head] = r.context_send[t]

    low = lane_low(rows)
    half_low = lane_low(half)

    def unpacked(source, pair):
        even, odd = source[2 * pair].astype(F32), source[2 * pair + 1].astype(F32)
        first = jnp.where(half_low, even, pltpu.roll(odd, HEAD_DIM, 1))
        second = jnp.where(half_low, pltpu.roll(even, HEAD_DIM, 1), odd)
        quarter = half // 2
        return jnp.concatenate(
            [first[:quarter], second[:quarter], first[quarter:], second[quarter:]], axis=0
        )

    dqs, dks, dvs = [], [], []
    for pair in range(HEADS // 2):
        dkv = [
            sum(r.dkv_in[(2 * pair + odd) * ratio + part].astype(F32) for part in range(ratio))
            for odd in range(2)
        ]
        dqs.append(unpacked(r.dq_in, pair))
        dks.append(jnp.where(low, dkv[0], pltpu.roll(dkv[1], HEAD_DIM, 1)))
        dvs.append(jnp.where(low, pltpu.roll(dkv[0], HEAD_DIM, 1), dkv[1]))
    dqkv = jnp.concatenate(dqs + dks + dvs, axis=1).astype(BF16)
    loaded("x1", "gains", "wh_all", "dout")
    for name in late + last:
        loads[name].start()
    x1 = r.x1[...]
    inverse = norm(x1)
    normal = x1 * inverse
    gain = r.gains[1:2, :]
    xn2 = (normal * gain).astype(BF16)
    wide = 3 * D // shards
    dxn2 = jnp.zeros((rows, D), F32)
    for s in range(shards):
        piece = dqkv[:, s * wide : (s + 1) * wide]
        put(0, s, dot_tn(xn2, piece))
        dxn2 = dxn2 + dot_nt(piece, r.wh_all[s])
    near_send(0)
    attention_gain = jnp.sum(dxn2 * normal, axis=0, keepdims=True)
    e2 = dxn2 * gain
    dx1 = r.dout[...].astype(F32) + inverse * (
        e2 - normal * jnp.mean(e2 * normal, axis=-1, keepdims=True)
    )
    r.dx1[...] = dx1
    dmixed = dx1.astype(BF16)
    loaded("gated", "wo_all")
    for s in range(shards):
        put(1, s, dot_tn(r.gated[:, s * width : (s + 1) * width], dmixed))
        r.dys[:, s * width : (s + 1) * width] = dot_nt(dmixed, r.wo_all[s])
    near_send(1)
    far_send(0)
    loaded("zgate", "yfull", "u", "x")

    def gate_step(pair, total):
        at = pl.ds(pl.multiple_of(pair * 2 * CHUNKS, 2 * CHUNKS), 2 * CHUNKS)
        dgated = r.dys[at, :].astype(BF16).astype(F32)
        gate = r.zgate[at, :]
        s = jax.nn.sigmoid(gate)
        dys = dgated * (gate * s)
        r.dys[at, :] = dys
        r.dzgate[at, :] = (dgated * r.yfull[at, :] * (s * (1.0 + gate * (1.0 - s)))).astype(BF16)
        return total + dys * r.u[at, :].astype(F32)

    total = lax.fori_loop(0, steps // 2, gate_step, jnp.zeros((2 * CHUNKS, DI), F32))
    r.small[SKIP : SKIP + 1, :] = jnp.sum(total, axis=0, keepdims=True)
    far_send(1)
    x = r.x[...]
    inverse_one = norm(x)
    normal_one = x * inverse_one
    gain_one = r.gains[0:1, :]
    xn1 = (normal_one * gain_one).astype(BF16)
    for s in range(shards):
        put(3, s, dot_tn(xn1, r.dzgate[:, s * width : (s + 1) * width]))
    near_send(3)
    loaded("wm_all", "packed", "cut", "cx", "totals", "span_totals")
    spread_decay(r.packed, r.amat, r.spread)

    def state_copy(by, at):
        to = lax.rem(me - by + spans, spans)
        return copy(
            r.grad_send.at[at], r.grads_in.at[me, at], r.state_sem, (by, at), at_seq(to)
        )

    def pair_step(pair, carry):
        for odd in range(2):
            lanes = lanes_of(pair * 2 + odd)
            amat = [r.spread[st * CHUNKS : (st + 1) * CHUNKS, lanes] for st in range(STATE)]

            def step_fn(turn, grads):
                step = steps - 1 - turn
                cut = r.cut[tile(step), lanes]
                dys = r.dys[tile(step), lanes]
                return tuple(
                    jnp.exp2(cut * amat[st]) * (grads[st] + dys * r.cx[tile(step), column(st)])
                    for st in range(STATE)
                )

            grads = lax.fori_loop(
                0, steps, step_fn, (jnp.zeros((CHUNKS, LANES), F32),) * STATE, unroll=8
            )
            for st in range(STATE):
                r.ends[st, :, lanes] = grads[st]
        lanes = pl.ds(pl.multiple_of(pair * 2 * LANES, 2 * LANES), 2 * LANES)
        amat = r.amat[:, lanes]
        state = jnp.zeros((STATE, 2 * LANES), F32)
        for k in reversed(range(CHUNKS)):
            state = jnp.exp2(amat * r.totals[k : k + 1, lanes]) * state + r.ends[:, k, lanes]
        r.grad_send[pair] = state.astype(BF16)
        for by in range(1, spans):

            @pl.when(me - by >= 0)
            def _():
                state_copy(by, pair).start()

        pl.when(pair == 0)(lambda: far_send(3))
        return carry

    lax.fori_loop(0, GROUPS_CH // 2, pair_step, 0)
    for h in range(HEADS):
        came = h * ratio + sub
        by = lax.rem(me - came + spans, spans)

        @pl.when(came != me)
        def _():
            context_copy(0, by, came).wait_recv()

    context = jnp.concatenate([unpacked(r.context, p) for p in range(HEADS // 2)], axis=1)
    context = context.astype(BF16)
    short = D // shards
    x2 = x1
    for s in range(shards):
        part = context[:, s * short : (s + 1) * short]
        x2 = x2 + dot_nn(part, r.wm_all[s])
        put(2, s, dot_tn(part, r.dout[...]))
    near_send(2)
    given = dot_tn(pick_rows(r.index, me, rows, steps), x2.astype(BF16))
    share = rows // spans
    for j in range(spans):
        r.given[j] = given[j * share : (j + 1) * share].astype(BF16)

    def given_copy(by):
        to = ring[by - 1]
        return copy(r.given.at[to], r.output.at[me], r.given_sem, (by,), at_seq(to))

    r.output[me] = r.given[me]

    loaded("init", "delta", "du", "bx", "xdbl", *last)
    r.db[...] = jnp.zeros_like(r.db)
    r.dc[...] = jnp.zeros_like(r.dc)
    for by in range(1, spans):
        for pair in range(GROUPS_CH // 2):

            @pl.when(me - by >= 0)
            def _():
                state_copy(by, pair).wait_send()

            @pl.when(me + by < spans)
            def _():
                state_copy(by, pair).wait_recv()

    for by in range(1, spans):
        given_copy(by).start()
    amat = r.amat[...]

    def chain(turn, state):
        k = spans - 1 - turn
        decay = jnp.exp2(amat * total_row(r.span_totals[k]))
        came = jnp.concatenate(
            [r.grads_in[k, g].astype(F32) for g in range(GROUPS_CH // 2)], axis=1
        )
        return decay * state + came

    state = lax.fori_loop(0, spans - 1 - me, chain, jnp.zeros((STATE, DI), F32))
    for k in reversed(range(CHUNKS)):
        r.arrive[:, k, :] = state
        if k:
            state = jnp.exp2(amat * r.totals[k : k + 1, :]) * state + r.ends[:, k, :]
    eight = STATE // 2

    def sum_of(terms):
        while len(terms) > 1:
            terms = [a + b for a, b in zip(terms[::2], terms[1::2])]
        return terms[0]

    def kept_at(step, i):
        return pl.ds(pl.multiple_of(step * (eight * CHUNKS) + i * CHUNKS, CHUNKS), CHUNKS)

    stages = {
        0: ((far_send, 2), (inner_send, 0),),
        2: ((inner_send, 1),),
        4: ((outer_send, 0),),
        6: ((inner_send, 3),),
        7: ((outer_send, 1),),
    }

    def run(todo):
        for stage, k in todo:
            stage(k)

    def group_step(group, carry):
        lanes = lanes_of(group)
        for part in range(2):
            states = range(part * eight, (part + 1) * eight)
            amat_g = [r.spread[st * CHUNKS : (st + 1) * CHUNKS, lanes] for st in states]

            def forward(step, held):
                cut = r.cut[tile(step), lanes]
                drive = r.du[tile(step), lanes]
                out = []
                for i, st in enumerate(states):
                    decay = jnp.exp2(cut * amat_g[i])
                    kept = decay * held[i]
                    new = kept + drive * r.bx[tile(step), column(st)]
                    r.decay[kept_at(step, i), :] = decay
                    r.held[kept_at(step, i), :] = kept
                    r.state[kept_at(step, i), :] = new
                    out.append(new)
                return tuple(out)

            lax.fori_loop(
                0, steps, forward, tuple(r.init[st, :, lanes] for st in states), unroll=8
            )

            def backward(turn, held):
                grads, sums = held
                step = steps - 1 - turn
                delta = r.delta[tile(step), lanes]
                drive = r.du[tile(step), lanes]
                dys = r.dys[tile(step), lanes]
                new, totals, by_b, by_a = [], [], [], []
                for i, st in enumerate(states):
                    at = tile(step)
                    grad = grads[i] + dys * r.cx[at, column(st)]
                    new.append(r.decay[kept_at(step, i), :] * grad)
                    through = grad * r.held[kept_at(step, i), :]
                    totals.append(sums[i] + through * delta)
                    by_a.append(amat_g[i] * through)
                    by_b.append(grad * r.bx[at, column(st)])
                    r.dc[at, column(st)] += r.state[kept_at(step, i), :] * dys
                    r.db[at, column(st)] += grad * drive
                if part:
                    r.bgrad[tile(step), lanes] += sum_of(by_b)
                    r.adelta[tile(step), lanes] += sum_of(by_a)
                else:
                    r.bgrad[tile(step), lanes] = sum_of(by_b)
                    r.adelta[tile(step), lanes] = sum_of(by_a)
                return (tuple(new), tuple(totals))

            _, sums = lax.fori_loop(
                0,
                steps,
                backward,
                (
                    tuple(r.arrive[st, :, lanes] for st in states),
                    (jnp.zeros((CHUNKS, LANES), F32),) * eight,
                ),
                unroll=8,
            )
            for i, st in enumerate(states):
                row = jnp.sum(sums[i], axis=0, keepdims=True)
                amat_row = amat_g[i][0:1, :] * math.log(2.0)
                r.small[DEC + st : DEC + st + 1, lanes] = row * amat_row
        for at, todo in stages.items():
            pl.when(group == at)(functools.partial(run, todo))
        return carry

    lax.fori_loop(0, GROUPS_CH, group_step, 0)
    small = r.packed[DEC:PACK, :].astype(F32)
    taps = small[TAPS - DEC : TAPS - DEC + CONV, :]
    skip = small[SKIP - DEC : SKIP - DEC + 1, :]

    def delta_step(step, total):
        at = tile(step)
        bgrad = r.bgrad[at, :]
        delta = r.delta[at, :]
        u = r.conv[at, :]
        u = (u * jax.nn.sigmoid(u)).astype(BF16).astype(F32)
        ddelta = u * bgrad + r.adelta[at, :] * math.log(2.0)
        dtpre = (ddelta * (1.0 - jnp.exp(-delta))).astype(BF16).astype(F32)
        r.adelta[at, :] = dtpre
        r.bgrad[at, :] = r.dys[at, :] * skip + delta * bgrad
        return total + dtpre

    total = lax.fori_loop(0, steps, delta_step, jnp.zeros((CHUNKS, DI), F32))
    run(((inner_send, 2),))
    r.small[STEPB : STEPB + 1, :] = jnp.sum(total, axis=0, keepdims=True)
    r.small[GAINS:, :] = jnp.zeros((PACK - GAINS, DI), F32)
    dtpre = r.adelta[...].astype(BF16)
    steplow = r.xdbl[:, 0:RANK].astype(BF16)
    r.small[STEP : STEP + RANK, :] = dot_tn(steplow, dtpre)
    r.dxdbl[:, 0:RANK] = dot_nt(dtpre, r.packed[STEP : STEP + RANK, :])
    for part in range(4):
        at = slice(part * rows // 4, (part + 1) * rows // 4)
        r.dxdbl[at, RANK : RANK + STATE] = gather_columns(r.db[at, :])
        r.dxdbl[at, RANK + STATE :] = gather_columns(r.dc[at, :])
    run(((outer_back, 0), (outer_send, 3),))
    dxdbl = r.dxdbl[...].astype(BF16)
    r.small[SEL : SEL + STEP, :] = dot_tn(dxdbl, r.u[...])
    r.bgrad[...] += dot_nn(dxdbl, r.packed[SEL : SEL + STEP, :])
    r.dext[...] = jnp.zeros_like(r.dext)
    r.spill[...] = jnp.zeros_like(r.spill)

    @pl.when(me == spans - 1)
    def _():
        r.spill_in[...] = jnp.zeros_like(r.spill_in)

    def conv_steps(first_step, last_step, ranges, totals):
        def one(step, totals):
            at = tile(step)
            places = lax.broadcasted_iota(jnp.int32, (CHUNKS, 1), 0) * steps + step + me * rows
            first = start_of(places, starts)
            inside = [places - (CONV - 1) + k >= first for k in range(CONV)]
            out = []
            for lanes, sums in zip(ranges, totals):
                dconv = r.bgrad[at, lanes] * silu_slope(r.conv[at, lanes])
                new = []
                for k in range(CONV):
                    to = pl.ds(pl.multiple_of((step + k) * CHUNKS, CHUNKS), CHUNKS)
                    counted = jnp.where(inside[k], dconv, 0.0)
                    new.append(sums[k] + counted * r.ext[to, lanes])
                    r.dext[to, lanes] += taps[k : k + 1, lanes] * counted
                out.append(tuple(new) + (sums[CONV] + dconv,))
            return tuple(out)

        return lax.fori_loop(first_step, last_step, one, totals)

    quarter = width // 2
    halves = [
        [slice((2 * o + part) * width, (2 * o + part + 1) * width) for o in range(chips)]
        for part in range(2)
    ]
    zero = jnp.zeros((CHUNKS, width), F32)
    firsts = [
        conv_steps(0, CONV - 1, ranges, tuple((zero,) * (CONV + 1) for _ in ranges))
        for ranges in halves
    ]
    for k in range(CONV - 1):
        r.spill[k : k + 1, :] = r.dext[k * CHUNKS : k * CHUNKS + 1, :]
    behind = lax.rem(me + spans - 1, spans)
    spill = copy(r.spill, r.spill_in, r.spill_sem, (), at_seq(behind))

    @pl.when(me > 0)
    def _():
        spill.start()

    chunk = lax.broadcasted_iota(jnp.int32, (CHUNKS, width), 0)
    dxin = []
    for part, ranges in enumerate(halves):
        totals = conv_steps(CONV - 1, steps, ranges, firsts[part])
        if part:
            far_send(4)
            run(((outer_send, 2),))
        else:
            run(((outer_back, 1),))

            @pl.when(me > 0)
            def _():
                spill.wait_send()

            @pl.when(me < spans - 1)
            def _():
                spill.wait_recv()

        for o, lanes in enumerate(ranges):
            for k in range(CONV):
                r.small[TAPS + k : TAPS + k + 1, lanes] = jnp.sum(
                    totals[o][k], axis=0, keepdims=True
                )
            r.small[BIAS : BIAS + 1, lanes] = jnp.sum(totals[o][CONV], axis=0, keepdims=True)
            for k in range(CONV - 1):
                block = r.dext[k * CHUNKS : (k + 1) * CHUNKS, lanes]
                edge = (steps - CONV + 1 + k) * CHUNKS + EDGE
                moved = pltpu.roll(block, CHUNKS - 1, 0)
                came = jnp.broadcast_to(r.spill_in[k : k + 1, lanes], (CHUNKS, width))
                r.dext[edge : edge + CHUNKS, lanes] += jnp.where(
                    chunk < CHUNKS - 1, moved, came
                )
            piece = r.dext[EDGE:, lanes].astype(BF16)
            dxin.append(piece)
            grad = dot_tn(xn1, piece)
            for parity_at in range(2):
                put(4 + part, 2 * o + parity_at, grad[:, parity_at * quarter : (parity_at + 1) * quarter])
        near_send(4 + part)
    run(((inner_back, 0), (outer_back, 3),))
    wide = 2 * width
    dxn1 = jnp.zeros((rows, D), F32)
    for s in range(shards):
        if s < chips:
            piece = jnp.concatenate([dxin[s], dxin[chips + s]], axis=1)
        else:
            at = (s - chips) * wide
            piece = r.dzgate[:, at : at + wide]
        dxn1 = dxn1 + dot_nt(piece, r.wi_all[s])
    mixer_gain = jnp.sum(dxn1 * normal_one, axis=0, keepdims=True)
    for s in range(shards):
        at = s * width
        gains = slice(s * short, (s + 1) * short)
        r.small[GAINS : GAINS + 1, at : at + short] = mixer_gain[:, gains]
        r.small[GAINS : GAINS + 1, at + short : at + 2 * short] = attention_gain[:, gains]
    for s in range(shards):
        put(SMALL, s, r.small[:, s * width : (s + 1) * width])
    near_send(SMALL)
    far_send(5)
    far_send(SMALL)
    run(((inner_back, 1), (outer_back, 2),))
    part_send(4)
    e1 = dxn1 * gain_one
    dx = r.dx1[...] + inverse_one * (
        e1 - normal_one * jnp.mean(e1 * normal_one, axis=-1, keepdims=True)
    )
    r.dx1[...] = dx
    for part in range(D // LANES):
        lanes = slice(part * LANES, (part + 1) * LANES)
        for step in range(steps):
            r.row[pl.ds(step, CHUNKS, stride=steps), :] = r.dx1[
                step * CHUNKS : (step + 1) * CHUNKS, lanes
            ]
        r.token_grad[:, lanes] = r.row[...]
    part_send(5)
    part_send(SMALL)
    run(((inner_back, 3), (inner_back, 2),))
    last_send(4)
    last_send(5)
    last_send(SMALL)
    for k in (0, 1, 2, 3):
        finish(k)
    for by in range(1, spans):
        given_copy(by).wait()
    for t in range(blocks):
        i = t * ratio + sub
        by = lax.rem(i - me + spans, spans)

        @pl.when(i != me)
        def _():
            context_copy(t, by, i).wait_send()

    finish(SMALL)
    finish(4)
    finish(5)


def final_kernel(*refs):
    r = Refs(tuple(k + "_in" for k in BACKWARD_OUT) + FINAL_OUT, refs)

    def whole(source):
        return jnp.concatenate([source[j].astype(F32) for j in range(source.shape[0])], axis=0)

    r.output[...] = r.output_in[...]
    r.token_grad[...] = r.token_grad_in[...]
    r.heads_grad[...] = whole(r.last_heads_in)
    r.output_grad[...] = whole(r.last_out_in)
    r.merge_grad[...] = whole(r.last_merge_in)
    small = whole(r.last_small_in)
    short = r.mixer_grad.shape[1]
    width = r.taps_grad.shape[1]
    r.select_grad[...] = small[SEL : SEL + STEP]
    r.stepw_grad[...] = small[STEP : STEP + RANK]
    r.decay_grad[...] = small[DEC : DEC + STATE]
    r.taps_grad[...] = small[TAPS : TAPS + CONV]
    r.bias_grad[...] = small[BIAS : BIAS + 1]
    r.stepb_grad[...] = small[STEPB : STEPB + 1]
    r.skip_grad[...] = small[SKIP : SKIP + 1]
    r.mixer_grad[...] = small[GAINS : GAINS + 1, :short]
    r.attention_grad[...] = small[GAINS : GAINS + 1, short:]
    late = jnp.concatenate([whole(r.pair_in_in.at[at]) for at in range(2)], axis=1)
    early = jnp.concatenate(
        [whole(source.at[at]) for source in (r.early_in_in, r.other_in_in) for at in range(2)], axis=1
    )
    inner_half = lax.axis_index("shard") < lax.axis_size("shard") // 2
    r.input_grad[...] = jnp.where(inner_half, early, late)


def shape(*dims, kind=F32):
    return jax.ShapeDtypeStruct(dims, kind)


def vmem(*dims, kind=F32):
    return pltpu.VMEM(dims, kind)


def per_device(
    tokens,
    cotangent,
    positions,
    lengths,
    mixer_gain,
    input_weight,
    kernel_weight,
    kernel_bias,
    select_weight,
    step_weight,
    step_bias,
    decay_log,
    skip_scale,
    output_weight,
    attention_gain,
    heads_weight,
    merge_weight,
):
    spans = lax.axis_size("seq")
    shards = lax.axis_size("shard")
    rows = tokens.shape[1]
    steps = rows // CHUNKS
    share = rows // spans
    nseq = lengths.shape[1]
    ratio = spans // HEADS
    part = rows // ratio
    width = DI // shards

    index = positions
    dma = pltpu.SemaphoreType.DMA
    spread = [vmem(STATE, DI), vmem(STATE * CHUNKS, DI)]
    columns = vmem(rows, STATE * LANES)
    plane = vmem(rows, DI)
    gain_len = D // shards
    halves = GROUPS_CH // 2
    weights = [(D, 2 * width), (width, D), (D, 3 * D // shards), (gain_len, D)]
    half = rows // 2
    blocks = spans // ratio
    slots = 2 if ratio == 1 else 1
    kept = (
        [shape(rows, D)]
        + [shape(shards, *w, kind=BF16) for w in weights]
        + [
            shape(PACK, DI, kind=BF16),
            shape(CHUNKS, D),
            shape(spans, GROUPS_CH, LANES),
            shape(EDGE + rows, DI),
            shape(rows, DI),
            shape(rows, DI),
            shape(rows, DI, kind=BF16),
            shape(rows, DI),
            shape(rows, STEP),
            shape(CHUNKS, DI),
            shape(rows, DI),
            shape(rows, DI, kind=BF16),
            shape(rows, D),
            shape(STATE, CHUNKS, DI),
            shape(rows, D, kind=BF16),
            shape(rows, STATE * LANES),
            shape(rows, STATE * LANES),
            shape(rows, DI),
            shape(rows, DI),
            shape(blocks, half, LANES, kind=BF16),
        ]
    )
    back = [shape(HEADS, half, LANES, kind=BF16), shape(spans, rows, LANES, kind=BF16)]
    inputs = [
        lengths[0],
        tokens[0],
        cotangent[0].reshape(spans, share, D),
        index,
        mixer_gain[None],
        attention_gain[None],
        select_weight.T,
        step_weight,
        decay_log.T,
        kernel_weight,
        kernel_bias[None],
        step_bias[None],
        skip_scale[None],
        input_weight,
        output_weight,
        heads_weight,
        merge_weight,
    ]
    anyspace = pl.BlockSpec(memory_space=pl.ANY)
    outs = pl.pallas_call(
        functools.partial(forward_kernel, steps, nseq, shards, spans),
        out_shape=kept + back,
        in_specs=[SMEM] + [VMEM] * (len(inputs) - 5) + [anyspace] * 4,
        out_specs=[anyspace] * len(kept) + [VMEM] * len(back),
        scratch_shapes=[vmem(*k.shape, kind=k.dtype) for k in kept]
        + [
            vmem(spans, share, D, kind=BF16),
            vmem(spans, halves, STATE, 2 * LANES, kind=BF16),
            vmem(STATE, CHUNKS, DI),
            vmem(rows, LANES),
            vmem(PACK, width),
        ]
        + [vmem(*w, kind=BF16) for w in weights]
        + [
            vmem(PACK, width, kind=BF16),
            vmem(2 * CHUNKS, gain_len, kind=BF16),
            vmem(shards, PACK, width, kind=BF16),
            vmem(shards, 2 * CHUNKS, gain_len, kind=BF16),
            vmem(2 * CHUNKS, D, kind=BF16),
            vmem(halves, STATE, 2 * LANES, kind=BF16),
            vmem(GROUPS_CH, LANES),
        ]
        + spread
        + [
            vmem(HEADS, half, LANES, kind=BF16),
            vmem(HEADS, half, LANES, kind=BF16),
            vmem(HEADS, rows, LANES, kind=BF16),
            vmem(blocks, half, LANES, kind=BF16),
            vmem(blocks, half, LANES, kind=BF16),
            vmem(spans * rows, LANES, kind=BF16),
            vmem(spans, LANES, rows, kind=BF16),
            vmem(slots, spans, rows, rows),
            vmem(slots, spans, rows, rows),
            vmem(spans * rows, LANES),
            vmem(blocks, half, LANES, kind=BF16),
            vmem(spans, rows, LANES, kind=BF16),
            vmem(rows, rows),
            dma((2, 6, shards - 1)),
            dma((2, max(shards // 2 - 1, 1), spans)),
            dma((2, spans)),
            dma((2,)),
            dma((2, spans, halves)),
        ]
        + [dma((2, spans)), dma((2, spans, 2)), dma((2, spans)), dma((2, spans, 2))]
        + [dma((2, spans))] * 2
        + [dma((len(kept),))]
        + [vmem(*w) for w in weights]
        + [dma((4,))],
        compiler_params=params(collective_id=0, has_side_effects=True),
        name="forward",
    )(*inputs)
    saved, back = outs[: len(kept)], outs[len(kept) :]
    parts = {
        "heads": (D // spans, 3 * D // shards),
        "out": (width // spans, D),
        "merge": (gain_len // spans, D),
        "late": (D // spans, width),
        "early": (D // spans, width // 2),
        "other": (D // spans, width // 2),
        "small": (PACK // spans, width),
    }
    chips = shards // 2
    sizes = [(spans, *parts[k]) for k in GRADS]
    count = len(GRADS)
    summed = [
        shape(spans, share, D, kind=BF16),
        shape(rows, D),
        shape(spans, *parts["heads"], kind=BF16),
        shape(spans, *parts["out"], kind=BF16),
        shape(spans, *parts["merge"], kind=BF16),
        shape(spans, *parts["small"], kind=BF16),
        shape(2, spans, *parts["late"], kind=BF16),
        shape(2, spans, *parts["early"], kind=BF16),
        shape(2, spans, *parts["other"], kind=BF16),
    ]
    few = vmem(rows * STATE // 2, LANES)
    state = vmem(STATE, CHUNKS, DI)
    summed = pl.pallas_call(
        functools.partial(backward_kernel, steps, nseq, shards, spans),
        out_shape=summed,
        in_specs=[SMEM] + [VMEM] * 3 + [anyspace] * len(kept),
        out_specs=[VMEM] * len(summed),
        scratch_shapes=[vmem(*k.shape, kind=k.dtype) for k in kept]
        + [
            vmem(HEADS, half, LANES, kind=BF16),
            vmem(spans, share, D, kind=BF16),
            vmem(rows, D),
            plane,
            vmem(rows, DI, kind=BF16),
            state,
            vmem(halves, STATE, 2 * LANES, kind=BF16),
            vmem(spans, halves, STATE, 2 * LANES, kind=BF16),
            columns,
            columns,
            few,
            few,
            few,
            plane,
            plane,
            state,
            vmem(rows, STEP),
            vmem(EDGE + rows, DI),
            vmem(CHUNKS, DI),
            vmem(CHUNKS, DI),
            vmem(PACK, DI),
            vmem(rows, LANES),
        ]
        + spread
        + [
            vmem(*parts["late"], kind=BF16),
            vmem(*parts["early"], kind=BF16),
            vmem(*parts["other"], kind=BF16),
        ]
        + [vmem(shards, *k, kind=BF16) for k in sizes]
        + [vmem(chips, *k, kind=BF16) for k in sizes] * 2
        + [vmem(max(chips - 1, 1), *k, kind=BF16) for k in sizes]
        + [vmem(spans + OUTER - 1, *k[1:], kind=BF16) for k in sizes]
        + [
            dma((len(kept),)),
            dma((2, spans)),
            dma((2, spans)),
            dma((2, spans, halves)),
            dma((2,)),
            dma((2, count, chips)),
            dma((2, count, chips)),
            dma((2, count, spans)),
            dma((2, count, spans)),
            dma((2, 2, 2, spans)),
            dma((2, 4, 2, spans // OUTER)),
            dma((2, 4, 2, OUTER)),
            dma((2, 2, OUTER)),
            dma((2, 2, spans // OUTER)),
        ],
        compiler_params=params(collective_id=1, has_side_effects=True),
        name="backward",
    )(lengths[0], index, *back, *saved)
    results = pl.pallas_call(
        final_kernel,
        out_shape=[
            shape(rows, D, kind=BF16),
            shape(rows, D),
            shape(1, gain_len),
            shape(D, 2 * width),
            shape(CONV, width),
            shape(1, width),
            shape(STEP, width),
            shape(RANK, width),
            shape(1, width),
            shape(STATE, width),
            shape(1, width),
            shape(width, D),
            shape(1, gain_len),
            shape(D, 3 * D // shards),
            shape(gain_len, D),
        ],
        in_specs=[VMEM] * len(summed),
        out_specs=[VMEM] * len(FINAL_OUT),
        compiler_params=params(),
        name="final",
    )(summed[0].reshape(rows, D), *summed[1:])
    flat, turned = {2, 5, 8, 10, 12}, {6, 9}
    return tuple(
        v[None] if i < 2 else v.reshape(-1) if i in flat else v.T if i in turned else v
        for i, v in enumerate(results)
    )


def solution(mesh):
    return jax.shard_map(
        per_device,
        mesh=mesh,
        in_specs=(
            P("shard", "seq", None),
            P("shard", "seq", None),
            P("shard", None),
            P("shard", None),
            P("shard"),
            P(None, "shard"),
            P(None, "shard"),
            P("shard"),
            P("shard", None),
            P(None, "shard"),
            P("shard"),
            P("shard", None),
            P("shard"),
            P("shard", None),
            P("shard"),
            P(None, "shard"),
            P("shard", None),
        ),
        out_specs=(
            P("shard", "seq", None),
            P("shard", "seq", None),
            P("shard"),
            P(None, "shard"),
            P(None, "shard"),
            P("shard"),
            P("shard", None),
            P(None, "shard"),
            P("shard"),
            P("shard", None),
            P("shard"),
            P("shard", None),
            P("shard"),
            P(None, "shard"),
            P("shard", None),
        ),
        check_vma=False,
    )
```

```python
import functools
import math
from typing import Any, NamedTuple

import jax
import jax.numpy as jnp
from jax import lax
from jax.experimental import pallas as pl
from jax.experimental.pallas import tpu as pltpu
from jax.sharding import PartitionSpec as P

D = 512
DI = 1024
RANK = 32
HEADS = 8
STATE = 16
HEAD_DIM = 64
CONV = 4
CHUNKS = 8
LANES = 128
GROUPS_CH = DI // LANES
EDGE = (CONV - 1) * CHUNKS
OUTER = 4

SEL = 0
STEP = RANK + 2 * STATE
DEC = STEP + RANK
TAPS = DEC + STATE
BIAS = TAPS + CONV
STEPB = BIAS + 1
SKIP = STEPB + 1
GAINS = SKIP + 1
PACK = 128

EPS = 1e-05
NEG = -1e30
CUT = 1e30
F32 = jnp.float32
BF16 = jnp.bfloat16

VMEM = pl.BlockSpec(memory_space=pltpu.VMEM)
SMEM = pl.BlockSpec(memory_space=pltpu.SMEM)


def params(**more):
    return pltpu.CompilerParams(vmem_limit_bytes=62 << 20, **more)


def dot_nn(left, right):
    return lax.dot_general(left, right, (((1,), (0,)), ((), ())), preferred_element_type=F32)


def dot_nt(left, right):
    return lax.dot_general(left, right, (((1,), (1,)), ((), ())), preferred_element_type=F32)


def dot_tn(left, right):
    return lax.dot_general(left, right, (((0,), (0,)), ((), ())), preferred_element_type=F32)


def row_places(rows, steps):
    return (rows & (CHUNKS - 1)) * steps + (rows >> 3)


def starts_of(lengths_ref, nseq):
    starts = [jnp.int32(0)]
    for k in range(nseq - 1):
        starts.append(starts[-1] + lengths_ref[k])
    return starts


def start_of(places, starts):
    first = jnp.zeros_like(places)
    for start in starts[1:]:
        first = jnp.where(places >= start, start, first)
    return first


def begin_of(places, starts):
    found = places == starts[0]
    for start in starts[1:]:
        found = found | (places == start)
    return found


def norm(value):
    return lax.rsqrt(jnp.mean(value * value, axis=-1, keepdims=True) + EPS)


def silu_slope(value):
    s = jax.nn.sigmoid(value)
    return s * (1.0 + value * (1.0 - s))


def tile(step):
    return pl.ds(pl.multiple_of(step * CHUNKS, CHUNKS), CHUNKS)


def lanes_of(group):
    return pl.ds(pl.multiple_of(group * LANES, LANES), LANES)


def spread_decay(packed_ref, amat_ref, spread_ref):
    amat = -jnp.exp(packed_ref[DEC : DEC + STATE, :].astype(F32)) * math.log2(math.e)
    amat_ref[...] = amat
    for st in range(STATE):
        spread_ref[st * CHUNKS : (st + 1) * CHUNKS, :] = jnp.broadcast_to(
            amat[st : st + 1, :], (CHUNKS, DI)
        )


def column(st):
    return slice(st * LANES, (st + 1) * LANES)


def thirds(value):
    high = value.astype(BF16)
    rest = value - high.astype(F32)
    middle = rest.astype(BF16)
    return high, middle, (rest - middle.astype(F32)).astype(BF16)


def spread_columns(values):
    terms = jnp.concatenate([t.astype(F32) for t in thirds(values)], axis=1).astype(BF16)
    count = terms.shape[1]
    line = lax.broadcasted_iota(jnp.int32, (count, STATE * LANES), 0)
    lane = lax.broadcasted_iota(jnp.int32, (count, STATE * LANES), 1)
    chosen = (line & (STATE - 1)) == lax.div(lane, LANES)
    return dot_nn(terms, chosen.astype(F32).astype(BF16))


def gather_columns(value):
    line = lax.broadcasted_iota(jnp.int32, (STATE * LANES, STATE), 0)
    lane = lax.broadcasted_iota(jnp.int32, (STATE * LANES, STATE), 1)
    chosen = (lax.div(line, LANES) == lane).astype(F32).astype(BF16)
    return sum(dot_nn(term, chosen) for term in thirds(value)[:2])


def at_seq(index):
    return {"device_id": {"seq": index}, "device_id_type": pl.DeviceIdType.MESH}


def at_shard(index):
    return {"device_id": {"shard": index}, "device_id_type": pl.DeviceIdType.MESH}


def greet(peers):
    barrier = pltpu.get_barrier_semaphore()
    for peer in peers:
        pl.semaphore_signal(barrier, inc=1, **peer)
    pl.semaphore_wait(barrier, len(peers))


def shard_peers(shards):
    shard = lax.axis_index("shard")
    core, chip = lax.rem(shard, 2), lax.div(shard, 2)
    partner = chip * 2 + 1 - core
    others = [lax.rem(chip + by, shards // 2) * 2 + core for by in range(1, shards // 2)]
    return shard, core, chip, partner, others


class Refs:
    def __init__(self, names, refs):
        for name, ref in zip(names, refs, strict=True):
            setattr(self, name, ref)


class ForwardIn(NamedTuple):
    lengths: Any
    tokens: Any
    cot: Any
    index: Any
    mixer: Any
    attention: Any
    select: Any
    stepw: Any
    decay: Any
    taps: Any
    bias: Any
    stepb: Any
    skip: Any
    wi_arg: Any
    wo_arg: Any
    wh_arg: Any
    wm_arg: Any


FORWARD_IN = ForwardIn._fields
class Kept(NamedTuple):
    x: Any
    wi_all: Any
    wo_all: Any
    wh_all: Any
    wm_all: Any
    packed: Any
    gains: Any
    span_totals: Any
    ext: Any
    zgate: Any
    conv: Any
    u: Any
    delta: Any
    xdbl: Any
    totals: Any
    yfull: Any
    gated: Any
    x1: Any
    init: Any
    dout: Any
    bx: Any
    cx: Any
    cut: Any
    du: Any
    context_send: Any


KEPT = Kept._fields
FORWARD_OUT = tuple(k + "_out" for k in KEPT) + ("dq_in", "dkv_in")
class ForwardScratch(NamedTuple):
    given: Any
    states: Any
    ends: Any
    row: Any
    small: Any
    wi_send: Any
    wo_send: Any
    wh_send: Any
    wm_send: Any
    packed_send: Any
    gains_send: Any
    packed_all: Any
    gains_all: Any
    before: Any
    state_send: Any
    total_send: Any
    amat: Any
    spread: Any
    q_send: Any
    d_send: Any
    kv_send: Any
    q_in: Any
    d_in: Any
    kv_in: Any
    kvt: Any
    score: Any
    dprob: Any
    dkv: Any
    dq_send: Any
    dkv_send: Any
    causal: Any
    gather_sem: Any
    share_sem: Any
    cot_sem: Any
    edge_sem: Any
    state_sem: Any
    total_sem: Any
    q_sem: Any
    d_sem: Any
    kv_sem: Any
    dq_sem: Any
    dkv_sem: Any
    keep_sem: Any
    wi: Any
    wo: Any
    wh: Any
    wm: Any
    arg_sem: Any


FORWARD_SCRATCH = KEPT + ForwardScratch._fields


def forward_kernel(steps, nseq, shards, spans, *refs):
    r = Refs(FORWARD_IN + FORWARD_OUT + FORWARD_SCRATCH, refs)
    rows = steps * CHUNKS
    width = DI // shards
    me = lax.axis_index("seq")
    shard, core, chip, partner, others = shard_peers(shards)
    far = len(others)
    ring = [lax.rem(me + by, spans) for by in range(1, spans)]
    arguments = [
        pltpu.make_async_copy(source, target, r.arg_sem.at[i])
        for i, (source, target) in enumerate(
            ((r.wi_arg, r.wi), (r.wo_arg, r.wo), (r.wh_arg, r.wh), (r.wm_arg, r.wm))
        )
    ]
    for argument in arguments:
        argument.start()
    greet([at_shard(partner)] + [at_shard(o) for o in others] + [at_seq(to) for to in ring])

    def copy(source, target, sems, at, to):
        return pltpu.make_async_remote_copy(
            src_ref=source, dst_ref=target, send_sem=sems.at[(0, *at)], recv_sem=sems.at[(1, *at)], **to
        )

    sources = (r.wi_send, r.packed_send, r.gains_send, r.wo_send, r.wh_send, r.wm_send)
    wholes = (r.wi_all, r.packed_all, r.gains_all, r.wo_all, r.wh_all, r.wm_all)

    share = D // 2 // spans
    straight = D - share * spans

    def own_share(index):
        return pl.ds(pl.multiple_of(straight + index * share, share), share)

    def sent(k, i):
        if i == far:
            return copy(sources[k], wholes[k].at[shard], r.gather_sem, (k, i), at_shard(partner))
        source, target = sources[k], wholes[k].at[shard]
        if k == 0:
            source, target = source.at[0:straight], wholes[k].at[shard, 0:straight]
        return copy(source, target, r.gather_sem, (k, i), at_shard(others[i]))

    def shared(i):
        return copy(
            r.wi_send.at[own_share(me)],
            r.wi_all.at[shard, own_share(me)],
            r.share_sem,
            (i, 0),
            at_shard(others[i]),
        )

    def fanned(i, by):
        came = lax.rem(chip + far - i, far + 1) * 2 + core
        held = r.wi_all.at[came, own_share(me)]
        return copy(held, held, r.share_sem, (i, by), at_seq(ring[by - 1]))

    def passed(k, i):
        came = lax.rem(chip + far - i, far + 1) * 2 + core
        return copy(
            wholes[k].at[came], wholes[k].at[came], r.gather_sem, (k, far + 1 + i), at_shard(partner)
        )

    def spread(*which):
        for k in which:
            for i in range(far + 1):
                sent(k, i).start()
        for k in which:
            wholes[k][shard] = sources[k][...]

    def pass_on(*which):
        for i in range(far):
            for k in which:
                sent(k, i).wait_recv()
                passed(k, i).start()

    def finish(*which):
        for k in which:
            for i in range(far):
                sent(k, i).wait_send()
                passed(k, i).wait()
            sent(k, far).wait()

    arguments[0].wait()
    r.wi_send[...] = r.wi[...].astype(BF16)
    r.small[...] = jnp.zeros_like(r.small)
    for source, first in (
        (r.select, SEL),
        (r.decay, DEC),
        (r.stepw, STEP),
        (r.taps, TAPS),
        (r.bias, BIAS),
        (r.stepb, STEPB),
        (r.skip, SKIP),
    ):
        r.small[first : first + source.shape[0], :] = source[...]
    r.packed_send[...] = r.small[...].astype(BF16)
    lane = lax.broadcasted_iota(jnp.int32, (2 * CHUNKS, D // shards), 0)
    r.gains_send[...] = jnp.where(lane == 0, r.mixer[...], r.attention[...]).astype(BF16)
    for i in range(far):
        shared(i).start()
    spread(0, 1, 2)
    last = r.tokens.at[pl.ds(rows - 2 * CHUNKS, 2 * CHUNKS)]
    edge = copy(last, r.before, r.edge_sem, (), at_seq(ring[0]))
    edge.start()

    def cot_copy(by):
        return copy(
            r.cot.at[ring[by - 1]], r.given.at[me], r.cot_sem, (by,), at_seq(ring[by - 1])
        )

    for i in range(far):
        shared(i).wait_recv()
        for by in range(1, spans):
            fanned(i, by).start()
    for argument in arguments[1:]:
        argument.wait()
    r.wo_send[...] = r.wo[...].astype(BF16)
    r.wh_send[...] = r.wh[...].astype(BF16)
    r.wm_send[...] = r.wm[...].astype(BF16)
    for part in range(D // LANES):
        lanes = slice(part * LANES, (part + 1) * LANES)
        r.row[...] = r.tokens[:, lanes].astype(F32)
        for step in range(steps):
            r.x[step * CHUNKS : (step + 1) * CHUNKS, lanes] = r.row[
                pl.ds(step, CHUNKS, stride=steps), :
            ]
    for i in range(far):
        shared(i).wait_send()
        for by in range(1, spans):
            fanned(i, by).wait()
    pass_on(0, 1, 2)
    for by in range(1, spans):
        cot_copy(by).start()
    r.given[me] = r.cot[me]
    spread(5, 3, 4)
    finish(0, 1, 2)
    edge.wait()

    starts = starts_of(r.lengths, nseq)
    r.packed[...] = jnp.concatenate([r.packed_all[s] for s in range(shards)], axis=1)
    gains = jnp.concatenate([r.gains_all[s].astype(F32) for s in range(shards)], axis=1)
    r.gains[...] = gains[:CHUNKS]
    gain = gains[0:1]
    x = r.x[...]
    xn1 = (x * norm(x) * gain).astype(BF16)
    before = r.before[...].astype(F32)
    edge_n = (before * norm(before) * gain).astype(BF16)
    wide = 2 * DI // shards
    for s in range(shards):
        piece = dot_nn(xn1, r.wi_all[s])
        if s < shards // 2:
            r.ext[EDGE:, s * wide : (s + 1) * wide] = piece
        else:
            at = (s - shards // 2) * wide
            r.zgate[:, at : at + wide] = piece
    edge_x = jnp.concatenate([dot_nn(edge_n, r.wi_all[s]) for s in range(shards // 2)], axis=1)
    count = r.before.shape[0]
    chunk = lax.broadcasted_iota(jnp.int32, (CHUNKS, DI), 0)
    for k in range(CONV - 1):
        late = (steps - CONV + 1 + k) * CHUNKS + EDGE
        moved = pltpu.roll(r.ext[late : late + CHUNKS, :], 1, 0)
        at = count - CONV + 1 + k
        r.ext[k * CHUNKS : (k + 1) * CHUNKS, :] = jnp.where(
            chunk == 0, jnp.broadcast_to(edge_x[at : at + 1, :], (CHUNKS, DI)), moved
        )
    small = r.packed[DEC:PACK, :].astype(F32)
    taps = small[TAPS - DEC : TAPS - DEC + CONV, :]
    bias = small[BIAS - DEC : BIAS - DEC + 1, :]

    def conv_step(step, carry):
        places = lax.broadcasted_iota(jnp.int32, (CHUNKS, 1), 0) * steps + step + me * rows
        first = start_of(places, starts)
        total = jnp.broadcast_to(bias, (CHUNKS, DI))
        for k in range(CONV):
            at = pl.ds(pl.multiple_of((step + k) * CHUNKS, CHUNKS), CHUNKS)
            inside = places - (CONV - 1) + k >= first
            total = total + jnp.where(inside, taps[k : k + 1, :] * r.ext[at, :], 0.0)
        r.conv[tile(step), :] = total
        r.du[tile(step), :] = total * jax.nn.sigmoid(total)
        return carry

    lax.fori_loop(0, steps, conv_step, 0, unroll=2)
    u = r.du[...].astype(BF16)
    r.u[...] = u
    xdbl = dot_nt(u, r.packed[SEL : SEL + STEP, :])
    r.xdbl[...] = xdbl
    r.delta[...] = dot_nn(
        xdbl[:, :RANK].astype(BF16), r.packed[STEP : STEP + RANK, :]
    )
    stepb = small[STEPB - DEC : STEPB - DEC + 1, :]

    def delta_step(step, total):
        places = lax.broadcasted_iota(jnp.int32, (CHUNKS, 1), 0) * steps + step + me * rows
        pre = r.delta[tile(step), :] + stepb
        delta = jnp.maximum(pre, 0.0) + jnp.log(1.0 + jnp.exp(-jnp.abs(pre)))
        r.delta[tile(step), :] = delta
        cut = jnp.where(begin_of(places, starts), CUT, delta)
        r.cut[tile(step), :] = cut
        r.du[tile(step), :] = delta * r.du[tile(step), :].astype(BF16).astype(F32)
        return total + cut

    totals = lax.fori_loop(0, steps, delta_step, jnp.zeros((CHUNKS, DI), F32), unroll=2)
    r.totals[...] = totals
    total = jnp.sum(totals, axis=0, keepdims=True)
    for group in range(GROUPS_CH):
        r.total_send[group : group + 1, :] = total[:, group * LANES : (group + 1) * LANES]
    r.span_totals[me] = r.total_send[...]

    def total_copy(by):
        return copy(
            r.total_send, r.span_totals.at[me], r.total_sem, (by,), at_seq(ring[by - 1])
        )

    for by in range(1, spans):
        total_copy(by).start()
    pass_on(5)
    spread_decay(r.packed, r.amat, r.spread)
    r.bx[...] = spread_columns(xdbl[:, RANK : RANK + STATE])

    def state_copy(by, at):
        return copy(
            r.state_send.at[at], r.states.at[me, at], r.state_sem, (by, at), at_seq(ring[by - 1])
        )

    def pair_step(pair, carry):
        for odd in range(2):
            lanes = lanes_of(pair * 2 + odd)
            amat = [r.spread[st * CHUNKS : (st + 1) * CHUNKS, lanes] for st in range(STATE)]

            def step_fn(step, states):
                cut = r.cut[tile(step), lanes]
                drive = r.du[tile(step), lanes]
                return tuple(
                    jnp.exp2(cut * amat[st]) * states[st] + drive * r.bx[tile(step), column(st)]
                    for st in range(STATE)
                )

            states = lax.fori_loop(
                0, steps, step_fn, (jnp.zeros((CHUNKS, LANES), F32),) * STATE, unroll=8
            )
            for st in range(STATE):
                r.ends[st, :, lanes] = states[st]
        lanes = pl.ds(pl.multiple_of(pair * 2 * LANES, 2 * LANES), 2 * LANES)
        amat = r.amat[:, lanes]
        state = jnp.zeros((STATE, 2 * LANES), F32)
        for k in range(CHUNKS):
            state = jnp.exp2(amat * r.totals[k : k + 1, lanes]) * state + r.ends[:, k, lanes]
        r.state_send[pair] = state.astype(BF16)
        for by in range(1, spans):

            @pl.when(me + by < spans)
            def _():
                state_copy(by, pair).start()

        return carry

    lax.fori_loop(0, GROUPS_CH // 2, pair_step, 0)
    pass_on(3)
    for by in range(1, spans):
        cot_copy(by).wait()
    finish(5)

    ratio = spans // HEADS
    sub = lax.rem(me, ratio)
    head = lax.div(me, ratio)
    half = rows // 2
    given = jnp.concatenate([r.given[j] for j in range(spans)], axis=0)
    dout = dot_nn(pick_rows(r.index, me, rows, steps), given).astype(BF16)
    r.dout[...] = dout
    merge = jnp.concatenate([r.wm_all[s] for s in range(shards)], axis=0)
    dcontext = dot_nt(dout, merge).astype(BF16).astype(F32)
    low = lane_low(half)

    quarter = half // 2
    quarter_low = lane_low(quarter)

    def packs(pair, target, first, part):
        above, below = pair[:quarter], pair[quarter:]
        at = slice(part * quarter, (part + 1) * quarter)
        even = jnp.where(quarter_low, above, pltpu.roll(below, HEAD_DIM, 1))
        odd = jnp.where(quarter_low, pltpu.roll(above, HEAD_DIM, 1), below)
        target[first, at] = even.astype(BF16)
        target[first + 1, at] = odd.astype(BF16)

    def half_rows(part):
        return slice(part * half, (part + 1) * half)

    for pair in range(HEADS // 2):
        for part in range(2):
            packs(dcontext[half_rows(part), pair * LANES : (pair + 1) * LANES], r.d_send, 2 * pair, part)

    def d_copy(by):
        to = lax.rem(me + by, spans)
        slot = lax.div(me, ratio)
        return copy(r.d_send.at[lax.div(to, ratio)], r.d_in.at[slot], r.d_sem, (by,), at_seq(to))

    def q_copy(by, part):
        to = lax.rem(me + by, spans)
        at = pl.ds(part * quarter, quarter)
        source, target = r.q_send.at[lax.div(to, ratio), at], r.q_in.at[lax.div(me, ratio), at]
        return copy(source, target, r.q_sem, (by, part), at_seq(to))

    def kv_copy(by, part):
        to = lax.rem(me + by, spans)
        return copy(
            r.kv_send.at[lax.div(to, ratio), pl.ds(part * half, half)],
            r.kv_in.at[pl.ds(pl.multiple_of(me * rows + part * half, half), half)],
            r.kv_sem,
            (by, part),
            at_seq(to),
        )

    def to_rows(made, act):
        for by in range(1, spans):
            if ratio == 1:
                act(made(by))
            else:
                pl.when(lax.rem(by, ratio) == 0)(lambda: act(made(by)))

    to_rows(d_copy, lambda c: c.start())
    r.d_in[lax.div(me, ratio)] = r.d_send[head]
    r.cx[...] = spread_columns(xdbl[:, RANK + STATE :])
    for by in range(1, spans):
        total_copy(by).wait()
        for pair in range(GROUPS_CH // 2):

            @pl.when(me + by < spans)
            def _():
                state_copy(by, pair).wait_send()

            @pl.when(me - by >= 0)
            def _():
                state_copy(by, pair).wait_recv()

    amat = r.amat[...]

    def chain(k, state):
        decay = jnp.exp2(amat * total_row(r.span_totals[k]))
        came = jnp.concatenate(
            [r.states[k, g].astype(F32) for g in range(GROUPS_CH // 2)], axis=1
        )
        return decay * state + came

    state = lax.fori_loop(0, me, chain, jnp.zeros((STATE, DI), F32))
    for k in range(CHUNKS):
        r.init[:, k, :] = state
        if k < CHUNKS - 1:
            state = jnp.exp2(amat * r.totals[k : k + 1, :]) * state + r.ends[:, k, :]

    skip = small[SKIP - DEC : SKIP - DEC + 1, :]
    wo = None
    scale = 1.0 / math.sqrt(HEAD_DIM)

    for part in range(2):
        entering, leaving = (r.init, r.ends) if part == 0 else (r.ends, None)

        def group_step(group, carry):
            lanes = lanes_of(group)
            amat_g = [r.spread[st * CHUNKS : (st + 1) * CHUNKS, lanes] for st in range(STATE)]

            def step_fn(step, states):
                cut = r.cut[tile(step), lanes]
                drive = r.du[tile(step), lanes]
                new = tuple(
                    jnp.exp2(cut * amat_g[st]) * states[st] + drive * r.bx[tile(step), column(st)]
                    for st in range(STATE)
                )
                terms = [new[st] * r.cx[tile(step), column(st)] for st in range(STATE)]
                while len(terms) > 1:
                    terms = [a + b for a, b in zip(terms[::2], terms[1::2])]
                r.yfull[tile(step), lanes] = terms[0]
                return new

            states = lax.fori_loop(
                part * steps // 2,
                (part + 1) * steps // 2,
                step_fn,
                tuple(entering[st, :, lanes] for st in range(STATE)),
                unroll=8,
            )
            if leaving is not None:
                for st in range(STATE):
                    leaving[st, :, lanes] = states[st]
            return carry

        lax.fori_loop(0, GROUPS_CH, group_step, 0)

        def gate_step(pair, carry):
            at = pl.ds(pl.multiple_of(pair * 2 * CHUNKS, 2 * CHUNKS), 2 * CHUNKS)
            yfull = r.yfull[at, :] + skip * r.u[at, :].astype(F32)
            r.yfull[at, :] = yfull
            gate = r.zgate[at, :]
            r.gated[at, :] = (yfull * (gate * jax.nn.sigmoid(gate))).astype(BF16)
            return carry

        lax.fori_loop(part * steps // 4, (part + 1) * steps // 4, gate_step, 0, unroll=2)
        if part == 0:
            pass_on(4)
            finish(3)
            wo = jnp.concatenate([r.wo_all[s] for s in range(shards)], axis=0)
        ours = half_rows(part)
        x1 = r.x[ours, :] + dot_nn(r.gated[ours, :], wo)
        r.x1[ours, :] = x1
        xn2 = (x1 * norm(x1) * gains[1:2, :]).astype(BF16)
        if part == 0:
            finish(4)
        qkv = jnp.concatenate([dot_nn(xn2, r.wh_all[s]) for s in range(shards)], axis=1)
        qkv = qkv.astype(BF16).astype(F32)
        for pair in range(HEADS // 2):
            at = pair * LANES
            packs(qkv[:, at : at + LANES] * scale, r.q_send, 2 * pair, part)
            k = qkv[:, D + at : D + at + LANES]
            v = qkv[:, 2 * D + at : 2 * D + at + LANES]
            even = jnp.where(low, k, pltpu.roll(v, HEAD_DIM, 1))
            odd = jnp.where(low, pltpu.roll(k, HEAD_DIM, 1), v)
            r.kv_send[2 * pair, ours] = even.astype(BF16)
            r.kv_send[2 * pair + 1, ours] = odd.astype(BF16)
        to_rows(functools.partial(q_copy, part=part), lambda c: c.start())
        for by in range(1, spans):
            kv_copy(by, part).start()
    r.q_in[lax.div(me, ratio)] = r.q_send[head]
    r.kv_in[pl.ds(pl.multiple_of(me * rows, rows), rows), :] = r.kv_send[head]
    keeps = [
        pltpu.make_async_copy(getattr(r, name), getattr(r, name + "_out"), r.keep_sem.at[i])
        for i, name in enumerate(KEPT)
    ]
    for keep in keeps[:-1]:
        keep.start()
    at = lax.broadcasted_iota(jnp.int32, (1, rows), 1)
    turn_at = lax.rem(lax.div(at, quarter), 2) * half + lax.div(at, half) * quarter + lax.rem(at, quarter)
    query_local = row_places(turn_at, steps)
    key_local = row_places(lax.broadcasted_iota(jnp.int32, (rows, 1), 0), steps)
    r.causal[...] = jnp.where(key_local <= query_local, 0.0, NEG)
    r.dkv[...] = jnp.zeros_like(r.dkv)
    if ratio > 1:
        to_rows(d_copy, lambda c: c.wait_recv())
        for part in range(2):
            to_rows(functools.partial(q_copy, part=part), lambda c: c.wait_recv())
            for by in range(1, spans):
                kv_copy(by, part).wait_recv()

    def arrived(source):
        by = lax.rem(me - source + spans, spans)

        @pl.when(source != me)
        def _():
            d_copy(by).wait_recv()
            for part in range(2):
                q_copy(by, part).wait_recv()
                kv_copy(by, part).wait_recv()


    static = ratio == 1
    blocks = spans // ratio

    def each(count, fn, carry):
        if not static:
            return lax.fori_loop(0, count, fn, carry)
        for j in range(count):
            carry = fn(j, carry)
        return carry

    def key_rows(j):
        return pl.ds(j * rows if static else pl.multiple_of(j * rows, rows), rows)

    def turn(j, carry):
        r.kvt[j] = r.kv_in[key_rows(j), :].astype(F32).T.astype(BF16)
        return carry

    if not static:
        each(spans, turn, 0)
    folded = (rows // CHUNKS, CHUNKS, rows)

    def dq_copy(to, by, t):
        return copy(r.dq_send.at[t], r.dq_in.at[head], r.dq_sem, (by,), at_seq(to))

    def query_block(t, carry):
        i = t * ratio + sub
        slot = t % 2 if static else 0
        if static:
            arrived(t)
            turn(t, 0)
        q = r.q_in[t].astype(F32)
        d = r.d_in[t].astype(F32)
        qt = q.T
        dt = d.T
        zero = jnp.zeros((HEAD_DIM, rows), F32)
        qt = jnp.concatenate([qt[:HEAD_DIM], qt[HEAD_DIM:]], axis=1)
        dt = jnp.concatenate([dt[:HEAD_DIM], dt[HEAD_DIM:]], axis=1)
        both = jnp.concatenate(
            [jnp.concatenate([qt, zero], axis=1), jnp.concatenate([zero, dt], axis=1)], axis=0
        ).astype(BF16)
        none = jnp.zeros((half, LANES), F32)
        natural = jnp.concatenate(
            [
                jnp.where(low, none, pltpu.roll(d, HEAD_DIM, 1)),
                jnp.where(low, none, d),
                jnp.where(low, q, none),
                jnp.where(low, pltpu.roll(q, HEAD_DIM, 1), none),
            ],
            axis=0,
        ).astype(BF16)
        first = start_of(query_local + i * rows, starts)

        def scores(j, top):
            joint = dot_nn(r.kv_in[key_rows(j), :], both)
            score = joint[:, :rows]
            if static:
                if j == t:
                    score = score + r.causal[...]
                if j in (0, t) or t == spans - 1:
                    score = jnp.where(key_local + j * rows >= first, score, NEG)
            else:
                query = query_local + i * rows
                key = key_local + j * rows
                score = jnp.where((key <= query) & (key >= first), score, NEG)
            r.score[slot, j] = score
            r.dprob[slot, j] = joint[:, rows:]
            return jnp.maximum(top, jnp.max(score.reshape(folded), axis=0))

        top = each(t + 1 if static else i + 1, scores, jnp.full((CHUNKS, rows), NEG, F32))
        top = jnp.max(top, axis=0, keepdims=True)

        def weigh(j, sums):
            total, dot = sums
            prob = jnp.exp(r.score[slot, j] - top)
            r.score[slot, j] = prob
            total = total + jnp.sum(prob.reshape(folded), axis=0)
            dot = dot + jnp.sum((prob * r.dprob[slot, j]).reshape(folded), axis=0)
            return total, dot

        zero = jnp.zeros((CHUNKS, rows), F32)
        total, dot = each(t + 1 if static else i + 1, weigh, (zero, zero))
        inverse = 1.0 / jnp.sum(total, axis=0, keepdims=True)
        datt = jnp.sum(dot, axis=0, keepdims=True) * inverse

        def back(j, sums):
            prob = r.score[slot, j] * inverse
            dscore = prob * (r.dprob[slot, j] - datt)
            joint = jnp.concatenate([prob.astype(BF16), dscore.astype(BF16)], axis=1)
            r.dkv[key_rows(j), :] += dot_nn(joint, natural)
            return sums + dot_nn(r.kvt[j], joint)

        sums = each(t + 1 if static else i + 1, back, jnp.zeros((LANES, 2 * rows), F32))
        dqt = sums[:HEAD_DIM, rows:] * scale
        ctx = sums[HEAD_DIM:, :rows]
        dqt = jnp.concatenate([dqt[:, :half], dqt[:, half:]], axis=0)
        ctx = jnp.concatenate([ctx[:, :half], ctx[:, half:]], axis=0)
        r.dq_send[t] = dqt.T.astype(BF16)
        r.context_send[t] = ctx.T.astype(BF16)
        by = lax.rem(i - me + spans, spans)

        @pl.when(i != me)
        def _():
            dq_copy(i, by, t).start()

        @pl.when(i == me)
        def _():
            r.dq_in[head] = r.dq_send[t]

        return carry

    if static:
        for t in range(blocks):
            query_block(t, 0)
    else:
        lax.fori_loop(0, blocks, query_block, 0)
    keeps[-1].start()
    to_rows(d_copy, lambda c: c.wait_send())
    for part in range(2):
        to_rows(functools.partial(q_copy, part=part), lambda c: c.wait_send())
        for by in range(1, spans):
            kv_copy(by, part).wait_send()

    def cast(j, carry):
        r.dkv_send[j] = r.dkv[key_rows(j), :].astype(BF16)
        return carry

    each(spans, cast, 0)

    def dkv_copy(by):
        to = ring[by - 1]
        return copy(r.dkv_send.at[to], r.dkv_in.at[me], r.dkv_sem, (by,), at_seq(to))

    for by in range(1, spans):
        dkv_copy(by).start()
    r.dkv_in[me] = r.dkv_send[me]
    for t in range(blocks):
        i = t * ratio + sub
        by = lax.rem(i - me + spans, spans)

        @pl.when(i != me)
        def _():
            dq_copy(i, by, t).wait_send()

    for h in range(HEADS):
        came = h * ratio + sub
        by = lax.rem(me - came + spans, spans)

        @pl.when(came != me)
        def _():
            dq_copy(came, by, 0).wait_recv()

    for by in range(1, spans):
        dkv_copy(by).wait()
    for keep in keeps:
        keep.wait()


def total_row(values):
    return jnp.concatenate([values[g : g + 1, :] for g in range(GROUPS_CH)], axis=1)


def lane_low(rows):
    return lax.broadcasted_iota(jnp.int32, (rows, LANES), 1) < HEAD_DIM


def pick_rows(table_ref, me, rows, steps):
    spans = table_ref.shape[1] // rows
    share = rows // spans
    lane = lax.broadcasted_iota(jnp.int32, (1, rows), 1)
    index = jnp.zeros((1, rows), F32)
    for j in range(spans):
        line = table_ref[:, j * rows : (j + 1) * rows].astype(F32)
        line = pltpu.roll(line, lax.rem((j + spans - me) * share, rows), 1)
        index = jnp.where(lane >= j * share, line, index)
    places = row_places(lax.broadcasted_iota(jnp.int32, (rows, 1), 0), steps) + me * rows
    return (index == places.astype(F32)).astype(F32).astype(BF16)


GRADS = ("heads", "out", "merge", "late", "early", "other", "small")
SMALL = 6
BACKWARD_IN = ("lengths", "index", "dq_in", "dkv_in") + tuple(k + "_kept" for k in KEPT)
class BackwardOut(NamedTuple):
    output: Any
    token_grad: Any
    last_heads: Any
    last_out: Any
    last_merge: Any
    last_small: Any
    pair_in: Any
    early_in: Any
    other_in: Any


BACKWARD_OUT = BackwardOut._fields
class FinalOut(NamedTuple):
    output: Any
    token_grad: Any
    mixer_grad: Any
    input_grad: Any
    taps_grad: Any
    bias_grad: Any
    select_grad: Any
    stepw_grad: Any
    stepb_grad: Any
    decay_grad: Any
    skip_grad: Any
    output_grad: Any
    attention_grad: Any
    heads_grad: Any
    merge_grad: Any


FINAL_OUT = FinalOut._fields
class BackwardScratch(NamedTuple):
    context: Any
    given: Any
    dx1: Any
    dys: Any
    dzgate: Any
    ends: Any
    grad_send: Any
    grads_in: Any
    db: Any
    dc: Any
    decay: Any
    held: Any
    state: Any
    bgrad: Any
    adelta: Any
    arrive: Any
    dxdbl: Any
    dext: Any
    spill: Any
    spill_in: Any
    small: Any
    row: Any
    amat: Any
    spread: Any
    sub_late: Any
    sub_early: Any
    sub_other: Any


class BackwardSems(NamedTuple):
    load_sem: Any
    context_sem: Any
    given_sem: Any
    state_sem: Any
    spill_sem: Any
    near_sem: Any
    far_sem: Any
    part_sem: Any
    last_sem: Any
    pair_sem: Any
    inner_sem: Any
    outer_sem: Any
    late_outer_sem: Any
    late_inner_sem: Any


BACKWARD_SCRATCH = (
    KEPT
    + BackwardScratch._fields
    + tuple(kind + name for kind in ("g_", "near_", "sum_", "far_", "part_") for name in GRADS)
    + BackwardSems._fields
)


def backward_kernel(steps, nseq, shards, spans, *refs):
    r = Refs(BACKWARD_IN + BACKWARD_OUT + BACKWARD_SCRATCH, refs)
    rows = steps * CHUNKS
    width = DI // shards
    me = lax.axis_index("seq")
    shard, core, chip, partner, others = shard_peers(shards)
    chips = shards // 2
    ring = [lax.rem(me + by, spans) for by in range(1, spans)]
    every = [me] + ring
    ratio = spans // HEADS
    sub = lax.rem(me, ratio)
    half = rows // 2
    blocks = spans // ratio
    starts = starts_of(r.lengths, nseq)
    loads = {
        name: pltpu.make_async_copy(getattr(r, name + "_kept"), getattr(r, name), r.load_sem.at[i])
        for i, name in enumerate(KEPT)
    }
    early = ("context_send", "dout", "x1", "gains", "wh_all")
    middle = ("gated", "wo_all", "zgate", "yfull", "u", "x")
    late = ("wm_all", "packed", "cut", "cx", "totals", "span_totals", "init", "delta", "du", "bx", "xdbl")
    last = ("conv", "ext", "wi_all")
    for name in early + middle:
        loads[name].start()

    def loaded(*names):
        for name in names:
            loads[name].wait()

    targets = [lax.div(shard, 2), shards // 2 + lax.div(shard, 2)]
    mine = lax.div(shard, shards // 2)
    first_piece = 2 * lax.rem(shard, shards // 2)

    def anywhere(index, at):
        return {"device_id": {"seq": index, "shard": at}, "device_id_type": pl.DeviceIdType.MESH}

    barrier = pltpu.get_barrier_semaphore()

    def signal(to):
        pl.semaphore_signal(barrier, inc=1, **to)

    peers = [at_shard(partner)] + [at_shard(o) for o in others] + [at_seq(to) for to in ring]
    for peer in peers:
        signal(peer)
    selves = jnp.int32(0)
    for by in range(spans):
        for at in targets + [first_piece, first_piece + 1]:
            if by:
                signal(anywhere(every[by], at))
            else:
                pl.when(at != shard)(lambda: signal(anywhere(me, at)))
                selves = selves + (at == shard).astype(jnp.int32)
    pl.semaphore_wait(barrier, len(peers) + 4 * spans - selves)

    def copy(source, target, sems, at, to):
        return pltpu.make_async_remote_copy(
            src_ref=source, dst_ref=target, send_sem=sems.at[(0, *at)], recv_sem=sems.at[(1, *at)], **to
        )

    def ref(kind, k):
        return getattr(r, kind + "_" + GRADS[k])

    def near_copy(k, x):
        return copy(
            ref("g", k).at[x * 2 + 1 - core], ref("near", k).at[x], r.near_sem, (k, x), at_shard(partner)
        )

    def far_copy(k, by):
        source = ref("sum", k).at[lax.rem(chip + by, chips)]
        return copy(source, ref("far", k).at[by - 1], r.far_sem, (k, by), at_shard(others[by - 1]))

    def part_copy(k, by):
        to = ring[by - 1]
        return copy(
            ref("near", k).at[0, to], ref("part", k).at[by], r.part_sem, (k, by), at_seq(to)
        )

    def last_copy(k, by):
        held = ref("last", k).at[me]
        return copy(held, held, r.last_sem, (k, by), at_seq(ring[by - 1]))

    def pair_refs(k):
        return (r.sub_early, r.early_in) if GRADS[k] == "early" else (r.sub_other, r.other_in)

    def pair_copy(k, by, at):
        source, target = pair_refs(k)
        to = anywhere(every[by], targets[0])
        return copy(source, target.at[at, me], r.pair_sem, (k - 4, at, by), to)

    def near_send(k):
        for x in range(chips):
            near_copy(k, x).start()

    def far_send(k):
        for x in range(chips):
            near_copy(k, x).wait_recv()
        for by in [*range(1, chips), 0]:
            x = lax.rem(chip + by, chips)
            ref("sum", k)[x] = (
                ref("g", k)[x * 2 + core].astype(F32) + ref("near", k)[x].astype(F32)
            ).astype(BF16)
            if by:
                far_copy(k, by).start()

    def part_send(k):
        total = ref("sum", k)[chip].astype(F32)
        for by in range(1, chips):
            far_copy(k, by).wait_recv()
            total = total + ref("far", k)[by - 1].astype(F32)
        ref("near", k)[0] = total.astype(BF16)
        for by in range(1, chips):
            far_copy(k, by).wait_send()
        for by in range(1, spans):
            part_copy(k, by).start()

    def last_send(k):
        total = ref("near", k)[0, me].astype(F32)
        for by in range(1, spans):
            part_copy(k, by).wait_recv()
            total = total + ref("part", k)[by].astype(F32)
        if k == SMALL:
            ref("last", k)[me] = total.astype(BF16)
            for by in range(1, spans):
                last_copy(k, by).start()
            return
        source, target = pair_refs(k)
        source[...] = total.astype(BF16)
        for by in range(spans):
            to_owner(by == 0, targets[0], pair_copy(k, by, parity), lambda c: c.start())

        @pl.when(targets[0] == shard)
        def _():
            target[parity, me] = source[...]

    def to_owner(same, to, made, act):
        if same:
            pl.when(to != shard)(lambda: act(made))
        else:
            act(made)

    inner = spans // OUTER
    low_me, high_me = lax.rem(me, inner), lax.div(me, inner)
    lows = [lax.rem(low_me + by, inner) for by in range(inner)]
    highs = [lax.rem(high_me + by, OUTER) for by in range(OUTER)]
    own_part = low_me * OUTER + high_me
    middle_at = (inner - 1) * OUTER
    parity = lax.rem(shard, 2)

    def inner_copy(k, by):
        return copy(
            ref("near", k).at[0, pl.ds(lows[by] * OUTER, OUTER)],
            ref("part", k).at[pl.ds((by - 1) * OUTER, OUTER)],
            r.inner_sem,
            (k, 0, by),
            at_seq(high_me * inner + lows[by]),
        )

    def outer_copy(k, by):
        return copy(
            ref("part", k).at[middle_at + highs[by]],
            ref("part", k).at[spans + by - 1],
            r.outer_sem,
            (k, 0, by),
            at_seq(highs[by] * inner + low_me),
        )

    def outer_last(k, by):
        held = ref("last", k).at[own_part]
        return copy(held, held, r.outer_sem, (k, 1, by), at_seq(highs[by] * inner + low_me))

    def inner_last(k, by):
        held = ref("last", k).at[pl.ds(low_me * OUTER, OUTER)]
        return copy(held, held, r.inner_sem, (k, 1, by), at_seq(high_me * inner + lows[by]))

    def late_outer(by, at):
        return copy(
            r.sub_late,
            r.pair_in.at[at, own_part],
            r.late_outer_sem,
            (at, by),
            anywhere(highs[by] * inner + low_me, targets[1]),
        )

    def late_inner(by, at):
        held = r.pair_in.at[at, pl.ds(low_me * OUTER, OUTER)]
        to = at_seq(high_me * inner + lows[by])
        return copy(held, held, r.late_inner_sem, (at, by), to)

    def inner_send(k):
        total = ref("sum", k)[chip].astype(F32)
        for by in range(1, chips):
            far_copy(k, by).wait_recv()
            total = total + ref("far", k)[by - 1].astype(F32)
        ref("near", k)[0] = total.astype(BF16)
        for by in range(1, inner):
            inner_copy(k, by).start()

    def outer_send(k):
        total = ref("near", k)[0, pl.ds(low_me * OUTER, OUTER)].astype(F32)
        for by in range(1, inner):
            inner_copy(k, by).wait_recv()
            total = total + ref("part", k)[(by - 1) * OUTER : by * OUTER].astype(F32)
        ref("part", k)[middle_at : middle_at + OUTER] = total.astype(BF16)
        for by in range(1, OUTER):
            outer_copy(k, by).start()

    def outer_back(k):
        total = ref("part", k)[middle_at + high_me].astype(F32)
        for by in range(1, OUTER):
            outer_copy(k, by).wait_recv()
            total = total + ref("part", k)[spans + by - 1].astype(F32)
        if k != 3:
            ref("last", k)[own_part] = total.astype(BF16)
            for by in range(1, OUTER):
                outer_last(k, by).start()
            return
        r.sub_late[...] = total.astype(BF16)
        for by in range(OUTER):
            to_owner(by == 0, targets[1], late_outer(by, parity), lambda c: c.start())

        @pl.when(targets[1] == shard)
        def _():
            r.pair_in[parity, own_part] = r.sub_late[...]

    def inner_back(k):
        if k != 3:
            for by in range(1, OUTER):
                outer_last(k, by).wait_recv()
            for by in range(1, inner):
                inner_last(k, by).start()
            return

        @pl.when(mine == 1)
        def _():
            for at in range(2):
                for by in range(OUTER):
                    to_owner(by == 0, first_piece + at, late_outer(by, at), lambda c: c.wait_recv())
                for by in range(1, inner):
                    late_inner(by, at).start()

    def finish(k):
        for x in range(chips):
            near_copy(k, x).wait_send()
        if k < 4:
            for by in range(1, chips):
                far_copy(k, by).wait_send()
            for by in range(1, inner):
                inner_copy(k, by).wait_send()
            for by in range(1, OUTER):
                outer_copy(k, by).wait_send()
        else:
            for by in range(1, spans):
                part_copy(k, by).wait_send()
        if k < 3:
            for by in range(1, OUTER):
                outer_last(k, by).wait_send()
            for by in range(1, inner):
                inner_last(k, by).wait()
        elif k == 3:
            for by in range(OUTER):
                to_owner(by == 0, targets[1], late_outer(by, parity), lambda c: c.wait_send())

            @pl.when(mine == 1)
            def _():
                for at in range(2):
                    for by in range(1, inner):
                        late_inner(by, at).wait()

        elif k == SMALL:
            for by in range(1, spans):
                last_copy(k, by).wait()
        else:
            for by in range(spans):
                to_owner(by == 0, targets[0], pair_copy(k, by, parity), lambda c: c.wait_send())

            @pl.when(mine == 0)
            def _():
                for at in range(2):
                    for by in range(spans):
                        made = pair_copy(k, by, at)
                        to_owner(by == 0, first_piece + at, made, lambda c: c.wait_recv())

    def put(k, piece, value):
        size = value.shape[0] // spans
        for j in range(spans):
            ref("g", k)[piece, j] = value[j * size : (j + 1) * size].astype(BF16)

    loaded("context_send")
    head = lax.div(me, ratio)

    def context_copy(t, by, to):
        return copy(r.context_send.at[t], r.context.at[head], r.context_sem, (by,), at_seq(to))

    for t in range(blocks):
        i = t * ratio + sub
        by = lax.rem(i - me + spans, spans)

        @pl.when(i != me)
        def _():
            context_copy(t, by, i).start()

        @pl.when(i == me)
        def _():
            r.context[head] = r.context_send[t]

    low = lane_low(rows)
    half_low = lane_low(half)

    def unpacked(source, pair):
        even, odd = source[2 * pair].astype(F32), source[2 * pair + 1].astype(F32)
        first = jnp.where(half_low, even, pltpu.roll(odd, HEAD_DIM, 1))
        second = jnp.where(half_low, pltpu.roll(even, HEAD_DIM, 1), odd)
        quarter = half // 2
        return jnp.concatenate(
            [first[:quarter], second[:quarter], first[quarter:], second[quarter:]], axis=0
        )

    dqs, dks, dvs = [], [], []
    for pair in range(HEADS // 2):
        dkv = [
            sum(r.dkv_in[(2 * pair + odd) * ratio + part].astype(F32) for part in range(ratio))
            for odd in range(2)
        ]
        dqs.append(unpacked(r.dq_in, pair))
        dks.append(jnp.where(low, dkv[0], pltpu.roll(dkv[1], HEAD_DIM, 1)))
        dvs.append(jnp.where(low, pltpu.roll(dkv[0], HEAD_DIM, 1), dkv[1]))
    dqkv = jnp.concatenate(dqs + dks + dvs, axis=1).astype(BF16)
    loaded("x1", "gains", "wh_all", "dout")
    for name in late + last:
        loads[name].start()
    x1 = r.x1[...]
    inverse = norm(x1)
    normal = x1 * inverse
    gain = r.gains[1:2, :]
    xn2 = (normal * gain).astype(BF16)
    wide = 3 * D // shards
    dxn2 = jnp.zeros((rows, D), F32)
    for s in range(shards):
        piece = dqkv[:, s * wide : (s + 1) * wide]
        put(0, s, dot_tn(xn2, piece))
        dxn2 = dxn2 + dot_nt(piece, r.wh_all[s])
    near_send(0)
    attention_gain = jnp.sum(dxn2 * normal, axis=0, keepdims=True)
    e2 = dxn2 * gain
    dx1 = r.dout[...].astype(F32) + inverse * (
        e2 - normal * jnp.mean(e2 * normal, axis=-1, keepdims=True)
    )
    r.dx1[...] = dx1
    dmixed = dx1.astype(BF16)
    loaded("gated", "wo_all")
    for s in range(shards):
        put(1, s, dot_tn(r.gated[:, s * width : (s + 1) * width], dmixed))
        r.dys[:, s * width : (s + 1) * width] = dot_nt(dmixed, r.wo_all[s])
    near_send(1)
    far_send(0)
    loaded("zgate", "yfull", "u", "x")

    def gate_step(pair, total):
        at = pl.ds(pl.multiple_of(pair * 2 * CHUNKS, 2 * CHUNKS), 2 * CHUNKS)
        dgated = r.dys[at, :].astype(BF16).astype(F32)
        gate = r.zgate[at, :]
        s = jax.nn.sigmoid(gate)
        dys = dgated * (gate * s)
        r.dys[at, :] = dys
        r.dzgate[at, :] = (dgated * r.yfull[at, :] * (s * (1.0 + gate * (1.0 - s)))).astype(BF16)
        return total + dys * r.u[at, :].astype(F32)

    total = lax.fori_loop(0, steps // 2, gate_step, jnp.zeros((2 * CHUNKS, DI), F32), unroll=2)
    r.small[SKIP : SKIP + 1, :] = jnp.sum(total, axis=0, keepdims=True)
    far_send(1)
    x = r.x[...]
    inverse_one = norm(x)
    normal_one = x * inverse_one
    gain_one = r.gains[0:1, :]
    xn1 = (normal_one * gain_one).astype(BF16)
    for s in range(shards):
        put(3, s, dot_tn(xn1, r.dzgate[:, s * width : (s + 1) * width]))
    near_send(3)
    loaded("wm_all", "packed", "cut", "cx", "totals", "span_totals")
    spread_decay(r.packed, r.amat, r.spread)

    def state_copy(by, at):
        to = lax.rem(me - by + spans, spans)
        return copy(
            r.grad_send.at[at], r.grads_in.at[me, at], r.state_sem, (by, at), at_seq(to)
        )

    def pair_step(pair, carry):
        for odd in range(2):
            lanes = lanes_of(pair * 2 + odd)
            amat = [r.spread[st * CHUNKS : (st + 1) * CHUNKS, lanes] for st in range(STATE)]

            def step_fn(turn, grads):
                step = steps - 1 - turn
                cut = r.cut[tile(step), lanes]
                dys = r.dys[tile(step), lanes]
                return tuple(
                    jnp.exp2(cut * amat[st]) * (grads[st] + dys * r.cx[tile(step), column(st)])
                    for st in range(STATE)
                )

            grads = lax.fori_loop(
                0, steps, step_fn, (jnp.zeros((CHUNKS, LANES), F32),) * STATE, unroll=8
            )
            for st in range(STATE):
                r.ends[st, :, lanes] = grads[st]
        lanes = pl.ds(pl.multiple_of(pair * 2 * LANES, 2 * LANES), 2 * LANES)
        amat = r.amat[:, lanes]
        state = jnp.zeros((STATE, 2 * LANES), F32)
        for k in reversed(range(CHUNKS)):
            state = jnp.exp2(amat * r.totals[k : k + 1, lanes]) * state + r.ends[:, k, lanes]
        r.grad_send[pair] = state.astype(BF16)
        for by in range(1, spans):

            @pl.when(me - by >= 0)
            def _():
                state_copy(by, pair).start()

        pl.when(pair == 0)(lambda: far_send(3))
        return carry

    lax.fori_loop(0, GROUPS_CH // 2, pair_step, 0)
    for h in range(HEADS):
        came = h * ratio + sub
        by = lax.rem(me - came + spans, spans)

        @pl.when(came != me)
        def _():
            context_copy(0, by, came).wait_recv()

    context = jnp.concatenate([unpacked(r.context, p) for p in range(HEADS // 2)], axis=1)
    context = context.astype(BF16)
    short = D // shards
    x2 = x1
    for s in range(shards):
        part = context[:, s * short : (s + 1) * short]
        x2 = x2 + dot_nn(part, r.wm_all[s])
        put(2, s, dot_tn(part, r.dout[...]))
    near_send(2)
    given = dot_tn(pick_rows(r.index, me, rows, steps), x2.astype(BF16))
    share = rows // spans
    for j in range(spans):
        r.given[j] = given[j * share : (j + 1) * share].astype(BF16)

    def given_copy(by):
        to = ring[by - 1]
        return copy(r.given.at[to], r.output.at[me], r.given_sem, (by,), at_seq(to))

    r.output[me] = r.given[me]

    loaded("init", "delta", "du", "bx", "xdbl", *last)
    r.db[...] = jnp.zeros_like(r.db)
    r.dc[...] = jnp.zeros_like(r.dc)
    for by in range(1, spans):
        for pair in range(GROUPS_CH // 2):

            @pl.when(me - by >= 0)
            def _():
                state_copy(by, pair).wait_send()

            @pl.when(me + by < spans)
            def _():
                state_copy(by, pair).wait_recv()

    for by in range(1, spans):
        given_copy(by).start()
    amat = r.amat[...]

    def chain(turn, state):
        k = spans - 1 - turn
        decay = jnp.exp2(amat * total_row(r.span_totals[k]))
        came = jnp.concatenate(
            [r.grads_in[k, g].astype(F32) for g in range(GROUPS_CH // 2)], axis=1
        )
        return decay * state + came

    state = lax.fori_loop(0, spans - 1 - me, chain, jnp.zeros((STATE, DI), F32))
    for k in reversed(range(CHUNKS)):
        r.arrive[:, k, :] = state
        if k:
            state = jnp.exp2(amat * r.totals[k : k + 1, :]) * state + r.ends[:, k, :]
    eight = STATE // 2

    def sum_of(terms):
        while len(terms) > 1:
            terms = [a + b for a, b in zip(terms[::2], terms[1::2])]
        return terms[0]

    def kept_at(step, i):
        return pl.ds(pl.multiple_of(step * (eight * CHUNKS) + i * CHUNKS, CHUNKS), CHUNKS)

    stages = {
        0: ((far_send, 2), (inner_send, 0),),
        2: ((inner_send, 1),),
        4: ((outer_send, 0),),
        6: ((inner_send, 3),),
        7: ((outer_send, 1),),
    }

    def run(todo):
        for stage, k in todo:
            stage(k)

    def group_step(group, carry):
        lanes = lanes_of(group)
        for part in range(2):
            states = range(part * eight, (part + 1) * eight)
            amat_g = [r.spread[st * CHUNKS : (st + 1) * CHUNKS, lanes] for st in states]

            def forward(step, held):
                cut = r.cut[tile(step), lanes]
                drive = r.du[tile(step), lanes]
                out = []
                for i, st in enumerate(states):
                    decay = jnp.exp2(cut * amat_g[i])
                    kept = decay * held[i]
                    new = kept + drive * r.bx[tile(step), column(st)]
                    r.decay[kept_at(step, i), :] = decay
                    r.held[kept_at(step, i), :] = kept
                    r.state[kept_at(step, i), :] = new
                    out.append(new)
                return tuple(out)

            lax.fori_loop(
                0, steps, forward, tuple(r.init[st, :, lanes] for st in states), unroll=8
            )

            def backward(turn, held):
                grads, sums = held
                step = steps - 1 - turn
                delta = r.delta[tile(step), lanes]
                drive = r.du[tile(step), lanes]
                dys = r.dys[tile(step), lanes]
                new, totals, by_b, by_a = [], [], [], []
                for i, st in enumerate(states):
                    at = tile(step)
                    grad = grads[i] + dys * r.cx[at, column(st)]
                    new.append(r.decay[kept_at(step, i), :] * grad)
                    through = grad * r.held[kept_at(step, i), :]
                    totals.append(sums[i] + through * delta)
                    by_a.append(amat_g[i] * through)
                    by_b.append(grad * r.bx[at, column(st)])
                    r.dc[at, column(st)] += r.state[kept_at(step, i), :] * dys
                    r.db[at, column(st)] += grad * drive
                if part:
                    r.bgrad[tile(step), lanes] += sum_of(by_b)
                    r.adelta[tile(step), lanes] += sum_of(by_a)
                else:
                    r.bgrad[tile(step), lanes] = sum_of(by_b)
                    r.adelta[tile(step), lanes] = sum_of(by_a)
                return (tuple(new), tuple(totals))

            _, sums = lax.fori_loop(
                0,
                steps,
                backward,
                (
                    tuple(r.arrive[st, :, lanes] for st in states),
                    (jnp.zeros((CHUNKS, LANES), F32),) * eight,
                ),
                unroll=8,
            )
            for i, st in enumerate(states):
                row = jnp.sum(sums[i], axis=0, keepdims=True)
                amat_row = amat_g[i][0:1, :] * math.log(2.0)
                r.small[DEC + st : DEC + st + 1, lanes] = row * amat_row
        for at, todo in stages.items():
            pl.when(group == at)(functools.partial(run, todo))
        return carry

    lax.fori_loop(0, GROUPS_CH, group_step, 0)
    small = r.packed[DEC:PACK, :].astype(F32)
    taps = small[TAPS - DEC : TAPS - DEC + CONV, :]
    skip = small[SKIP - DEC : SKIP - DEC + 1, :]

    def delta_step(step, total):
        at = tile(step)
        bgrad = r.bgrad[at, :]
        delta = r.delta[at, :]
        u = r.conv[at, :]
        u = (u * jax.nn.sigmoid(u)).astype(BF16).astype(F32)
        ddelta = u * bgrad + r.adelta[at, :] * math.log(2.0)
        dtpre = (ddelta * (1.0 - jnp.exp(-delta))).astype(BF16).astype(F32)
        r.adelta[at, :] = dtpre
        r.bgrad[at, :] = r.dys[at, :] * skip + delta * bgrad
        return total + dtpre

    total = lax.fori_loop(0, steps, delta_step, jnp.zeros((CHUNKS, DI), F32), unroll=2)
    run(((inner_send, 2),))
    r.small[STEPB : STEPB + 1, :] = jnp.sum(total, axis=0, keepdims=True)
    r.small[GAINS:, :] = jnp.zeros((PACK - GAINS, DI), F32)
    dtpre = r.adelta[...].astype(BF16)
    steplow = r.xdbl[:, 0:RANK].astype(BF16)
    r.small[STEP : STEP + RANK, :] = dot_tn(steplow, dtpre)
    r.dxdbl[:, 0:RANK] = dot_nt(dtpre, r.packed[STEP : STEP + RANK, :])
    for part in range(4):
        at = slice(part * rows // 4, (part + 1) * rows // 4)
        r.dxdbl[at, RANK : RANK + STATE] = gather_columns(r.db[at, :])
        r.dxdbl[at, RANK + STATE :] = gather_columns(r.dc[at, :])
    run(((outer_back, 0), (outer_send, 3),))
    dxdbl = r.dxdbl[...].astype(BF16)
    r.small[SEL : SEL + STEP, :] = dot_tn(dxdbl, r.u[...])
    r.bgrad[...] += dot_nn(dxdbl, r.packed[SEL : SEL + STEP, :])
    r.dext[...] = jnp.zeros_like(r.dext)
    r.spill[...] = jnp.zeros_like(r.spill)

    @pl.when(me == spans - 1)
    def _():
        r.spill_in[...] = jnp.zeros_like(r.spill_in)

    def conv_steps(first_step, last_step, ranges, totals):
        def one(step, totals):
            at = tile(step)
            places = lax.broadcasted_iota(jnp.int32, (CHUNKS, 1), 0) * steps + step + me * rows
            first = start_of(places, starts)
            inside = [places - (CONV - 1) + k >= first for k in range(CONV)]
            out = []
            for lanes, sums in zip(ranges, totals):
                dconv = r.bgrad[at, lanes] * silu_slope(r.conv[at, lanes])
                new = []
                for k in range(CONV):
                    to = pl.ds(pl.multiple_of((step + k) * CHUNKS, CHUNKS), CHUNKS)
                    counted = jnp.where(inside[k], dconv, 0.0)
                    new.append(sums[k] + counted * r.ext[to, lanes])
                    r.dext[to, lanes] += taps[k : k + 1, lanes] * counted
                out.append(tuple(new) + (sums[CONV] + dconv,))
            return tuple(out)

        return lax.fori_loop(first_step, last_step, one, totals, unroll=2)

    quarter = width // 2
    halves = [
        [slice((2 * o + part) * width, (2 * o + part + 1) * width) for o in range(chips)]
        for part in range(2)
    ]
    zero = jnp.zeros((CHUNKS, width), F32)
    firsts = [
        conv_steps(0, CONV, ranges, tuple((zero,) * (CONV + 1) for _ in ranges))
        for ranges in halves
    ]
    for k in range(CONV - 1):
        r.spill[k : k + 1, :] = r.dext[k * CHUNKS : k * CHUNKS + 1, :]
    behind = lax.rem(me + spans - 1, spans)
    spill = copy(r.spill, r.spill_in, r.spill_sem, (), at_seq(behind))

    @pl.when(me > 0)
    def _():
        spill.start()

    chunk = lax.broadcasted_iota(jnp.int32, (CHUNKS, width), 0)
    dxin = []
    for part, ranges in enumerate(halves):
        totals = conv_steps(CONV, steps, ranges, firsts[part])
        if part:
            far_send(4)
            run(((outer_send, 2),))
        else:
            run(((outer_back, 1),))

            @pl.when(me > 0)
            def _():
                spill.wait_send()

            @pl.when(me < spans - 1)
            def _():
                spill.wait_recv()

        for o, lanes in enumerate(ranges):
            for k in range(CONV):
                r.small[TAPS + k : TAPS + k + 1, lanes] = jnp.sum(
                    totals[o][k], axis=0, keepdims=True
                )
            r.small[BIAS : BIAS + 1, lanes] = jnp.sum(totals[o][CONV], axis=0, keepdims=True)
            for k in range(CONV - 1):
                block = r.dext[k * CHUNKS : (k + 1) * CHUNKS, lanes]
                edge = (steps - CONV + 1 + k) * CHUNKS + EDGE
                moved = pltpu.roll(block, CHUNKS - 1, 0)
                came = jnp.broadcast_to(r.spill_in[k : k + 1, lanes], (CHUNKS, width))
                r.dext[edge : edge + CHUNKS, lanes] += jnp.where(
                    chunk < CHUNKS - 1, moved, came
                )
            piece = r.dext[EDGE:, lanes].astype(BF16)
            dxin.append(piece)
            grad = dot_tn(xn1, piece)
            for parity_at in range(2):
                put(4 + part, 2 * o + parity_at, grad[:, parity_at * quarter : (parity_at + 1) * quarter])
        near_send(4 + part)
    run(((inner_back, 0), (outer_back, 3),))
    wide = 2 * width
    dxn1 = jnp.zeros((rows, D), F32)
    for s in range(shards):
        if s < chips:
            piece = jnp.concatenate([dxin[s], dxin[chips + s]], axis=1)
        else:
            at = (s - chips) * wide
            piece = r.dzgate[:, at : at + wide]
        dxn1 = dxn1 + dot_nt(piece, r.wi_all[s])
    mixer_gain = jnp.sum(dxn1 * normal_one, axis=0, keepdims=True)
    for s in range(shards):
        at = s * width
        gains = slice(s * short, (s + 1) * short)
        r.small[GAINS : GAINS + 1, at : at + short] = mixer_gain[:, gains]
        r.small[GAINS : GAINS + 1, at + short : at + 2 * short] = attention_gain[:, gains]
    for s in range(shards):
        put(SMALL, s, r.small[:, s * width : (s + 1) * width])
    near_send(SMALL)
    far_send(5)
    far_send(SMALL)
    run(((inner_back, 1), (outer_back, 2),))
    part_send(4)
    e1 = dxn1 * gain_one
    dx = r.dx1[...] + inverse_one * (
        e1 - normal_one * jnp.mean(e1 * normal_one, axis=-1, keepdims=True)
    )
    r.dx1[...] = dx
    for part in range(D // LANES):
        lanes = slice(part * LANES, (part + 1) * LANES)
        for step in range(steps):
            r.row[pl.ds(step, CHUNKS, stride=steps), :] = r.dx1[
                step * CHUNKS : (step + 1) * CHUNKS, lanes
            ]
        r.token_grad[:, lanes] = r.row[...]
    part_send(5)
    part_send(SMALL)
    run(((inner_back, 3), (inner_back, 2),))
    last_send(4)
    last_send(5)
    last_send(SMALL)
    for k in (0, 1, 2, 3):
        finish(k)
    for by in range(1, spans):
        given_copy(by).wait()
    for t in range(blocks):
        i = t * ratio + sub
        by = lax.rem(i - me + spans, spans)

        @pl.when(i != me)
        def _():
            context_copy(t, by, i).wait_send()

    finish(SMALL)
    finish(4)
    finish(5)


def final_kernel(*refs):
    r = Refs(tuple(k + "_in" for k in BACKWARD_OUT) + FINAL_OUT, refs)

    def whole(source):
        return jnp.concatenate([source[j].astype(F32) for j in range(source.shape[0])], axis=0)

    r.output[...] = r.output_in[...]
    r.token_grad[...] = r.token_grad_in[...]
    r.heads_grad[...] = whole(r.last_heads_in)
    r.output_grad[...] = whole(r.last_out_in)
    r.merge_grad[...] = whole(r.last_merge_in)
    small = whole(r.last_small_in)
    short = r.mixer_grad.shape[1]
    width = r.taps_grad.shape[1]
    r.select_grad[...] = small[SEL : SEL + STEP]
    r.stepw_grad[...] = small[STEP : STEP + RANK]
    r.decay_grad[...] = small[DEC : DEC + STATE]
    r.taps_grad[...] = small[TAPS : TAPS + CONV]
    r.bias_grad[...] = small[BIAS : BIAS + 1]
    r.stepb_grad[...] = small[STEPB : STEPB + 1]
    r.skip_grad[...] = small[SKIP : SKIP + 1]
    r.mixer_grad[...] = small[GAINS : GAINS + 1, :short]
    r.attention_grad[...] = small[GAINS : GAINS + 1, short:]
    late = jnp.concatenate([whole(r.pair_in_in.at[at]) for at in range(2)], axis=1)
    early = jnp.concatenate(
        [whole(source.at[at]) for source in (r.early_in_in, r.other_in_in) for at in range(2)], axis=1
    )
    inner_half = lax.axis_index("shard") < lax.axis_size("shard") // 2
    r.input_grad[...] = jnp.where(inner_half, early, late)


def shape(*dims, kind=F32):
    return jax.ShapeDtypeStruct(dims, kind)


def vmem(*dims, kind=F32):
    return pltpu.VMEM(dims, kind)


def per_device(
    tokens,
    cotangent,
    positions,
    lengths,
    mixer_gain,
    input_weight,
    kernel_weight,
    kernel_bias,
    select_weight,
    step_weight,
    step_bias,
    decay_log,
    skip_scale,
    output_weight,
    attention_gain,
    heads_weight,
    merge_weight,
):
    spans = lax.axis_size("seq")
    shards = lax.axis_size("shard")
    rows = tokens.shape[1]
    steps = rows // CHUNKS
    share = rows // spans
    nseq = lengths.shape[1]
    ratio = spans // HEADS
    part = rows // ratio
    width = DI // shards

    index = positions
    dma = pltpu.SemaphoreType.DMA
    spread = [vmem(STATE, DI), vmem(STATE * CHUNKS, DI)]
    columns = vmem(rows, STATE * LANES)
    plane = vmem(rows, DI)
    gain_len = D // shards
    halves = GROUPS_CH // 2
    weights = [(D, 2 * width), (width, D), (D, 3 * D // shards), (gain_len, D)]
    half = rows // 2
    blocks = spans // ratio
    slots = 2 if ratio == 1 else 1
    kept = (
        [shape(rows, D)]
        + [shape(shards, *w, kind=BF16) for w in weights]
        + [
            shape(PACK, DI, kind=BF16),
            shape(CHUNKS, D),
            shape(spans, GROUPS_CH, LANES),
            shape(EDGE + rows, DI),
            shape(rows, DI),
            shape(rows, DI),
            shape(rows, DI, kind=BF16),
            shape(rows, DI),
            shape(rows, STEP),
            shape(CHUNKS, DI),
            shape(rows, DI),
            shape(rows, DI, kind=BF16),
            shape(rows, D),
            shape(STATE, CHUNKS, DI),
            shape(rows, D, kind=BF16),
            shape(rows, STATE * LANES),
            shape(rows, STATE * LANES),
            shape(rows, DI),
            shape(rows, DI),
            shape(blocks, half, LANES, kind=BF16),
        ]
    )
    back = [shape(HEADS, half, LANES, kind=BF16), shape(spans, rows, LANES, kind=BF16)]
    inputs = [
        lengths[0],
        tokens[0],
        cotangent[0].reshape(spans, share, D),
        index,
        mixer_gain[None],
        attention_gain[None],
        select_weight.T,
        step_weight,
        decay_log.T,
        kernel_weight,
        kernel_bias[None],
        step_bias[None],
        skip_scale[None],
        input_weight,
        output_weight,
        heads_weight,
        merge_weight,
    ]
    anyspace = pl.BlockSpec(memory_space=pl.ANY)
    outs = pl.pallas_call(
        functools.partial(forward_kernel, steps, nseq, shards, spans),
        out_shape=kept + back,
        in_specs=[SMEM] + [VMEM] * (len(inputs) - 5) + [anyspace] * 4,
        out_specs=[anyspace] * len(kept) + [VMEM] * len(back),
        scratch_shapes=[vmem(*k.shape, kind=k.dtype) for k in kept]
        + [
            vmem(spans, share, D, kind=BF16),
            vmem(spans, halves, STATE, 2 * LANES, kind=BF16),
            vmem(STATE, CHUNKS, DI),
            vmem(rows, LANES),
            vmem(PACK, width),
        ]
        + [vmem(*w, kind=BF16) for w in weights]
        + [
            vmem(PACK, width, kind=BF16),
            vmem(2 * CHUNKS, gain_len, kind=BF16),
            vmem(shards, PACK, width, kind=BF16),
            vmem(shards, 2 * CHUNKS, gain_len, kind=BF16),
            vmem(2 * CHUNKS, D, kind=BF16),
            vmem(halves, STATE, 2 * LANES, kind=BF16),
            vmem(GROUPS_CH, LANES),
        ]
        + spread
        + [
            vmem(HEADS, half, LANES, kind=BF16),
            vmem(HEADS, half, LANES, kind=BF16),
            vmem(HEADS, rows, LANES, kind=BF16),
            vmem(blocks, half, LANES, kind=BF16),
            vmem(blocks, half, LANES, kind=BF16),
            vmem(spans * rows, LANES, kind=BF16),
            vmem(spans, LANES, rows, kind=BF16),
            vmem(slots, spans, rows, rows),
            vmem(slots, spans, rows, rows),
            vmem(spans * rows, LANES),
            vmem(blocks, half, LANES, kind=BF16),
            vmem(spans, rows, LANES, kind=BF16),
            vmem(rows, rows),
            dma((2, 6, shards - 1)),
            dma((2, max(shards // 2 - 1, 1), spans)),
            dma((2, spans)),
            dma((2,)),
            dma((2, spans, halves)),
        ]
        + [dma((2, spans)), dma((2, spans, 2)), dma((2, spans)), dma((2, spans, 2))]
        + [dma((2, spans))] * 2
        + [dma((len(kept),))]
        + [vmem(*w) for w in weights]
        + [dma((4,))],
        compiler_params=params(collective_id=0, has_side_effects=True),
        name="forward",
    )(*inputs)
    saved, back = outs[: len(kept)], outs[len(kept) :]
    parts = {
        "heads": (D // spans, 3 * D // shards),
        "out": (width // spans, D),
        "merge": (gain_len // spans, D),
        "late": (D // spans, width),
        "early": (D // spans, width // 2),
        "other": (D // spans, width // 2),
        "small": (PACK // spans, width),
    }
    chips = shards // 2
    sizes = [(spans, *parts[k]) for k in GRADS]
    count = len(GRADS)
    summed = [
        shape(spans, share, D, kind=BF16),
        shape(rows, D),
        shape(spans, *parts["heads"], kind=BF16),
        shape(spans, *parts["out"], kind=BF16),
        shape(spans, *parts["merge"], kind=BF16),
        shape(spans, *parts["small"], kind=BF16),
        shape(2, spans, *parts["late"], kind=BF16),
        shape(2, spans, *parts["early"], kind=BF16),
        shape(2, spans, *parts["other"], kind=BF16),
    ]
    few = vmem(rows * STATE // 2, LANES)
    state = vmem(STATE, CHUNKS, DI)
    summed = pl.pallas_call(
        functools.partial(backward_kernel, steps, nseq, shards, spans),
        out_shape=summed,
        in_specs=[SMEM] + [VMEM] * 3 + [anyspace] * len(kept),
        out_specs=[VMEM] * len(summed),
        scratch_shapes=[vmem(*k.shape, kind=k.dtype) for k in kept]
        + [
            vmem(HEADS, half, LANES, kind=BF16),
            vmem(spans, share, D, kind=BF16),
            vmem(rows, D),
            plane,
            vmem(rows, DI, kind=BF16),
            state,
            vmem(halves, STATE, 2 * LANES, kind=BF16),
            vmem(spans, halves, STATE, 2 * LANES, kind=BF16),
            columns,
            columns,
            few,
            few,
            few,
            plane,
            plane,
            state,
            vmem(rows, STEP),
            vmem(EDGE + rows, DI),
            vmem(CHUNKS, DI),
            vmem(CHUNKS, DI),
            vmem(PACK, DI),
            vmem(rows, LANES),
        ]
        + spread
        + [
            vmem(*parts["late"], kind=BF16),
            vmem(*parts["early"], kind=BF16),
            vmem(*parts["other"], kind=BF16),
        ]
        + [vmem(shards, *k, kind=BF16) for k in sizes]
        + [vmem(chips, *k, kind=BF16) for k in sizes] * 2
        + [vmem(max(chips - 1, 1), *k, kind=BF16) for k in sizes]
        + [vmem(spans + OUTER - 1, *k[1:], kind=BF16) for k in sizes]
        + [
            dma((len(kept),)),
            dma((2, spans)),
            dma((2, spans)),
            dma((2, spans, halves)),
            dma((2,)),
            dma((2, count, chips)),
            dma((2, count, chips)),
            dma((2, count, spans)),
            dma((2, count, spans)),
            dma((2, 2, 2, spans)),
            dma((2, 4, 2, spans // OUTER)),
            dma((2, 4, 2, OUTER)),
            dma((2, 2, OUTER)),
            dma((2, 2, spans // OUTER)),
        ],
        compiler_params=params(collective_id=1, has_side_effects=True),
        name="backward",
    )(lengths[0], index, *back, *saved)
    results = pl.pallas_call(
        final_kernel,
        out_shape=[
            shape(rows, D, kind=BF16),
            shape(rows, D),
            shape(1, gain_len),
            shape(D, 2 * width),
            shape(CONV, width),
            shape(1, width),
            shape(STEP, width),
            shape(RANK, width),
            shape(1, width),
            shape(STATE, width),
            shape(1, width),
            shape(width, D),
            shape(1, gain_len),
            shape(D, 3 * D // shards),
            shape(gain_len, D),
        ],
        in_specs=[VMEM] * len(summed),
        out_specs=[VMEM] * len(FINAL_OUT),
        compiler_params=params(),
        name="final",
    )(summed[0].reshape(rows, D), *summed[1:])
    flat, turned = {2, 5, 8, 10, 12}, {6, 9}
    return tuple(
        v[None] if i < 2 else v.reshape(-1) if i in flat else v.T if i in turned else v
        for i, v in enumerate(results)
    )


def solution(mesh):
    return jax.shard_map(
        per_device,
        mesh=mesh,
        in_specs=(
            P("shard", "seq", None),
            P("shard", "seq", None),
            P("shard", None),
            P("shard", None),
            P("shard"),
            P(None, "shard"),
            P(None, "shard"),
            P("shard"),
            P("shard", None),
            P(None, "shard"),
            P("shard"),
            P("shard", None),
            P("shard"),
            P("shard", None),
            P("shard"),
            P(None, "shard"),
            P("shard", None),
        ),
        out_specs=(
            P("shard", "seq", None),
            P("shard", "seq", None),
            P("shard"),
            P(None, "shard"),
            P(None, "shard"),
            P("shard"),
            P("shard", None),
            P(None, "shard"),
            P("shard"),
            P("shard", None),
            P("shard"),
            P("shard", None),
            P("shard"),
            P(None, "shard"),
            P("shard", None),
        ),
        check_vma=False,
    )
```

```python
import functools
import math
from typing import Any, NamedTuple

import jax
import jax.numpy as jnp
from jax import lax
from jax.experimental import pallas as pl
from jax.experimental.pallas import tpu as pltpu
from jax.sharding import PartitionSpec as P

D = 512
DI = 1024
RANK = 32
HEADS = 8
STATE = 16
HEAD_DIM = 64
CONV = 4
CHUNKS = 8
LANES = 128
GROUPS_CH = DI // LANES
EDGE = (CONV - 1) * CHUNKS
OUTER = 4

SEL = 0
STEP = RANK + 2 * STATE
DEC = STEP + RANK
TAPS = DEC + STATE
BIAS = TAPS + CONV
STEPB = BIAS + 1
SKIP = STEPB + 1
GAINS = SKIP + 1
PACK = 128

EPS = 1e-05
NEG = -1e30
CUT = 1e30
F32 = jnp.float32
BF16 = jnp.bfloat16

VMEM = pl.BlockSpec(memory_space=pltpu.VMEM)
SMEM = pl.BlockSpec(memory_space=pltpu.SMEM)


def params(**more):
    return pltpu.CompilerParams(vmem_limit_bytes=62 << 20, **more)


def dot_nn(left, right):
    return lax.dot_general(left, right, (((1,), (0,)), ((), ())), preferred_element_type=F32)


def dot_nt(left, right):
    return lax.dot_general(left, right, (((1,), (1,)), ((), ())), preferred_element_type=F32)


def dot_tn(left, right):
    return lax.dot_general(left, right, (((0,), (0,)), ((), ())), preferred_element_type=F32)


def row_places(rows, steps):
    return (rows & (CHUNKS - 1)) * steps + (rows >> 3)


def starts_of(lengths_ref, nseq):
    starts = [jnp.int32(0)]
    for k in range(nseq - 1):
        starts.append(starts[-1] + lengths_ref[k])
    return starts


def start_of(places, starts):
    first = jnp.zeros_like(places)
    for start in starts[1:]:
        first = jnp.where(places >= start, start, first)
    return first


def begin_of(places, starts):
    found = places == starts[0]
    for start in starts[1:]:
        found = found | (places == start)
    return found


def norm(value):
    return lax.rsqrt(jnp.mean(value * value, axis=-1, keepdims=True) + EPS)


def silu_slope(value):
    s = jax.nn.sigmoid(value)
    return s * (1.0 + value * (1.0 - s))


def tile(step):
    return pl.ds(pl.multiple_of(step * CHUNKS, CHUNKS), CHUNKS)


def lanes_of(group):
    return pl.ds(pl.multiple_of(group * LANES, LANES), LANES)


def spread_decay(packed_ref, amat_ref, spread_ref):
    amat = -jnp.exp(packed_ref[DEC : DEC + STATE, :].astype(F32)) * math.log2(math.e)
    amat_ref[...] = amat
    for st in range(STATE):
        spread_ref[st * CHUNKS : (st + 1) * CHUNKS, :] = jnp.broadcast_to(
            amat[st : st + 1, :], (CHUNKS, DI)
        )


def column(st):
    return slice(st * LANES, (st + 1) * LANES)


def thirds(value):
    high = value.astype(BF16)
    rest = value - high.astype(F32)
    middle = rest.astype(BF16)
    return high, middle, (rest - middle.astype(F32)).astype(BF16)


def spread_columns(values):
    terms = jnp.concatenate([t.astype(F32) for t in thirds(values)], axis=1).astype(BF16)
    count = terms.shape[1]
    line = lax.broadcasted_iota(jnp.int32, (count, STATE * LANES), 0)
    lane = lax.broadcasted_iota(jnp.int32, (count, STATE * LANES), 1)
    chosen = (line & (STATE - 1)) == lax.div(lane, LANES)
    return dot_nn(terms, chosen.astype(F32).astype(BF16))


def gather_columns(value):
    line = lax.broadcasted_iota(jnp.int32, (STATE * LANES, STATE), 0)
    lane = lax.broadcasted_iota(jnp.int32, (STATE * LANES, STATE), 1)
    chosen = (lax.div(line, LANES) == lane).astype(F32).astype(BF16)
    return sum(dot_nn(term, chosen) for term in thirds(value)[:2])


def at_seq(index):
    return {"device_id": {"seq": index}, "device_id_type": pl.DeviceIdType.MESH}


def at_shard(index):
    return {"device_id": {"shard": index}, "device_id_type": pl.DeviceIdType.MESH}


def greet(peers):
    barrier = pltpu.get_barrier_semaphore()
    for peer in peers:
        pl.semaphore_signal(barrier, inc=1, **peer)
    pl.semaphore_wait(barrier, len(peers))


def shard_peers(shards):
    shard = lax.axis_index("shard")
    core, chip = lax.rem(shard, 2), lax.div(shard, 2)
    partner = chip * 2 + 1 - core
    others = [lax.rem(chip + by, shards // 2) * 2 + core for by in range(1, shards // 2)]
    return shard, core, chip, partner, others


class Refs:
    def __init__(self, names, refs):
        for name, ref in zip(names, refs, strict=True):
            setattr(self, name, ref)


class ForwardIn(NamedTuple):
    lengths: Any
    tokens: Any
    cot: Any
    index: Any
    mixer: Any
    attention: Any
    select: Any
    stepw: Any
    decay: Any
    taps: Any
    bias: Any
    stepb: Any
    skip: Any
    wi_arg: Any
    wo_arg: Any
    wh_arg: Any
    wm_arg: Any


FORWARD_IN = ForwardIn._fields
class Kept(NamedTuple):
    x: Any
    wi_all: Any
    wo_all: Any
    wh_all: Any
    wm_all: Any
    packed: Any
    gains: Any
    span_totals: Any
    ext: Any
    zgate: Any
    conv: Any
    u: Any
    delta: Any
    xdbl: Any
    totals: Any
    yfull: Any
    gated: Any
    x1: Any
    init: Any
    dout: Any
    bx: Any
    cx: Any
    cut: Any
    du: Any
    context_send: Any


KEPT = Kept._fields
FORWARD_OUT = tuple(k + "_out" for k in KEPT) + ("dq_in", "dkv_in")
class ForwardScratch(NamedTuple):
    given: Any
    states: Any
    ends: Any
    row: Any
    small: Any
    wi_send: Any
    wo_send: Any
    wh_send: Any
    wm_send: Any
    packed_send: Any
    gains_send: Any
    packed_all: Any
    gains_all: Any
    before: Any
    state_send: Any
    total_send: Any
    amat: Any
    spread: Any
    q_send: Any
    d_send: Any
    kv_send: Any
    q_in: Any
    d_in: Any
    kv_in: Any
    kvt: Any
    score: Any
    dprob: Any
    dkv: Any
    dq_send: Any
    dkv_send: Any
    causal: Any
    gather_sem: Any
    share_sem: Any
    cot_sem: Any
    edge_sem: Any
    state_sem: Any
    total_sem: Any
    q_sem: Any
    d_sem: Any
    kv_sem: Any
    dq_sem: Any
    dkv_sem: Any
    keep_sem: Any
    wi: Any
    wo: Any
    wh: Any
    wm: Any
    arg_sem: Any


FORWARD_SCRATCH = KEPT + ForwardScratch._fields


def forward_kernel(steps, nseq, shards, spans, *refs):
    r = Refs(FORWARD_IN + FORWARD_OUT + FORWARD_SCRATCH, refs)
    rows = steps * CHUNKS
    width = DI // shards
    me = lax.axis_index("seq")
    shard, core, chip, partner, others = shard_peers(shards)
    far = len(others)
    ring = [lax.rem(me + by, spans) for by in range(1, spans)]
    arguments = [
        pltpu.make_async_copy(source, target, r.arg_sem.at[i])
        for i, (source, target) in enumerate(
            ((r.wi_arg, r.wi), (r.wo_arg, r.wo), (r.wh_arg, r.wh), (r.wm_arg, r.wm))
        )
    ]
    for argument in arguments:
        argument.start()
    greet([at_shard(partner)] + [at_shard(o) for o in others] + [at_seq(to) for to in ring])

    def copy(source, target, sems, at, to):
        return pltpu.make_async_remote_copy(
            src_ref=source, dst_ref=target, send_sem=sems.at[(0, *at)], recv_sem=sems.at[(1, *at)], **to
        )

    sources = (r.wi_send, r.packed_send, r.gains_send, r.wo_send, r.wh_send, r.wm_send)
    wholes = (r.wi_all, r.packed_all, r.gains_all, r.wo_all, r.wh_all, r.wm_all)

    share = D // 2 // spans
    straight = D - share * spans

    def own_share(index):
        return pl.ds(pl.multiple_of(straight + index * share, share), share)

    def sent(k, i):
        if i == far:
            return copy(sources[k], wholes[k].at[shard], r.gather_sem, (k, i), at_shard(partner))
        source, target = sources[k], wholes[k].at[shard]
        if k == 0:
            source, target = source.at[0:straight], wholes[k].at[shard, 0:straight]
        return copy(source, target, r.gather_sem, (k, i), at_shard(others[i]))

    def shared(i):
        return copy(
            r.wi_send.at[own_share(me)],
            r.wi_all.at[shard, own_share(me)],
            r.share_sem,
            (i, 0),
            at_shard(others[i]),
        )

    def fanned(i, by):
        came = lax.rem(chip + far - i, far + 1) * 2 + core
        held = r.wi_all.at[came, own_share(me)]
        return copy(held, held, r.share_sem, (i, by), at_seq(ring[by - 1]))

    def passed(k, i):
        came = lax.rem(chip + far - i, far + 1) * 2 + core
        return copy(
            wholes[k].at[came], wholes[k].at[came], r.gather_sem, (k, far + 1 + i), at_shard(partner)
        )

    def spread(*which):
        for k in which:
            for i in range(far + 1):
                sent(k, i).start()
        for k in which:
            wholes[k][shard] = sources[k][...]

    def pass_on(*which):
        for i in range(far):
            for k in which:
                sent(k, i).wait_recv()
                passed(k, i).start()

    def finish(*which):
        for k in which:
            for i in range(far):
                sent(k, i).wait_send()
                passed(k, i).wait()
            sent(k, far).wait()

    arguments[0].wait()
    r.wi_send[...] = r.wi[...].astype(BF16)
    r.small[...] = jnp.zeros_like(r.small)
    for source, first in (
        (r.select, SEL),
        (r.decay, DEC),
        (r.stepw, STEP),
        (r.taps, TAPS),
        (r.bias, BIAS),
        (r.stepb, STEPB),
        (r.skip, SKIP),
    ):
        r.small[first : first + source.shape[0], :] = source[...]
    r.packed_send[...] = r.small[...].astype(BF16)
    lane = lax.broadcasted_iota(jnp.int32, (2 * CHUNKS, D // shards), 0)
    r.gains_send[...] = jnp.where(lane == 0, r.mixer[...], r.attention[...]).astype(BF16)
    for i in range(far):
        shared(i).start()
    spread(0, 1, 2)
    last = r.tokens.at[pl.ds(rows - 2 * CHUNKS, 2 * CHUNKS)]
    edge = copy(last, r.before, r.edge_sem, (), at_seq(ring[0]))
    edge.start()

    def cot_copy(by):
        return copy(
            r.cot.at[ring[by - 1]], r.given.at[me], r.cot_sem, (by,), at_seq(ring[by - 1])
        )

    for i in range(far):
        shared(i).wait_recv()
        for by in range(1, spans):
            fanned(i, by).start()
    for argument in arguments[1:]:
        argument.wait()
    r.wo_send[...] = r.wo[...].astype(BF16)
    r.wh_send[...] = r.wh[...].astype(BF16)
    r.wm_send[...] = r.wm[...].astype(BF16)
    for part in range(D // LANES):
        lanes = slice(part * LANES, (part + 1) * LANES)
        r.row[...] = r.tokens[:, lanes].astype(F32)
        for step in range(steps):
            r.x[step * CHUNKS : (step + 1) * CHUNKS, lanes] = r.row[
                pl.ds(step, CHUNKS, stride=steps), :
            ]
    for i in range(far):
        shared(i).wait_send()
        for by in range(1, spans):
            fanned(i, by).wait()
    pass_on(0, 1, 2)
    for by in range(1, spans):
        cot_copy(by).start()
    r.given[me] = r.cot[me]
    spread(5, 3, 4)
    finish(0, 1, 2)
    edge.wait()

    starts = starts_of(r.lengths, nseq)
    r.packed[...] = jnp.concatenate([r.packed_all[s] for s in range(shards)], axis=1)
    gains = jnp.concatenate([r.gains_all[s].astype(F32) for s in range(shards)], axis=1)
    r.gains[...] = gains[:CHUNKS]
    gain = gains[0:1]
    x = r.x[...]
    xn1 = (x * norm(x) * gain).astype(BF16)
    before = r.before[...].astype(F32)
    edge_n = (before * norm(before) * gain).astype(BF16)
    wide = 2 * DI // shards
    for s in range(shards):
        piece = dot_nn(xn1, r.wi_all[s])
        if s < shards // 2:
            r.ext[EDGE:, s * wide : (s + 1) * wide] = piece
        else:
            at = (s - shards // 2) * wide
            r.zgate[:, at : at + wide] = piece
    edge_x = jnp.concatenate([dot_nn(edge_n, r.wi_all[s]) for s in range(shards // 2)], axis=1)
    count = r.before.shape[0]
    chunk = lax.broadcasted_iota(jnp.int32, (CHUNKS, DI), 0)
    for k in range(CONV - 1):
        late = (steps - CONV + 1 + k) * CHUNKS + EDGE
        moved = pltpu.roll(r.ext[late : late + CHUNKS, :], 1, 0)
        at = count - CONV + 1 + k
        r.ext[k * CHUNKS : (k + 1) * CHUNKS, :] = jnp.where(
            chunk == 0, jnp.broadcast_to(edge_x[at : at + 1, :], (CHUNKS, DI)), moved
        )
    small = r.packed[DEC:PACK, :].astype(F32)
    taps = small[TAPS - DEC : TAPS - DEC + CONV, :]
    bias = small[BIAS - DEC : BIAS - DEC + 1, :]

    def conv_step(step, carry):
        places = lax.broadcasted_iota(jnp.int32, (CHUNKS, 1), 0) * steps + step + me * rows
        first = start_of(places, starts)
        total = jnp.broadcast_to(bias, (CHUNKS, DI))
        for k in range(CONV):
            at = pl.ds(pl.multiple_of((step + k) * CHUNKS, CHUNKS), CHUNKS)
            inside = places - (CONV - 1) + k >= first
            total = total + jnp.where(inside, taps[k : k + 1, :] * r.ext[at, :], 0.0)
        r.conv[tile(step), :] = total
        r.du[tile(step), :] = total * jax.nn.sigmoid(total)
        return carry

    lax.fori_loop(0, steps, conv_step, 0, unroll=2)
    u = r.du[...].astype(BF16)
    r.u[...] = u
    xdbl = dot_nt(u, r.packed[SEL : SEL + STEP, :])
    r.xdbl[...] = xdbl
    r.delta[...] = dot_nn(
        xdbl[:, :RANK].astype(BF16), r.packed[STEP : STEP + RANK, :]
    )
    stepb = small[STEPB - DEC : STEPB - DEC + 1, :]

    def delta_step(step, total):
        places = lax.broadcasted_iota(jnp.int32, (CHUNKS, 1), 0) * steps + step + me * rows
        pre = r.delta[tile(step), :] + stepb
        delta = jnp.maximum(pre, 0.0) + jnp.log(1.0 + jnp.exp(-jnp.abs(pre)))
        r.delta[tile(step), :] = delta
        cut = jnp.where(begin_of(places, starts), CUT, delta)
        r.cut[tile(step), :] = cut
        r.du[tile(step), :] = delta * r.du[tile(step), :].astype(BF16).astype(F32)
        return total + cut

    totals = lax.fori_loop(0, steps, delta_step, jnp.zeros((CHUNKS, DI), F32), unroll=2)
    r.totals[...] = totals
    total = jnp.sum(totals, axis=0, keepdims=True)
    for group in range(GROUPS_CH):
        r.total_send[group : group + 1, :] = total[:, group * LANES : (group + 1) * LANES]
    r.span_totals[me] = r.total_send[...]

    def total_copy(by):
        return copy(
            r.total_send, r.span_totals.at[me], r.total_sem, (by,), at_seq(ring[by - 1])
        )

    for by in range(1, spans):
        total_copy(by).start()
    pass_on(5)
    spread_decay(r.packed, r.amat, r.spread)
    r.bx[...] = spread_columns(xdbl[:, RANK : RANK + STATE])

    def state_copy(by, at):
        return copy(
            r.state_send.at[at], r.states.at[me, at], r.state_sem, (by, at), at_seq(ring[by - 1])
        )

    def pair_step(pair, carry):
        for odd in range(2):
            lanes = lanes_of(pair * 2 + odd)
            amat = [r.spread[st * CHUNKS : (st + 1) * CHUNKS, lanes] for st in range(STATE)]

            def step_fn(step, states):
                cut = r.cut[tile(step), lanes]
                drive = r.du[tile(step), lanes]
                return tuple(
                    jnp.exp2(cut * amat[st]) * states[st] + drive * r.bx[tile(step), column(st)]
                    for st in range(STATE)
                )

            states = lax.fori_loop(
                0, steps, step_fn, (jnp.zeros((CHUNKS, LANES), F32),) * STATE, unroll=8
            )
            for st in range(STATE):
                r.ends[st, :, lanes] = states[st]
        lanes = pl.ds(pl.multiple_of(pair * 2 * LANES, 2 * LANES), 2 * LANES)
        amat = r.amat[:, lanes]
        state = jnp.zeros((STATE, 2 * LANES), F32)
        for k in range(CHUNKS):
            state = jnp.exp2(amat * r.totals[k : k + 1, lanes]) * state + r.ends[:, k, lanes]
        r.state_send[pair] = state.astype(BF16)
        for by in range(1, spans):

            @pl.when(me + by < spans)
            def _():
                state_copy(by, pair).start()

        return carry

    lax.fori_loop(0, GROUPS_CH // 2, pair_step, 0)
    pass_on(3)
    for by in range(1, spans):
        cot_copy(by).wait()
    finish(5)

    ratio = spans // HEADS
    sub = lax.rem(me, ratio)
    head = lax.div(me, ratio)
    half = rows // 2
    given = jnp.concatenate([r.given[j] for j in range(spans)], axis=0)
    dout = dot_nn(pick_rows(r.index, me, rows, steps), given).astype(BF16)
    r.dout[...] = dout
    merge = jnp.concatenate([r.wm_all[s] for s in range(shards)], axis=0)
    dcontext = dot_nt(dout, merge).astype(BF16).astype(F32)
    low = lane_low(half)

    quarter = half // 2
    quarter_low = lane_low(quarter)

    def packs(pair, target, first, part):
        above, below = pair[:quarter], pair[quarter:]
        at = slice(part * quarter, (part + 1) * quarter)
        even = jnp.where(quarter_low, above, pltpu.roll(below, HEAD_DIM, 1))
        odd = jnp.where(quarter_low, pltpu.roll(above, HEAD_DIM, 1), below)
        target[first, at] = even.astype(BF16)
        target[first + 1, at] = odd.astype(BF16)

    def half_rows(part):
        return slice(part * half, (part + 1) * half)

    for pair in range(HEADS // 2):
        for part in range(2):
            packs(dcontext[half_rows(part), pair * LANES : (pair + 1) * LANES], r.d_send, 2 * pair, part)

    def d_copy(by):
        to = lax.rem(me + by, spans)
        slot = lax.div(me, ratio)
        return copy(r.d_send.at[lax.div(to, ratio)], r.d_in.at[slot], r.d_sem, (by,), at_seq(to))

    def q_copy(by, part):
        to = lax.rem(me + by, spans)
        at = pl.ds(part * quarter, quarter)
        source, target = r.q_send.at[lax.div(to, ratio), at], r.q_in.at[lax.div(me, ratio), at]
        return copy(source, target, r.q_sem, (by, part), at_seq(to))

    def kv_copy(by, part):
        to = lax.rem(me + by, spans)
        return copy(
            r.kv_send.at[lax.div(to, ratio), pl.ds(part * half, half)],
            r.kv_in.at[pl.ds(pl.multiple_of(me * rows + part * half, half), half)],
            r.kv_sem,
            (by, part),
            at_seq(to),
        )

    def to_rows(made, act):
        for by in range(1, spans):
            if ratio == 1:
                act(made(by))
            else:
                pl.when(lax.rem(by, ratio) == 0)(lambda: act(made(by)))

    to_rows(d_copy, lambda c: c.start())
    r.d_in[lax.div(me, ratio)] = r.d_send[head]
    r.cx[...] = spread_columns(xdbl[:, RANK + STATE :])
    for by in range(1, spans):
        total_copy(by).wait()
        for pair in range(GROUPS_CH // 2):

            @pl.when(me + by < spans)
            def _():
                state_copy(by, pair).wait_send()

            @pl.when(me - by >= 0)
            def _():
                state_copy(by, pair).wait_recv()

    amat = r.amat[...]

    def chain(k, state):
        decay = jnp.exp2(amat * total_row(r.span_totals[k]))
        came = jnp.concatenate(
            [r.states[k, g].astype(F32) for g in range(GROUPS_CH // 2)], axis=1
        )
        return decay * state + came

    state = lax.fori_loop(0, me, chain, jnp.zeros((STATE, DI), F32))
    for k in range(CHUNKS):
        r.init[:, k, :] = state
        if k < CHUNKS - 1:
            state = jnp.exp2(amat * r.totals[k : k + 1, :]) * state + r.ends[:, k, :]

    skip = small[SKIP - DEC : SKIP - DEC + 1, :]
    wo = None
    scale = 1.0 / math.sqrt(HEAD_DIM)

    for part in range(2):
        entering, leaving = (r.init, r.ends) if part == 0 else (r.ends, None)

        def group_step(group, carry):
            lanes = lanes_of(group)
            amat_g = [r.spread[st * CHUNKS : (st + 1) * CHUNKS, lanes] for st in range(STATE)]

            def step_fn(step, states):
                cut = r.cut[tile(step), lanes]
                drive = r.du[tile(step), lanes]
                new = tuple(
                    jnp.exp2(cut * amat_g[st]) * states[st] + drive * r.bx[tile(step), column(st)]
                    for st in range(STATE)
                )
                terms = [new[st] * r.cx[tile(step), column(st)] for st in range(STATE)]
                while len(terms) > 1:
                    terms = [a + b for a, b in zip(terms[::2], terms[1::2])]
                r.yfull[tile(step), lanes] = terms[0]
                return new

            states = lax.fori_loop(
                part * steps // 2,
                (part + 1) * steps // 2,
                step_fn,
                tuple(entering[st, :, lanes] for st in range(STATE)),
                unroll=8,
            )
            if leaving is not None:
                for st in range(STATE):
                    leaving[st, :, lanes] = states[st]
            return carry

        lax.fori_loop(0, GROUPS_CH, group_step, 0)

        def gate_step(pair, carry):
            at = pl.ds(pl.multiple_of(pair * 2 * CHUNKS, 2 * CHUNKS), 2 * CHUNKS)
            yfull = r.yfull[at, :] + skip * r.u[at, :].astype(F32)
            r.yfull[at, :] = yfull
            gate = r.zgate[at, :]
            r.gated[at, :] = (yfull * (gate * jax.nn.sigmoid(gate))).astype(BF16)
            return carry

        lax.fori_loop(part * steps // 4, (part + 1) * steps // 4, gate_step, 0, unroll=2)
        if part == 0:
            pass_on(4)
            finish(3)
            wo = jnp.concatenate([r.wo_all[s] for s in range(shards)], axis=0)
        ours = half_rows(part)
        x1 = r.x[ours, :] + dot_nn(r.gated[ours, :], wo)
        r.x1[ours, :] = x1
        xn2 = (x1 * norm(x1) * gains[1:2, :]).astype(BF16)
        if part == 0:
            finish(4)
        qkv = jnp.concatenate([dot_nn(xn2, r.wh_all[s]) for s in range(shards)], axis=1)
        qkv = qkv.astype(BF16).astype(F32)
        for pair in range(HEADS // 2):
            at = pair * LANES
            packs(qkv[:, at : at + LANES] * scale, r.q_send, 2 * pair, part)
            k = qkv[:, D + at : D + at + LANES]
            v = qkv[:, 2 * D + at : 2 * D + at + LANES]
            even = jnp.where(low, k, pltpu.roll(v, HEAD_DIM, 1))
            odd = jnp.where(low, pltpu.roll(k, HEAD_DIM, 1), v)
            r.kv_send[2 * pair, ours] = even.astype(BF16)
            r.kv_send[2 * pair + 1, ours] = odd.astype(BF16)
        to_rows(functools.partial(q_copy, part=part), lambda c: c.start())
        for by in range(1, spans):
            kv_copy(by, part).start()
    r.q_in[lax.div(me, ratio)] = r.q_send[head]
    r.kv_in[pl.ds(pl.multiple_of(me * rows, rows), rows), :] = r.kv_send[head]
    keeps = [
        pltpu.make_async_copy(getattr(r, name), getattr(r, name + "_out"), r.keep_sem.at[i])
        for i, name in enumerate(KEPT)
    ]
    for keep in keeps[:-1]:
        keep.start()
    at = lax.broadcasted_iota(jnp.int32, (1, rows), 1)
    turn_at = lax.rem(lax.div(at, quarter), 2) * half + lax.div(at, half) * quarter + lax.rem(at, quarter)
    query_local = row_places(turn_at, steps)
    key_local = row_places(lax.broadcasted_iota(jnp.int32, (rows, 1), 0), steps)
    r.causal[...] = jnp.where(key_local <= query_local, 0.0, NEG)
    r.dkv[...] = jnp.zeros_like(r.dkv)
    if ratio > 1:
        to_rows(d_copy, lambda c: c.wait_recv())
        for part in range(2):
            to_rows(functools.partial(q_copy, part=part), lambda c: c.wait_recv())
            for by in range(1, spans):
                kv_copy(by, part).wait_recv()

    def arrived(source):
        by = lax.rem(me - source + spans, spans)

        @pl.when(source != me)
        def _():
            d_copy(by).wait_recv()
            for part in range(2):
                q_copy(by, part).wait_recv()
                kv_copy(by, part).wait_recv()


    static = ratio == 1
    blocks = spans // ratio

    def each(count, fn, carry):
        if not static:
            return lax.fori_loop(0, count, fn, carry)
        for j in range(count):
            carry = fn(j, carry)
        return carry

    def key_rows(j):
        return pl.ds(j * rows if static else pl.multiple_of(j * rows, rows), rows)

    def turn(j, carry):
        r.kvt[j] = r.kv_in[key_rows(j), :].astype(F32).T.astype(BF16)
        return carry

    if not static:
        each(spans, turn, 0)
    folded = (rows // CHUNKS, CHUNKS, rows)

    def dq_copy(to, by, t):
        return copy(r.dq_send.at[t], r.dq_in.at[head], r.dq_sem, (by,), at_seq(to))

    def query_block(t, carry):
        i = t * ratio + sub
        slot = t % 2 if static else 0
        if static:
            arrived(t)
            turn(t, 0)
        q = r.q_in[t].astype(F32)
        d = r.d_in[t].astype(F32)
        qt = q.T
        dt = d.T
        zero = jnp.zeros((HEAD_DIM, rows), F32)
        qt = jnp.concatenate([qt[:HEAD_DIM], qt[HEAD_DIM:]], axis=1)
        dt = jnp.concatenate([dt[:HEAD_DIM], dt[HEAD_DIM:]], axis=1)
        both = jnp.concatenate(
            [jnp.concatenate([qt, zero], axis=1), jnp.concatenate([zero, dt], axis=1)], axis=0
        ).astype(BF16)
        none = jnp.zeros((half, LANES), F32)
        natural = jnp.concatenate(
            [
                jnp.where(low, none, pltpu.roll(d, HEAD_DIM, 1)),
                jnp.where(low, none, d),
                jnp.where(low, q, none),
                jnp.where(low, pltpu.roll(q, HEAD_DIM, 1), none),
            ],
            axis=0,
        ).astype(BF16)
        first = start_of(query_local + i * rows, starts)

        def scores(j, top):
            joint = dot_nn(r.kv_in[key_rows(j), :], both)
            score = joint[:, :rows]
            if static:
                if j == t:
                    score = score + r.causal[...]
                if j in (0, t) or t == spans - 1:
                    score = jnp.where(key_local + j * rows >= first, score, NEG)
            else:
                query = query_local + i * rows
                key = key_local + j * rows
                score = jnp.where((key <= query) & (key >= first), score, NEG)
            r.score[slot, j] = score
            r.dprob[slot, j] = joint[:, rows:]
            return jnp.maximum(top, jnp.max(score.reshape(folded), axis=0))

        top = each(t + 1 if static else i + 1, scores, jnp.full((CHUNKS, rows), NEG, F32))
        top = jnp.max(top, axis=0, keepdims=True)

        def weigh(j, sums):
            total, dot = sums
            prob = jnp.exp(r.score[slot, j] - top)
            r.score[slot, j] = prob
            total = total + jnp.sum(prob.reshape(folded), axis=0)
            dot = dot + jnp.sum((prob * r.dprob[slot, j]).reshape(folded), axis=0)
            return total, dot

        zero = jnp.zeros((CHUNKS, rows), F32)
        total, dot = each(t + 1 if static else i + 1, weigh, (zero, zero))
        inverse = 1.0 / jnp.sum(total, axis=0, keepdims=True)
        datt = jnp.sum(dot, axis=0, keepdims=True) * inverse

        def back(j, sums):
            prob = r.score[slot, j] * inverse
            dscore = prob * (r.dprob[slot, j] - datt)
            joint = jnp.concatenate([prob.astype(BF16), dscore.astype(BF16)], axis=1)
            r.dkv[key_rows(j), :] += dot_nn(joint, natural)
            return sums + dot_nn(r.kvt[j], joint)

        sums = each(t + 1 if static else i + 1, back, jnp.zeros((LANES, 2 * rows), F32))
        dqt = sums[:HEAD_DIM, rows:] * scale
        ctx = sums[HEAD_DIM:, :rows]
        dqt = jnp.concatenate([dqt[:, :half], dqt[:, half:]], axis=0)
        ctx = jnp.concatenate([ctx[:, :half], ctx[:, half:]], axis=0)
        r.dq_send[t] = dqt.T.astype(BF16)
        r.context_send[t] = ctx.T.astype(BF16)
        by = lax.rem(i - me + spans, spans)

        @pl.when(i != me)
        def _():
            dq_copy(i, by, t).start()

        @pl.when(i == me)
        def _():
            r.dq_in[head] = r.dq_send[t]

        return carry

    if static:
        for t in range(blocks):
            query_block(t, 0)
    else:
        lax.fori_loop(0, blocks, query_block, 0)
    keeps[-1].start()
    to_rows(d_copy, lambda c: c.wait_send())
    for part in range(2):
        to_rows(functools.partial(q_copy, part=part), lambda c: c.wait_send())
        for by in range(1, spans):
            kv_copy(by, part).wait_send()

    def cast(j, carry):
        r.dkv_send[j] = r.dkv[key_rows(j), :].astype(BF16)
        return carry

    each(spans, cast, 0)

    def dkv_copy(by):
        to = ring[by - 1]
        return copy(r.dkv_send.at[to], r.dkv_in.at[me], r.dkv_sem, (by,), at_seq(to))

    for by in range(1, spans):
        dkv_copy(by).start()
    r.dkv_in[me] = r.dkv_send[me]
    for t in range(blocks):
        i = t * ratio + sub
        by = lax.rem(i - me + spans, spans)

        @pl.when(i != me)
        def _():
            dq_copy(i, by, t).wait_send()

    for h in range(HEADS):
        came = h * ratio + sub
        by = lax.rem(me - came + spans, spans)

        @pl.when(came != me)
        def _():
            dq_copy(came, by, 0).wait_recv()

    for by in range(1, spans):
        dkv_copy(by).wait()
    for keep in keeps:
        keep.wait()


def total_row(values):
    return jnp.concatenate([values[g : g + 1, :] for g in range(GROUPS_CH)], axis=1)


def lane_low(rows):
    return lax.broadcasted_iota(jnp.int32, (rows, LANES), 1) < HEAD_DIM


def pick_rows(table_ref, me, rows, steps):
    spans = table_ref.shape[1] // rows
    share = rows // spans
    lane = lax.broadcasted_iota(jnp.int32, (1, rows), 1)
    index = jnp.zeros((1, rows), F32)
    for j in range(spans):
        line = table_ref[:, j * rows : (j + 1) * rows].astype(F32)
        line = pltpu.roll(line, lax.rem((j + spans - me) * share, rows), 1)
        index = jnp.where(lane >= j * share, line, index)
    places = row_places(lax.broadcasted_iota(jnp.int32, (rows, 1), 0), steps) + me * rows
    return (index == places.astype(F32)).astype(F32).astype(BF16)


GRADS = ("heads", "out", "merge", "late", "early", "other", "small")
SMALL = 6
BACKWARD_IN = ("lengths", "index", "dq_in", "dkv_in") + tuple(k + "_kept" for k in KEPT)
class BackwardOut(NamedTuple):
    output: Any
    token_grad: Any
    last_heads: Any
    last_out: Any
    last_merge: Any
    last_small: Any
    pair_in: Any
    early_in: Any
    other_in: Any


BACKWARD_OUT = BackwardOut._fields
class FinalOut(NamedTuple):
    output: Any
    token_grad: Any
    mixer_grad: Any
    input_grad: Any
    taps_grad: Any
    bias_grad: Any
    select_grad: Any
    stepw_grad: Any
    stepb_grad: Any
    decay_grad: Any
    skip_grad: Any
    output_grad: Any
    attention_grad: Any
    heads_grad: Any
    merge_grad: Any


FINAL_OUT = FinalOut._fields
class BackwardScratch(NamedTuple):
    context: Any
    given: Any
    dx1: Any
    dys: Any
    dzgate: Any
    ends: Any
    grad_send: Any
    grads_in: Any
    db: Any
    dc: Any
    decay: Any
    held: Any
    state: Any
    bgrad: Any
    adelta: Any
    arrive: Any
    dxdbl: Any
    dext: Any
    spill: Any
    spill_in: Any
    small: Any
    row: Any
    amat: Any
    spread: Any
    sub_late: Any
    sub_early: Any
    sub_other: Any


class BackwardSems(NamedTuple):
    load_sem: Any
    context_sem: Any
    given_sem: Any
    state_sem: Any
    spill_sem: Any
    near_sem: Any
    far_sem: Any
    part_sem: Any
    last_sem: Any
    pair_sem: Any
    inner_sem: Any
    outer_sem: Any
    late_outer_sem: Any
    late_inner_sem: Any


BACKWARD_SCRATCH = (
    KEPT
    + BackwardScratch._fields
    + tuple(kind + name for kind in ("g_", "near_", "sum_", "far_", "part_") for name in GRADS)
    + BackwardSems._fields
)


def backward_kernel(steps, nseq, shards, spans, *refs):
    r = Refs(BACKWARD_IN + BACKWARD_OUT + BACKWARD_SCRATCH, refs)
    rows = steps * CHUNKS
    width = DI // shards
    me = lax.axis_index("seq")
    shard, core, chip, partner, others = shard_peers(shards)
    chips = shards // 2
    ring = [lax.rem(me + by, spans) for by in range(1, spans)]
    every = [me] + ring
    ratio = spans // HEADS
    sub = lax.rem(me, ratio)
    half = rows // 2
    blocks = spans // ratio
    starts = starts_of(r.lengths, nseq)
    loads = {
        name: pltpu.make_async_copy(getattr(r, name + "_kept"), getattr(r, name), r.load_sem.at[i])
        for i, name in enumerate(KEPT)
    }
    early = ("context_send", "dout", "x1", "gains", "wh_all")
    middle = ("gated", "wo_all", "zgate", "yfull", "u", "x")
    late = ("wm_all", "packed", "cut", "cx", "totals", "span_totals", "init", "delta", "du", "bx", "xdbl")
    last = ("conv", "ext", "wi_all")
    for name in early + middle:
        loads[name].start()

    def loaded(*names):
        for name in names:
            loads[name].wait()

    targets = [lax.div(shard, 2), shards // 2 + lax.div(shard, 2)]
    mine = lax.div(shard, shards // 2)
    first_piece = 2 * lax.rem(shard, shards // 2)

    def anywhere(index, at):
        return {"device_id": {"seq": index, "shard": at}, "device_id_type": pl.DeviceIdType.MESH}

    barrier = pltpu.get_barrier_semaphore()

    def signal(to):
        pl.semaphore_signal(barrier, inc=1, **to)

    peers = [at_shard(partner)] + [at_shard(o) for o in others] + [at_seq(to) for to in ring]
    for peer in peers:
        signal(peer)
    selves = jnp.int32(0)
    for by in range(spans):
        for at in targets + [first_piece, first_piece + 1]:
            if by:
                signal(anywhere(every[by], at))
            else:
                pl.when(at != shard)(lambda: signal(anywhere(me, at)))
                selves = selves + (at == shard).astype(jnp.int32)
    pl.semaphore_wait(barrier, len(peers) + 4 * spans - selves)

    def copy(source, target, sems, at, to):
        return pltpu.make_async_remote_copy(
            src_ref=source, dst_ref=target, send_sem=sems.at[(0, *at)], recv_sem=sems.at[(1, *at)], **to
        )

    def ref(kind, k):
        return getattr(r, kind + "_" + GRADS[k])

    def near_copy(k, x):
        return copy(
            ref("g", k).at[x * 2 + 1 - core], ref("near", k).at[x], r.near_sem, (k, x), at_shard(partner)
        )

    def far_copy(k, by):
        source = ref("sum", k).at[lax.rem(chip + by, chips)]
        return copy(source, ref("far", k).at[by - 1], r.far_sem, (k, by), at_shard(others[by - 1]))

    def part_copy(k, by):
        to = ring[by - 1]
        return copy(
            ref("near", k).at[0, to], ref("part", k).at[by], r.part_sem, (k, by), at_seq(to)
        )

    def last_copy(k, by):
        held = ref("last", k).at[me]
        return copy(held, held, r.last_sem, (k, by), at_seq(ring[by - 1]))

    def pair_refs(k):
        return (r.sub_early, r.early_in) if GRADS[k] == "early" else (r.sub_other, r.other_in)

    def pair_copy(k, by, at):
        source, target = pair_refs(k)
        to = anywhere(every[by], targets[0])
        return copy(source, target.at[at, me], r.pair_sem, (k - 4, at, by), to)

    def near_send(k):
        for x in range(chips):
            near_copy(k, x).start()

    def far_send(k):
        for x in range(chips):
            near_copy(k, x).wait_recv()
        for by in [*range(1, chips), 0]:
            x = lax.rem(chip + by, chips)
            ref("sum", k)[x] = (
                ref("g", k)[x * 2 + core].astype(F32) + ref("near", k)[x].astype(F32)
            ).astype(BF16)
            if by:
                far_copy(k, by).start()

    def part_send(k):
        total = ref("sum", k)[chip].astype(F32)
        for by in range(1, chips):
            far_copy(k, by).wait_recv()
            total = total + ref("far", k)[by - 1].astype(F32)
        ref("near", k)[0] = total.astype(BF16)
        for by in range(1, chips):
            far_copy(k, by).wait_send()
        for by in range(1, spans):
            part_copy(k, by).start()

    def last_send(k):
        total = ref("near", k)[0, me].astype(F32)
        for by in range(1, spans):
            part_copy(k, by).wait_recv()
            total = total + ref("part", k)[by].astype(F32)
        if k == SMALL:
            ref("last", k)[me] = total.astype(BF16)
            for by in range(1, spans):
                last_copy(k, by).start()
            return
        source, target = pair_refs(k)
        source[...] = total.astype(BF16)
        for by in range(spans):
            to_owner(by == 0, targets[0], pair_copy(k, by, parity), lambda c: c.start())

        @pl.when(targets[0] == shard)
        def _():
            target[parity, me] = source[...]

    def to_owner(same, to, made, act):
        if same:
            pl.when(to != shard)(lambda: act(made))
        else:
            act(made)

    inner = spans // OUTER
    low_me, high_me = lax.rem(me, inner), lax.div(me, inner)
    lows = [lax.rem(low_me + by, inner) for by in range(inner)]
    highs = [lax.rem(high_me + by, OUTER) for by in range(OUTER)]
    own_part = low_me * OUTER + high_me
    middle_at = (inner - 1) * OUTER
    parity = lax.rem(shard, 2)

    def inner_copy(k, by):
        return copy(
            ref("near", k).at[0, pl.ds(lows[by] * OUTER, OUTER)],
            ref("part", k).at[pl.ds((by - 1) * OUTER, OUTER)],
            r.inner_sem,
            (k, 0, by),
            at_seq(high_me * inner + lows[by]),
        )

    def outer_copy(k, by):
        return copy(
            ref("part", k).at[middle_at + highs[by]],
            ref("part", k).at[spans + by - 1],
            r.outer_sem,
            (k, 0, by),
            at_seq(highs[by] * inner + low_me),
        )

    def outer_last(k, by):
        held = ref("last", k).at[own_part]
        return copy(held, held, r.outer_sem, (k, 1, by), at_seq(highs[by] * inner + low_me))

    def inner_last(k, by):
        held = ref("last", k).at[pl.ds(low_me * OUTER, OUTER)]
        return copy(held, held, r.inner_sem, (k, 1, by), at_seq(high_me * inner + lows[by]))

    def late_outer(by, at):
        return copy(
            r.sub_late,
            r.pair_in.at[at, own_part],
            r.late_outer_sem,
            (at, by),
            anywhere(highs[by] * inner + low_me, targets[1]),
        )

    def late_inner(by, at):
        held = r.pair_in.at[at, pl.ds(low_me * OUTER, OUTER)]
        to = at_seq(high_me * inner + lows[by])
        return copy(held, held, r.late_inner_sem, (at, by), to)

    def inner_send(k):
        total = ref("sum", k)[chip].astype(F32)
        for by in range(1, chips):
            far_copy(k, by).wait_recv()
            total = total + ref("far", k)[by - 1].astype(F32)
        ref("near", k)[0] = total.astype(BF16)
        for by in range(1, inner):
            inner_copy(k, by).start()

    def outer_send(k):
        total = ref("near", k)[0, pl.ds(low_me * OUTER, OUTER)].astype(F32)
        for by in range(1, inner):
            inner_copy(k, by).wait_recv()
            total = total + ref("part", k)[(by - 1) * OUTER : by * OUTER].astype(F32)
        ref("part", k)[middle_at : middle_at + OUTER] = total.astype(BF16)
        for by in range(1, OUTER):
            outer_copy(k, by).start()

    def outer_back(k):
        total = ref("part", k)[middle_at + high_me].astype(F32)
        for by in range(1, OUTER):
            outer_copy(k, by).wait_recv()
            total = total + ref("part", k)[spans + by - 1].astype(F32)
        if k != 3:
            ref("last", k)[own_part] = total.astype(BF16)
            for by in range(1, OUTER):
                outer_last(k, by).start()
            return
        r.sub_late[...] = total.astype(BF16)
        for by in range(OUTER):
            to_owner(by == 0, targets[1], late_outer(by, parity), lambda c: c.start())

        @pl.when(targets[1] == shard)
        def _():
            r.pair_in[parity, own_part] = r.sub_late[...]

    def inner_back(k):
        if k != 3:
            for by in range(1, OUTER):
                outer_last(k, by).wait_recv()
            for by in range(1, inner):
                inner_last(k, by).start()
            return

        @pl.when(mine == 1)
        def _():
            for at in range(2):
                for by in range(OUTER):
                    to_owner(by == 0, first_piece + at, late_outer(by, at), lambda c: c.wait_recv())
                for by in range(1, inner):
                    late_inner(by, at).start()

    def finish(k):
        for x in range(chips):
            near_copy(k, x).wait_send()
        if k < 4:
            for by in range(1, chips):
                far_copy(k, by).wait_send()
            for by in range(1, inner):
                inner_copy(k, by).wait_send()
            for by in range(1, OUTER):
                outer_copy(k, by).wait_send()
        else:
            for by in range(1, spans):
                part_copy(k, by).wait_send()
        if k < 3:
            for by in range(1, OUTER):
                outer_last(k, by).wait_send()
            for by in range(1, inner):
                inner_last(k, by).wait()
        elif k == 3:
            for by in range(OUTER):
                to_owner(by == 0, targets[1], late_outer(by, parity), lambda c: c.wait_send())

            @pl.when(mine == 1)
            def _():
                for at in range(2):
                    for by in range(1, inner):
                        late_inner(by, at).wait()

        elif k == SMALL:
            for by in range(1, spans):
                last_copy(k, by).wait()
        else:
            for by in range(spans):
                to_owner(by == 0, targets[0], pair_copy(k, by, parity), lambda c: c.wait_send())

            @pl.when(mine == 0)
            def _():
                for at in range(2):
                    for by in range(spans):
                        made = pair_copy(k, by, at)
                        to_owner(by == 0, first_piece + at, made, lambda c: c.wait_recv())

    def put(k, piece, value):
        size = value.shape[0] // spans
        for j in range(spans):
            ref("g", k)[piece, j] = value[j * size : (j + 1) * size].astype(BF16)

    loaded("context_send")
    head = lax.div(me, ratio)

    def context_copy(t, by, to):
        return copy(r.context_send.at[t], r.context.at[head], r.context_sem, (by,), at_seq(to))

    for t in range(blocks):
        i = t * ratio + sub
        by = lax.rem(i - me + spans, spans)

        @pl.when(i != me)
        def _():
            context_copy(t, by, i).start()

        @pl.when(i == me)
        def _():
            r.context[head] = r.context_send[t]

    low = lane_low(rows)
    half_low = lane_low(half)

    def unpacked(source, pair):
        even, odd = source[2 * pair].astype(F32), source[2 * pair + 1].astype(F32)
        first = jnp.where(half_low, even, pltpu.roll(odd, HEAD_DIM, 1))
        second = jnp.where(half_low, pltpu.roll(even, HEAD_DIM, 1), odd)
        quarter = half // 2
        return jnp.concatenate(
            [first[:quarter], second[:quarter], first[quarter:], second[quarter:]], axis=0
        )

    dqs, dks, dvs = [], [], []
    for pair in range(HEADS // 2):
        dkv = [
            sum(r.dkv_in[(2 * pair + odd) * ratio + part].astype(F32) for part in range(ratio))
            for odd in range(2)
        ]
        dqs.append(unpacked(r.dq_in, pair))
        dks.append(jnp.where(low, dkv[0], pltpu.roll(dkv[1], HEAD_DIM, 1)))
        dvs.append(jnp.where(low, pltpu.roll(dkv[0], HEAD_DIM, 1), dkv[1]))
    dqkv = jnp.concatenate(dqs + dks + dvs, axis=1).astype(BF16)
    loaded("x1", "gains", "wh_all", "dout")
    for name in late + last:
        loads[name].start()
    x1 = r.x1[...]
    inverse = norm(x1)
    normal = x1 * inverse
    gain = r.gains[1:2, :]
    xn2 = (normal * gain).astype(BF16)
    wide = 3 * D // shards
    dxn2 = jnp.zeros((rows, D), F32)
    for s in range(shards):
        piece = dqkv[:, s * wide : (s + 1) * wide]
        put(0, s, dot_tn(xn2, piece))
        dxn2 = dxn2 + dot_nt(piece, r.wh_all[s])
    near_send(0)
    attention_gain = jnp.sum(dxn2 * normal, axis=0, keepdims=True)
    e2 = dxn2 * gain
    dx1 = r.dout[...].astype(F32) + inverse * (
        e2 - normal * jnp.mean(e2 * normal, axis=-1, keepdims=True)
    )
    r.dx1[...] = dx1
    dmixed = dx1.astype(BF16)
    loaded("gated", "wo_all")
    for s in range(shards):
        put(1, s, dot_tn(r.gated[:, s * width : (s + 1) * width], dmixed))
        r.dys[:, s * width : (s + 1) * width] = dot_nt(dmixed, r.wo_all[s])
    near_send(1)
    far_send(0)
    loaded("zgate", "yfull", "u", "x")

    def gate_step(pair, total):
        at = pl.ds(pl.multiple_of(pair * 2 * CHUNKS, 2 * CHUNKS), 2 * CHUNKS)
        dgated = r.dys[at, :].astype(BF16).astype(F32)
        gate = r.zgate[at, :]
        s = jax.nn.sigmoid(gate)
        dys = dgated * (gate * s)
        r.dys[at, :] = dys
        r.dzgate[at, :] = (dgated * r.yfull[at, :] * (s * (1.0 + gate * (1.0 - s)))).astype(BF16)
        return total + dys * r.u[at, :].astype(F32)

    total = lax.fori_loop(0, steps // 2, gate_step, jnp.zeros((2 * CHUNKS, DI), F32), unroll=2)
    r.small[SKIP : SKIP + 1, :] = jnp.sum(total, axis=0, keepdims=True)
    far_send(1)
    x = r.x[...]
    inverse_one = norm(x)
    normal_one = x * inverse_one
    gain_one = r.gains[0:1, :]
    xn1 = (normal_one * gain_one).astype(BF16)
    for s in range(shards):
        put(3, s, dot_tn(xn1, r.dzgate[:, s * width : (s + 1) * width]))
    near_send(3)
    loaded("wm_all", "packed", "cut", "cx", "totals", "span_totals")
    spread_decay(r.packed, r.amat, r.spread)

    def state_copy(by, at):
        to = lax.rem(me - by + spans, spans)
        return copy(
            r.grad_send.at[at], r.grads_in.at[me, at], r.state_sem, (by, at), at_seq(to)
        )

    def pair_step(pair, carry):
        for odd in range(2):
            lanes = lanes_of(pair * 2 + odd)
            amat = [r.spread[st * CHUNKS : (st + 1) * CHUNKS, lanes] for st in range(STATE)]

            def step_fn(turn, grads):
                step = steps - 1 - turn
                cut = r.cut[tile(step), lanes]
                dys = r.dys[tile(step), lanes]
                return tuple(
                    jnp.exp2(cut * amat[st]) * (grads[st] + dys * r.cx[tile(step), column(st)])
                    for st in range(STATE)
                )

            grads = lax.fori_loop(
                0, steps, step_fn, (jnp.zeros((CHUNKS, LANES), F32),) * STATE, unroll=16
            )
            for st in range(STATE):
                r.ends[st, :, lanes] = grads[st]
        lanes = pl.ds(pl.multiple_of(pair * 2 * LANES, 2 * LANES), 2 * LANES)
        amat = r.amat[:, lanes]
        state = jnp.zeros((STATE, 2 * LANES), F32)
        for k in reversed(range(CHUNKS)):
            state = jnp.exp2(amat * r.totals[k : k + 1, lanes]) * state + r.ends[:, k, lanes]
        r.grad_send[pair] = state.astype(BF16)
        for by in range(1, spans):

            @pl.when(me - by >= 0)
            def _():
                state_copy(by, pair).start()

        pl.when(pair == 0)(lambda: far_send(3))
        return carry

    lax.fori_loop(0, GROUPS_CH // 2, pair_step, 0)
    for h in range(HEADS):
        came = h * ratio + sub
        by = lax.rem(me - came + spans, spans)

        @pl.when(came != me)
        def _():
            context_copy(0, by, came).wait_recv()

    context = jnp.concatenate([unpacked(r.context, p) for p in range(HEADS // 2)], axis=1)
    context = context.astype(BF16)
    short = D // shards
    x2 = x1
    for s in range(shards):
        part = context[:, s * short : (s + 1) * short]
        x2 = x2 + dot_nn(part, r.wm_all[s])
        put(2, s, dot_tn(part, r.dout[...]))
    near_send(2)
    given = dot_tn(pick_rows(r.index, me, rows, steps), x2.astype(BF16))
    share = rows // spans
    for j in range(spans):
        r.given[j] = given[j * share : (j + 1) * share].astype(BF16)

    def given_copy(by):
        to = ring[by - 1]
        return copy(r.given.at[to], r.output.at[me], r.given_sem, (by,), at_seq(to))

    r.output[me] = r.given[me]

    loaded("init", "delta", "du", "bx", "xdbl", *last)
    r.db[...] = jnp.zeros_like(r.db)
    r.dc[...] = jnp.zeros_like(r.dc)
    for by in range(1, spans):
        for pair in range(GROUPS_CH // 2):

            @pl.when(me - by >= 0)
            def _():
                state_copy(by, pair).wait_send()

            @pl.when(me + by < spans)
            def _():
                state_copy(by, pair).wait_recv()

    for by in range(1, spans):
        given_copy(by).start()
    amat = r.amat[...]

    def chain(turn, state):
        k = spans - 1 - turn
        decay = jnp.exp2(amat * total_row(r.span_totals[k]))
        came = jnp.concatenate(
            [r.grads_in[k, g].astype(F32) for g in range(GROUPS_CH // 2)], axis=1
        )
        return decay * state + came

    state = lax.fori_loop(0, spans - 1 - me, chain, jnp.zeros((STATE, DI), F32))
    for k in reversed(range(CHUNKS)):
        r.arrive[:, k, :] = state
        if k:
            state = jnp.exp2(amat * r.totals[k : k + 1, :]) * state + r.ends[:, k, :]
    eight = STATE // 2

    def sum_of(terms):
        while len(terms) > 1:
            terms = [a + b for a, b in zip(terms[::2], terms[1::2])]
        return terms[0]

    def kept_at(step, i):
        return pl.ds(pl.multiple_of(step * (eight * CHUNKS) + i * CHUNKS, CHUNKS), CHUNKS)

    stages = {
        0: ((far_send, 2), (inner_send, 0),),
        2: ((inner_send, 1),),
        4: ((outer_send, 0),),
        6: ((inner_send, 3),),
        7: ((outer_send, 1),),
    }

    def run(todo):
        for stage, k in todo:
            stage(k)

    def group_step(group, carry):
        lanes = lanes_of(group)
        for part in range(2):
            states = range(part * eight, (part + 1) * eight)
            amat_g = [r.spread[st * CHUNKS : (st + 1) * CHUNKS, lanes] for st in states]

            def forward(step, held):
                cut = r.cut[tile(step), lanes]
                drive = r.du[tile(step), lanes]
                out = []
                for i, st in enumerate(states):
                    decay = jnp.exp2(cut * amat_g[i])
                    kept = decay * held[i]
                    new = kept + drive * r.bx[tile(step), column(st)]
                    r.decay[kept_at(step, i), :] = decay
                    r.held[kept_at(step, i), :] = kept
                    r.state[kept_at(step, i), :] = new
                    out.append(new)
                return tuple(out)

            lax.fori_loop(
                0, steps, forward, tuple(r.init[st, :, lanes] for st in states), unroll=16
            )

            def backward(turn, held):
                grads, sums = held
                step = steps - 1 - turn
                delta = r.delta[tile(step), lanes]
                drive = r.du[tile(step), lanes]
                dys = r.dys[tile(step), lanes]
                new, totals, by_b, by_a = [], [], [], []
                for i, st in enumerate(states):
                    at = tile(step)
                    grad = grads[i] + dys * r.cx[at, column(st)]
                    new.append(r.decay[kept_at(step, i), :] * grad)
                    through = grad * r.held[kept_at(step, i), :]
                    totals.append(sums[i] + through * delta)
                    by_a.append(amat_g[i] * through)
                    by_b.append(grad * r.bx[at, column(st)])
                    r.dc[at, column(st)] += r.state[kept_at(step, i), :] * dys
                    r.db[at, column(st)] += grad * drive
                if part:
                    r.bgrad[tile(step), lanes] += sum_of(by_b)
                    r.adelta[tile(step), lanes] += sum_of(by_a)
                else:
                    r.bgrad[tile(step), lanes] = sum_of(by_b)
                    r.adelta[tile(step), lanes] = sum_of(by_a)
                return (tuple(new), tuple(totals))

            _, sums = lax.fori_loop(
                0,
                steps,
                backward,
                (
                    tuple(r.arrive[st, :, lanes] for st in states),
                    (jnp.zeros((CHUNKS, LANES), F32),) * eight,
                ),
                unroll=16,
            )
            for i, st in enumerate(states):
                row = jnp.sum(sums[i], axis=0, keepdims=True)
                amat_row = amat_g[i][0:1, :] * math.log(2.0)
                r.small[DEC + st : DEC + st + 1, lanes] = row * amat_row
        for at, todo in stages.items():
            pl.when(group == at)(functools.partial(run, todo))
        return carry

    lax.fori_loop(0, GROUPS_CH, group_step, 0)
    small = r.packed[DEC:PACK, :].astype(F32)
    taps = small[TAPS - DEC : TAPS - DEC + CONV, :]
    skip = small[SKIP - DEC : SKIP - DEC + 1, :]

    def delta_step(step, total):
        at = tile(step)
        bgrad = r.bgrad[at, :]
        delta = r.delta[at, :]
        u = r.conv[at, :]
        u = (u * jax.nn.sigmoid(u)).astype(BF16).astype(F32)
        ddelta = u * bgrad + r.adelta[at, :] * math.log(2.0)
        dtpre = (ddelta * (1.0 - jnp.exp(-delta))).astype(BF16).astype(F32)
        r.adelta[at, :] = dtpre
        r.bgrad[at, :] = r.dys[at, :] * skip + delta * bgrad
        return total + dtpre

    total = lax.fori_loop(0, steps, delta_step, jnp.zeros((CHUNKS, DI), F32), unroll=2)
    run(((inner_send, 2),))
    r.small[STEPB : STEPB + 1, :] = jnp.sum(total, axis=0, keepdims=True)
    r.small[GAINS:, :] = jnp.zeros((PACK - GAINS, DI), F32)
    dtpre = r.adelta[...].astype(BF16)
    steplow = r.xdbl[:, 0:RANK].astype(BF16)
    r.small[STEP : STEP + RANK, :] = dot_tn(steplow, dtpre)
    r.dxdbl[:, 0:RANK] = dot_nt(dtpre, r.packed[STEP : STEP + RANK, :])
    for part in range(4):
        at = slice(part * rows // 4, (part + 1) * rows // 4)
        r.dxdbl[at, RANK : RANK + STATE] = gather_columns(r.db[at, :])
        r.dxdbl[at, RANK + STATE :] = gather_columns(r.dc[at, :])
    run(((outer_back, 0), (outer_send, 3),))
    dxdbl = r.dxdbl[...].astype(BF16)
    r.small[SEL : SEL + STEP, :] = dot_tn(dxdbl, r.u[...])
    r.bgrad[...] += dot_nn(dxdbl, r.packed[SEL : SEL + STEP, :])
    r.dext[...] = jnp.zeros_like(r.dext)
    r.spill[...] = jnp.zeros_like(r.spill)

    @pl.when(me == spans - 1)
    def _():
        r.spill_in[...] = jnp.zeros_like(r.spill_in)

    def conv_steps(first_step, last_step, ranges, totals):
        def one(step, totals):
            at = tile(step)
            places = lax.broadcasted_iota(jnp.int32, (CHUNKS, 1), 0) * steps + step + me * rows
            first = start_of(places, starts)
            inside = [places - (CONV - 1) + k >= first for k in range(CONV)]
            out = []
            for lanes, sums in zip(ranges, totals):
                dconv = r.bgrad[at, lanes] * silu_slope(r.conv[at, lanes])
                new = []
                for k in range(CONV):
                    to = pl.ds(pl.multiple_of((step + k) * CHUNKS, CHUNKS), CHUNKS)
                    counted = jnp.where(inside[k], dconv, 0.0)
                    new.append(sums[k] + counted * r.ext[to, lanes])
                    r.dext[to, lanes] += taps[k : k + 1, lanes] * counted
                out.append(tuple(new) + (sums[CONV] + dconv,))
            return tuple(out)

        return lax.fori_loop(first_step, last_step, one, totals, unroll=2)

    quarter = width // 2
    halves = [
        [slice((2 * o + part) * width, (2 * o + part + 1) * width) for o in range(chips)]
        for part in range(2)
    ]
    zero = jnp.zeros((CHUNKS, width), F32)
    firsts = [
        conv_steps(0, CONV, ranges, tuple((zero,) * (CONV + 1) for _ in ranges))
        for ranges in halves
    ]
    for k in range(CONV - 1):
        r.spill[k : k + 1, :] = r.dext[k * CHUNKS : k * CHUNKS + 1, :]
    behind = lax.rem(me + spans - 1, spans)
    spill = copy(r.spill, r.spill_in, r.spill_sem, (), at_seq(behind))

    @pl.when(me > 0)
    def _():
        spill.start()

    chunk = lax.broadcasted_iota(jnp.int32, (CHUNKS, width), 0)
    dxin = []
    for part, ranges in enumerate(halves):
        totals = conv_steps(CONV, steps, ranges, firsts[part])
        if part:
            far_send(4)
            run(((outer_send, 2),))
        else:
            run(((outer_back, 1),))

            @pl.when(me > 0)
            def _():
                spill.wait_send()

            @pl.when(me < spans - 1)
            def _():
                spill.wait_recv()

        for o, lanes in enumerate(ranges):
            for k in range(CONV):
                r.small[TAPS + k : TAPS + k + 1, lanes] = jnp.sum(
                    totals[o][k], axis=0, keepdims=True
                )
            r.small[BIAS : BIAS + 1, lanes] = jnp.sum(totals[o][CONV], axis=0, keepdims=True)
            for k in range(CONV - 1):
                block = r.dext[k * CHUNKS : (k + 1) * CHUNKS, lanes]
                edge = (steps - CONV + 1 + k) * CHUNKS + EDGE
                moved = pltpu.roll(block, CHUNKS - 1, 0)
                came = jnp.broadcast_to(r.spill_in[k : k + 1, lanes], (CHUNKS, width))
                r.dext[edge : edge + CHUNKS, lanes] += jnp.where(
                    chunk < CHUNKS - 1, moved, came
                )
            piece = r.dext[EDGE:, lanes].astype(BF16)
            dxin.append(piece)
            grad = dot_tn(xn1, piece)
            for parity_at in range(2):
                put(4 + part, 2 * o + parity_at, grad[:, parity_at * quarter : (parity_at + 1) * quarter])
        near_send(4 + part)
    run(((inner_back, 0), (outer_back, 3),))
    wide = 2 * width
    dxn1 = jnp.zeros((rows, D), F32)
    for s in range(shards):
        if s < chips:
            piece = jnp.concatenate([dxin[s], dxin[chips + s]], axis=1)
        else:
            at = (s - chips) * wide
            piece = r.dzgate[:, at : at + wide]
        dxn1 = dxn1 + dot_nt(piece, r.wi_all[s])
    mixer_gain = jnp.sum(dxn1 * normal_one, axis=0, keepdims=True)
    for s in range(shards):
        at = s * width
        gains = slice(s * short, (s + 1) * short)
        r.small[GAINS : GAINS + 1, at : at + short] = mixer_gain[:, gains]
        r.small[GAINS : GAINS + 1, at + short : at + 2 * short] = attention_gain[:, gains]
    for s in range(shards):
        put(SMALL, s, r.small[:, s * width : (s + 1) * width])
    near_send(SMALL)
    far_send(5)
    far_send(SMALL)
    run(((inner_back, 1), (outer_back, 2),))
    part_send(4)
    e1 = dxn1 * gain_one
    dx = r.dx1[...] + inverse_one * (
        e1 - normal_one * jnp.mean(e1 * normal_one, axis=-1, keepdims=True)
    )
    r.dx1[...] = dx
    for part in range(D // LANES):
        lanes = slice(part * LANES, (part + 1) * LANES)
        for step in range(steps):
            r.row[pl.ds(step, CHUNKS, stride=steps), :] = r.dx1[
                step * CHUNKS : (step + 1) * CHUNKS, lanes
            ]
        r.token_grad[:, lanes] = r.row[...]
    part_send(5)
    part_send(SMALL)
    run(((inner_back, 3), (inner_back, 2),))
    last_send(4)
    last_send(5)
    last_send(SMALL)
    for k in (0, 1, 2, 3):
        finish(k)
    for by in range(1, spans):
        given_copy(by).wait()
    for t in range(blocks):
        i = t * ratio + sub
        by = lax.rem(i - me + spans, spans)

        @pl.when(i != me)
        def _():
            context_copy(t, by, i).wait_send()

    finish(SMALL)
    finish(4)
    finish(5)


def final_kernel(*refs):
    r = Refs(tuple(k + "_in" for k in BACKWARD_OUT) + FINAL_OUT, refs)

    def whole(source):
        return jnp.concatenate([source[j].astype(F32) for j in range(source.shape[0])], axis=0)

    r.output[...] = r.output_in[...]
    r.token_grad[...] = r.token_grad_in[...]
    r.heads_grad[...] = whole(r.last_heads_in)
    r.output_grad[...] = whole(r.last_out_in)
    r.merge_grad[...] = whole(r.last_merge_in)
    small = whole(r.last_small_in)
    short = r.mixer_grad.shape[1]
    width = r.taps_grad.shape[1]
    r.select_grad[...] = small[SEL : SEL + STEP]
    r.stepw_grad[...] = small[STEP : STEP + RANK]
    r.decay_grad[...] = small[DEC : DEC + STATE]
    r.taps_grad[...] = small[TAPS : TAPS + CONV]
    r.bias_grad[...] = small[BIAS : BIAS + 1]
    r.stepb_grad[...] = small[STEPB : STEPB + 1]
    r.skip_grad[...] = small[SKIP : SKIP + 1]
    r.mixer_grad[...] = small[GAINS : GAINS + 1, :short]
    r.attention_grad[...] = small[GAINS : GAINS + 1, short:]
    late = jnp.concatenate([whole(r.pair_in_in.at[at]) for at in range(2)], axis=1)
    early = jnp.concatenate(
        [whole(source.at[at]) for source in (r.early_in_in, r.other_in_in) for at in range(2)], axis=1
    )
    inner_half = lax.axis_index("shard") < lax.axis_size("shard") // 2
    r.input_grad[...] = jnp.where(inner_half, early, late)


def shape(*dims, kind=F32):
    return jax.ShapeDtypeStruct(dims, kind)


def vmem(*dims, kind=F32):
    return pltpu.VMEM(dims, kind)


def per_device(
    tokens,
    cotangent,
    positions,
    lengths,
    mixer_gain,
    input_weight,
    kernel_weight,
    kernel_bias,
    select_weight,
    step_weight,
    step_bias,
    decay_log,
    skip_scale,
    output_weight,
    attention_gain,
    heads_weight,
    merge_weight,
):
    spans = lax.axis_size("seq")
    shards = lax.axis_size("shard")
    rows = tokens.shape[1]
    steps = rows // CHUNKS
    share = rows // spans
    nseq = lengths.shape[1]
    ratio = spans // HEADS
    part = rows // ratio
    width = DI // shards

    index = positions
    dma = pltpu.SemaphoreType.DMA
    spread = [vmem(STATE, DI), vmem(STATE * CHUNKS, DI)]
    columns = vmem(rows, STATE * LANES)
    plane = vmem(rows, DI)
    gain_len = D // shards
    halves = GROUPS_CH // 2
    weights = [(D, 2 * width), (width, D), (D, 3 * D // shards), (gain_len, D)]
    half = rows // 2
    blocks = spans // ratio
    slots = 2 if ratio == 1 else 1
    kept = (
        [shape(rows, D)]
        + [shape(shards, *w, kind=BF16) for w in weights]
        + [
            shape(PACK, DI, kind=BF16),
            shape(CHUNKS, D),
            shape(spans, GROUPS_CH, LANES),
            shape(EDGE + rows, DI),
            shape(rows, DI),
            shape(rows, DI),
            shape(rows, DI, kind=BF16),
            shape(rows, DI),
            shape(rows, STEP),
            shape(CHUNKS, DI),
            shape(rows, DI),
            shape(rows, DI, kind=BF16),
            shape(rows, D),
            shape(STATE, CHUNKS, DI),
            shape(rows, D, kind=BF16),
            shape(rows, STATE * LANES),
            shape(rows, STATE * LANES),
            shape(rows, DI),
            shape(rows, DI),
            shape(blocks, half, LANES, kind=BF16),
        ]
    )
    back = [shape(HEADS, half, LANES, kind=BF16), shape(spans, rows, LANES, kind=BF16)]
    inputs = [
        lengths[0],
        tokens[0],
        cotangent[0].reshape(spans, share, D),
        index,
        mixer_gain[None],
        attention_gain[None],
        select_weight.T,
        step_weight,
        decay_log.T,
        kernel_weight,
        kernel_bias[None],
        step_bias[None],
        skip_scale[None],
        input_weight,
        output_weight,
        heads_weight,
        merge_weight,
    ]
    anyspace = pl.BlockSpec(memory_space=pl.ANY)
    outs = pl.pallas_call(
        functools.partial(forward_kernel, steps, nseq, shards, spans),
        out_shape=kept + back,
        in_specs=[SMEM] + [VMEM] * (len(inputs) - 5) + [anyspace] * 4,
        out_specs=[anyspace] * len(kept) + [VMEM] * len(back),
        scratch_shapes=[vmem(*k.shape, kind=k.dtype) for k in kept]
        + [
            vmem(spans, share, D, kind=BF16),
            vmem(spans, halves, STATE, 2 * LANES, kind=BF16),
            vmem(STATE, CHUNKS, DI),
            vmem(rows, LANES),
            vmem(PACK, width),
        ]
        + [vmem(*w, kind=BF16) for w in weights]
        + [
            vmem(PACK, width, kind=BF16),
            vmem(2 * CHUNKS, gain_len, kind=BF16),
            vmem(shards, PACK, width, kind=BF16),
            vmem(shards, 2 * CHUNKS, gain_len, kind=BF16),
            vmem(2 * CHUNKS, D, kind=BF16),
            vmem(halves, STATE, 2 * LANES, kind=BF16),
            vmem(GROUPS_CH, LANES),
        ]
        + spread
        + [
            vmem(HEADS, half, LANES, kind=BF16),
            vmem(HEADS, half, LANES, kind=BF16),
            vmem(HEADS, rows, LANES, kind=BF16),
            vmem(blocks, half, LANES, kind=BF16),
            vmem(blocks, half, LANES, kind=BF16),
            vmem(spans * rows, LANES, kind=BF16),
            vmem(spans, LANES, rows, kind=BF16),
            vmem(slots, spans, rows, rows),
            vmem(slots, spans, rows, rows),
            vmem(spans * rows, LANES),
            vmem(blocks, half, LANES, kind=BF16),
            vmem(spans, rows, LANES, kind=BF16),
            vmem(rows, rows),
            dma((2, 6, shards - 1)),
            dma((2, max(shards // 2 - 1, 1), spans)),
            dma((2, spans)),
            dma((2,)),
            dma((2, spans, halves)),
        ]
        + [dma((2, spans)), dma((2, spans, 2)), dma((2, spans)), dma((2, spans, 2))]
        + [dma((2, spans))] * 2
        + [dma((len(kept),))]
        + [vmem(*w) for w in weights]
        + [dma((4,))],
        compiler_params=params(collective_id=0, has_side_effects=True),
        name="forward",
    )(*inputs)
    saved, back = outs[: len(kept)], outs[len(kept) :]
    parts = {
        "heads": (D // spans, 3 * D // shards),
        "out": (width // spans, D),
        "merge": (gain_len // spans, D),
        "late": (D // spans, width),
        "early": (D // spans, width // 2),
        "other": (D // spans, width // 2),
        "small": (PACK // spans, width),
    }
    chips = shards // 2
    sizes = [(spans, *parts[k]) for k in GRADS]
    count = len(GRADS)
    summed = [
        shape(spans, share, D, kind=BF16),
        shape(rows, D),
        shape(spans, *parts["heads"], kind=BF16),
        shape(spans, *parts["out"], kind=BF16),
        shape(spans, *parts["merge"], kind=BF16),
        shape(spans, *parts["small"], kind=BF16),
        shape(2, spans, *parts["late"], kind=BF16),
        shape(2, spans, *parts["early"], kind=BF16),
        shape(2, spans, *parts["other"], kind=BF16),
    ]
    few = vmem(rows * STATE // 2, LANES)
    state = vmem(STATE, CHUNKS, DI)
    summed = pl.pallas_call(
        functools.partial(backward_kernel, steps, nseq, shards, spans),
        out_shape=summed,
        in_specs=[SMEM] + [VMEM] * 3 + [anyspace] * len(kept),
        out_specs=[VMEM] * len(summed),
        scratch_shapes=[vmem(*k.shape, kind=k.dtype) for k in kept]
        + [
            vmem(HEADS, half, LANES, kind=BF16),
            vmem(spans, share, D, kind=BF16),
            vmem(rows, D),
            plane,
            vmem(rows, DI, kind=BF16),
            state,
            vmem(halves, STATE, 2 * LANES, kind=BF16),
            vmem(spans, halves, STATE, 2 * LANES, kind=BF16),
            columns,
            columns,
            few,
            few,
            few,
            plane,
            plane,
            state,
            vmem(rows, STEP),
            vmem(EDGE + rows, DI),
            vmem(CHUNKS, DI),
            vmem(CHUNKS, DI),
            vmem(PACK, DI),
            vmem(rows, LANES),
        ]
        + spread
        + [
            vmem(*parts["late"], kind=BF16),
            vmem(*parts["early"], kind=BF16),
            vmem(*parts["other"], kind=BF16),
        ]
        + [vmem(shards, *k, kind=BF16) for k in sizes]
        + [vmem(chips, *k, kind=BF16) for k in sizes] * 2
        + [vmem(max(chips - 1, 1), *k, kind=BF16) for k in sizes]
        + [vmem(spans + OUTER - 1, *k[1:], kind=BF16) for k in sizes]
        + [
            dma((len(kept),)),
            dma((2, spans)),
            dma((2, spans)),
            dma((2, spans, halves)),
            dma((2,)),
            dma((2, count, chips)),
            dma((2, count, chips)),
            dma((2, count, spans)),
            dma((2, count, spans)),
            dma((2, 2, 2, spans)),
            dma((2, 4, 2, spans // OUTER)),
            dma((2, 4, 2, OUTER)),
            dma((2, 2, OUTER)),
            dma((2, 2, spans // OUTER)),
        ],
        compiler_params=params(collective_id=1, has_side_effects=True),
        name="backward",
    )(lengths[0], index, *back, *saved)
    results = pl.pallas_call(
        final_kernel,
        out_shape=[
            shape(rows, D, kind=BF16),
            shape(rows, D),
            shape(1, gain_len),
            shape(D, 2 * width),
            shape(CONV, width),
            shape(1, width),
            shape(STEP, width),
            shape(RANK, width),
            shape(1, width),
            shape(STATE, width),
            shape(1, width),
            shape(width, D),
            shape(1, gain_len),
            shape(D, 3 * D // shards),
            shape(gain_len, D),
        ],
        in_specs=[VMEM] * len(summed),
        out_specs=[VMEM] * len(FINAL_OUT),
        compiler_params=params(),
        name="final",
    )(summed[0].reshape(rows, D), *summed[1:])
    flat, turned = {2, 5, 8, 10, 12}, {6, 9}
    return tuple(
        v[None] if i < 2 else v.reshape(-1) if i in flat else v.T if i in turned else v
        for i, v in enumerate(results)
    )


def solution(mesh):
    return jax.shard_map(
        per_device,
        mesh=mesh,
        in_specs=(
            P("shard", "seq", None),
            P("shard", "seq", None),
            P("shard", None),
            P("shard", None),
            P("shard"),
            P(None, "shard"),
            P(None, "shard"),
            P("shard"),
            P("shard", None),
            P(None, "shard"),
            P("shard"),
            P("shard", None),
            P("shard"),
            P("shard", None),
            P("shard"),
            P(None, "shard"),
            P("shard", None),
        ),
        out_specs=(
            P("shard", "seq", None),
            P("shard", "seq", None),
            P("shard"),
            P(None, "shard"),
            P(None, "shard"),
            P("shard"),
            P("shard", None),
            P(None, "shard"),
            P("shard"),
            P("shard", None),
            P("shard"),
            P("shard", None),
            P("shard"),
            P(None, "shard"),
            P("shard", None),
        ),
        check_vma=False,
    )
```
